32 devices in a mesh: dp: 8 (over z, x), fsdp: 4 (over y, core).
Axes of the slice: x: 2, y: 2, z: 4, core: 2. Of those that a mesh axis runs over, the one named last changes fastest.
Arguments:
- hidden_in: float32 [32, 496, 768], P(('dp', 'fsdp')), may hold values from -6 to 6
- cotangent: float32 [32, 496, 768], P(('dp', 'fsdp')), may hold values from -6 to 6
- lengths: int32 [32], P(('dp', 'fsdp')), may hold values from 397 to 496, as said below
- qkv_weight: float32 [2, 768, 2304], P(None, ('dp', 'fsdp')), may hold values from -0.21875 to 0.21875
- out_weight: float32 [2, 768, 768], P(None, ('dp', 'fsdp')), may hold values from -6 to 6
- up_weight: float32 [2, 768, 3072], P(None, ('dp', 'fsdp')), may hold values from -0.21875 to 0.21875
- down_weight: float32 [2, 3072, 768], P(None, None, ('dp', 'fsdp')), may hold values from -0.109375 to 0.109375
- norm_gains: float32 [2, 2, 768], P(None, None, ('dp', 'fsdp')), may hold values from 0.5 to 1.5
- biases: float32 [2, 6, 768], P(None, None, ('dp', 'fsdp')), may hold values from -1.2 to 1.2
- up_bias: float32 [2, 3072], P(None, ('dp', 'fsdp')), may hold values from -1.2 to 1.2
Outputs:
- output: float32 [32, 496, 768], P(('dp', 'fsdp'))
- input_grad: float32 [32, 496, 768], P(('dp', 'fsdp'))
- qkv_grad: float32 [2, 768, 2304], P(None, ('dp', 'fsdp'))
- out_grad: float32 [2, 768, 768], P(None, ('dp', 'fsdp'))
- up_grad: float32 [2, 768, 3072], P(None, ('dp', 'fsdp'))
- down_grad: float32 [2, 3072, 768], P(None, None, ('dp', 'fsdp'))
- gains_grad: float32 [2, 2, 768], P(None, None, ('dp', 'fsdp'))
- biases_grad: float32 [2, 6, 768], P(None, None, ('dp', 'fsdp'))
- up_bias_grad: float32 [2, 3072], P(None, ('dp', 'fsdp'))
The draws below stay inside these ranges and needn't reach their ends.
Inputs may be any that keep to these rules, and one draw needn't show every extreme that they name: `lengths`: valid patches of each clip; some clip has exactly 496.
All inputs are finite; a program needn't handle non-finite values.
Results may differ from the reference program's by a relative error of at most 0.013.
Values may be sent and summed in bfloat16 or wider, within the bound.
No kernel may reach another device: no remote copies, remote signals or barrier semaphores. Data moves between devices by JAX's collectives and lax.ppermute only.
A program may use at most 320 MiB of HBM per device.

```python
import jax
import jax.numpy as jnp
from jax import lax

D = 768
FF = 3072
HEADS = 12
HEAD_WIDTH = 64
LAYERS = 2
L = 496
CLIPS = 32
SHORTEST = 397


def draw_lengths(key, part):
    first_key, second_key = jax.random.split(key)
    counts = jax.random.randint(first_key, (CLIPS,), SHORTEST, L + 1)
    position = jax.random.randint(second_key, (), 0, CLIPS)
    return counts.at[position].set(L).astype(jnp.int32)


def raised(entries, own_key, source, target, blocks, factor):
    def block_of(dim):
        return (jnp.arange(entries.shape[dim]) // (entries.shape[dim] // blocks)).reshape((-1,) + (1,) * (entries.ndim - 1 - dim))

    one_side = jax.random.permutation(own_key, blocks)[block_of(target)]
    far = (block_of(target) + blocks // 2) % blocks
    return jnp.where((block_of(source) == one_side) | (block_of(source) == far), factor * entries, entries)


def steps_of(rng, extent, cuts, least, top_value):
    def one(axis_at, blocks):
        draws = jax.random.uniform(jax.random.fold_in(jax.random.fold_in(rng, 6), axis_at), (blocks,), jnp.float32, least / len(cuts), top_value / len(cuts))
        return jnp.repeat(jnp.exp(draws), extent[axis_at] // blocks).reshape((-1,) + (1,) * (len(extent) - axis_at - 1))

    factor_of = one(*cuts[0])
    for cut in cuts[1:]:
        factor_of = factor_of * one(*cut)
    return factor_of


def gaussian(key, dims, scale, bound, shards=(), held_as=jnp.bfloat16):
    entries = jax.random.normal(key, dims, jnp.float32) * scale
    if len(shards) > 0:
        entries = steps_of(key, dims, shards, -0.22, 0.18) * entries
    return jnp.clip(entries, min=-bound, max=bound).astype(held_as)


def bell_draw_with(own_key, extent, deviation, bound, cuts, heavy, kind=jnp.bfloat16):
    values = deviation * jax.random.normal(own_key, extent, jnp.float32)
    if cuts:
        values = values * steps_of(own_key, extent, cuts, -0.22, 0.18)
    return jnp.clip(raised(values, jax.random.fold_in(own_key, 3), *heavy), -bound, bound).astype(kind)


def setup_inputs(seed: int = 0) -> dict:
    splits = jax.random.split(jax.random.key(seed), 11)
    return {
        "hidden_in": gaussian(splits[0], (CLIPS, L, D), 1.0, 6.0, ((0, 32),), jnp.float32),
        "cotangent": bell_draw_with(splits[1], (CLIPS, L, D), 1.0, 6.0, ((0, 32),), (0, 2, 32, 2.75), jnp.float32),
        "lengths": draw_lengths(jax.random.fold_in(splits[10], 71), 0),
        "qkv_weight": gaussian(splits[3], (LAYERS, D, 3 * D), D ** -0.5, 0.21875, ((1, 32),), jnp.float32),
        "out_weight": gaussian(splits[4], (LAYERS, D, D), (max(1, D // L)) ** -0.5, 6.0, ((1, 32),), jnp.float32),
        "up_weight": gaussian(splits[5], (LAYERS, D, FF), D ** -0.5, 0.21875, ((1, 32),), jnp.float32),
        "down_weight": gaussian(splits[6], (LAYERS, FF, D), FF ** -0.5, 0.109375, ((2, 32),), jnp.float32),
        "norm_gains": jnp.clip(1.0 + 0.1 * jax.random.normal(splits[7], (LAYERS, 2, D), jnp.float32), 0.5, 1.5),
        "biases": gaussian(splits[8], (LAYERS, 6, D), 0.2, 1.2, ((2, 32),), jnp.float32),
        "up_bias": gaussian(splits[9], (LAYERS, FF), 0.2, 1.2, ((1, 32),), jnp.float32),
    }


@jax.custom_vjp
def low(v):
    return lax.optimization_barrier(v.astype(jnp.bfloat16)).astype(jnp.float32)

@jax.custom_vjp
def low_back(v):
    return v

def low_keep(v):
    return (low(v), None)

def low_pass(kept, grad):
    return (grad,)

def back_keep(v):
    return (v, None)

def back_low(kept, grad):
    return (low(grad),)
low.defvjp(low_keep, low_pass)
low_back.defvjp(back_keep, back_low)
norm_eps = 1e-06
highest_precision = lax.Precision.HIGHEST

def layer_norm(values, gain, shift):
    center = values - lax.optimization_barrier(jnp.mean(values, axis=-1, keepdims=True))
    spread = lax.optimization_barrier(jnp.mean(center * center, axis=-1, keepdims=True))
    return center * lax.rsqrt(spread + norm_eps) * gain + shift

def matmul(left, right):
    return jnp.dot(left, right, precision=highest_precision, preferred_element_type=jnp.float32)

def attend_clip(inputs):
    query_matrix, key_matrix, value_matrix, keep = inputs
    attention_scores = low_back(jnp.einsum('qtx,jtx->tqj', query_matrix, key_matrix, precision=highest_precision) * HEAD_WIDTH ** (-0.5))
    masked = jnp.where(keep[None, None, :], attention_scores, -1e+30)
    attention_probabilities = low(jax.nn.softmax(masked, axis=-1))
    return jnp.einsum('ies,sin->ein', attention_probabilities, value_matrix, precision=highest_precision)

def block(residual, w_qkv, w_out, w_up, w_down, gains, shifts, up_shift, valid):
    normed = low(layer_norm(residual, gains[0], shifts[4]))
    qkv_bias = jnp.concatenate([shifts[0], jnp.zeros_like(shifts[0]), shifts[1]])
    qkv_rows = low(low_back(matmul(normed, w_qkv) + qkv_bias))
    parts = qkv_rows.reshape(CLIPS, L, 3, HEADS, HEAD_WIDTH)
    mixed = lax.map(jax.checkpoint(attend_clip), (parts[:, :, 0], parts[:, :, 1], parts[:, :, 2], valid))
    mixed_rows = low(low_back(mixed.reshape(CLIPS * L, D)))
    middle = residual + low_back(matmul(mixed_rows, w_out) + shifts[2])
    normed_two = low(layer_norm(middle, gains[1], shifts[5]))
    hidden_pre = low_back(matmul(normed_two, w_up) + up_shift)
    hidden = low(jax.nn.gelu(hidden_pre, approximate=False))
    return middle + low_back(matmul(hidden, w_down) + shifts[3])

def reference(hidden_in, cotangent, lengths, qkv_weight, out_weight, up_weight, down_weight, norm_gains, biases, up_bias):
    valid = jnp.arange(L, dtype=jnp.int32)[None, :] < lengths[:, None].astype(jnp.int32)

    def forward(start, w_qkv, w_out, w_up, w_down, gains, shifts, up_shift):
        residual = start.reshape(CLIPS * L, D)
        for layer_index in range(LAYERS):
            residual = block(residual, low(w_qkv[layer_index]), low(w_out[layer_index]), low(w_up[layer_index]), low(w_down[layer_index]), low(gains[layer_index]), low(shifts[layer_index]), low(up_shift[layer_index]), valid)
        return residual.reshape(CLIPS, L, D)
    result, pull = jax.vjp(forward, hidden_in, qkv_weight, out_weight, up_weight, down_weight, norm_gains, biases, up_bias)
    grads = pull(cotangent)
    return (result, grads[0], grads[1], grads[2], grads[3], grads[4], grads[5], grads[6], grads[7])
```

```python
import jax
import jax.numpy as jnp
from jax import lax
from jax.experimental import pallas as pl
from jax.experimental.pallas import tpu as pltpu
from jax.sharding import PartitionSpec as P

HEADS = 12
HEAD_WIDTH = 64
AXES = ("dp", "fsdp")
LANES = 128


norm_eps = 1e-06


def linear(z, x, y, c):
    return ((z * 2 + x) * 2 + y) * 2 + c


def pairs_of(step):
    result = []
    for z in range(4):
        for x in range(2):
            for y in range(2):
                for c in range(2):
                    result.append((linear(z, x, y, c), linear(*step(z, x, y, c))))
    return result


TO_CORE = pairs_of(lambda z, x, y, c: (z, x, y, 1 - c))
TO_RING = pairs_of(lambda z, x, y, c: ((z + 1) % 4, x, y, c))
TO_XY = pairs_of(lambda z, x, y, c: (z, x, 1 - y, c) if c else (z, 1 - x, y, c))
TO_YX = pairs_of(lambda z, x, y, c: (z, 1 - x, y, c) if c else (z, x, 1 - y, c))


def send(value, pairs):
    return lax.ppermute(value, AXES, pairs)


def place():
    dp = lax.axis_index("dp")
    fsdp = lax.axis_index("fsdp")
    return dp // 2, dp % 2, fsdp // 2, fsdp % 2


def blocked():
    return lax.axis_size("dp") == 8 and lax.axis_size("fsdp") == 4


def assemble(own, other, widths, rows):
    z, x, y, c = place()
    spots = jnp.stack([z, x, y, c]).astype(jnp.int32)
    halves = [width // 2 for width in widths]
    count = 32 * len(widths)

    def body(spot, own_ref, other_ref, *rest):
        outs, sems = rest[:-1], rest[-1]
        z, x, y, c = spot[0], spot[1], spot[2], spot[3]
        copies = []
        for side, ref in enumerate((own_ref, other_ref)):
            owner = c if side == 0 else 1 - c
            for block in range(16):
                bz, bx, by = block // 4, (block // 2) % 2, block % 2
                zr = lax.rem(z - bz + 4, 4)
                xr = lax.rem(x + bx, 2)
                yr = lax.rem(y + by, 2)
                first = jnp.where(owner == 0, yr, xr)
                second = jnp.where(owner == 0, xr, yr)
                start = pl.multiple_of(((first * 2 + second) * 4 + zr) * rows, 8)
                column = 0
                for half, out in zip(halves, outs):
                    target = pl.multiple_of(owner * half, LANES)
                    copies.append(
                        pltpu.make_async_copy(
                            ref.at[pl.ds(start, rows), pl.ds(column, half)],
                            out.at[pl.ds(block * rows, rows), pl.ds(target, half)],
                            sems.at[len(copies)],
                        )
                    )
                    column = column + half
        for copy in copies:
            copy.start()
        for copy in copies:
            copy.wait()

    return pl.pallas_call(
        body,
        out_shape=[jax.ShapeDtypeStruct((16 * rows, width), own.dtype) for width in widths],
        in_specs=[
            pl.BlockSpec(memory_space=pltpu.SMEM),
            pl.BlockSpec(memory_space=pl.ANY),
            pl.BlockSpec(memory_space=pl.ANY),
        ],
        out_specs=[pl.BlockSpec(memory_space=pl.ANY) for width in widths],
        scratch_shapes=[pltpu.SemaphoreType.DMA((count,))],
        cost_estimate=pl.CostEstimate(
            flops=0, bytes_accessed=4 * own.size * own.dtype.itemsize, transcendentals=0
        ),
    )(spots, own, other)


def gather_rows(pieces):
    if not blocked():
        return [lax.all_gather(piece, AXES, axis=0, tiled=True) for piece in pieces]
    z, x, y, c = place()
    widths = [piece.shape[1] for piece in pieces]
    low = jnp.concatenate([piece[:, : piece.shape[1] // 2] for piece in pieces], axis=1)
    high = jnp.concatenate([piece[:, piece.shape[1] // 2 :] for piece in pieces], axis=1)
    mine = jnp.where(c == 0, low, high)
    got = send(jnp.where(c == 0, high, low), TO_CORE)
    block = jnp.where(
        c == 0, jnp.concatenate([mine, got], axis=0), jnp.concatenate([got, mine], axis=0)
    )
    ring = [block]
    for step in range(3):
        ring.append(send(ring[-1], TO_RING))
    stack = jnp.concatenate(ring, axis=0)
    stack = jnp.concatenate([stack, send(stack, TO_XY)], axis=0)
    stack = jnp.concatenate([stack, send(stack, TO_YX)], axis=0)
    other = send(stack, TO_CORE)
    return assemble(stack, other, widths, block.shape[0])


def add_up(kept, got):
    return (kept.astype(jnp.float32) + got.astype(jnp.float32)).astype(jnp.bfloat16)


def scatter_rows(grads):
    if not blocked():
        return [
            lax.psum_scatter(
                grad.astype(jnp.bfloat16), AXES, scatter_dimension=0, tiled=True
            ).astype(jnp.float32)
            for grad in grads
        ]
    z, x, y, c = place()
    halves = [grad.shape[1] // 2 for grad in grads]
    low = jnp.concatenate([g[:, :half] for g, half in zip(grads, halves)], axis=1)
    high = jnp.concatenate([g[:, half:] for g, half in zip(grads, halves)], axis=1)
    low = low.astype(jnp.bfloat16)
    high = high.astype(jnp.bfloat16)
    width = low.shape[1]
    got = send(jnp.where(c == 0, high, low), TO_CORE)
    part = add_up(jnp.where(c == 0, low, high), got)
    rows = part.shape[0] // 16
    part = part.reshape(4, 2, 2, rows, width)

    def pick(block_x, block_y):
        along_y = lax.dynamic_index_in_dim(part, block_y, axis=2, keepdims=False)
        along_x = lax.dynamic_index_in_dim(part, block_x, axis=1, keepdims=False)
        return jnp.where(c == 0, along_y, along_x)

    got = send(pick(1 - x, 1 - y), TO_YX)
    part = add_up(pick(x, y), got)
    spot = jnp.where(c == 0, x, y)
    got = send(lax.dynamic_index_in_dim(part, 1 - spot, axis=1, keepdims=False), TO_XY)
    part = add_up(lax.dynamic_index_in_dim(part, spot, axis=1, keepdims=False), got)

    def block_at(step):
        return lax.dynamic_index_in_dim(part, (z + 3 - step) % 4, axis=0, keepdims=False)

    moving = block_at(0)
    for step in range(3):
        moving = add_up(block_at(step + 1), send(moving, TO_RING))
    half_rows = rows // 2
    kept = jnp.where(c == 0, moving[:half_rows], moving[half_rows:])
    got = send(jnp.where(c == 0, moving[half_rows:], moving[:half_rows]), TO_CORE)
    result = []
    start = 0
    for half in halves:
        a = kept[:, start : start + half]
        b = got[:, start : start + half]
        result.append(
            jnp.where(
                c == 0, jnp.concatenate([a, b], axis=1), jnp.concatenate([b, a], axis=1)
            ).astype(jnp.float32)
        )
        start = start + half
    return result


def layer_norm(values, gain, shift):
    center = values - jnp.mean(values, axis=-1, keepdims=True)
    spread = jnp.mean(center * center, axis=-1, keepdims=True)
    return center * lax.rsqrt(spread + norm_eps) * gain + shift


def gelu_exact(values):
    return jax.nn.gelu(values, approximate=False)


def pack_small(gains, shifts, up_bias):
    rows = gains.shape[1]
    packed = jnp.concatenate([gains.T, shifts.T, up_bias.reshape(rows, -1)], axis=1)
    packed = jnp.pad(packed, ((0, 0), (0, LANES - packed.shape[1])))
    return jnp.concatenate([packed, packed], axis=1)


def unpack_small(packed):
    rows = packed.shape[0]
    return packed[:, :2].T, packed[:, 2:8].T, packed[:, 8:12].reshape(4 * rows)


def split_heads(qkv_rows, clips, slots):
    parts = qkv_rows.reshape(clips, slots, 3, HEADS, HEAD_WIDTH)
    return (parts[:, :, 0], parts[:, :, 1], parts[:, :, 2])


def masked_scores(query_matrix, key_matrix, valid):
    attention_scores = jnp.einsum(
        "clhd,cmhd->chlm", query_matrix, key_matrix, preferred_element_type=jnp.float32
    ) * HEAD_WIDTH ** (-0.5)
    return jnp.where(valid[:, None, None, :], attention_scores, -1e30)


def forward_layer(residual, matrices, valid, clips, slots):
    w_qkv, w_out, w_up, w_down_t, gains_low, up_low, shifts_low = matrices
    gains = gains_low.astype(jnp.float32)
    shifts = shifts_low.astype(jnp.float32)
    normed = layer_norm(residual, gains[0], shifts[4]).astype(jnp.bfloat16)
    qkv_bias = jnp.concatenate([shifts[0], jnp.zeros_like(shifts[0]), shifts[1]])
    qkv_rows = (jnp.dot(normed, w_qkv, preferred_element_type=jnp.float32) + qkv_bias).astype(
        jnp.bfloat16
    )
    query_matrix, key_matrix, value_matrix = split_heads(qkv_rows, clips, slots)
    masked = masked_scores(query_matrix, key_matrix, valid)
    peak = jnp.max(masked, axis=-1, keepdims=True)
    expo = jnp.exp(masked - peak)
    total = jnp.sum(expo, axis=-1, keepdims=True)
    attention_probabilities = (expo / total).astype(jnp.bfloat16)
    log_total = peak + jnp.log(total)
    mixed = jnp.einsum(
        "chlm,cmhd->clhd", attention_probabilities, value_matrix, preferred_element_type=jnp.float32
    )
    mixed = mixed.reshape(clips * slots, residual.shape[1]).astype(jnp.bfloat16)
    middle = residual + (jnp.dot(mixed, w_out, preferred_element_type=jnp.float32) + shifts[2])
    normed_two = layer_norm(middle, gains[1], shifts[5]).astype(jnp.bfloat16)
    hidden_pre = jnp.dot(normed_two, w_up, preferred_element_type=jnp.float32) + up_low.astype(
        jnp.float32
    )
    hidden = gelu_exact(hidden_pre).astype(jnp.bfloat16)
    result = middle + (jnp.einsum("tf,df->td", hidden, w_down_t, preferred_element_type=jnp.float32) + shifts[3])
    return (
        result,
        (residual, normed, qkv_rows, log_total, mixed, middle, normed_two, hidden_pre, hidden),
    )


def backward_layer(grad_result, matrices, record, valid, clips, slots):
    w_qkv, w_out, w_up, w_down_t, gains_low, up_low, shifts_low = matrices
    gains = gains_low.astype(jnp.float32)
    shifts = shifts_low.astype(jnp.float32)
    residual, normed, qkv_rows, log_total, mixed, middle, normed_two, hidden_pre, hidden = record
    width = residual.shape[1]
    down_low = grad_result.astype(jnp.bfloat16)
    grad_down = jnp.einsum("td,tf->df", down_low, hidden, preferred_element_type=jnp.float32)
    grad_down_bias = jnp.sum(down_low, axis=0, dtype=jnp.float32)
    grad_hidden = jnp.dot(down_low, w_down_t, preferred_element_type=jnp.float32)
    unused, gelu_pull = jax.vjp(gelu_exact, hidden_pre)
    grad_pre = gelu_pull(grad_hidden)[0].astype(jnp.bfloat16)
    grad_up = jnp.einsum("td,tf->df", normed_two, grad_pre, preferred_element_type=jnp.float32)
    grad_up_bias = jnp.sum(grad_pre, axis=0, dtype=jnp.float32)
    grad_normed_two = jnp.einsum("tf,df->td", grad_pre, w_up, preferred_element_type=jnp.float32)
    unused_two, norm_pull_two = jax.vjp(layer_norm, middle, gains[1], shifts[5])
    grad_mid_part, grad_gain_two, grad_shift_two = norm_pull_two(grad_normed_two)
    grad_middle = grad_result + grad_mid_part
    branch_low = grad_middle.astype(jnp.bfloat16)
    grad_out_weight = jnp.einsum("te,td->ed", mixed, branch_low, preferred_element_type=jnp.float32)
    grad_out_bias = jnp.sum(branch_low, axis=0, dtype=jnp.float32)
    grad_mixed = jnp.einsum(
        "td,ed->te", branch_low, w_out, preferred_element_type=jnp.float32
    ).astype(jnp.bfloat16)
    query_matrix, key_matrix, value_matrix = split_heads(qkv_rows, clips, slots)
    masked = masked_scores(query_matrix, key_matrix, valid)
    attention_probabilities = jnp.exp(masked - log_total)
    grad_heads = grad_mixed.reshape(clips, slots, HEADS, HEAD_WIDTH)
    grad_probs = jnp.einsum(
        "clhd,cmhd->chlm", grad_heads, value_matrix, preferred_element_type=jnp.float32
    )
    grad_values = jnp.einsum(
        "chlm,clhd->cmhd",
        attention_probabilities.astype(jnp.bfloat16),
        grad_heads,
        preferred_element_type=jnp.float32,
    )
    row_terms = jnp.sum(attention_probabilities * grad_probs, axis=-1, keepdims=True)
    grad_scores = (attention_probabilities * (grad_probs - row_terms)).astype(jnp.bfloat16)
    grad_queries = jnp.einsum(
        "chlm,cmhd->clhd", grad_scores, key_matrix, preferred_element_type=jnp.float32
    ) * HEAD_WIDTH ** (-0.5)
    grad_keys = jnp.einsum(
        "chlm,clhd->cmhd", grad_scores, query_matrix, preferred_element_type=jnp.float32
    ) * HEAD_WIDTH ** (-0.5)
    grad_qkv_rows = (
        jnp.stack([grad_queries, grad_keys, grad_values], axis=2)
        .reshape(clips * slots, 3 * width)
        .astype(jnp.bfloat16)
    )
    grad_qkv = jnp.einsum("td,te->de", normed, grad_qkv_rows, preferred_element_type=jnp.float32)
    grad_query_bias = jnp.sum(grad_qkv_rows[:, :width], axis=0, dtype=jnp.float32)
    grad_value_bias = jnp.sum(grad_qkv_rows[:, 2 * width :], axis=0, dtype=jnp.float32)
    grad_normed = jnp.einsum("te,de->td", grad_qkv_rows, w_qkv, preferred_element_type=jnp.float32)
    unused_one, norm_pull_one = jax.vjp(layer_norm, residual, gains[0], shifts[4])
    grad_res_part, grad_gain_one, grad_shift_one = norm_pull_one(grad_normed)
    grad_input = grad_middle + grad_res_part
    grad_gains = jnp.stack([grad_gain_one, grad_gain_two])
    grad_shifts = jnp.stack(
        [
            grad_query_bias,
            grad_value_bias,
            grad_out_bias,
            grad_down_bias,
            grad_shift_one,
            grad_shift_two,
        ]
    )
    return (
        grad_input,
        (grad_qkv, grad_out_weight, grad_up, grad_down, grad_gains, grad_up_bias, grad_shifts),
    )


def local(
    hidden_in,
    cotangent,
    lengths,
    qkv_weight,
    out_weight,
    up_weight,
    down_weight,
    norm_gains,
    biases,
    up_bias,
):
    clips, slots, width = hidden_in.shape
    layers = qkv_weight.shape[0]
    valid = lax.broadcasted_iota(jnp.int32, (clips, slots), 1) < lengths[:, None]
    low = jnp.bfloat16
    small = [
        pack_small(norm_gains[i], biases[i], up_bias[i]).astype(low) for i in range(layers)
    ]
    down_t = jnp.swapaxes(down_weight, 1, 2).astype(low)
    matrices = []
    for i in range(layers):
        qkv, packed = gather_rows([qkv_weight[i].astype(low), small[i]])
        out, up = gather_rows([out_weight[i].astype(low), up_weight[i].astype(low)])
        (down,) = gather_rows([down_t[i]])
        gains, shifts, up_shift = unpack_small(packed)
        matrices.append((qkv, out, up, down, gains, up_shift, shifts))

    residual = hidden_in.reshape(clips * slots, width)
    records = []
    for i in range(layers):
        residual, record = forward_layer(residual, matrices[i], valid, clips, slots)
        records.append(record)
    result = residual.reshape(clips, slots, width)
    grad_rows = cotangent.reshape(clips * slots, width)
    owned = [None] * layers
    for i in reversed(range(layers)):
        grad_rows, terms = backward_layer(
            grad_rows, matrices[i], records[i], valid, clips, slots
        )
        grad_qkv, grad_out, grad_up, grad_down, grad_gains, grad_up_bias, grad_shifts = terms
        (own_down,) = scatter_rows([grad_down])
        own_out, own_up = scatter_rows([grad_out, grad_up])
        grad_small = pack_small(grad_gains, grad_shifts, grad_up_bias)
        own_qkv, own_small = scatter_rows([grad_qkv, grad_small])
        gains, shifts, up_shift = unpack_small(own_small)
        owned[i] = (own_qkv, own_out, own_up, own_down.T, gains, shifts, up_shift)

    def stacked(member):
        return jnp.stack([owned[i][member] for i in range(layers)])

    return (
        result,
        grad_rows.reshape(clips, slots, width),
        stacked(0),
        stacked(1),
        stacked(2),
        stacked(3),
        stacked(4),
        stacked(5),
        stacked(6),
    )


def solution(mesh):
    return jax.shard_map(
        local,
        mesh=mesh,
        in_specs=(
            P(("dp", "fsdp"), None, None),
            P(("dp", "fsdp"), None, None),
            P(("dp", "fsdp")),
            P(None, ("dp", "fsdp"), None),
            P(None, ("dp", "fsdp"), None),
            P(None, ("dp", "fsdp"), None),
            P(None, None, ("dp", "fsdp")),
            P(None, None, ("dp", "fsdp")),
            P(None, None, ("dp", "fsdp")),
            P(None, ("dp", "fsdp")),
        ),
        out_specs=(
            P(("dp", "fsdp"), None, None),
            P(("dp", "fsdp"), None, None),
            P(None, ("dp", "fsdp"), None),
            P(None, ("dp", "fsdp"), None),
            P(None, ("dp", "fsdp"), None),
            P(None, None, ("dp", "fsdp")),
            P(None, None, ("dp", "fsdp")),
            P(None, None, ("dp", "fsdp")),
            P(None, ("dp", "fsdp")),
        ),
        check_vma=False,
    )
```

```python
import jax
import jax.numpy as jnp
from jax import lax
from jax.experimental import pallas as pl
from jax.experimental.pallas import tpu as pltpu
from jax.sharding import PartitionSpec as P

HEADS = 12
HEAD_WIDTH = 64
LANES = 128
PAIRS = HEADS * HEAD_WIDTH // LANES
LOW = jnp.bfloat16
WIDE = jnp.float32
norm_eps = 1e-06
AXES = ("dp", "fsdp")
VMEM_LIMIT = 60 * 1024 * 1024


def cost(flops, moved, hard=0):
    return pl.CostEstimate(flops=int(flops), bytes_accessed=int(moved), transcendentals=int(hard))


def params():
    return pltpu.CompilerParams(vmem_limit_bytes=VMEM_LIMIT)


def vmem_specs(count):
    return [pl.BlockSpec(memory_space=pltpu.VMEM)] * count


def any_specs(count):
    return [pl.BlockSpec(memory_space=pl.ANY)] * count


def dot(a, b):
    return jnp.dot(a, b, preferred_element_type=WIDE)


def dot_nt(a, b):
    return lax.dot_general(a, b, (((1,), (1,)), ((), ())), preferred_element_type=WIDE)


def dot_tn(a, b):
    return lax.dot_general(a, b, (((0,), (0,)), ((), ())), preferred_element_type=WIDE)


def piece_copies(spot, own_ref, other_ref, target, sems, column, half):
    z, x, y, c = spot[0], spot[1], spot[2], spot[3]
    rows = own_ref.shape[0] // 16
    copies = []
    for side, ref in enumerate((own_ref, other_ref)):
        owner = c if side == 0 else 1 - c
        to = pl.multiple_of(owner * half, LANES)
        for block in range(16):
            bz, bx, by = block // 4, (block // 2) % 2, block % 2
            zr = lax.rem(z - bz + 4, 4)
            xr = lax.rem(x + bx, 2)
            yr = lax.rem(y + by, 2)
            first = jnp.where(owner == 0, yr, xr)
            second = jnp.where(owner == 0, xr, yr)
            start = pl.multiple_of(((first * 2 + second) * 4 + zr) * rows, 8)
            copies.append(
                pltpu.make_async_copy(
                    ref.at[pl.ds(start, rows), pl.ds(column, half)],
                    target.at[pl.ds(block * rows, rows), pl.ds(to, half)],
                    sems.at[len(copies)],
                )
            )
    return copies


def norm_rows(v):
    center = v - jnp.mean(v, axis=-1, keepdims=True)
    r = lax.rsqrt(jnp.mean(center * center, axis=-1, keepdims=True) + norm_eps)
    return center * r, r


def norm_back(v, gain, d):
    xh, r = norm_rows(v)
    dg = d * gain
    m1 = jnp.mean(dg, axis=-1, keepdims=True)
    m2 = jnp.mean(dg * xh, axis=-1, keepdims=True)
    return (
        r * (dg - m1 - xh * m2),
        jnp.sum(d * xh, axis=0, keepdims=True),
        jnp.sum(d, axis=0, keepdims=True),
    )


GAIN1, GAIN2, BQ, BV, BO, BD, SH1, SH2 = range(8)


def qkv_forward(spot, own, other, column, h, table):
    rows, width = h.shape
    wide = 3 * width
    tile = 256

    def body(spot_ref, own_ref, other_ref, h_ref, t_ref, qkv_ref, a_ref, w_ref, sems):
        copies = piece_copies(spot_ref, own_ref, other_ref, w_ref, sems, column, wide // 2)
        for copy in copies:
            copy.start()
        xh, r = norm_rows(h_ref[...])
        a_ref[...] = (xh * t_ref[GAIN1 : GAIN1 + 1, :] + t_ref[SH1 : SH1 + 1, :]).astype(LOW)
        for copy in copies:
            copy.wait()
        a = a_ref[...]
        for n in range(wide // tile):
            s = n * tile
            out = dot(a, w_ref[:, s : s + tile])
            if s < width:
                out = out + t_ref[BQ : BQ + 1, s : s + tile]
            elif s >= 2 * width:
                out = out + t_ref[BV : BV + 1, s - 2 * width : s - 2 * width + tile]
            qkv_ref[:, s : s + tile] = out.astype(LOW)

    return pl.pallas_call(
        body,
        out_shape=[
            jax.ShapeDtypeStruct((rows, wide), LOW),
            jax.ShapeDtypeStruct((rows, width), LOW),
        ],
        in_specs=[pl.BlockSpec(memory_space=pltpu.SMEM)] + any_specs(2) + vmem_specs(2),
        out_specs=vmem_specs(2),
        scratch_shapes=[pltpu.VMEM((width, wide), LOW), pltpu.SemaphoreType.DMA((32,))],
        compiler_params=params(),
        cost_estimate=cost(2 * rows * width * wide, 2 * width * wide + 9 * rows * width),
        name="qkv_forward",
    )(spot, own, other, h, table)


def attention_forward(lengths, qkv):
    rows, wide = qkv.shape
    width = wide // 3

    def body(len_ref, q_ref, k_ref, v_ref, o_ref, lse_ref):
        pair = pl.program_id(0)
        lane = lax.broadcasted_iota(jnp.int32, (1, LANES), 1)
        key = lax.broadcasted_iota(jnp.int32, (1, rows), 1)
        shut = jnp.where(key < len_ref[0], 0.0, -1e30)
        q = q_ref[...] * jnp.asarray(HEAD_WIDTH**-0.5, LOW)
        k = k_ref[...]
        v = v_ref[...]
        outs = []
        stats = jnp.where(pair == 0, jnp.zeros((rows, LANES), WIDE), lse_ref[...])
        for side in range(2):
            inside = (lane >= HEAD_WIDTH) == (side == 1)
            qs = jnp.where(inside, q, jnp.zeros_like(q))
            s = dot_nt(qs, k) + shut
            peak = jnp.max(s, axis=1, keepdims=True)
            e = jnp.exp(s - peak)
            total = jnp.sum(e, axis=1, keepdims=True)
            p = (e * (1.0 / total)).astype(LOW)
            outs.append(dot(p, v))
            stats = jnp.where(lane == pair * 2 + side, peak + jnp.log(total), stats)
        lse_ref[...] = stats
        o_ref[...] = jnp.where(lane < HEAD_WIDTH, outs[0], outs[1]).astype(LOW)

    return pl.pallas_call(
        body,
        out_shape=[
            jax.ShapeDtypeStruct((rows, width), LOW),
            jax.ShapeDtypeStruct((rows, LANES), WIDE),
        ],
        grid_spec=pltpu.PrefetchScalarGridSpec(
            num_scalar_prefetch=1,
            grid=(PAIRS,),
            in_specs=[
                pl.BlockSpec((rows, LANES), lambda p, n: (0, p)),
                pl.BlockSpec((rows, LANES), lambda p, n: (0, p + PAIRS)),
                pl.BlockSpec((rows, LANES), lambda p, n: (0, p + 2 * PAIRS)),
            ],
            out_specs=[
                pl.BlockSpec((rows, LANES), lambda p, n: (0, p)),
                pl.BlockSpec((rows, LANES), lambda p, n: (0, 0)),
            ],
        ),
        compiler_params=params(),
        cost_estimate=cost(16 * rows * rows * width, 8 * rows * width, HEADS * rows * rows),
        name="attention_forward",
    )(lengths, qkv, qkv, qkv)


def out_forward(spot, own, other, column, h, mixed, table):
    rows, width = h.shape

    def body(spot_ref, own_ref, other_ref, h_ref, m_ref, t_ref, h2_ref, a_ref, w_ref, sems):
        copies = piece_copies(spot_ref, own_ref, other_ref, w_ref, sems, column, width // 2)
        for copy in copies:
            copy.start()
        for copy in copies:
            copy.wait()
        h2 = h_ref[...] + (dot(m_ref[...], w_ref[...]) + t_ref[BO : BO + 1, :])
        h2_ref[...] = h2
        xh, r = norm_rows(h2)
        a_ref[...] = (xh * t_ref[GAIN2 : GAIN2 + 1, :] + t_ref[SH2 : SH2 + 1, :]).astype(LOW)

    return pl.pallas_call(
        body,
        out_shape=[
            jax.ShapeDtypeStruct((rows, width), WIDE),
            jax.ShapeDtypeStruct((rows, width), LOW),
        ],
        in_specs=[pl.BlockSpec(memory_space=pltpu.SMEM)] + any_specs(2) + vmem_specs(3),
        out_specs=vmem_specs(2),
        scratch_shapes=[pltpu.VMEM((width, width), LOW), pltpu.SemaphoreType.DMA((32,))],
        compiler_params=params(),
        cost_estimate=cost(2 * rows * width * width, 2 * width * width + 12 * rows * width),
        name="out_forward",
    )(spot, own, other, h, mixed, table)


def gelu_parts(u):
    cdf = 0.5 * (1.0 + lax.erf(u * (0.5**0.5)))
    pdf = jnp.exp(-0.5 * u * u) * (0.3989422804014327)
    return cdf, pdf


def mlp_forward(spot, up, down, h2, a2, up_bias, table):
    rows, width = h2.shape
    hidden = up_bias.shape[1]
    tile = 512
    (up_own, up_other, up_col), (down_own, down_other, down_col) = up, down

    def body(
        spot_ref, uo_ref, up_ref, do_ref, dp_ref, h_ref, a_ref, b_ref, t_ref,
        z_ref, g_ref, o_ref, wu_ref, wd_ref, sems_u, sems_d,
    ):
        ups = piece_copies(spot_ref, uo_ref, up_ref, wu_ref, sems_u, up_col, hidden // 2)
        downs = piece_copies(spot_ref, do_ref, dp_ref, wd_ref, sems_d, down_col, hidden // 2)
        for copy in ups + downs:
            copy.start()
        o_ref[...] = h_ref[...] + t_ref[BD : BD + 1, :]
        for copy in ups + downs:
            copy.wait()

        def step(n, carry):
            at = pl.ds(pl.multiple_of(n * tile, tile), tile)
            u = dot(a_ref[...], wu_ref[:, at]) + b_ref[:, at]
            cdf, pdf = gelu_parts(u)
            z = (u * cdf).astype(LOW)
            z_ref[:, at] = z
            g_ref[:, at] = (cdf + u * pdf).astype(LOW)
            o_ref[...] += dot_nt(z, wd_ref[:, at])
            return carry

        lax.fori_loop(0, hidden // tile, step, 0)

    return pl.pallas_call(
        body,
        out_shape=[
            jax.ShapeDtypeStruct((rows, hidden), LOW),
            jax.ShapeDtypeStruct((rows, hidden), LOW),
            jax.ShapeDtypeStruct((rows, width), WIDE),
        ],
        in_specs=[pl.BlockSpec(memory_space=pltpu.SMEM)] + any_specs(4) + vmem_specs(4),
        out_specs=vmem_specs(3),
        scratch_shapes=[
            pltpu.VMEM((width, hidden), LOW),
            pltpu.VMEM((width, hidden), LOW),
            pltpu.SemaphoreType.DMA((32,)),
            pltpu.SemaphoreType.DMA((32,)),
        ],
        compiler_params=params(),
        cost_estimate=cost(
            4 * rows * width * hidden, 4 * width * hidden + 4 * rows * hidden, 2 * rows * hidden
        ),
        name="mlp_forward",
    )(spot, up_own, up_other, down_own, down_other, h2, a2, up_bias, table)


def block_starts(spot, owner, rows):
    z, x, y = spot[0], spot[1], spot[2]
    result = []
    for block in range(16):
        bz, bx, by = block // 4, (block // 2) % 2, block % 2
        zr = lax.rem(z - bz + 4, 4)
        xr = lax.rem(x + bx, 2)
        yr = lax.rem(y + by, 2)
        first = jnp.where(owner == 0, yr, xr)
        second = jnp.where(owner == 0, xr, yr)
        result.append(pl.multiple_of(((first * 2 + second) * 4 + zr) * rows, 16))
    return result


def put_blocks(value, out_ref, starts, column, width):
    rows = value.shape[0] // 16
    low = value.astype(LOW)
    for block, start in enumerate(starts):
        out_ref[pl.ds(start, rows), pl.ds(column, width)] = low[block * rows : (block + 1) * rows]


def column_sum(value):
    return jnp.sum(value.astype(WIDE), axis=0, keepdims=True)


def down_backward(spot, down, e, z, slope):
    rows, width = e.shape
    hidden = z.shape[1]
    half = hidden // 2
    tile = 512
    own, other, column = down

    def body(
        spot_ref, own_ref, other_ref, e_ref, z_ref, s_ref,
        du_ref, mine_ref, rest_ref, bd_ref, bu_ref, w_ref, em_ref, emt_ref, sems,
    ):
        copies = piece_copies(spot_ref, own_ref, other_ref, w_ref, sems, column, half)
        for copy in copies:
            copy.start()
        em = e_ref[...].astype(LOW)
        em_ref[...] = em
        bd_ref[...] = column_sum(em)
        emt_ref[...] = em.T
        for copy in copies:
            copy.wait()
        c = spot_ref[3]
        for owner, out_ref in ((c, mine_ref), (1 - c, rest_ref)):
            starts = block_starts(spot_ref, owner, width // 16)

            def step(n, carry):
                at = pl.ds(pl.multiple_of(owner * half + n * tile, LANES), tile)
                dz = dot(em_ref[...], w_ref[:, at])
                du = (dz * s_ref[:, at].astype(WIDE)).astype(LOW)
                du_ref[:, at] = du
                bu_ref[:, at] = column_sum(du)
                grad = dot(emt_ref[...], z_ref[:, at])
                put_blocks(grad, out_ref, starts, pl.multiple_of(n * tile, LANES), tile)
                return carry

            lax.fori_loop(0, half // tile, step, 0)

    return pl.pallas_call(
        body,
        out_shape=[
            jax.ShapeDtypeStruct((rows, hidden), LOW),
            jax.ShapeDtypeStruct((width, half), LOW),
            jax.ShapeDtypeStruct((width, half), LOW),
            jax.ShapeDtypeStruct((1, width), WIDE),
            jax.ShapeDtypeStruct((1, hidden), WIDE),
        ],
        in_specs=[pl.BlockSpec(memory_space=pltpu.SMEM)] + any_specs(2) + vmem_specs(3),
        out_specs=vmem_specs(5),
        scratch_shapes=[
            pltpu.VMEM((width, hidden), LOW),
            pltpu.VMEM((rows, width), LOW),
            pltpu.VMEM((width, rows), LOW),
            pltpu.SemaphoreType.DMA((32,)),
        ],
        compiler_params=params(),
        cost_estimate=cost(4 * rows * width * hidden, 4 * width * hidden + 6 * rows * hidden),
        name="down_backward",
    )(spot, own, other, e, z, slope)


def up_backward(spot, up, out, e, h2, a2, mixed, du, table):
    rows, width = e.shape
    hidden = du.shape[1]
    half = hidden // 2
    tile = 512
    (up_own, up_other, up_col), (out_own, out_other, out_col) = up, out

    def body(
        spot_ref, uo_ref, up_ref, oo_ref, op_ref, e_ref, h_ref, a_ref, m_ref, du_ref, t_ref,
        e2_ref, da_ref, mine_ref, rest_ref, omine_ref, orest_ref, sums_ref,
        wu_ref, wo_ref, at_ref, mt_ref, ey_ref, acc_ref, sems_u, sems_o,
    ):
        ups = piece_copies(spot_ref, uo_ref, up_ref, wu_ref, sems_u, up_col, half)
        outs = piece_copies(spot_ref, oo_ref, op_ref, wo_ref, sems_o, out_col, width // 2)
        for copy in ups + outs:
            copy.start()
        at_ref[...] = a_ref[...].T
        mt_ref[...] = m_ref[...].T
        acc_ref[...] = jnp.zeros_like(acc_ref)
        for copy in ups:
            copy.wait()
        c = spot_ref[3]
        for owner, out_ref in ((c, mine_ref), (1 - c, rest_ref)):
            starts = block_starts(spot_ref, owner, width // 16)

            def step(n, carry):
                at = pl.ds(pl.multiple_of(owner * half + n * tile, LANES), tile)
                d = du_ref[:, at]
                put_blocks(
                    dot(at_ref[...], d), out_ref, starts, pl.multiple_of(n * tile, LANES), tile
                )
                acc_ref[...] += dot_nt(d, wu_ref[:, at])
                return carry

            lax.fori_loop(0, half // tile, step, 0)
        dv, gain, shift = norm_back(h_ref[...], t_ref[GAIN2 : GAIN2 + 1, :], acc_ref[...])
        e2 = e_ref[...] + dv
        e2_ref[...] = e2
        ey = e2.astype(LOW)
        ey_ref[...] = ey
        sums_ref[0:1, :] = gain
        sums_ref[1:2, :] = shift
        sums_ref[2:3, :] = column_sum(ey)
        for copy in outs:
            copy.wait()
        da_ref[...] = dot_nt(ey, wo_ref[...]).astype(LOW)
        for owner, out_ref in ((c, omine_ref), (1 - c, orest_ref)):
            starts = block_starts(spot_ref, owner, width // 16)
            at = pl.ds(pl.multiple_of(owner * (width // 2), LANES), width // 2)
            put_blocks(dot(mt_ref[...], ey_ref[:, at]), out_ref, starts, 0, width // 2)

    return pl.pallas_call(
        body,
        out_shape=[
            jax.ShapeDtypeStruct((rows, width), WIDE),
            jax.ShapeDtypeStruct((rows, width), LOW),
            jax.ShapeDtypeStruct((width, half), LOW),
            jax.ShapeDtypeStruct((width, half), LOW),
            jax.ShapeDtypeStruct((width, width // 2), LOW),
            jax.ShapeDtypeStruct((width, width // 2), LOW),
            jax.ShapeDtypeStruct((8, width), WIDE),
        ],
        in_specs=[pl.BlockSpec(memory_space=pltpu.SMEM)] + any_specs(4) + vmem_specs(6),
        out_specs=vmem_specs(7),
        scratch_shapes=[
            pltpu.VMEM((width, hidden), LOW),
            pltpu.VMEM((width, width), LOW),
            pltpu.VMEM((width, rows), LOW),
            pltpu.VMEM((width, rows), LOW),
            pltpu.VMEM((rows, width), LOW),
            pltpu.VMEM((rows, width), WIDE),
            pltpu.SemaphoreType.DMA((32,)),
            pltpu.SemaphoreType.DMA((32,)),
        ],
        compiler_params=params(),
        cost_estimate=cost(
            4 * rows * width * (hidden + width), 4 * width * (hidden + width) + 2 * rows * hidden
        ),
        name="up_backward",
    )(spot, up_own, up_other, out_own, out_other, e, h2, a2, mixed, du, table)


def attention_backward(lengths, qkv, da, mixed, lse):
    rows, wide = qkv.shape
    width = wide // 3

    def body(len_ref, q_ref, k_ref, v_ref, d_ref, m_ref, lse_ref, out_ref, row_ref):
        pair = pl.program_id(0)

        @pl.when(pair == 0)
        def start():
            row_ref[...] = lse_ref[...].T

        lane = lax.broadcasted_iota(jnp.int32, (1, LANES), 1)
        sub = lax.broadcasted_iota(jnp.int32, (LANES, 1), 0)
        key = lax.broadcasted_iota(jnp.int32, (rows, 1), 0)
        shut = jnp.where(key < len_ref[0], 0.0, -1e30)
        scale = jnp.asarray(HEAD_WIDTH**-0.5, LOW)
        q = q_ref[...] * scale
        k = k_ref[...]
        v = v_ref[...]
        d = d_ref[...]
        kt = k.T * scale
        prod = (d.astype(WIDE) * m_ref[...].astype(WIDE)).T
        dks, dvs = [], []
        dqt = jnp.zeros((LANES, rows), WIDE)
        for side in range(2):
            inside = (lane >= HEAD_WIDTH) == (side == 1)
            down = (sub >= HEAD_WIDTH) == (side == 1)
            ks = jnp.where(inside, k, jnp.zeros_like(k))
            vs = jnp.where(inside, v, jnp.zeros_like(v))
            kts = jnp.where(down, kt, jnp.zeros_like(kt))
            first = side * HEAD_WIDTH
            delta = jnp.sum(prod[first : first + HEAD_WIDTH], axis=0, keepdims=True)
            log_total = row_ref[pl.ds(pair * 2 + side, 1), :]
            p = jnp.exp((dot_nt(ks, q) + shut) - log_total)
            dp = dot_nt(vs, d)
            dvs.append(dot(p.astype(LOW), d))
            ds = (p * (dp - delta)).astype(LOW)
            dks.append(dot(ds, q))
            dqt = dqt + dot(kts, ds)
        dq = dqt.T
        dk = jnp.where(lane < HEAD_WIDTH, dks[0], dks[1])
        dv = jnp.where(lane < HEAD_WIDTH, dvs[0], dvs[1])
        for n, value in enumerate((dq, dk, dv)):
            at = pl.ds(pl.multiple_of(n * width + pair * LANES, LANES), LANES)
            out_ref[:, at] = value.astype(LOW)

    return pl.pallas_call(
        body,
        out_shape=jax.ShapeDtypeStruct((rows, wide), LOW),
        grid_spec=pltpu.PrefetchScalarGridSpec(
            num_scalar_prefetch=1,
            grid=(PAIRS,),
            in_specs=[
                pl.BlockSpec((rows, LANES), lambda p, n: (0, p)),
                pl.BlockSpec((rows, LANES), lambda p, n: (0, p + PAIRS)),
                pl.BlockSpec((rows, LANES), lambda p, n: (0, p + 2 * PAIRS)),
                pl.BlockSpec((rows, LANES), lambda p, n: (0, p)),
                pl.BlockSpec((rows, LANES), lambda p, n: (0, p)),
                pl.BlockSpec((rows, LANES), lambda p, n: (0, 0)),
            ],
            out_specs=pl.BlockSpec((rows, wide), lambda p, n: (0, 0)),
            scratch_shapes=[pltpu.VMEM((LANES, rows), WIDE)],
        ),
        compiler_params=params(),
        cost_estimate=cost(40 * rows * rows * width, 16 * rows * width, HEADS * rows * rows),
        name="attention_backward",
    )(lengths, qkv, qkv, qkv, da, mixed, lse)


def qkv_backward(spot, own, other, column, dqkv, e2, h, a1, table):
    rows, wide = dqkv.shape
    width = wide // 3
    half = wide // 2
    tile = 384

    def body(
        spot_ref, own_ref, other_ref, d_ref, e_ref, h_ref, a_ref, t_ref,
        o_ref, mine_ref, rest_ref, sums_ref, w_ref, at_ref, acc_ref, sems,
    ):
        copies = piece_copies(spot_ref, own_ref, other_ref, w_ref, sems, column, half)
        for copy in copies:
            copy.start()
        at_ref[...] = a_ref[...].T
        acc_ref[...] = jnp.zeros_like(acc_ref)
        for copy in copies:
            copy.wait()
        c = spot_ref[3]
        for owner, out_ref in ((c, mine_ref), (1 - c, rest_ref)):
            starts = block_starts(spot_ref, owner, width // 16)

            def step(n, carry):
                at = pl.ds(pl.multiple_of(owner * half + n * tile, LANES), tile)
                d = d_ref[:, at]
                put_blocks(
                    dot(at_ref[...], d), out_ref, starts, pl.multiple_of(n * tile, LANES), tile
                )
                acc_ref[...] += dot_nt(d, w_ref[:, at])
                return carry

            lax.fori_loop(0, half // tile, step, 0)
        dv, gain, shift = norm_back(h_ref[...], t_ref[GAIN1 : GAIN1 + 1, :], acc_ref[...])
        o_ref[...] = e_ref[...] + dv
        sums_ref[0:1, :] = gain
        sums_ref[1:2, :] = shift
        sums_ref[2:3, :] = column_sum(d_ref[:, :width])
        sums_ref[3:4, :] = column_sum(d_ref[:, 2 * width :])

    return pl.pallas_call(
        body,
        out_shape=[
            jax.ShapeDtypeStruct((rows, width), WIDE),
            jax.ShapeDtypeStruct((width, half), LOW),
            jax.ShapeDtypeStruct((width, half), LOW),
            jax.ShapeDtypeStruct((8, width), WIDE),
        ],
        in_specs=[pl.BlockSpec(memory_space=pltpu.SMEM)] + any_specs(2) + vmem_specs(5),
        out_specs=vmem_specs(4),
        scratch_shapes=[
            pltpu.VMEM((width, wide), LOW),
            pltpu.VMEM((width, rows), LOW),
            pltpu.VMEM((rows, width), WIDE),
            pltpu.SemaphoreType.DMA((32,)),
        ],
        compiler_params=params(),
        cost_estimate=cost(4 * rows * width * wide, 4 * width * wide + 16 * rows * width),
        name="qkv_backward",
    )(spot, own, other, dqkv, e2, h, a1, table)


def small_forward(spot, own, column, hidden):
    width = own.shape[0]

    def body(spot_ref, own_ref, t_ref, b_ref, w_ref, sems):
        rows = width // 16
        starts = block_starts(spot_ref, spot_ref[3], rows)
        copies = [
            pltpu.make_async_copy(
                own_ref.at[pl.ds(start, rows), pl.ds(column, LANES)],
                w_ref.at[pl.ds(block * rows, rows), :],
                sems.at[block],
            )
            for block, start in enumerate(starts)
        ]
        for copy in copies:
            copy.start()
        for copy in copies:
            copy.wait()
        values = w_ref[...].astype(WIDE)
        t_ref[...] = values.T[0:8, :]
        share = hidden // 32
        for device in range(32):
            at = device * (width // 32)
            b_ref[0:1, device * share : (device + 1) * share] = values[
                at : at + 1, LANES - share :
            ]

    return pl.pallas_call(
        body,
        out_shape=[
            jax.ShapeDtypeStruct((8, width), WIDE),
            jax.ShapeDtypeStruct((1, hidden), WIDE),
        ],
        in_specs=[pl.BlockSpec(memory_space=pltpu.SMEM)] + any_specs(1),
        out_specs=vmem_specs(2),
        scratch_shapes=[pltpu.VMEM((width, LANES), LOW), pltpu.SemaphoreType.DMA((16,))],
        compiler_params=params(),
        cost_estimate=cost(0, 4 * width * LANES),
        name="small_forward",
    )(spot, own)


def small_backward(spot, first, second, down_sum, up_sum):
    width = first.shape[1]
    hidden = up_sum.shape[1]

    def body(spot_ref, f_ref, s_ref, d_ref, u_ref, mine_ref, rest_ref, w_ref, p_ref):
        w_ref[...] = jnp.zeros_like(w_ref)
        for row, value in (
            (GAIN1, s_ref[0:1, :]),
            (GAIN2, f_ref[0:1, :]),
            (BQ, s_ref[2:3, :]),
            (BV, s_ref[3:4, :]),
            (BO, f_ref[2:3, :]),
            (BD, d_ref[...]),
            (SH1, s_ref[1:2, :]),
            (SH2, f_ref[1:2, :]),
        ):
            w_ref[row : row + 1, :] = value
        p_ref[...] = w_ref[...].T
        share = hidden // 32
        for device in range(32):
            at = device * (width // 32)
            p_ref[at : at + 1, LANES - share :] = u_ref[
                0:1, device * share : (device + 1) * share
            ]
        packed = p_ref[...]
        c = spot_ref[3]
        for owner, out_ref in ((c, mine_ref), (1 - c, rest_ref)):
            put_blocks(packed, out_ref, block_starts(spot_ref, owner, width // 16), 0, LANES)

    return pl.pallas_call(
        body,
        out_shape=[jax.ShapeDtypeStruct((width, LANES), LOW)] * 2,
        in_specs=[pl.BlockSpec(memory_space=pltpu.SMEM)] + vmem_specs(4),
        out_specs=vmem_specs(2),
        scratch_shapes=[pltpu.VMEM((LANES, width), WIDE), pltpu.VMEM((width, LANES), WIDE)],
        compiler_params=params(),
        cost_estimate=cost(0, 8 * width * LANES),
        name="small_backward",
    )(spot, first, second, down_sum, up_sum)


def linear(z, x, y, c):
    return ((z * 2 + x) * 2 + y) * 2 + c


def pairs_of(step):
    result = []
    for z in range(4):
        for x in range(2):
            for y in range(2):
                for c in range(2):
                    result.append((linear(z, x, y, c), linear(*step(z, x, y, c))))
    return result


TO_CORE = pairs_of(lambda z, x, y, c: (z, x, y, 1 - c))
TO_RING = pairs_of(lambda z, x, y, c: ((z + 1) % 4, x, y, c))
TO_XY = pairs_of(lambda z, x, y, c: (z, x, 1 - y, c) if c else (z, 1 - x, y, c))
TO_YX = pairs_of(lambda z, x, y, c: (z, 1 - x, y, c) if c else (z, x, 1 - y, c))


def send(value, pairs):
    return lax.ppermute(value, AXES, pairs)


def blocked():
    return lax.axis_size("dp") == 8 and lax.axis_size("fsdp") == 4


def place():
    if not blocked():
        return jnp.zeros((4,), jnp.int32)
    dp = lax.axis_index("dp")
    fsdp = lax.axis_index("fsdp")
    return jnp.stack([dp // 2, dp % 2, fsdp // 2, fsdp % 2]).astype(jnp.int32)


def halves(pieces):
    low = [piece[:, : piece.shape[1] // 2] for piece in pieces]
    high = [piece[:, piece.shape[1] // 2 :] for piece in pieces]
    return jnp.concatenate(low, axis=1), jnp.concatenate(high, axis=1)


def gather_rows(spot, pieces):
    offsets = [0]
    for piece in pieces:
        offsets.append(offsets[-1] + piece.shape[1] // 2)
    if not blocked():
        whole = [lax.all_gather(piece, AXES, axis=0, tiled=True) for piece in pieces]
        low, high = [
            part.reshape(4, 2, 2, -1, part.shape[1])[jnp.array([0, 3, 2, 1])]
            for part in halves(whole)
        ]
        width = low.shape[-1]
        own = low.transpose(2, 1, 0, 3, 4).reshape(-1, width)
        other = high.transpose(1, 2, 0, 3, 4).reshape(-1, width)
        return own, other, offsets
    c = spot[3]
    low, high = halves(pieces)
    mine = jnp.where(c == 0, low, high)
    got = send(jnp.where(c == 0, high, low), TO_CORE)
    block = jnp.where(
        c == 0, jnp.concatenate([mine, got], axis=0), jnp.concatenate([got, mine], axis=0)
    )
    ring = [block]
    for step in range(3):
        ring.append(send(ring[-1], TO_RING))
    stack = jnp.concatenate(ring, axis=0)
    stack = jnp.concatenate([stack, send(stack, TO_XY)], axis=0)
    stack = jnp.concatenate([stack, send(stack, TO_YX)], axis=0)
    return stack, send(stack, TO_CORE), offsets


def added(parts):
    total = parts[0].astype(WIDE)
    for part in parts[1:]:
        total = total + part.astype(WIDE)
    return total


def scatter_rows(spot, mines, rests):
    if not blocked():
        result = []
        for mine, rest in zip(mines, rests):
            rows, half = mine.shape[0] // 16, mine.shape[1]
            low = mine.reshape(2, 2, 4, rows, half).transpose(2, 1, 0, 3, 4)
            high = rest.reshape(2, 2, 4, rows, half).transpose(2, 0, 1, 3, 4)
            whole = jnp.concatenate([low, high], axis=-1)[jnp.array([0, 3, 2, 1])]
            whole = whole.reshape(16 * rows, 2 * half)
            result.append(
                lax.psum_scatter(whole, AXES, scatter_dimension=0, tiled=True).astype(WIDE)
            )
        return result
    c = spot[3]
    height = mines[0].shape[0]
    a = height // 2
    b = height // 4
    rows = height // 16
    gots = [send(rest, TO_CORE) for rest in rests]

    def part(start, stop):
        return jnp.concatenate(
            [added([mine[start:stop], got[start:stop]]) for mine, got in zip(mines, gots)], axis=1
        )

    got_a = send(part(a, 2 * a).astype(LOW), TO_YX)
    got_b = send(added([part(b, 2 * b), got_a[b : 2 * b]]).astype(LOW), TO_XY)

    def block_at(step):
        at = slice(step * rows, (step + 1) * rows)
        return added([part(at.start, at.stop), got_a[at], got_b[at]])

    moving = block_at(1)
    for step in (2, 3, 0):
        moving = added([block_at(step), send(moving.astype(LOW), TO_RING)])
    low, high = moving[: rows // 2], moving[rows // 2 :]
    kept = jnp.where(c == 0, low, high)
    got = send(jnp.where(c == 0, high, low).astype(LOW), TO_CORE).astype(WIDE)
    result = []
    start = 0
    for mine in mines:
        half = mine.shape[1]
        ours = kept[:, start : start + half]
        theirs = got[:, start : start + half]
        result.append(
            jnp.where(
                c == 0,
                jnp.concatenate([ours, theirs], axis=1),
                jnp.concatenate([theirs, ours], axis=1),
            )
        )
        start = start + half
    return result


def pack_small(gains, shifts, up_bias):
    rows = gains.shape[1]
    columns = jnp.concatenate([gains, shifts], axis=0).T
    share = up_bias.shape[0]
    first = jnp.pad(columns, ((0, 0), (0, LANES - share - columns.shape[1])))
    second = jnp.pad(up_bias[None, :], ((0, rows - 1), (0, 0)))
    packed = jnp.concatenate([first, second], axis=1)
    return jnp.concatenate([packed, packed], axis=1)


def unpack_small(packed, share):
    return packed[:, 0:2].T, packed[:, 2:8].T, packed[0, LANES - share : LANES]


def whole_small(gains, shifts, up_bias):
    both = jnp.concatenate([gains, shifts], axis=0)
    table = lax.all_gather(both, AXES, axis=1, tiled=True)
    return table.astype(WIDE), lax.all_gather(up_bias, AXES, axis=0, tiled=True)[None].astype(WIDE)


def spread_small(first, second, down_sum, up_sum):
    table = jnp.concatenate(
        [
            second[0:1],
            first[0:1],
            second[2:4],
            first[2:3],
            down_sum,
            second[1:2],
            first[1:2],
        ],
        axis=0,
    )
    own = lax.psum_scatter(table, AXES, scatter_dimension=1, tiled=True)
    return own[0:2], own[2:8], lax.psum_scatter(up_sum[0], AXES, scatter_dimension=0, tiled=True)


def local(
    hidden_in,
    cotangent,
    lengths,
    qkv_weight,
    out_weight,
    up_weight,
    down_weight,
    norm_gains,
    biases,
    up_bias,
):
    clips, slots, width = hidden_in.shape
    layers = qkv_weight.shape[0]
    share = up_bias.shape[1]
    hidden = down_weight.shape[1]
    assert clips == 1
    spot = place()
    down_t = jnp.swapaxes(down_weight, 1, 2).astype(LOW)
    weights = []
    for i in range(layers):
        gains, shifts, bias = (v[i].astype(LOW) for v in (norm_gains, biases, up_bias))
        pieces = [qkv_weight[i].astype(LOW)]
        if blocked():
            pieces.append(pack_small(gains, shifts, bias))
        own, other, at = gather_rows(spot, pieces)
        qkv = (own, other, at[0])
        if blocked():
            table, bias = small_forward(spot, own, at[1], hidden)
        else:
            table, bias = whole_small(gains, shifts, bias)
        own, other, at = gather_rows(spot, [out_weight[i].astype(LOW), up_weight[i].astype(LOW)])
        out, up = (own, other, at[0]), (own, other, at[1])
        own, other, at = gather_rows(spot, [down_t[i]])
        weights.append((qkv, out, up, (own, other, at[0]), table, bias))

    h = hidden_in[0]
    records = []
    for i in range(layers):
        qkv_w, out_w, up_w, down_w, table, bias = weights[i]
        qkv, a1 = qkv_forward(spot, *qkv_w, h, table)
        mixed, lse = attention_forward(lengths, qkv)
        h2, a2 = out_forward(spot, *out_w, h, mixed, table)
        z, slope, result = mlp_forward(spot, up_w, down_w, h2, a2, bias, table)
        records.append((h, a1, qkv, mixed, lse, h2, a2, z, slope))
        h = result
    output = h[None]
    e = cotangent[0]
    owned = [None] * layers
    for i in reversed(range(layers)):
        qkv_w, out_w, up_w, down_w, table, bias = weights[i]
        h, a1, qkv, mixed, lse, h2, a2, z, slope = records[i]
        du, mine, rest, down_sum, up_sum = down_backward(spot, down_w, e, z, slope)
        (own_down,) = scatter_rows(spot, [mine], [rest])
        e2, da, mine, rest, out_mine, out_rest, first = up_backward(
            spot, up_w, out_w, e, h2, a2, mixed, du, table
        )
        own_out, own_up = scatter_rows(spot, [out_mine, mine], [out_rest, rest])
        dqkv = attention_backward(lengths, qkv, da, mixed, lse)
        e, mine, rest, second = qkv_backward(spot, *qkv_w, dqkv, e2, h, a1, table)
        if blocked():
            small_mine, small_rest = small_backward(spot, first, second, down_sum, up_sum)
            own_qkv, packed = scatter_rows(spot, [mine, small_mine], [rest, small_rest])
            small = unpack_small(packed, share)
        else:
            (own_qkv,) = scatter_rows(spot, [mine], [rest])
            small = spread_small(first, second, down_sum, up_sum)
        owned[i] = (own_qkv, own_out, own_up, own_down.T, *small)

    stacked = [jnp.stack([owned[i][n] for i in range(layers)]) for n in range(7)]
    return (output, e[None], *stacked)


def solution(mesh):
    return jax.shard_map(
        local,
        mesh=mesh,
        in_specs=(
            P(("dp", "fsdp"), None, None),
            P(("dp", "fsdp"), None, None),
            P(("dp", "fsdp")),
            P(None, ("dp", "fsdp"), None),
            P(None, ("dp", "fsdp"), None),
            P(None, ("dp", "fsdp"), None),
            P(None, None, ("dp", "fsdp")),
            P(None, None, ("dp", "fsdp")),
            P(None, None, ("dp", "fsdp")),
            P(None, ("dp", "fsdp")),
        ),
        out_specs=(
            P(("dp", "fsdp"), None, None),
            P(("dp", "fsdp"), None, None),
            P(None, ("dp", "fsdp"), None),
            P(None, ("dp", "fsdp"), None),
            P(None, ("dp", "fsdp"), None),
            P(None, None, ("dp", "fsdp")),
            P(None, None, ("dp", "fsdp")),
            P(None, None, ("dp", "fsdp")),
            P(None, ("dp", "fsdp")),
        ),
        check_vma=False,
    )
```

```python
import jax
import jax.numpy as jnp
from jax import lax
from jax.experimental import pallas as pl
from jax.experimental.pallas import tpu as pltpu
from jax.sharding import PartitionSpec as P

HEADS = 12
HEAD_WIDTH = 64
LANES = 128
PAIRS = HEADS * HEAD_WIDTH // LANES
LOW = jnp.bfloat16
WIDE = jnp.float32
norm_eps = 1e-06
AXES = ("dp", "fsdp")
VMEM_LIMIT = 60 * 1024 * 1024


def cost(flops, moved, hard=0):
    return pl.CostEstimate(flops=int(flops), bytes_accessed=int(moved), transcendentals=int(hard))


def params():
    return pltpu.CompilerParams(vmem_limit_bytes=VMEM_LIMIT)


def vmem_specs(count):
    return [pl.BlockSpec(memory_space=pltpu.VMEM)] * count


def any_specs(count):
    return [pl.BlockSpec(memory_space=pl.ANY)] * count


def dot(a, b):
    return jnp.dot(a, b, preferred_element_type=WIDE)


def dot_nt(a, b):
    return lax.dot_general(a, b, (((1,), (1,)), ((), ())), preferred_element_type=WIDE)


def dot_tn(a, b):
    return lax.dot_general(a, b, (((0,), (0,)), ((), ())), preferred_element_type=WIDE)


def piece_copies(spot, own_ref, other_ref, target, sems, column, half):
    z, x, y, c = spot[0], spot[1], spot[2], spot[3]
    rows = own_ref.shape[0] // 16
    copies = []
    for side, ref in enumerate((own_ref, other_ref)):
        owner = c if side == 0 else 1 - c
        to = pl.multiple_of(owner * half, LANES)
        for block in range(16):
            bz, bx, by = block // 4, (block // 2) % 2, block % 2
            zr = lax.rem(z - bz + 4, 4)
            xr = lax.rem(x + bx, 2)
            yr = lax.rem(y + by, 2)
            first = jnp.where(owner == 0, yr, xr)
            second = jnp.where(owner == 0, xr, yr)
            start = pl.multiple_of(((first * 2 + second) * 4 + zr) * rows, 8)
            copies.append(
                pltpu.make_async_copy(
                    ref.at[pl.ds(start, rows), pl.ds(column, half)],
                    target.at[pl.ds(block * rows, rows), pl.ds(to, half)],
                    sems.at[len(copies)],
                )
            )
    return copies


def norm_rows(v):
    center = v - jnp.mean(v, axis=-1, keepdims=True)
    r = lax.rsqrt(jnp.mean(center * center, axis=-1, keepdims=True) + norm_eps)
    return center * r, r


def norm_back(v, gain, d):
    xh, r = norm_rows(v)
    dg = d * gain
    m1 = jnp.mean(dg, axis=-1, keepdims=True)
    m2 = jnp.mean(dg * xh, axis=-1, keepdims=True)
    return (
        r * (dg - m1 - xh * m2),
        jnp.sum(d * xh, axis=0, keepdims=True),
        jnp.sum(d, axis=0, keepdims=True),
    )


GAIN1, GAIN2, BQ, BV, BO, BD, SH1, SH2 = range(8)


def qkv_forward(spot, own, other, column, h, table):
    rows, width = h.shape
    wide = 3 * width
    tile = 256

    def body(spot_ref, own_ref, other_ref, h_ref, t_ref, qkv_ref, a_ref, w_ref, sems):
        copies = piece_copies(spot_ref, own_ref, other_ref, w_ref, sems, column, wide // 2)
        for copy in copies:
            copy.start()
        xh, r = norm_rows(h_ref[...])
        a_ref[...] = (xh * t_ref[GAIN1 : GAIN1 + 1, :] + t_ref[SH1 : SH1 + 1, :]).astype(LOW)
        for copy in copies:
            copy.wait()
        a = a_ref[...]
        for n in range(wide // tile):
            s = n * tile
            out = dot(a, w_ref[:, s : s + tile])
            if s < width:
                out = out + t_ref[BQ : BQ + 1, s : s + tile]
            elif s >= 2 * width:
                out = out + t_ref[BV : BV + 1, s - 2 * width : s - 2 * width + tile]
            qkv_ref[:, s : s + tile] = out.astype(LOW)

    return pl.pallas_call(
        body,
        out_shape=[
            jax.ShapeDtypeStruct((rows, wide), LOW),
            jax.ShapeDtypeStruct((rows, width), LOW),
        ],
        in_specs=[pl.BlockSpec(memory_space=pltpu.SMEM)] + any_specs(2) + vmem_specs(2),
        out_specs=vmem_specs(2),
        scratch_shapes=[pltpu.VMEM((width, wide), LOW), pltpu.SemaphoreType.DMA((32,))],
        compiler_params=params(),
        cost_estimate=cost(2 * rows * width * wide, 2 * width * wide + 9 * rows * width),
        name="qkv_forward",
    )(spot, own, other, h, table)


def attention_forward(lengths, qkv, begin, pairs):
    rows, wide = qkv.shape
    width = pairs * LANES

    def body(len_ref, q_ref, k_ref, v_ref, o_ref, lse_ref):
        pair = pl.program_id(0)
        lane = lax.broadcasted_iota(jnp.int32, (1, LANES), 1)
        key = lax.broadcasted_iota(jnp.int32, (1, rows), 1)
        shut = jnp.where(key < len_ref[0], 0.0, -1e30)
        q = q_ref[...] * jnp.asarray(HEAD_WIDTH**-0.5, LOW)
        k = k_ref[...]
        v = v_ref[...]
        outs = []
        stats = jnp.where(pair == 0, jnp.zeros((rows, LANES), WIDE), lse_ref[...])
        for side in range(2):
            inside = (lane >= HEAD_WIDTH) == (side == 1)
            qs = jnp.where(inside, q, jnp.zeros_like(q))
            s = dot_nt(qs, k) + shut
            peak = jnp.max(s, axis=1, keepdims=True)
            e = jnp.exp(s - peak)
            total = jnp.sum(e, axis=1, keepdims=True)
            p = (e * (1.0 / total)).astype(LOW)
            outs.append(dot(p, v))
            stats = jnp.where(lane == pair * 2 + side, peak + jnp.log(total), stats)
        lse_ref[...] = stats
        o_ref[...] = jnp.where(lane < HEAD_WIDTH, outs[0], outs[1]).astype(LOW)

    return pl.pallas_call(
        body,
        out_shape=[
            jax.ShapeDtypeStruct((rows, width), LOW),
            jax.ShapeDtypeStruct((rows, LANES), WIDE),
        ],
        grid_spec=pltpu.PrefetchScalarGridSpec(
            num_scalar_prefetch=1,
            grid=(pairs,),
            in_specs=[
                pl.BlockSpec((rows, LANES), lambda p, n: (0, p + begin)),
                pl.BlockSpec((rows, LANES), lambda p, n: (0, p + begin + PAIRS)),
                pl.BlockSpec((rows, LANES), lambda p, n: (0, p + begin + 2 * PAIRS)),
            ],
            out_specs=[
                pl.BlockSpec((rows, LANES), lambda p, n: (0, p)),
                pl.BlockSpec((rows, LANES), lambda p, n: (0, 0)),
            ],
        ),
        compiler_params=params(),
        cost_estimate=cost(16 * rows * rows * width, 8 * rows * width, 2 * pairs * rows * rows),
        name="attention_forward",
    )(lengths, qkv, qkv, qkv)


def out_forward(spot, own, other, column, h, mixed, table):
    rows, width = h.shape
    part = width // 2

    def body(
        spot_ref, own_ref, other_ref, h_ref, m0_ref, m1_ref, t_ref, h2_ref, a_ref, w_ref, sems
    ):
        copies = piece_copies(spot_ref, own_ref, other_ref, w_ref, sems, column, width // 2)
        for copy in copies:
            copy.start()
        for copy in copies:
            copy.wait()
        product = dot(m0_ref[...], w_ref[:part, :]) + dot(m1_ref[...], w_ref[part:, :])
        h2 = h_ref[...] + (product + t_ref[BO : BO + 1, :])
        h2_ref[...] = h2
        xh, r = norm_rows(h2)
        a_ref[...] = (xh * t_ref[GAIN2 : GAIN2 + 1, :] + t_ref[SH2 : SH2 + 1, :]).astype(LOW)

    return pl.pallas_call(
        body,
        out_shape=[
            jax.ShapeDtypeStruct((rows, width), WIDE),
            jax.ShapeDtypeStruct((rows, width), LOW),
        ],
        in_specs=[pl.BlockSpec(memory_space=pltpu.SMEM)] + any_specs(2) + vmem_specs(4),
        out_specs=vmem_specs(2),
        scratch_shapes=[pltpu.VMEM((width, width), LOW), pltpu.SemaphoreType.DMA((32,))],
        compiler_params=params(),
        cost_estimate=cost(2 * rows * width * width, 2 * width * width + 12 * rows * width),
        name="out_forward",
    )(spot, own, other, h, *mixed, table)


def gelu_parts(u):
    cdf = 0.5 * (1.0 + lax.erf(u * (0.5**0.5)))
    pdf = jnp.exp(-0.5 * u * u) * (0.3989422804014327)
    return cdf, pdf


def mlp_forward(spot, up, down, base, a2, up_bias, table, first):
    rows, width = base.shape
    hidden = up_bias.shape[1]
    tile = 512
    (up_own, up_other, up_col), (down_own, down_other, down_col) = up, down

    def body(
        spot_ref, uo_ref, up_ref, do_ref, dp_ref, h_ref, a_ref, b_ref, t_ref,
        z_ref, g_ref, o_ref, wu_ref, wd_ref, sems_u, sems_d,
    ):
        ups = piece_copies(spot_ref, uo_ref, up_ref, wu_ref, sems_u, up_col, hidden // 2)
        downs = piece_copies(spot_ref, do_ref, dp_ref, wd_ref, sems_d, down_col, hidden // 2)
        for copy in ups + downs:
            copy.start()
        if first:
            o_ref[...] = h_ref[...] + t_ref[BD : BD + 1, :]
        else:
            o_ref[...] = h_ref[...]
        for copy in ups + downs:
            copy.wait()

        def step(n, carry):
            at = pl.ds(pl.multiple_of(n * tile, tile), tile)
            u = dot(a_ref[...], wu_ref[:, at]) + b_ref[:, at]
            cdf, pdf = gelu_parts(u)
            z = (u * cdf).astype(LOW)
            z_ref[:, at] = z
            g_ref[:, at] = (cdf + u * pdf).astype(LOW)
            o_ref[...] += dot_nt(z, wd_ref[:, at])
            return carry

        lax.fori_loop(0, hidden // tile, step, 0)

    return pl.pallas_call(
        body,
        out_shape=[
            jax.ShapeDtypeStruct((rows, hidden), LOW),
            jax.ShapeDtypeStruct((rows, hidden), LOW),
            jax.ShapeDtypeStruct((rows, width), WIDE),
        ],
        in_specs=[pl.BlockSpec(memory_space=pltpu.SMEM)] + any_specs(4) + vmem_specs(4),
        out_specs=vmem_specs(3),
        scratch_shapes=[
            pltpu.VMEM((width, hidden), LOW),
            pltpu.VMEM((width, hidden), LOW),
            pltpu.SemaphoreType.DMA((32,)),
            pltpu.SemaphoreType.DMA((32,)),
        ],
        compiler_params=params(),
        cost_estimate=cost(
            4 * rows * width * hidden, 4 * width * hidden + 4 * rows * hidden, 2 * rows * hidden
        ),
        name="mlp_forward",
    )(spot, up_own, up_other, down_own, down_other, base, a2, up_bias, table)


def block_starts(spot, owner, rows):
    z, x, y = spot[0], spot[1], spot[2]
    result = []
    for block in range(16):
        bz, bx, by = block // 4, (block // 2) % 2, block % 2
        zr = lax.rem(z - bz + 4, 4)
        xr = lax.rem(x + bx, 2)
        yr = lax.rem(y + by, 2)
        first = jnp.where(owner == 0, yr, xr)
        second = jnp.where(owner == 0, xr, yr)
        result.append(pl.multiple_of(((first * 2 + second) * 4 + zr) * rows, 16))
    return result


def put_blocks(value, out_ref, starts, column, width):
    rows = value.shape[0] // 16
    low = value.astype(LOW)
    for block, start in enumerate(starts):
        out_ref[pl.ds(start, rows), pl.ds(column, width)] = low[block * rows : (block + 1) * rows]


def column_sum(value):
    return jnp.sum(value.astype(WIDE), axis=0, keepdims=True)


def down_backward(spot, down, e, z, slope):
    rows, width = e.shape
    hidden = z.shape[1]
    half = hidden // 2
    tile = 384
    own, other, column = down

    def body(
        spot_ref, own_ref, other_ref, e_ref, z_ref, s_ref,
        du_ref, mine_ref, rest_ref, bd_ref, bu_ref, w_ref, em_ref, emt_ref, sems,
    ):
        copies = piece_copies(spot_ref, own_ref, other_ref, w_ref, sems, column, half)
        for copy in copies:
            copy.start()
        em = e_ref[...].astype(LOW)
        em_ref[...] = em
        bd_ref[...] = column_sum(em)
        emt_ref[...] = em.T
        for copy in copies:
            copy.wait()
        c = spot_ref[3]
        for owner, out_ref in ((c, mine_ref), (1 - c, rest_ref)):
            starts = block_starts(spot_ref, owner, width // 16)

            def step(n, carry):
                at = pl.ds(pl.multiple_of(owner * half + n * tile, LANES), tile)
                dz = dot(em_ref[...], w_ref[:, at])
                du = (dz * s_ref[:, at].astype(WIDE)).astype(LOW)
                du_ref[:, at] = du
                bu_ref[:, at] = column_sum(du)
                grad = dot(emt_ref[...], z_ref[:, at])
                put_blocks(grad, out_ref, starts, pl.multiple_of(n * tile, LANES), tile)
                return carry

            lax.fori_loop(0, half // tile, step, 0)

    return pl.pallas_call(
        body,
        out_shape=[
            jax.ShapeDtypeStruct((rows, hidden), LOW),
            jax.ShapeDtypeStruct((width, half), LOW),
            jax.ShapeDtypeStruct((width, half), LOW),
            jax.ShapeDtypeStruct((1, width), WIDE),
            jax.ShapeDtypeStruct((1, hidden), WIDE),
        ],
        in_specs=[pl.BlockSpec(memory_space=pltpu.SMEM)] + any_specs(2) + vmem_specs(3),
        out_specs=vmem_specs(5),
        scratch_shapes=[
            pltpu.VMEM((width, hidden), LOW),
            pltpu.VMEM((rows, width), LOW),
            pltpu.VMEM((width, rows), LOW),
            pltpu.SemaphoreType.DMA((32,)),
        ],
        compiler_params=params(),
        cost_estimate=cost(4 * rows * width * hidden, 4 * width * hidden + 6 * rows * hidden),
        name="down_backward",
    )(spot, own, other, e, z, slope)


def up_backward(spot, up, a2, du):
    rows, width = a2.shape
    hidden = du.shape[1]
    half = hidden // 2
    tile = 384
    own, other, column = up

    def body(
        spot_ref, own_ref, other_ref, a_ref, du_ref, acc_ref, mine_ref, rest_ref, w_ref, at_ref, sems
    ):
        copies = piece_copies(spot_ref, own_ref, other_ref, w_ref, sems, column, half)
        for copy in copies:
            copy.start()
        at_ref[...] = a_ref[...].T
        acc_ref[...] = jnp.zeros_like(acc_ref)
        for copy in copies:
            copy.wait()
        up_steps(spot_ref, w_ref, at_ref, du_ref, acc_ref, (mine_ref, rest_ref), half, tile)

    return pl.pallas_call(
        body,
        out_shape=[
            jax.ShapeDtypeStruct((rows, width), WIDE),
            jax.ShapeDtypeStruct((width, half), LOW),
            jax.ShapeDtypeStruct((width, half), LOW),
        ],
        in_specs=[pl.BlockSpec(memory_space=pltpu.SMEM)] + any_specs(2) + vmem_specs(2),
        out_specs=vmem_specs(3),
        scratch_shapes=[
            pltpu.VMEM((width, hidden), LOW),
            pltpu.VMEM((width, rows), LOW),
            pltpu.SemaphoreType.DMA((32,)),
        ],
        compiler_params=params(),
        cost_estimate=cost(4 * rows * width * hidden, 4 * width * hidden + 2 * rows * hidden),
        name="up_backward",
    )(spot, own, other, a2, du)


def up_steps(spot_ref, w_ref, at_ref, d_ref, acc_ref, out_refs, half, tile):
    c = spot_ref[3]
    for owner, out_ref in zip((c, 1 - c), out_refs):
        starts = block_starts(spot_ref, owner, at_ref.shape[0] // 16)

        def step(n, carry):
            at = pl.ds(pl.multiple_of(owner * half + n * tile, LANES), tile)
            d = d_ref[:, at]
            put_blocks(
                dot(at_ref[...], d), out_ref, starts, pl.multiple_of(n * tile, LANES), tile
            )
            acc_ref[...] += dot_nt(d, w_ref[:, at])
            return carry

        lax.fori_loop(0, half // tile, step, 0)


def middle_backward(spot, up, out, e, h2, a2, mixed, du, acc, table):
    rows, width = e.shape
    hidden = du.shape[1]
    half = hidden // 2
    part = width // 2
    tile = 384
    (up_own, up_other, up_col), (out_own, out_other, out_col) = up, out

    def body(
        spot_ref, uo_ref, up_ref, oo_ref, op_ref,
        e_ref, h_ref, a_ref, m0_ref, m1_ref, du_ref, before_ref, t_ref,
        e2_ref, da_ref, mine_ref, rest_ref, omine_ref, orest_ref, sums_ref,
        wu_ref, wo_ref, at_ref, mt_ref, ey_ref, acc_ref, sems_u, sems_o,
    ):
        ups = piece_copies(spot_ref, uo_ref, up_ref, wu_ref, sems_u, up_col, half)
        outs = piece_copies(spot_ref, oo_ref, op_ref, wo_ref, sems_o, out_col, part)
        for copy in ups + outs:
            copy.start()
        at_ref[...] = a_ref[...].T
        mt_ref[:part, :] = m0_ref[...].T
        mt_ref[part:, :] = m1_ref[...].T
        acc_ref[...] = before_ref[...]
        for copy in ups:
            copy.wait()
        up_steps(spot_ref, wu_ref, at_ref, du_ref, acc_ref, (mine_ref, rest_ref), half, tile)
        dv, gain, shift = norm_back(h_ref[...], t_ref[GAIN2 : GAIN2 + 1, :], acc_ref[...])
        e2 = e_ref[...] + dv
        e2_ref[...] = e2
        ey = e2.astype(LOW)
        ey_ref[...] = ey
        sums_ref[0:1, :] = gain
        sums_ref[1:2, :] = shift
        sums_ref[2:3, :] = column_sum(ey)
        for copy in outs:
            copy.wait()
        da_ref[...] = dot_nt(ey, wo_ref[...]).astype(LOW)
        c = spot_ref[3]
        for owner, out_ref in ((c, omine_ref), (1 - c, orest_ref)):
            starts = block_starts(spot_ref, owner, width // 16)
            at = pl.ds(pl.multiple_of(owner * part, LANES), part)
            put_blocks(dot(mt_ref[...], ey_ref[:, at]), out_ref, starts, 0, part)

    return pl.pallas_call(
        body,
        out_shape=[
            jax.ShapeDtypeStruct((rows, width), WIDE),
            jax.ShapeDtypeStruct((rows, width), LOW),
            jax.ShapeDtypeStruct((width, half), LOW),
            jax.ShapeDtypeStruct((width, half), LOW),
            jax.ShapeDtypeStruct((width, part), LOW),
            jax.ShapeDtypeStruct((width, part), LOW),
            jax.ShapeDtypeStruct((8, width), WIDE),
        ],
        in_specs=[pl.BlockSpec(memory_space=pltpu.SMEM)] + any_specs(4) + vmem_specs(8),
        out_specs=vmem_specs(7),
        scratch_shapes=[
            pltpu.VMEM((width, hidden), LOW),
            pltpu.VMEM((width, width), LOW),
            pltpu.VMEM((width, rows), LOW),
            pltpu.VMEM((width, rows), LOW),
            pltpu.VMEM((rows, width), LOW),
            pltpu.VMEM((rows, width), WIDE),
            pltpu.SemaphoreType.DMA((32,)),
            pltpu.SemaphoreType.DMA((32,)),
        ],
        compiler_params=params(),
        cost_estimate=cost(
            4 * rows * width * (hidden + width), 4 * width * (hidden + width) + 2 * rows * hidden
        ),
        name="middle_backward",
    )(spot, up_own, up_other, out_own, out_other, e, h2, a2, *mixed, du, acc, table)


def attention_backward(lengths, qkv, da, mixed, lse, begin, pairs):
    rows, wide = qkv.shape
    width = pairs * LANES

    def body(len_ref, q_ref, k_ref, v_ref, d_ref, m_ref, lse_ref, out_ref, row_ref):
        pair = pl.program_id(0)

        @pl.when(pair == 0)
        def start():
            row_ref[...] = lse_ref[...].T

        lane = lax.broadcasted_iota(jnp.int32, (1, LANES), 1)
        sub = lax.broadcasted_iota(jnp.int32, (LANES, 1), 0)
        key = lax.broadcasted_iota(jnp.int32, (rows, 1), 0)
        shut = jnp.where(key < len_ref[0], 0.0, -1e30)
        scale = jnp.asarray(HEAD_WIDTH**-0.5, LOW)
        q = q_ref[...] * scale
        k = k_ref[...]
        v = v_ref[...]
        d = d_ref[...]
        kt = k.T * scale
        prod = (d.astype(WIDE) * m_ref[...].astype(WIDE)).T
        dks, dvs = [], []
        dqt = jnp.zeros((LANES, rows), WIDE)
        for side in range(2):
            inside = (lane >= HEAD_WIDTH) == (side == 1)
            down = (sub >= HEAD_WIDTH) == (side == 1)
            ks = jnp.where(inside, k, jnp.zeros_like(k))
            vs = jnp.where(inside, v, jnp.zeros_like(v))
            kts = jnp.where(down, kt, jnp.zeros_like(kt))
            first = side * HEAD_WIDTH
            delta = jnp.sum(prod[first : first + HEAD_WIDTH], axis=0, keepdims=True)
            log_total = row_ref[pl.ds(pair * 2 + side, 1), :]
            p = jnp.exp((dot_nt(ks, q) + shut) - log_total)
            dp = dot_nt(vs, d)
            dvs.append(dot(p.astype(LOW), d))
            ds = (p * (dp - delta)).astype(LOW)
            dks.append(dot(ds, q))
            dqt = dqt + dot(kts, ds)
        dq = dqt.T
        dk = jnp.where(lane < HEAD_WIDTH, dks[0], dks[1])
        dv = jnp.where(lane < HEAD_WIDTH, dvs[0], dvs[1])
        for n, value in enumerate((dq, dk, dv)):
            at = pl.ds(pl.multiple_of(n * width + pair * LANES, LANES), LANES)
            out_ref[:, at] = value.astype(LOW)

    return pl.pallas_call(
        body,
        out_shape=jax.ShapeDtypeStruct((rows, 3 * width), LOW),
        grid_spec=pltpu.PrefetchScalarGridSpec(
            num_scalar_prefetch=1,
            grid=(pairs,),
            in_specs=[
                pl.BlockSpec((rows, LANES), lambda p, n: (0, p + begin)),
                pl.BlockSpec((rows, LANES), lambda p, n: (0, p + begin + PAIRS)),
                pl.BlockSpec((rows, LANES), lambda p, n: (0, p + begin + 2 * PAIRS)),
                pl.BlockSpec((rows, LANES), lambda p, n: (0, p + begin)),
                pl.BlockSpec((rows, LANES), lambda p, n: (0, p)),
                pl.BlockSpec((rows, LANES), lambda p, n: (0, 0)),
            ],
            out_specs=pl.BlockSpec((rows, 3 * width), lambda p, n: (0, 0)),
            scratch_shapes=[pltpu.VMEM((LANES, rows), WIDE)],
        ),
        compiler_params=params(),
        cost_estimate=cost(40 * rows * rows * width, 16 * rows * width, 2 * pairs * rows * rows),
        name="attention_backward",
    )(lengths, qkv, qkv, qkv, da, mixed, lse)


def qkv_backward(spot, own, other, column, dqkv, e2, h, a1, table):
    rows, width = e2.shape
    wide = 3 * width
    half = wide // 2
    part = width // 2
    tile = 384

    def body(
        spot_ref, own_ref, other_ref, d0_ref, d1_ref, e_ref, h_ref, a_ref, t_ref,
        o_ref, mine_ref, rest_ref, sums_ref, w_ref, at_ref, d_ref, acc_ref, sems,
    ):
        copies = piece_copies(spot_ref, own_ref, other_ref, w_ref, sems, column, half)
        for copy in copies:
            copy.start()
        at_ref[...] = a_ref[...].T
        acc_ref[...] = jnp.zeros_like(acc_ref)
        for n in range(3):
            for side, ref in enumerate((d0_ref, d1_ref)):
                start = n * width + side * part
                d_ref[:, start : start + part] = ref[:, n * part : (n + 1) * part]
        for copy in copies:
            copy.wait()
        up_steps(spot_ref, w_ref, at_ref, d_ref, acc_ref, (mine_ref, rest_ref), half, tile)
        dv, gain, shift = norm_back(h_ref[...], t_ref[GAIN1 : GAIN1 + 1, :], acc_ref[...])
        o_ref[...] = e_ref[...] + dv
        sums_ref[0:1, :] = gain
        sums_ref[1:2, :] = shift
        sums_ref[2:3, :] = column_sum(d_ref[:, :width])
        sums_ref[3:4, :] = column_sum(d_ref[:, 2 * width :])

    return pl.pallas_call(
        body,
        out_shape=[
            jax.ShapeDtypeStruct((rows, width), WIDE),
            jax.ShapeDtypeStruct((width, half), LOW),
            jax.ShapeDtypeStruct((width, half), LOW),
            jax.ShapeDtypeStruct((8, width), WIDE),
        ],
        in_specs=[pl.BlockSpec(memory_space=pltpu.SMEM)] + any_specs(2) + vmem_specs(6),
        out_specs=vmem_specs(4),
        scratch_shapes=[
            pltpu.VMEM((width, wide), LOW),
            pltpu.VMEM((width, rows), LOW),
            pltpu.VMEM((rows, wide), LOW),
            pltpu.VMEM((rows, width), WIDE),
            pltpu.SemaphoreType.DMA((32,)),
        ],
        compiler_params=params(),
        cost_estimate=cost(4 * rows * width * wide, 4 * width * wide + 16 * rows * width),
        name="qkv_backward",
    )(spot, own, other, *dqkv, e2, h, a1, table)


def small_forward(spot, own, column, hidden):
    width = own.shape[0]

    def body(spot_ref, own_ref, t_ref, b_ref, w_ref, sems):
        rows = width // 16
        starts = block_starts(spot_ref, spot_ref[3], rows)
        copies = [
            pltpu.make_async_copy(
                own_ref.at[pl.ds(start, rows), pl.ds(column, LANES)],
                w_ref.at[pl.ds(block * rows, rows), :],
                sems.at[block],
            )
            for block, start in enumerate(starts)
        ]
        for copy in copies:
            copy.start()
        for copy in copies:
            copy.wait()
        values = w_ref[...].astype(WIDE)
        t_ref[...] = values.T[0:8, :]
        share = hidden // 32
        for device in range(32):
            at = device * (width // 32)
            b_ref[0:1, device * share : (device + 1) * share] = values[
                at : at + 1, LANES - share :
            ]

    return pl.pallas_call(
        body,
        out_shape=[
            jax.ShapeDtypeStruct((8, width), WIDE),
            jax.ShapeDtypeStruct((1, hidden), WIDE),
        ],
        in_specs=[pl.BlockSpec(memory_space=pltpu.SMEM)] + any_specs(1),
        out_specs=vmem_specs(2),
        scratch_shapes=[pltpu.VMEM((width, LANES), LOW), pltpu.SemaphoreType.DMA((16,))],
        compiler_params=params(),
        cost_estimate=cost(0, 4 * width * LANES),
        name="small_forward",
    )(spot, own)


def small_backward(spot, first, second, down_sum, up_sum):
    width = first.shape[1]
    hidden = up_sum.shape[1]

    def body(spot_ref, f_ref, s_ref, d_ref, u_ref, mine_ref, rest_ref, w_ref, p_ref):
        w_ref[...] = jnp.zeros_like(w_ref)
        for row, value in (
            (GAIN1, s_ref[0:1, :]),
            (GAIN2, f_ref[0:1, :]),
            (BQ, s_ref[2:3, :]),
            (BV, s_ref[3:4, :]),
            (BO, f_ref[2:3, :]),
            (BD, d_ref[...]),
            (SH1, s_ref[1:2, :]),
            (SH2, f_ref[1:2, :]),
        ):
            w_ref[row : row + 1, :] = value
        p_ref[...] = w_ref[...].T
        share = hidden // 32
        for device in range(32):
            at = device * (width // 32)
            p_ref[at : at + 1, LANES - share :] = u_ref[
                0:1, device * share : (device + 1) * share
            ]
        packed = p_ref[...]
        c = spot_ref[3]
        for owner, out_ref in ((c, mine_ref), (1 - c, rest_ref)):
            put_blocks(packed, out_ref, block_starts(spot_ref, owner, width // 16), 0, LANES)

    return pl.pallas_call(
        body,
        out_shape=[jax.ShapeDtypeStruct((width, LANES), LOW)] * 2,
        in_specs=[pl.BlockSpec(memory_space=pltpu.SMEM)] + vmem_specs(4),
        out_specs=vmem_specs(2),
        scratch_shapes=[pltpu.VMEM((LANES, width), WIDE), pltpu.VMEM((width, LANES), WIDE)],
        compiler_params=params(),
        cost_estimate=cost(0, 8 * width * LANES),
        name="small_backward",
    )(spot, first, second, down_sum, up_sum)


def linear(z, x, y, c):
    return ((z * 2 + x) * 2 + y) * 2 + c


def pairs_of(step):
    result = []
    for z in range(4):
        for x in range(2):
            for y in range(2):
                for c in range(2):
                    result.append((linear(z, x, y, c), linear(*step(z, x, y, c))))
    return result


TO_CORE = pairs_of(lambda z, x, y, c: (z, x, y, 1 - c))
TO_Z = [pairs_of(lambda z, x, y, c, n=n: ((z + n) % 4, x, y, c)) for n in range(4)]
TO_XY = pairs_of(lambda z, x, y, c: (z, x, 1 - y, c) if c else (z, 1 - x, y, c))
TO_YX = pairs_of(lambda z, x, y, c: (z, 1 - x, y, c) if c else (z, x, 1 - y, c))


def send(value, pairs):
    return lax.ppermute(value, AXES, pairs)


def blocked():
    return lax.axis_size("dp") == 8 and lax.axis_size("fsdp") == 4


def place():
    if not blocked():
        return jnp.zeros((4,), jnp.int32)
    dp = lax.axis_index("dp")
    fsdp = lax.axis_index("fsdp")
    return jnp.stack([dp // 2, dp % 2, fsdp // 2, fsdp % 2]).astype(jnp.int32)


def halves(pieces):
    low = [piece[:, : piece.shape[1] // 2] for piece in pieces]
    high = [piece[:, piece.shape[1] // 2 :] for piece in pieces]
    return jnp.concatenate(low, axis=1), jnp.concatenate(high, axis=1)


class Chain:
    def __init__(self, steps):
        self.steps = steps
        self.result = None
        self.flying = None
        self.resume(None)

    def resume(self, arrived):
        try:
            self.waiting = self.steps.send(arrived)
        except StopIteration as end:
            self.waiting = None
            self.result = end.value

    def start(self):
        if self.waiting is not None:
            self.flying = [send(value, pairs) for value, pairs in self.waiting]


def stage(begin, work=None, hold=()):
    for chain in begin:
        chain.start()
    landing = [chain for chain in begin if chain.flying is not None and chain not in hold]
    outs = work() if work is not None else ()
    arrived, outs = lax.optimization_barrier(([chain.flying for chain in landing], outs))
    for chain, values in zip(landing, arrived):
        chain.flying = None
        chain.resume(values)
    return outs


def land(chain):
    class Held:
        flying = chain.flying

        def start(self):
            pass

        def resume(self, values):
            chain.flying = None
            chain.resume(values)

    return Held()


def offsets_of(widths):
    offsets = [0]
    for width in widths:
        offsets.append(offsets[-1] + width // 2)
    return offsets


def gather_whole(pieces):
    whole = [lax.all_gather(piece, AXES, axis=0, tiled=True) for piece in pieces]
    low, high = [
        part.reshape(4, 2, 2, -1, part.shape[1])[jnp.array([0, 3, 2, 1])] for part in halves(whole)
    ]
    width = low.shape[-1]
    own = low.transpose(2, 1, 0, 3, 4).reshape(-1, width)
    return own, high.transpose(1, 2, 0, 3, 4).reshape(-1, width)


def gather_steps(pieces, block):
    if not blocked():
        return gather_whole(pieces)
    ring = yield [(block, TO_Z[n]) for n in (1, 2, 3)]
    stack = jnp.concatenate([block, *ring], axis=0)
    for pairs in (TO_XY, TO_YX):
        (got,) = yield [(stack, pairs)]
        stack = jnp.concatenate([stack, got], axis=0)
    (got,) = yield [(stack, TO_CORE)]
    return stack, got


def added(parts):
    total = parts[0].astype(WIDE)
    for part in parts[1:]:
        total = total + part.astype(WIDE)
    return total


def scatter_whole(mines, rests):
    result = []
    for mine, rest in zip(mines, rests):
        rows, half = mine.shape[0] // 16, mine.shape[1]
        low = mine.reshape(2, 2, 4, rows, half).transpose(2, 1, 0, 3, 4)
        high = rest.reshape(2, 2, 4, rows, half).transpose(2, 0, 1, 3, 4)
        whole = jnp.concatenate([low, high], axis=-1)[jnp.array([0, 3, 2, 1])]
        whole = whole.reshape(16 * rows, 2 * half)
        result.append(lax.psum_scatter(whole, AXES, scatter_dimension=0, tiled=True).astype(WIDE))
    return result


def cross_steps(rest):
    if not blocked():
        return rest
    (got,) = yield [(rest, TO_CORE)]
    return got


def scatter_steps(spot, mines, gots):
    if not blocked():
        return scatter_whole(mines, gots)
    c = spot[3]
    height = mines[0].shape[0]
    a = height // 2
    b = height // 4
    rows = height // 16

    def part(start, stop):
        return jnp.concatenate(
            [added([mine[start:stop], got[start:stop]]) for mine, got in zip(mines, gots)], axis=1
        )

    (got_a,) = yield [(part(a, 2 * a).astype(LOW), TO_YX)]
    (got_b,) = yield [(added([part(b, 2 * b), got_a[b : 2 * b]]).astype(LOW), TO_XY)]

    def block_at(step):
        at = slice(step * rows, (step + 1) * rows)
        return added([part(at.start, at.stop), got_a[at], got_b[at]])

    got_z = yield [(block_at(n).astype(LOW), TO_Z[4 - n]) for n in (1, 2, 3)]
    total = added([block_at(0), *got_z])
    low, high = total[: rows // 2], total[rows // 2 :]
    kept = jnp.where(c == 0, low, high)
    (got,) = yield [(jnp.where(c == 0, high, low).astype(LOW), TO_CORE)]
    got = got.astype(WIDE)
    result = []
    start = 0
    for mine in mines:
        half = mine.shape[1]
        ours = kept[:, start : start + half]
        theirs = got[:, start : start + half]
        result.append(
            jnp.where(
                c == 0,
                jnp.concatenate([ours, theirs], axis=1),
                jnp.concatenate([theirs, ours], axis=1),
            )
        )
        start = start + half
    return result


def pack_small(gains, shifts, up_bias):
    rows = gains.shape[1]
    columns = jnp.concatenate([gains, shifts], axis=0).T
    share = up_bias.shape[0]
    first = jnp.pad(columns, ((0, 0), (0, LANES - share - columns.shape[1])))
    second = jnp.pad(up_bias[None, :], ((0, rows - 1), (0, 0)))
    packed = jnp.concatenate([first, second], axis=1)
    return jnp.concatenate([packed, packed], axis=1)


def unpack_small(packed, share):
    return packed[:, 0:2].T, packed[:, 2:8].T, packed[0, LANES - share : LANES]


def whole_small(gains, shifts, up_bias):
    both = jnp.concatenate([gains, shifts], axis=0)
    table = lax.all_gather(both, AXES, axis=1, tiled=True)
    return table.astype(WIDE), lax.all_gather(up_bias, AXES, axis=0, tiled=True)[None].astype(WIDE)


def spread_small(first, second, down_sum, up_sum):
    table = jnp.concatenate(
        [
            second[0:1],
            first[0:1],
            second[2:4],
            first[2:3],
            down_sum,
            second[1:2],
            first[1:2],
        ],
        axis=0,
    )
    own = lax.psum_scatter(table, AXES, scatter_dimension=1, tiled=True)
    return own[0:2], own[2:8], lax.psum_scatter(up_sum[0], AXES, scatter_dimension=0, tiled=True)


def local(
    hidden_in,
    cotangent,
    lengths,
    qkv_weight,
    out_weight,
    up_weight,
    down_weight,
    norm_gains,
    biases,
    up_bias,
):
    clips, slots, width = hidden_in.shape
    layers = qkv_weight.shape[0]
    share = up_bias.shape[1]
    hidden = down_weight.shape[1]
    half = hidden // 2
    assert clips == 1 and layers == 2
    spot = place()
    chunks = []
    for i in range(layers):
        gains, shifts, bias = (v[i].astype(LOW) for v in (norm_gains, biases, up_bias))
        up = up_weight[i].astype(LOW)
        down = down_weight[i].T.astype(LOW)
        first = [qkv_weight[i].astype(LOW)]
        if blocked():
            first.append(pack_small(gains, shifts, bias))
        chunks.append(first)
        chunks.append([out_weight[i].astype(LOW), up[:, :half], down[:, :half]])
        chunks.append([up[:, half:], down[:, half:]])
    spots = [offsets_of([piece.shape[1] for piece in pieces]) for pieces in chunks]

    def both_cores(pieces):
        low, high = halves(pieces)
        mine = jnp.where(spot[3] == 0, low, high)
        got = send(jnp.where(spot[3] == 0, high, low), TO_CORE)
        upper = jnp.concatenate([mine, got], axis=0)
        return jnp.where(spot[3] == 0, upper, jnp.concatenate([got, mine], axis=0))

    if blocked():
        rest = both_cores([piece for pieces in chunks[1:] for piece in pieces])
        blocks = [both_cores(chunks[0])]
        start = 0
        for at in spots[1:]:
            blocks.append(rest[:, start : start + at[-1]])
            start = start + at[-1]
    else:
        blocks = [None] * len(chunks)
    q0, a0, b0, q1, a1, b1 = [Chain(gather_steps(p, block)) for p, block in zip(chunks, blocks)]

    def weight(index, member):
        chain = (q0, a0, b0, q1, a1, b1)[index]
        return (*chain.result, spots[index][member])

    def small_of(i):
        if blocked():
            return small_forward(spot, weight(3 * i, 0)[0], spots[3 * i][1], hidden)
        return whole_small(norm_gains[i].astype(LOW), biases[i].astype(LOW), up_bias[i].astype(LOW))

    pairs = PAIRS // 2
    rec = [{"h": hidden_in[0]}, {}]

    def norm_and_qkv(i):
        r = rec[i]
        table, bias = small_of(i)
        qkv, first = qkv_forward(spot, *weight(3 * i, 0), r["h"], table)
        return {"table": table, "bias": bias, "qkv": qkv, "a1": first}

    def attend(i, side):
        mixed, lse = attention_forward(lengths, rec[i]["qkv"], side * pairs, pairs)
        return {f"mixed{side}": mixed, f"lse{side}": lse}

    def project(i):
        r = rec[i]
        h2, second = out_forward(
            spot, *weight(3 * i + 1, 0), r["h"], (r["mixed0"], r["mixed1"]), r["table"]
        )
        return {"h2": h2, "a2": second}

    def feed(i, side):
        r = rec[i]
        z, slope, total = mlp_forward(
            spot,
            weight(3 * i + 1 + side, 1 - side),
            weight(3 * i + 1 + side, 2 - side),
            r["total"] if side else r["h2"],
            r["a2"],
            r["bias"][:, side * half : (side + 1) * half],
            r["table"],
            side == 0,
        )
        return {f"z{side}": z, f"slope{side}": slope, "total": total}

    def down_back(i, side):
        r = rec[i]
        du, mine, rest, down_sum, up_sum = down_backward(
            spot, weight(3 * i + 1 + side, 2 - side), r["e"], r[f"z{side}"], r[f"slope{side}"]
        )
        return {
            f"du{side}": du,
            f"down{side}": (mine, rest),
            "down_sum": down_sum,
            f"up_sum{side}": up_sum,
        }

    def up_back(i):
        r = rec[i]
        acc, mine, rest = up_backward(spot, weight(3 * i + 1, 1), r["a2"], r["du0"])
        return {"acc": acc, "up0": (mine, rest)}

    def middle_back(i):
        r = rec[i]
        e2, da, mine, rest, out_mine, out_rest, sums = middle_backward(
            spot,
            weight(3 * i + 2, 0),
            weight(3 * i + 1, 0),
            r["e"],
            r["h2"],
            r["a2"],
            (r["mixed0"], r["mixed1"]),
            r["du1"],
            r["acc"],
            r["table"],
        )
        return {
            "e2": e2,
            "da": da,
            "up1": (mine, rest),
            "out": (out_mine, out_rest),
            "sums2": sums,
        }

    def attend_back(i, side):
        r = rec[i]
        dqkv = attention_backward(
            lengths, r["qkv"], r["da"], r[f"mixed{side}"], r[f"lse{side}"], side * pairs, pairs
        )
        return {f"dqkv{side}": dqkv}

    def qkv_back(i):
        r = rec[i]
        e, mine, rest, sums = qkv_backward(
            spot,
            *weight(3 * i, 0),
            (r["dqkv0"], r["dqkv1"]),
            r["e2"],
            r["h"],
            r["a1"],
            r["table"],
        )
        found = {"e_in": e, "qkv_grad": (mine, rest), "sums1": sums}
        if blocked():
            up_sum = jnp.concatenate([r["up_sum0"], r["up_sum1"]], axis=1)
            found["small"] = small_backward(spot, r["sums2"], sums, r["down_sum"], up_sum)
        return found

    def run(begin, *work, hold=()):
        def todo():
            before = [dict(r) for r in rec]
            found = []
            for function, i, *rest in work:
                new = function(i, *rest)
                rec[i].update(new)
                found.append(new)
            for r, old in zip(rec, before):
                r.clear()
                r.update(old)
            return found

        for (function, i, *rest), new in zip(work, stage(begin, todo, hold)):
            rec[i].update(new)

    run([q0])
    run([q0, a0], hold=[a0])
    run([q0, land(a0)])
    run([q0, a0, b0], hold=[b0])
    run([a0, land(b0)], (norm_and_qkv, 0), (attend, 0, 0))
    run([a0, b0], (attend, 0, 1))
    run([b0, q1], (project, 0), (feed, 0, 0))
    run([b0, q1])
    run([q1, a1], (feed, 0, 1))
    rec[1]["h"] = rec[0]["total"]
    run([q1, a1, b1], hold=[b1])
    run([a1, land(b1)], (norm_and_qkv, 1))
    run([a1, b1], (attend, 1, 0))
    run([b1], (attend, 1, 1), (project, 1))
    run([b1], (feed, 1, 0))
    run([], (feed, 1, 1))
    output = rec[1]["total"][None]

    def cross(i, *members):
        return [Chain(cross_steps(rec[i][member][1])) for member in members]

    def scatter(i, members, crossed):
        mines = [rec[i][member][0] for member in members]
        return Chain(scatter_steps(spot, mines, [chain.result for chain in crossed]))

    small_parts = ["small"] if blocked() else []
    rec[1]["e"] = cotangent[0]
    run([], (down_back, 1, 0))
    down_a = cross(1, "down0")
    run(down_a, (down_back, 1, 1))
    down_b = cross(1, "down1")
    run(down_b, (up_back, 1))
    d1 = scatter(1, ["down0", "down1"], down_a + down_b)
    up_a = cross(1, "up0")
    run([d1, *up_a], (middle_back, 1))
    up_b = cross(1, "out", "up1")
    run([d1, *up_b], (attend_back, 1, 0))
    u1 = scatter(1, ["out", "up0", "up1"], [up_b[0], up_a[0], up_b[1]])
    run([d1, u1], (attend_back, 1, 1), (qkv_back, 1))
    rec[0]["e"] = rec[1]["e_in"]
    qkv_a = cross(1, "qkv_grad", *small_parts)
    run([d1, u1, *qkv_a], (down_back, 0, 0))
    q1 = scatter(1, ["qkv_grad", *small_parts], qkv_a)
    down_a = cross(0, "down0")
    run([u1, q1, *down_a], (down_back, 0, 1))
    down_b = cross(0, "down1")
    run([u1, q1, *down_b], (up_back, 0))
    d0 = scatter(0, ["down0", "down1"], down_a + down_b)
    up_a = cross(0, "up0")
    run([d0, q1, *up_a], (middle_back, 0))
    up_b = cross(0, "out", "up1")
    run([d0, q1, *up_b], (attend_back, 0, 0))
    u0 = scatter(0, ["out", "up0", "up1"], [up_b[0], up_a[0], up_b[1]])
    run([d0, u0], (attend_back, 0, 1), (qkv_back, 0))
    qkv_a = cross(0, "qkv_grad", *small_parts)
    run([d0, u0, *qkv_a])
    q0 = scatter(0, ["qkv_grad", *small_parts], qkv_a)
    run([u0, q0])
    run([u0, q0])
    run([q0])
    run([q0])

    owned = []
    for i, (q, u, d) in enumerate(((q0, u0, d0), (q1, u1, d1))):
        r = rec[i]
        own_down = jnp.concatenate(d.result, axis=1).T
        own_up = jnp.concatenate(u.result[1:], axis=1)
        if blocked():
            found = unpack_small(q.result[1], share)
        else:
            up_sum = jnp.concatenate([r["up_sum0"], r["up_sum1"]], axis=1)
            found = spread_small(r["sums2"], r["sums1"], r["down_sum"], up_sum)
        owned.append((q.result[0], u.result[0], own_up, own_down, *found))
    stacked = [jnp.stack([owned[i][n] for i in range(layers)]) for n in range(7)]
    return (output, rec[0]["e_in"][None], *stacked)


def solution(mesh):
    return jax.shard_map(
        local,
        mesh=mesh,
        in_specs=(
            P(("dp", "fsdp"), None, None),
            P(("dp", "fsdp"), None, None),
            P(("dp", "fsdp")),
            P(None, ("dp", "fsdp"), None),
            P(None, ("dp", "fsdp"), None),
            P(None, ("dp", "fsdp"), None),
            P(None, None, ("dp", "fsdp")),
            P(None, None, ("dp", "fsdp")),
            P(None, None, ("dp", "fsdp")),
            P(None, ("dp", "fsdp")),
        ),
        out_specs=(
            P(("dp", "fsdp"), None, None),
            P(("dp", "fsdp"), None, None),
            P(None, ("dp", "fsdp"), None),
            P(None, ("dp", "fsdp"), None),
            P(None, ("dp", "fsdp"), None),
            P(None, None, ("dp", "fsdp")),
            P(None, None, ("dp", "fsdp")),
            P(None, None, ("dp", "fsdp")),
            P(None, ("dp", "fsdp")),
        ),
        check_vma=False,
    )
```

```python
import jax
import jax.numpy as jnp
from jax import lax
from jax.experimental import pallas as pl
from jax.experimental.pallas import tpu as pltpu
from jax.sharding import PartitionSpec as P

HEADS = 12
HEAD_WIDTH = 64
LANES = 128
PAIRS = HEADS * HEAD_WIDTH // LANES
LOW = jnp.bfloat16
WIDE = jnp.float32
norm_eps = 1e-06
AXES = ("dp", "fsdp")
VMEM_LIMIT = 60 * 1024 * 1024
FORWARD_TILE = 768
BACKWARD_TILE = 768


def cost(flops, moved, hard=0):
    return pl.CostEstimate(flops=int(flops), bytes_accessed=int(moved), transcendentals=int(hard))


def params():
    return pltpu.CompilerParams(vmem_limit_bytes=VMEM_LIMIT)


def vmem_specs(count):
    return [pl.BlockSpec(memory_space=pltpu.VMEM)] * count


def any_specs(count):
    return [pl.BlockSpec(memory_space=pl.ANY)] * count


def dot(a, b):
    return jnp.dot(a, b, preferred_element_type=WIDE)


def dot_nt(a, b):
    return lax.dot_general(a, b, (((1,), (1,)), ((), ())), preferred_element_type=WIDE)


def dot_tn(a, b):
    return lax.dot_general(a, b, (((0,), (0,)), ((), ())), preferred_element_type=WIDE)


def place_of(spot, owner, block):
    z, x, y = spot[0], spot[1], spot[2]
    first, second, zr = block // 8, (block // 4) % 2, block % 4
    bz = lax.rem(z - zr + 4, 4)
    bx = lax.rem(x + jnp.where(owner == 0, second, first), 2)
    by = lax.rem(y + jnp.where(owner == 0, first, second), 2)
    return (bz * 2 + bx) * 2 + by


def piece_copies(spot, refs, target, sems, column, half, sides=(0, 1)):
    c = spot[3]
    rows = refs[0].shape[0] // 8
    copies = []
    for side in sides:
        owner = c if side == 0 else 1 - c
        to = pl.multiple_of(owner * half, LANES)
        for block in range(16):
            start = pl.multiple_of(place_of(spot, owner, block) * rows, 16)
            copies.append(
                pltpu.make_async_copy(
                    refs[2 * side + block // 8].at[
                        pl.ds((block % 8) * rows, rows), pl.ds(column, half)
                    ],
                    target.at[pl.ds(start, rows), pl.ds(to, half)],
                    sems.at[side * 16 + block],
                )
            )
    return copies


def norm_rows(v):
    center = v - jnp.mean(v, axis=-1, keepdims=True)
    r = lax.rsqrt(jnp.mean(center * center, axis=-1, keepdims=True) + norm_eps)
    return center * r, r


def norm_back(v, gain, d):
    xh, r = norm_rows(v)
    dg = d * gain
    m1 = jnp.mean(dg, axis=-1, keepdims=True)
    m2 = jnp.mean(dg * xh, axis=-1, keepdims=True)
    return (
        r * (dg - m1 - xh * m2),
        jnp.sum(d * xh, axis=0, keepdims=True),
        jnp.sum(d, axis=0, keepdims=True),
    )


GAIN1, GAIN2, BQ, BV, BO, BD, SH1, SH2 = range(8)


def qkv_forward(spot, weight, h, table):
    refs, column = weight
    rows, width = h.shape
    wide = 3 * width
    tile = width

    def body(spot_ref, r0, r1, r2, r3, h_ref, t_ref, qkv_ref, a_ref, w_ref, sems):
        copies = piece_copies(spot_ref, (r0, r1, r2, r3), w_ref, sems, column, wide // 2)
        for copy in copies:
            copy.start()
        xh, r = norm_rows(h_ref[...])
        a_ref[...] = (xh * t_ref[GAIN1 : GAIN1 + 1, :] + t_ref[SH1 : SH1 + 1, :]).astype(LOW)
        for copy in copies:
            copy.wait()
        a = a_ref[...]
        for n in range(wide // tile):
            s = n * tile
            out = dot(a, w_ref[:, s : s + tile])
            if s < width:
                out = out + t_ref[BQ : BQ + 1, s : s + tile]
            elif s >= 2 * width:
                out = out + t_ref[BV : BV + 1, s - 2 * width : s - 2 * width + tile]
            qkv_ref[:, s : s + tile] = out.astype(LOW)

    return pl.pallas_call(
        body,
        out_shape=[
            jax.ShapeDtypeStruct((rows, wide), LOW),
            jax.ShapeDtypeStruct((rows, width), LOW),
        ],
        in_specs=[pl.BlockSpec(memory_space=pltpu.SMEM)] + any_specs(4) + vmem_specs(2),
        out_specs=vmem_specs(2),
        scratch_shapes=[pltpu.VMEM((width, wide), LOW), pltpu.SemaphoreType.DMA((32,))],
        compiler_params=params(),
        cost_estimate=cost(2 * rows * width * wide, 2 * width * wide + 9 * rows * width),
        name="qkv_forward",
    )(spot, *refs, h, table)


def attention_forward(lengths, qkv, begin, pairs):
    rows, wide = qkv.shape
    width = pairs * LANES

    def body(len_ref, q_ref, k_ref, v_ref, o_ref, lse_ref):
        pair = pl.program_id(0)
        lane = lax.broadcasted_iota(jnp.int32, (1, LANES), 1)
        key = lax.broadcasted_iota(jnp.int32, (1, rows), 1)
        shut = jnp.where(key < len_ref[0], 0.0, -1e30)
        q = q_ref[...] * jnp.asarray(HEAD_WIDTH**-0.5, LOW)
        k = k_ref[...]
        v = v_ref[...]
        outs = []
        stats = jnp.where(pair == 0, jnp.zeros((rows, LANES), WIDE), lse_ref[...])
        for side in range(2):
            inside = (lane >= HEAD_WIDTH) == (side == 1)
            qs = jnp.where(inside, q, jnp.zeros_like(q))
            s = dot_nt(qs, k) + shut
            peak = jnp.max(s, axis=1, keepdims=True)
            e = jnp.exp(s - peak)
            total = jnp.sum(e, axis=1, keepdims=True)
            p = (e * (1.0 / total)).astype(LOW)
            outs.append(dot(p, v))
            stats = jnp.where(lane == pair * 2 + side, peak + jnp.log(total), stats)
        lse_ref[...] = stats
        o_ref[...] = jnp.where(lane < HEAD_WIDTH, outs[0], outs[1]).astype(LOW)

    return pl.pallas_call(
        body,
        out_shape=[
            jax.ShapeDtypeStruct((rows, width), LOW),
            jax.ShapeDtypeStruct((rows, LANES), WIDE),
        ],
        grid_spec=pltpu.PrefetchScalarGridSpec(
            num_scalar_prefetch=1,
            grid=(pairs,),
            in_specs=[
                pl.BlockSpec((rows, LANES), lambda p, n: (0, p + begin)),
                pl.BlockSpec((rows, LANES), lambda p, n: (0, p + begin + PAIRS)),
                pl.BlockSpec((rows, LANES), lambda p, n: (0, p + begin + 2 * PAIRS)),
            ],
            out_specs=[
                pl.BlockSpec((rows, LANES), lambda p, n: (0, p)),
                pl.BlockSpec((rows, LANES), lambda p, n: (0, 0)),
            ],
        ),
        compiler_params=params(),
        cost_estimate=cost(16 * rows * rows * width, 8 * rows * width, 2 * pairs * rows * rows),
        name="attention_forward",
    )(lengths, qkv, qkv, qkv)


def out_forward(spot, weight, h, mixed, table):
    refs, column = weight
    rows, width = h.shape
    part = width // 2

    def body(
        spot_ref, r0, r1, r2, r3, h_ref, m0_ref, m1_ref, t_ref, h2_ref, a_ref, w_ref, sems
    ):
        copies = piece_copies(spot_ref, (r0, r1, r2, r3), w_ref, sems, column, width // 2)
        for copy in copies:
            copy.start()
        for copy in copies:
            copy.wait()
        product = dot(m0_ref[...], w_ref[:part, :]) + dot(m1_ref[...], w_ref[part:, :])
        h2 = h_ref[...] + (product + t_ref[BO : BO + 1, :])
        h2_ref[...] = h2
        xh, r = norm_rows(h2)
        a_ref[...] = (xh * t_ref[GAIN2 : GAIN2 + 1, :] + t_ref[SH2 : SH2 + 1, :]).astype(LOW)

    return pl.pallas_call(
        body,
        out_shape=[
            jax.ShapeDtypeStruct((rows, width), WIDE),
            jax.ShapeDtypeStruct((rows, width), LOW),
        ],
        in_specs=[pl.BlockSpec(memory_space=pltpu.SMEM)] + any_specs(4) + vmem_specs(4),
        out_specs=vmem_specs(2),
        scratch_shapes=[pltpu.VMEM((width, width), LOW), pltpu.SemaphoreType.DMA((32,))],
        compiler_params=params(),
        cost_estimate=cost(2 * rows * width * width, 2 * width * width + 12 * rows * width),
        name="out_forward",
    )(spot, *refs, h, *mixed, table)


def gelu_parts(u):
    cdf = 0.5 * (1.0 + lax.erf(u * (0.5**0.5)))
    pdf = jnp.exp(-0.5 * u * u) * (0.3989422804014327)
    return cdf, pdf


def side_tiles(tiles):
    def whole(s, n, spot):
        owner = jnp.where(s == 0, spot[3], 1 - spot[3])
        return 0, owner * tiles + n

    def mine(s, n, spot):
        return 0, jnp.where(s == 0, n, tiles - 1)

    def rest(s, n, spot):
        return 0, jnp.where(s == 0, 0, n)

    def fixed(s, n, spot):
        return 0, 0

    return whole, mine, rest, fixed


def mlp_forward(spot, up, down, base, a2, up_bias, table, first):
    rows, width = base.shape
    hidden = up_bias.shape[1]
    half = hidden // 2
    tile = FORWARD_TILE
    tiles = half // tile
    whole, mine, rest, fixed = side_tiles(tiles)
    (up_refs, up_col), (down_refs, down_col) = up, down

    def body(
        spot_ref, h_ref, a_ref, b_ref, t_ref, u0, u1, u2, u3, d0, d1, d2, d3,
        z_ref, g_ref, o_ref, wu_ref, wd_ref, sems_u, sems_d,
    ):
        side, n = pl.program_id(0), pl.program_id(1)
        ups = piece_copies(spot_ref, (u0, u1, u2, u3), wu_ref, sems_u, up_col, half)
        downs = piece_copies(spot_ref, (d0, d1, d2, d3), wd_ref, sems_d, down_col, half)

        @pl.when((side == 0) & (n == 0))
        def begin():
            for copy in ups[:16] + downs[:16] + ups[16:] + downs[16:]:
                copy.start()
            if first:
                o_ref[...] = h_ref[...] + t_ref[BD : BD + 1, :]
            else:
                o_ref[...] = h_ref[...]
            for copy in ups[:16] + downs[:16]:
                copy.wait()

        @pl.when((side == 1) & (n == 0))
        def more():
            for copy in ups[16:] + downs[16:]:
                copy.wait()

        owner = jnp.where(side == 0, spot_ref[3], 1 - spot_ref[3])
        at = pl.ds(pl.multiple_of(owner * half + n * tile, LANES), tile)
        u = dot(a_ref[...], wu_ref[:, at]) + b_ref[...]
        cdf, pdf = gelu_parts(u)
        z = (u * cdf).astype(LOW)
        z_ref[...] = z
        g_ref[...] = (cdf + u * pdf).astype(LOW)
        o_ref[...] += dot_nt(z, wd_ref[:, at])

    return pl.pallas_call(
        body,
        out_shape=[
            jax.ShapeDtypeStruct((rows, hidden), LOW),
            jax.ShapeDtypeStruct((rows, hidden), LOW),
            jax.ShapeDtypeStruct((rows, width), WIDE),
        ],
        grid_spec=pltpu.PrefetchScalarGridSpec(
            num_scalar_prefetch=1,
            grid=(2, tiles),
            in_specs=[
                pl.BlockSpec((rows, width), fixed),
                pl.BlockSpec((rows, width), fixed),
                pl.BlockSpec((1, tile), whole),
                pl.BlockSpec((8, width), fixed),
            ]
            + any_specs(8),
            out_specs=[
                pl.BlockSpec((rows, tile), whole),
                pl.BlockSpec((rows, tile), whole),
                pl.BlockSpec((rows, width), fixed),
            ],
            scratch_shapes=[
                pltpu.VMEM((width, hidden), LOW),
                pltpu.VMEM((width, hidden), LOW),
                pltpu.SemaphoreType.DMA((32,)),
                pltpu.SemaphoreType.DMA((32,)),
            ],
        ),
        compiler_params=params(),
        cost_estimate=cost(
            4 * rows * width * hidden, 4 * width * hidden + 4 * rows * hidden, 2 * rows * hidden
        ),
        name="mlp_forward",
    )(spot, base, a2, up_bias, table, *up_refs, *down_refs)


def block_starts(spot, owner, rows):
    z, x, y = spot[0], spot[1], spot[2]
    result = []
    for block in range(16):
        bz, bx, by = block // 4, (block // 2) % 2, block % 2
        zr = lax.rem(z - bz + 4, 4)
        xr = lax.rem(x + bx, 2)
        yr = lax.rem(y + by, 2)
        first = jnp.where(owner == 0, yr, xr)
        second = jnp.where(owner == 0, xr, yr)
        result.append(pl.multiple_of(((first * 2 + second) * 4 + zr) * rows, 16))
    return result


def put_blocks(value, out_ref, starts, column, width):
    rows = value.shape[0] // 16
    low = value.astype(LOW)
    for block, start in enumerate(starts):
        out_ref[pl.ds(start, rows), pl.ds(column, width)] = low[block * rows : (block + 1) * rows]


def column_sum(value):
    return jnp.sum(value.astype(WIDE), axis=0, keepdims=True)


def mlp_backward(spot, up, down, e, a2, z, slope, before):
    rows, width = e.shape
    hidden = z.shape[1]
    half = hidden // 2
    tile = BACKWARD_TILE
    tiles = half // tile
    whole, mine, rest, fixed = side_tiles(tiles)
    (up_refs, up_col), (down_refs, down_col) = up, down
    extra = [] if before is None else [before]

    def body(spot_ref, e_ref, a_ref, z_ref, s_ref, *refs):
        if extra:
            before_ref, refs = refs[0], refs[1:]
        (
            u0, u1, u2, u3, d0, d1, d2, d3,
            acc_ref, um_ref, ur_ref, dm_ref, dr_ref, bd_ref, bu_ref,
            wu_ref, wd_ref, em_ref, emt_ref, at_ref, sems_u, sems_d,
        ) = refs
        side, n = pl.program_id(0), pl.program_id(1)
        ups = piece_copies(spot_ref, (u0, u1, u2, u3), wu_ref, sems_u, up_col, half)
        downs = piece_copies(spot_ref, (d0, d1, d2, d3), wd_ref, sems_d, down_col, half)

        @pl.when((side == 0) & (n == 0))
        def begin():
            for copy in downs[:16] + ups[:16] + downs[16:] + ups[16:]:
                copy.start()
            em = e_ref[...].astype(LOW)
            em_ref[...] = em
            bd_ref[...] = column_sum(em)
            emt_ref[...] = em.T
            at_ref[...] = a_ref[...].T
            acc_ref[...] = before_ref[...] if extra else jnp.zeros_like(acc_ref)
            for copy in downs[:16] + ups[:16]:
                copy.wait()

        @pl.when((side == 1) & (n == 0))
        def more():
            for copy in downs[16:] + ups[16:]:
                copy.wait()

        owner = jnp.where(side == 0, spot_ref[3], 1 - spot_ref[3])
        at = pl.ds(pl.multiple_of(owner * half + n * tile, LANES), tile)
        starts = block_starts(spot_ref, owner, width // 16)
        du = (dot(em_ref[...], wd_ref[:, at]) * s_ref[...].astype(WIDE)).astype(LOW)
        bu_ref[...] = column_sum(du)
        down_grad = dot(emt_ref[...], z_ref[...])
        up_grad = dot(at_ref[...], du)
        acc_ref[...] += dot_nt(du, wu_ref[:, at])

        @pl.when(side == 0)
        def first_half():
            put_blocks(down_grad, dm_ref, starts, 0, tile)
            put_blocks(up_grad, um_ref, starts, 0, tile)

        @pl.when(side == 1)
        def second_half():
            put_blocks(down_grad, dr_ref, starts, 0, tile)
            put_blocks(up_grad, ur_ref, starts, 0, tile)

    return pl.pallas_call(
        body,
        out_shape=[
            jax.ShapeDtypeStruct((rows, width), WIDE),
            jax.ShapeDtypeStruct((width, half), LOW),
            jax.ShapeDtypeStruct((width, half), LOW),
            jax.ShapeDtypeStruct((width, half), LOW),
            jax.ShapeDtypeStruct((width, half), LOW),
            jax.ShapeDtypeStruct((1, width), WIDE),
            jax.ShapeDtypeStruct((1, hidden), WIDE),
        ],
        grid_spec=pltpu.PrefetchScalarGridSpec(
            num_scalar_prefetch=1,
            grid=(2, tiles),
            in_specs=[
                pl.BlockSpec((rows, width), fixed),
                pl.BlockSpec((rows, width), fixed),
                pl.BlockSpec((rows, tile), whole),
                pl.BlockSpec((rows, tile), whole),
            ]
            + [pl.BlockSpec((rows, width), fixed)] * len(extra)
            + any_specs(8),
            out_specs=[
                pl.BlockSpec((rows, width), fixed),
                pl.BlockSpec((width, tile), mine),
                pl.BlockSpec((width, tile), rest),
                pl.BlockSpec((width, tile), mine),
                pl.BlockSpec((width, tile), rest),
                pl.BlockSpec((1, width), fixed),
                pl.BlockSpec((1, tile), whole),
            ],
            scratch_shapes=[
                pltpu.VMEM((width, hidden), LOW),
                pltpu.VMEM((width, hidden), LOW),
                pltpu.VMEM((rows, width), LOW),
                pltpu.VMEM((width, rows), LOW),
                pltpu.VMEM((width, rows), LOW),
                pltpu.SemaphoreType.DMA((32,)),
                pltpu.SemaphoreType.DMA((32,)),
            ],
        ),
        compiler_params=params(),
        cost_estimate=cost(8 * rows * width * hidden, 8 * width * hidden + 4 * rows * hidden),
        name="mlp_backward",
    )(spot, e, a2, z, slope, *extra, *up_refs, *down_refs)


def middle_backward(spot, out, e, h2, mixed, acc, table):
    rows, width = e.shape
    part = width // 2
    refs, column = out

    def body(
        spot_ref, r0, r1, r2, r3, e_ref, h_ref, m0_ref, m1_ref, acc_ref, t_ref,
        e2_ref, da_ref, mine_ref, rest_ref, sums_ref, w_ref, mt_ref, ey_ref, sems,
    ):
        copies = piece_copies(spot_ref, (r0, r1, r2, r3), w_ref, sems, column, part)
        for copy in copies:
            copy.start()
        mt_ref[:part, :] = m0_ref[...].T
        mt_ref[part:, :] = m1_ref[...].T
        dv, gain, shift = norm_back(h_ref[...], t_ref[GAIN2 : GAIN2 + 1, :], acc_ref[...])
        e2 = e_ref[...] + dv
        e2_ref[...] = e2
        ey = e2.astype(LOW)
        ey_ref[...] = ey
        sums_ref[0:1, :] = gain
        sums_ref[1:2, :] = shift
        sums_ref[2:3, :] = column_sum(ey)
        for copy in copies:
            copy.wait()
        da_ref[...] = dot_nt(ey, w_ref[...]).astype(LOW)
        c = spot_ref[3]
        for owner, out_ref in ((c, mine_ref), (1 - c, rest_ref)):
            starts = block_starts(spot_ref, owner, width // 16)
            at = pl.ds(pl.multiple_of(owner * part, LANES), part)
            put_blocks(dot(mt_ref[...], ey_ref[:, at]), out_ref, starts, 0, part)

    return pl.pallas_call(
        body,
        out_shape=[
            jax.ShapeDtypeStruct((rows, width), WIDE),
            jax.ShapeDtypeStruct((rows, width), LOW),
            jax.ShapeDtypeStruct((width, part), LOW),
            jax.ShapeDtypeStruct((width, part), LOW),
            jax.ShapeDtypeStruct((8, width), WIDE),
        ],
        in_specs=[pl.BlockSpec(memory_space=pltpu.SMEM)] + any_specs(4) + vmem_specs(6),
        out_specs=vmem_specs(5),
        scratch_shapes=[
            pltpu.VMEM((width, width), LOW),
            pltpu.VMEM((width, rows), LOW),
            pltpu.VMEM((rows, width), LOW),
            pltpu.SemaphoreType.DMA((32,)),
        ],
        compiler_params=params(),
        cost_estimate=cost(4 * rows * width * width, 4 * width * width + 20 * rows * width),
        name="middle_backward",
    )(spot, *refs, e, h2, *mixed, acc, table)


def attention_backward(lengths, qkv, da, mixed, lse, begin, pairs):
    rows, wide = qkv.shape
    width = pairs * LANES

    def body(len_ref, q_ref, k_ref, v_ref, d_ref, m_ref, lse_ref, out_ref, row_ref):
        pair = pl.program_id(0)

        @pl.when(pair == 0)
        def start():
            row_ref[...] = lse_ref[...].T

        lane = lax.broadcasted_iota(jnp.int32, (1, LANES), 1)
        sub = lax.broadcasted_iota(jnp.int32, (LANES, 1), 0)
        key = lax.broadcasted_iota(jnp.int32, (rows, 1), 0)
        shut = jnp.where(key < len_ref[0], 0.0, -1e30)
        scale = jnp.asarray(HEAD_WIDTH**-0.5, LOW)
        q = q_ref[...] * scale
        k = k_ref[...]
        v = v_ref[...]
        d = d_ref[...]
        kt = k.T * scale
        prod = (d.astype(WIDE) * m_ref[...].astype(WIDE)).T
        dks, dvs = [], []
        dqt = jnp.zeros((LANES, rows), WIDE)
        for side in range(2):
            inside = (lane >= HEAD_WIDTH) == (side == 1)
            down = (sub >= HEAD_WIDTH) == (side == 1)
            ks = jnp.where(inside, k, jnp.zeros_like(k))
            vs = jnp.where(inside, v, jnp.zeros_like(v))
            kts = jnp.where(down, kt, jnp.zeros_like(kt))
            first = side * HEAD_WIDTH
            delta = jnp.sum(prod[first : first + HEAD_WIDTH], axis=0, keepdims=True)
            log_total = row_ref[pl.ds(pair * 2 + side, 1), :]
            p = jnp.exp((dot_nt(ks, q) + shut) - log_total)
            dp = dot_nt(vs, d)
            dvs.append(dot(p.astype(LOW), d))
            ds = (p * (dp - delta)).astype(LOW)
            dks.append(dot(ds, q))
            dqt = dqt + dot(kts, ds)
        dq = dqt.T
        dk = jnp.where(lane < HEAD_WIDTH, dks[0], dks[1])
        dv = jnp.where(lane < HEAD_WIDTH, dvs[0], dvs[1])
        for n, value in enumerate((dq, dk, dv)):
            at = pl.ds(pl.multiple_of(n * width + pair * LANES, LANES), LANES)
            out_ref[:, at] = value.astype(LOW)

    return pl.pallas_call(
        body,
        out_shape=jax.ShapeDtypeStruct((rows, 3 * width), LOW),
        grid_spec=pltpu.PrefetchScalarGridSpec(
            num_scalar_prefetch=1,
            grid=(pairs,),
            in_specs=[
                pl.BlockSpec((rows, LANES), lambda p, n: (0, p + begin)),
                pl.BlockSpec((rows, LANES), lambda p, n: (0, p + begin + PAIRS)),
                pl.BlockSpec((rows, LANES), lambda p, n: (0, p + begin + 2 * PAIRS)),
                pl.BlockSpec((rows, LANES), lambda p, n: (0, p + begin)),
                pl.BlockSpec((rows, LANES), lambda p, n: (0, p)),
                pl.BlockSpec((rows, LANES), lambda p, n: (0, 0)),
            ],
            out_specs=pl.BlockSpec((rows, 3 * width), lambda p, n: (0, 0)),
            scratch_shapes=[pltpu.VMEM((LANES, rows), WIDE)],
        ),
        compiler_params=params(),
        cost_estimate=cost(40 * rows * rows * width, 16 * rows * width, 2 * pairs * rows * rows),
        name="attention_backward",
    )(lengths, qkv, qkv, qkv, da, mixed, lse)


def qkv_backward(spot, weight, dqkv, e2, h, a1, table, others):
    rows, width = e2.shape
    wide = 3 * width
    half = wide // 2
    part = width // 2
    refs, column = weight
    sums, down_sum, up_sums = others
    hidden = sum(value.shape[1] for value in up_sums)

    def body(
        spot_ref, r0, r1, r2, r3, d0_ref, d1_ref, e_ref, h_ref, a_ref, t_ref,
        s_ref, ds_ref, u0_ref, u1_ref, o_ref, mine_ref, rest_ref, sums_ref,
        w_ref, at_ref, d_ref, acc_ref, row_ref, pack_ref, sems,
    ):
        copies = piece_copies(spot_ref, (r0, r1, r2, r3), w_ref, sems, column, half)
        for copy in copies:
            copy.start()
        at_ref[...] = a_ref[...].T
        for n in range(3):
            for side, ref in enumerate((d0_ref, d1_ref)):
                start = n * width + side * part
                d_ref[:, start : start + part] = ref[:, n * part : (n + 1) * part]
        for copy in copies:
            copy.wait()
        c = spot_ref[3]
        order = []
        for owner, out_ref in ((c, mine_ref), (1 - c, rest_ref)):
            starts = block_starts(spot_ref, owner, width // 16)
            at = pl.ds(pl.multiple_of(owner * half, LANES), half)
            put_blocks(dot(at_ref[...], d_ref[:, at]), out_ref, starts, 0, half)
            order.append((starts, out_ref))
        acc_ref[...] = dot_nt(d_ref[...], w_ref[...])
        dv, gain, shift = norm_back(h_ref[...], t_ref[GAIN1 : GAIN1 + 1, :], acc_ref[...])
        o_ref[...] = e_ref[...] + dv
        row_ref[...] = jnp.zeros_like(row_ref)
        for row, value in (
            (GAIN1, gain),
            (GAIN2, s_ref[0:1, :]),
            (BQ, column_sum(d_ref[:, :width])),
            (BV, column_sum(d_ref[:, 2 * width :])),
            (BO, s_ref[2:3, :]),
            (BD, ds_ref[...]),
            (SH1, shift),
            (SH2, s_ref[1:2, :]),
        ):
            row_ref[row : row + 1, :] = value
        sums_ref[...] = row_ref[0:8, :]
        pack_ref[...] = row_ref[...].T
        share = hidden // 32
        per = u0_ref.shape[1] // share
        for device in range(32):
            at = device * (width // 32)
            ref, start = (u0_ref, u1_ref)[device // per], (device % per) * share
            pack_ref[at : at + 1, LANES - share :] = ref[0:1, start : start + share]
        for starts, out_ref in order:
            put_blocks(pack_ref[...], out_ref, starts, half, LANES)

    return pl.pallas_call(
        body,
        out_shape=[
            jax.ShapeDtypeStruct((rows, width), WIDE),
            jax.ShapeDtypeStruct((width, half + LANES), LOW),
            jax.ShapeDtypeStruct((width, half + LANES), LOW),
            jax.ShapeDtypeStruct((8, width), WIDE),
        ],
        in_specs=[pl.BlockSpec(memory_space=pltpu.SMEM)] + any_specs(4) + vmem_specs(10),
        out_specs=vmem_specs(4),
        scratch_shapes=[
            pltpu.VMEM((width, wide), LOW),
            pltpu.VMEM((width, rows), LOW),
            pltpu.VMEM((rows, wide), LOW),
            pltpu.VMEM((rows, width), WIDE),
            pltpu.VMEM((LANES, width), WIDE),
            pltpu.VMEM((width, LANES), WIDE),
            pltpu.SemaphoreType.DMA((32,)),
        ],
        compiler_params=params(),
        cost_estimate=cost(4 * rows * width * wide, 4 * width * wide + 16 * rows * width),
        name="qkv_backward",
    )(spot, *refs, *dqkv, e2, h, a1, table, sums, down_sum, *up_sums)


def small_forward(spot, refs, column, hidden):
    rows = refs[0].shape[0] // 8
    width = 16 * rows

    def body(spot_ref, r0, r1, t_ref, b_ref, w_ref, sems):
        copies = []
        for block in range(16):
            start = pl.multiple_of(place_of(spot_ref, spot_ref[3], block) * rows, 16)
            copies.append(
                pltpu.make_async_copy(
                    (r0, r1)[block // 8].at[pl.ds((block % 8) * rows, rows), pl.ds(column, LANES)],
                    w_ref.at[pl.ds(start, rows), :],
                    sems.at[block],
                )
            )
        for copy in copies:
            copy.start()
        for copy in copies:
            copy.wait()
        values = w_ref[...].astype(WIDE)
        t_ref[...] = values.T[0:8, :]
        share = hidden // 32
        for device in range(32):
            at = device * (width // 32)
            b_ref[0:1, device * share : (device + 1) * share] = values[
                at : at + 1, LANES - share :
            ]

    return pl.pallas_call(
        body,
        out_shape=[
            jax.ShapeDtypeStruct((8, width), WIDE),
            jax.ShapeDtypeStruct((1, hidden), WIDE),
        ],
        in_specs=[pl.BlockSpec(memory_space=pltpu.SMEM)] + any_specs(2),
        out_specs=vmem_specs(2),
        scratch_shapes=[pltpu.VMEM((width, LANES), LOW), pltpu.SemaphoreType.DMA((16,))],
        compiler_params=params(),
        cost_estimate=cost(0, 4 * width * LANES),
        name="small_forward",
    )(spot, *refs[:2])


def rows_spec(height, width, index):
    return pl.BlockSpec((height, width), lambda i: (index, 0))


def sum_call(body, ins, outs, out_specs, name, spot=None):
    specs = [rows_spec(height, value.shape[1], index) for value, height, index in ins]
    moved = sum(2 * height * value.shape[1] for value, height, index in ins)
    first = [] if spot is None else [spot]
    return pl.pallas_call(
        body,
        out_shape=outs,
        grid=(1,),
        in_specs=[pl.BlockSpec(memory_space=pltpu.SMEM)] * len(first) + specs,
        out_specs=out_specs,
        compiler_params=params(),
        cost_estimate=cost(0, 2 * moved),
        name=name,
    )(*first, *(value for value, height, index in ins))


def wide_sum(refs):
    total = refs[0][...].astype(WIDE)
    for ref in refs[1:]:
        total = total + ref[...].astype(WIDE)
    return total


def sum_pieces(mines, gots, arrived, height, index):
    count = len(mines)
    width = sum(mine.shape[1] for mine in mines)

    def body(*refs):
        out_ref = refs[-1]
        start = 0
        for n in range(count):
            half = refs[n].shape[1]
            total = wide_sum((refs[n], refs[count + n]))
            for ref in refs[2 * count : -1]:
                total = total + ref[:, start : start + half].astype(WIDE)
            out_ref[:, start : start + half] = total.astype(LOW)
            start = start + half

    ins = [(value, height, index) for value in (*mines, *gots, *arrived)]
    out = jax.ShapeDtypeStruct((height, width), LOW)
    return sum_call(body, ins, out, rows_spec(height, width, 0), "sum_pieces")


def sum_blocks(mines, gots, arrived):
    count = len(mines)
    height = mines[0].shape[0] // 4
    rows = height // 4
    width = sum(mine.shape[1] for mine in mines)

    def body(*refs):
        outs = refs[-4:]
        start = 0
        for n in range(count):
            half = refs[n].shape[1]
            total = wide_sum((refs[n], refs[count + n]))
            for ref in refs[2 * count : -4]:
                total = total + ref[:, start : start + half].astype(WIDE)
            for block, out_ref in enumerate(outs):
                out_ref[:, start : start + half] = total[
                    block * rows : (block + 1) * rows
                ].astype(out_ref.dtype)
            start = start + half

    ins = [(value, height, 0) for value in (*mines, *gots, *arrived)]
    outs = [jax.ShapeDtypeStruct((rows, width), WIDE)]
    outs += [jax.ShapeDtypeStruct((rows, width), LOW)] * 3
    return sum_call(body, ins, outs, [rows_spec(rows, width, 0)] * 4, "sum_blocks")


def sum_last(spot, own, arrived):
    rows, width = own.shape

    def body(spot_ref, *refs):
        kept_ref, sent_ref = refs[-2:]
        total = wide_sum(refs[:-2])
        low, high = total[: rows // 2], total[rows // 2 :]
        c = spot_ref[3]
        kept_ref[...] = jnp.where(c == 0, low, high)
        sent_ref[...] = jnp.where(c == 0, high, low).astype(LOW)

    ins = [(value, rows, 0) for value in (own, *arrived)]
    outs = [jax.ShapeDtypeStruct((rows // 2, width), kind) for kind in (WIDE, LOW)]
    return sum_call(body, ins, outs, [rows_spec(rows // 2, width, 0)] * 2, "sum_last", spot)


def finish_mlp(spot, parts, shapes):
    down_shape, up_shape, out_shape = shapes
    layers = len(parts)
    half = up_shape[2] // 4
    small = out_shape[2] // 2

    def body(spot_ref, *refs):
        down_ref, up_ref, out_ref = refs[-3:]
        c = spot_ref[3]
        at = 0
        for layer in range(layers):
            for part in range(2):
                for owner, ref in ((c, refs[at]), (1 - c, refs[at + 1])):
                    start = pl.multiple_of(part * 2 * half + owner * half, LANES)
                    values = ref[:, :half].astype(WIDE)
                    down_ref[layer, pl.ds(start, half), :] = values.T
                    up_ref[layer, :, pl.ds(start, half)] = ref[:, half : 2 * half].astype(WIDE)
                    if part == 0:
                        start = pl.multiple_of(owner * small, LANES)
                        out_ref[layer, :, pl.ds(start, small)] = ref[
                            :, 2 * half : 2 * half + small
                        ].astype(WIDE)
                at = at + 2

    flat = [value for layer in parts for part in layer for value in part]
    return pl.pallas_call(
        body,
        out_shape=[jax.ShapeDtypeStruct(shape, WIDE) for shape in shapes],
        in_specs=[pl.BlockSpec(memory_space=pltpu.SMEM)] + vmem_specs(len(flat)),
        out_specs=vmem_specs(3),
        compiler_params=params(),
        cost_estimate=cost(0, 16 * sum(value.size for value in flat)),
        name="finish_mlp",
    )(spot, *flat)


def finish_qkv(spot, parts, shapes):
    share = shapes[3][1]
    half = shapes[0][2] // 2

    def body(spot_ref, *refs):
        qkv_ref, gain_ref, bias_ref, up_ref = refs[-4:]
        c = spot_ref[3]
        for layer in range(len(parts)):
            kept_ref, got_ref = refs[2 * layer], refs[2 * layer + 1]
            for owner, ref in ((c, kept_ref), (1 - c, got_ref)):
                start = pl.multiple_of(owner * half, LANES)
                qkv_ref[layer, :, pl.ds(start, half)] = ref[:, :half].astype(WIDE)
            packed = kept_ref[:, half : half + LANES]
            columns = packed.T
            gain_ref[layer] = columns[0:2, :]
            bias_ref[layer] = columns[2:8, :]
            up_ref[layer : layer + 1, :] = packed[0:1, LANES - share :]

    flat = [value for part in parts for value in part]
    return pl.pallas_call(
        body,
        out_shape=[jax.ShapeDtypeStruct(shape, WIDE) for shape in shapes],
        in_specs=[pl.BlockSpec(memory_space=pltpu.SMEM)] + vmem_specs(len(flat)),
        out_specs=vmem_specs(4),
        compiler_params=params(),
        cost_estimate=cost(0, 8 * sum(value.size for value in flat)),
        name="finish_qkv",
    )(spot, *flat)


def linear(z, x, y, c):
    return ((z * 2 + x) * 2 + y) * 2 + c


def pairs_of(step):
    result = []
    for z in range(4):
        for x in range(2):
            for y in range(2):
                for c in range(2):
                    result.append((linear(z, x, y, c), linear(*step(z, x, y, c))))
    return result


TO_CORE = pairs_of(lambda z, x, y, c: (z, x, y, 1 - c))
TO_Z = [pairs_of(lambda z, x, y, c, n=n: ((z + n) % 4, x, y, c)) for n in range(4)]
TO_XY = pairs_of(lambda z, x, y, c: (z, x, 1 - y, c) if c else (z, 1 - x, y, c))
TO_YX = pairs_of(lambda z, x, y, c: (z, 1 - x, y, c) if c else (z, x, 1 - y, c))


def send(value, pairs):
    return lax.ppermute(value, AXES, pairs)


def blocked():
    return lax.axis_size("dp") == 8 and lax.axis_size("fsdp") == 4


def place():
    if not blocked():
        return jnp.zeros((4,), jnp.int32)
    dp = lax.axis_index("dp")
    fsdp = lax.axis_index("fsdp")
    return jnp.stack([dp // 2, dp % 2, fsdp // 2, fsdp % 2]).astype(jnp.int32)


def halves(pieces):
    low = [piece[:, : piece.shape[1] // 2] for piece in pieces]
    high = [piece[:, piece.shape[1] // 2 :] for piece in pieces]
    return jnp.concatenate(low, axis=1), jnp.concatenate(high, axis=1)


class Chain:
    def __init__(self, steps):
        self.steps = steps
        self.result = None
        self.flying = None
        self.resume(None)

    def resume(self, arrived):
        try:
            self.waiting = self.steps.send(arrived)
        except StopIteration as end:
            self.waiting = None
            self.result = end.value

    def start(self):
        if self.waiting is not None:
            self.flying = [send(value, pairs) for value, pairs in self.waiting]


def stage(begin, work=None, hold=()):
    for chain in begin:
        chain.start()
    landing = [chain for chain in begin if chain.flying is not None and chain not in hold]
    outs = work() if work is not None else ()
    arrived, outs = lax.optimization_barrier(([chain.flying for chain in landing], outs))
    for chain, values in zip(landing, arrived):
        chain.flying = None
        chain.resume(values)
    return outs


def land(chain):
    class Held:
        flying = chain.flying

        def start(self):
            pass

        def resume(self, values):
            chain.flying = None
            chain.resume(values)

    return Held()


def offsets_of(widths):
    offsets = [0]
    for width in widths:
        offsets.append(offsets[-1] + width // 2)
    return offsets


def gather_whole(pieces):
    whole = [lax.all_gather(piece, AXES, axis=0, tiled=True) for piece in pieces]
    low, high = [
        part.reshape(4, 2, 2, -1, part.shape[1])[jnp.array([0, 3, 2, 1])] for part in halves(whole)
    ]
    width = low.shape[-1]
    own = low.transpose(2, 1, 0, 3, 4).reshape(2, -1, width)
    other = high.transpose(1, 2, 0, 3, 4).reshape(2, -1, width)
    return own[0], own[1], other[0], other[1]


def gather_steps(pieces, block):
    if not blocked():
        return gather_whole(pieces)
    ring = yield [(block, TO_Z[n]) for n in (1, 2, 3)]
    stack = jnp.concatenate([block, *ring], axis=0)
    (got,) = yield [(stack, TO_XY)]
    near = jnp.concatenate([stack, got], axis=0)
    far, near_got = yield [(near, TO_YX), (near, TO_CORE)]
    (far_got,) = yield [(far, TO_CORE)]
    return near, far, near_got, far_got


def scatter_whole(mines, rests):
    result = []
    for mine, rest in zip(mines, rests):
        rows = mine.shape[0] // 16
        half = mine.shape[1] // (3 * LANES) * (3 * LANES)
        mine, rest = mine[:, :half], rest[:, :half]
        low = mine.reshape(2, 2, 4, rows, half).transpose(2, 1, 0, 3, 4)
        high = rest.reshape(2, 2, 4, rows, half).transpose(2, 0, 1, 3, 4)
        whole = jnp.concatenate([low, high], axis=-1)[jnp.array([0, 3, 2, 1])]
        whole = whole.reshape(16 * rows, 2 * half)
        result.append(lax.psum_scatter(whole, AXES, scatter_dimension=0, tiled=True).astype(WIDE))
    return result


def cross_steps(rest):
    if not blocked():
        return rest
    (got,) = yield [(rest, TO_CORE)]
    return got


def scatter_steps(spot, mines, gots):
    if not blocked():
        return scatter_whole(mines, gots)
    height = mines[0].shape[0]
    (got_a,) = yield [(sum_pieces(mines, gots, (), height // 2, 1), TO_YX)]
    (got_b,) = yield [(sum_pieces(mines, gots, (got_a,), height // 4, 1), TO_XY)]
    own, *blocks = sum_blocks(mines, gots, (got_a, got_b))
    arrived = yield [(block, TO_Z[3 - n]) for n, block in enumerate(blocks)]
    kept, sent = sum_last(spot, own, arrived)
    (got,) = yield [(sent, TO_CORE)]
    return kept, got


def pack_small(gains, shifts, up_bias):
    rows = gains.shape[1]
    columns = jnp.concatenate([gains, shifts], axis=0).T
    share = up_bias.shape[0]
    first = jnp.pad(columns, ((0, 0), (0, LANES - share - columns.shape[1])))
    second = jnp.pad(up_bias[None, :], ((0, rows - 1), (0, 0)))
    packed = jnp.concatenate([first, second], axis=1)
    return jnp.concatenate([packed, packed], axis=1)


def whole_small(gains, shifts, up_bias):
    both = jnp.concatenate([gains, shifts], axis=0)
    table = lax.all_gather(both, AXES, axis=1, tiled=True)
    return table.astype(WIDE), lax.all_gather(up_bias, AXES, axis=0, tiled=True)[None].astype(WIDE)


def local(
    hidden_in,
    cotangent,
    lengths,
    qkv_weight,
    out_weight,
    up_weight,
    down_weight,
    norm_gains,
    biases,
    up_bias,
):
    clips, slots, width = hidden_in.shape
    layers = qkv_weight.shape[0]
    share = up_bias.shape[1]
    hidden = down_weight.shape[1]
    half = hidden // 2
    assert clips == 1 and layers == 2
    spot = place()
    chunks = []
    for i in range(layers):
        gains, shifts, bias = (v[i].astype(LOW) for v in (norm_gains, biases, up_bias))
        up = up_weight[i].astype(LOW)
        down = down_weight[i].T.astype(LOW)
        first = [qkv_weight[i].astype(LOW)]
        if blocked():
            first.append(pack_small(gains, shifts, bias))
        chunks.append(first)
        chunks.append([out_weight[i].astype(LOW), up[:, :half], down[:, :half]])
        chunks.append([up[:, half:], down[:, half:]])
    spots = [offsets_of([piece.shape[1] for piece in pieces]) for pieces in chunks]

    def both_cores(pieces):
        low, high = halves(pieces)
        mine = jnp.where(spot[3] == 0, low, high)
        got = send(jnp.where(spot[3] == 0, high, low), TO_CORE)
        upper = jnp.concatenate([mine, got], axis=0)
        return jnp.where(spot[3] == 0, upper, jnp.concatenate([got, mine], axis=0))

    if blocked():
        rest = both_cores([piece for pieces in chunks[1:] for piece in pieces])
        blocks = [both_cores(chunks[0])]
        start = 0
        for at in spots[1:]:
            blocks.append(rest[:, start : start + at[-1]])
            start = start + at[-1]
    else:
        blocks = [None] * len(chunks)
    q0, a0, b0, q1, a1, b1 = [Chain(gather_steps(p, block)) for p, block in zip(chunks, blocks)]

    def weight(index, member):
        chain = (q0, a0, b0, q1, a1, b1)[index]
        return chain.result, spots[index][member]

    def small_of(i):
        if blocked():
            return small_forward(spot, q0.result if i == 0 else q1.result, spots[3 * i][1], hidden)
        return whole_small(norm_gains[i].astype(LOW), biases[i].astype(LOW), up_bias[i].astype(LOW))

    pairs = PAIRS // 2
    rec = [{"h": hidden_in[0]}, {}]

    def norm_and_qkv(i):
        r = rec[i]
        table, bias = small_of(i)
        qkv, first = qkv_forward(spot, weight(3 * i, 0), r["h"], table)
        return {"table": table, "bias": bias, "qkv": qkv, "a1": first}

    def attend(i, side):
        mixed, lse = attention_forward(lengths, rec[i]["qkv"], side * pairs, pairs)
        return {f"mixed{side}": mixed, f"lse{side}": lse}

    def project(i):
        r = rec[i]
        h2, second = out_forward(
            spot, weight(3 * i + 1, 0), r["h"], (r["mixed0"], r["mixed1"]), r["table"]
        )
        return {"h2": h2, "a2": second}

    def feed_weights(i, side):
        return weight(3 * i + 1 + side, 1 - side), weight(3 * i + 1 + side, 2 - side)

    def feed(i, side):
        r = rec[i]
        z, slope, total = mlp_forward(
            spot,
            *feed_weights(i, side),
            r["total"] if side else r["h2"],
            r["a2"],
            r["bias"][:, side * half : (side + 1) * half],
            r["table"],
            side == 0,
        )
        return {f"z{side}": z, f"slope{side}": slope, "total": total}

    def feed_back(i, side):
        r = rec[i]
        acc, up_mine, up_rest, down_mine, down_rest, down_sum, up_sum = mlp_backward(
            spot,
            *feed_weights(i, side),
            r["e"],
            r["a2"],
            r[f"z{side}"],
            r[f"slope{side}"],
            None if side else r["acc"],
        )
        return {
            "acc": acc,
            f"up{side}": (up_mine, up_rest),
            f"down{side}": (down_mine, down_rest),
            "down_sum": down_sum,
            f"up_sum{side}": up_sum,
        }

    def middle_back(i):
        r = rec[i]
        mixed = (r["mixed0"], r["mixed1"])
        e2, da, mine, rest, sums = middle_backward(
            spot, weight(3 * i + 1, 0), r["e"], r["h2"], mixed, r["acc"], r["table"]
        )
        return {"e2": e2, "da": da, "out": (mine, rest), "sums2": sums}

    def attend_back(i, side):
        r = rec[i]
        dqkv = attention_backward(
            lengths, r["qkv"], r["da"], r[f"mixed{side}"], r[f"lse{side}"], side * pairs, pairs
        )
        return {f"dqkv{side}": dqkv}

    def qkv_back(i):
        r = rec[i]
        e, mine, rest, table = qkv_backward(
            spot,
            weight(3 * i, 0),
            (r["dqkv0"], r["dqkv1"]),
            r["e2"],
            r["h"],
            r["a1"],
            r["table"],
            (r["sums2"], r["down_sum"], (r["up_sum0"], r["up_sum1"])),
        )
        return {"e_in": e, "qkv": (mine, rest), "small": table}

    def run(begin, *work, hold=()):
        def todo():
            before = [dict(r) for r in rec]
            found = []
            for function, i, *rest in work:
                new = function(i, *rest)
                rec[i].update(new)
                found.append(new)
            for r, old in zip(rec, before):
                r.clear()
                r.update(old)
            return found

        for (function, i, *rest), new in zip(work, stage(begin, todo, hold)):
            rec[i].update(new)

    run([q0])
    run([q0, a0], hold=[a0])
    run([q0, land(a0)])
    run([q0, a0, b0], hold=[b0])
    run([a0, land(b0)], (norm_and_qkv, 0), (attend, 0, 0))
    run([a0, b0], (attend, 0, 1))
    run([b0, q1], (project, 0), (feed, 0, 0))
    run([b0, q1])
    run([q1, a1], (feed, 0, 1))
    rec[1]["h"] = rec[0]["total"]
    run([q1, a1, b1], hold=[b1])
    run([a1, land(b1)], (norm_and_qkv, 1))
    run([a1, b1], (attend, 1, 0))
    run([b1], (attend, 1, 1), (project, 1))
    run([b1], (feed, 1, 0))
    run([], (feed, 1, 1))
    output = rec[1]["total"][None]

    def cross(i, *members):
        return [Chain(cross_steps(rec[i][member][1])) for member in members]

    def scatter(i, members, crossed):
        mines = [rec[i][member][0] for member in members]
        return Chain(scatter_steps(spot, mines, [chain.result for chain in crossed]))

    first_members, second_members = ["down1", "up1"], ["down0", "up0", "out"]
    rec[1]["e"] = cotangent[0]
    run([], (feed_back, 1, 1))
    first = cross(1, *first_members)
    run(first, (feed_back, 1, 0))
    b1 = scatter(1, first_members, first)
    second = cross(1, "down0", "up0")
    run([b1, *second], (middle_back, 1), (attend_back, 1, 0))
    second += cross(1, "out")
    run([b1, *second], (attend_back, 1, 1))
    a1 = scatter(1, second_members, second)
    run([b1, a1], (qkv_back, 1))
    rec[0]["e"] = rec[1]["e_in"]
    third = cross(1, "qkv")
    run([b1, a1, *third], (feed_back, 0, 1))
    q1 = scatter(1, ["qkv"], third)
    first = cross(0, *first_members)
    run([a1, q1, *first], (feed_back, 0, 0))
    b0 = scatter(0, first_members, first)
    second = cross(0, "down0", "up0")
    run([a1, q1, b0, *second], (middle_back, 0), (attend_back, 0, 0))
    second += cross(0, "out")
    run([q1, b0, *second], (attend_back, 0, 1))
    a0 = scatter(0, second_members, second)
    run([q1, b0, a0], (qkv_back, 0))
    third = cross(0, "qkv")
    run([b0, a0, *third])
    q0 = scatter(0, ["qkv"], third)
    run([a0, q0])
    run([a0, q0])

    input_grad = rec[0]["e_in"][None]
    mlp_shapes = [(layers, hidden, down_weight.shape[2]), up_weight.shape, out_weight.shape]
    qkv_shapes = [qkv_weight.shape, norm_gains.shape, biases.shape, up_bias.shape]
    if blocked():
        down_grad, up_grad, out_grad = finish_mlp(
            spot, [(a0.result, b0.result), (a1.result, b1.result)], mlp_shapes
        )
        run([q0])
        run([q0])
        qkv_grad, gains, shifts, up_sums = finish_qkv(spot, [q0.result, q1.result], qkv_shapes)
        return output, input_grad, qkv_grad, out_grad, up_grad, down_grad, gains, shifts, up_sums
    owned = []
    for r, q, a, b in ((rec[0], q0, a0, b0), (rec[1], q1, a1, b1)):
        down = jnp.concatenate([a.result[0], b.result[0]], axis=1).T
        up = jnp.concatenate([a.result[1], b.result[1]], axis=1)
        up_sum = jnp.concatenate([r["up_sum0"], r["up_sum1"]], axis=1)
        table = lax.psum_scatter(r["small"], AXES, scatter_dimension=1, tiled=True)
        up_sum = lax.psum_scatter(up_sum[0], AXES, scatter_dimension=0, tiled=True)
        owned.append((q.result[0], a.result[2], up, down, table[0:2], table[2:8], up_sum))
    stacked = [jnp.stack([pair[n] for pair in owned]) for n in range(7)]
    return (output, input_grad, *stacked)


def solution(mesh):
    return jax.shard_map(
        local,
        mesh=mesh,
        in_specs=(
            P(("dp", "fsdp"), None, None),
            P(("dp", "fsdp"), None, None),
            P(("dp", "fsdp")),
            P(None, ("dp", "fsdp"), None),
            P(None, ("dp", "fsdp"), None),
            P(None, ("dp", "fsdp"), None),
            P(None, None, ("dp", "fsdp")),
            P(None, None, ("dp", "fsdp")),
            P(None, None, ("dp", "fsdp")),
            P(None, ("dp", "fsdp")),
        ),
        out_specs=(
            P(("dp", "fsdp"), None, None),
            P(("dp", "fsdp"), None, None),
            P(None, ("dp", "fsdp"), None),
            P(None, ("dp", "fsdp"), None),
            P(None, ("dp", "fsdp"), None),
            P(None, None, ("dp", "fsdp")),
            P(None, None, ("dp", "fsdp")),
            P(None, None, ("dp", "fsdp")),
            P(None, ("dp", "fsdp")),
        ),
        check_vma=False,
    )
```

```python
import jax
import jax.numpy as jnp
from jax import lax
from jax.experimental import pallas as pl
from jax.experimental.pallas import tpu as pltpu
from jax.sharding import PartitionSpec as P

HEADS = 12
HEAD_WIDTH = 64
LANES = 128
PAIRS = HEADS * HEAD_WIDTH // LANES
LOW = jnp.bfloat16
WIDE = jnp.float32
norm_eps = 1e-06
AXES = ("dp", "fsdp")
VMEM_LIMIT = 60 * 1024 * 1024
FORWARD_TILE = 768


def cost(flops, moved, hard=0):
    return pl.CostEstimate(flops=int(flops), bytes_accessed=int(moved), transcendentals=int(hard))


def params():
    return pltpu.CompilerParams(vmem_limit_bytes=VMEM_LIMIT)


def vmem_specs(count):
    return [pl.BlockSpec(memory_space=pltpu.VMEM)] * count


def any_specs(count):
    return [pl.BlockSpec(memory_space=pl.ANY)] * count


def dot(a, b):
    return jnp.dot(a, b, preferred_element_type=WIDE)


def dot_nt(a, b):
    return lax.dot_general(a, b, (((1,), (1,)), ((), ())), preferred_element_type=WIDE)


def dot_tn(a, b):
    return lax.dot_general(a, b, (((0,), (0,)), ((), ())), preferred_element_type=WIDE)


def place_of(spot, owner, block):
    z, x, y = spot[0], spot[1], spot[2]
    first, second, zr = block // 8, (block // 4) % 2, block % 4
    bz = lax.rem(z - zr + 4, 4)
    bx = lax.rem(x + jnp.where(owner == 0, second, first), 2)
    by = lax.rem(y + jnp.where(owner == 0, first, second), 2)
    return (bz * 2 + bx) * 2 + by


def piece_copies(spot, refs, target, sems, column, half, sides=(0, 1)):
    c = spot[3]
    rows = refs[0].shape[0] // 8
    copies = []
    for side in sides:
        owner = c if side == 0 else 1 - c
        to = pl.multiple_of(owner * half, LANES)
        for block in range(16):
            start = pl.multiple_of(place_of(spot, owner, block) * rows, 16)
            copies.append(
                pltpu.make_async_copy(
                    refs[2 * side + block // 8].at[
                        pl.ds((block % 8) * rows, rows), pl.ds(column, half)
                    ],
                    target.at[pl.ds(start, rows), pl.ds(to, half)],
                    sems.at[side * 16 + block],
                )
            )
    return copies


def norm_rows(v):
    center = v - jnp.mean(v, axis=-1, keepdims=True)
    r = lax.rsqrt(jnp.mean(center * center, axis=-1, keepdims=True) + norm_eps)
    return center * r, r


def norm_back(v, gain, d):
    xh, r = norm_rows(v)
    dg = d * gain
    m1 = jnp.mean(dg, axis=-1, keepdims=True)
    m2 = jnp.mean(dg * xh, axis=-1, keepdims=True)
    return (
        r * (dg - m1 - xh * m2),
        jnp.sum(d * xh, axis=0, keepdims=True),
        jnp.sum(d, axis=0, keepdims=True),
    )


GAIN1, GAIN2, BQ, BV, BO, BD, SH1, SH2 = range(8)


def qkv_forward(spot, weight, h, table):
    refs, column = weight
    rows, width = h.shape
    wide = 3 * width
    tile = width

    def body(spot_ref, r0, r1, r2, r3, h_ref, t_ref, qkv_ref, a_ref, w_ref, sems):
        copies = piece_copies(spot_ref, (r0, r1, r2, r3), w_ref, sems, column, wide // 2)
        for copy in copies:
            copy.start()
        xh, r = norm_rows(h_ref[...])
        a_ref[...] = (xh * t_ref[GAIN1 : GAIN1 + 1, :] + t_ref[SH1 : SH1 + 1, :]).astype(LOW)
        for copy in copies:
            copy.wait()
        a = a_ref[...]
        for n in range(wide // tile):
            s = n * tile
            out = dot(a, w_ref[:, s : s + tile])
            if s < width:
                out = out + t_ref[BQ : BQ + 1, s : s + tile]
            elif s >= 2 * width:
                out = out + t_ref[BV : BV + 1, s - 2 * width : s - 2 * width + tile]
            qkv_ref[:, s : s + tile] = out.astype(LOW)

    return pl.pallas_call(
        body,
        out_shape=[
            jax.ShapeDtypeStruct((rows, wide), LOW),
            jax.ShapeDtypeStruct((rows, width), LOW),
        ],
        in_specs=[pl.BlockSpec(memory_space=pltpu.SMEM)] + any_specs(4) + vmem_specs(2),
        out_specs=vmem_specs(2),
        scratch_shapes=[pltpu.VMEM((width, wide), LOW), pltpu.SemaphoreType.DMA((32,))],
        compiler_params=params(),
        cost_estimate=cost(2 * rows * width * wide, 2 * width * wide + 9 * rows * width),
        name="qkv_forward",
    )(spot, *refs, h, table)


def attention_forward(lengths, qkv, begin, pairs):
    rows, wide = qkv.shape
    width = pairs * LANES

    def body(len_ref, q_ref, k_ref, v_ref, o_ref, lse_ref):
        pair = pl.program_id(0)
        lane = lax.broadcasted_iota(jnp.int32, (1, LANES), 1)
        key = lax.broadcasted_iota(jnp.int32, (1, rows), 1)
        shut = jnp.where(key < len_ref[0], 0.0, -1e30)
        q = q_ref[...] * jnp.asarray(HEAD_WIDTH**-0.5, LOW)
        k = k_ref[...]
        v = v_ref[...]
        outs = []
        stats = jnp.where(pair == 0, jnp.zeros((rows, LANES), WIDE), lse_ref[...])
        for side in range(2):
            inside = (lane >= HEAD_WIDTH) == (side == 1)
            qs = jnp.where(inside, q, jnp.zeros_like(q))
            s = dot_nt(qs, k) + shut
            peak = jnp.max(s, axis=1, keepdims=True)
            e = jnp.exp(s - peak)
            total = jnp.sum(e, axis=1, keepdims=True)
            p = (e * (1.0 / total)).astype(LOW)
            outs.append(dot(p, v))
            stats = jnp.where(lane == pair * 2 + side, peak + jnp.log(total), stats)
        lse_ref[...] = stats
        o_ref[...] = jnp.where(lane < HEAD_WIDTH, outs[0], outs[1]).astype(LOW)

    return pl.pallas_call(
        body,
        out_shape=[
            jax.ShapeDtypeStruct((rows, width), LOW),
            jax.ShapeDtypeStruct((rows, LANES), WIDE),
        ],
        grid_spec=pltpu.PrefetchScalarGridSpec(
            num_scalar_prefetch=1,
            grid=(pairs,),
            in_specs=[
                pl.BlockSpec((rows, LANES), lambda p, n: (0, p + begin)),
                pl.BlockSpec((rows, LANES), lambda p, n: (0, p + begin + PAIRS)),
                pl.BlockSpec((rows, LANES), lambda p, n: (0, p + begin + 2 * PAIRS)),
            ],
            out_specs=[
                pl.BlockSpec((rows, LANES), lambda p, n: (0, p)),
                pl.BlockSpec((rows, LANES), lambda p, n: (0, 0)),
            ],
        ),
        compiler_params=params(),
        cost_estimate=cost(16 * rows * rows * width, 8 * rows * width, 2 * pairs * rows * rows),
        name="attention_forward",
    )(lengths, qkv, qkv, qkv)


def out_forward(spot, weight, h, mixed, table):
    refs, column = weight
    rows, width = h.shape
    part = width // 2

    def body(
        spot_ref, r0, r1, r2, r3, h_ref, m0_ref, m1_ref, t_ref, h2_ref, a_ref, w_ref, sems
    ):
        copies = piece_copies(spot_ref, (r0, r1, r2, r3), w_ref, sems, column, width // 2)
        for copy in copies:
            copy.start()
        for copy in copies:
            copy.wait()
        product = dot(m0_ref[...], w_ref[:part, :]) + dot(m1_ref[...], w_ref[part:, :])
        h2 = h_ref[...] + (product + t_ref[BO : BO + 1, :])
        h2_ref[...] = h2
        xh, r = norm_rows(h2)
        a_ref[...] = (xh * t_ref[GAIN2 : GAIN2 + 1, :] + t_ref[SH2 : SH2 + 1, :]).astype(LOW)

    return pl.pallas_call(
        body,
        out_shape=[
            jax.ShapeDtypeStruct((rows, width), WIDE),
            jax.ShapeDtypeStruct((rows, width), LOW),
        ],
        in_specs=[pl.BlockSpec(memory_space=pltpu.SMEM)] + any_specs(4) + vmem_specs(4),
        out_specs=vmem_specs(2),
        scratch_shapes=[pltpu.VMEM((width, width), LOW), pltpu.SemaphoreType.DMA((32,))],
        compiler_params=params(),
        cost_estimate=cost(2 * rows * width * width, 2 * width * width + 12 * rows * width),
        name="out_forward",
    )(spot, *refs, h, *mixed, table)


def gelu_parts(u):
    cdf = 0.5 * (1.0 + lax.erf(u * (0.5**0.5)))
    pdf = jnp.exp(-0.5 * u * u) * (0.3989422804014327)
    return cdf, pdf


def side_tiles(tiles):
    def whole(s, n, spot):
        owner = jnp.where(s == 0, spot[3], 1 - spot[3])
        return 0, owner * tiles + n

    def mine(s, n, spot):
        return 0, jnp.where(s == 0, n, tiles - 1)

    def rest(s, n, spot):
        return 0, jnp.where(s == 0, 0, n)

    def fixed(s, n, spot):
        return 0, 0

    return whole, mine, rest, fixed


def mlp_forward(spot, up, down, base, a2, up_bias, table, first):
    rows, width = base.shape
    hidden = up_bias.shape[1]
    half = hidden // 2
    tile = FORWARD_TILE
    tiles = half // tile
    whole, mine, rest, fixed = side_tiles(tiles)
    (up_refs, up_col), (down_refs, down_col) = up, down

    def body(
        spot_ref, h_ref, a_ref, b_ref, t_ref, u0, u1, u2, u3, d0, d1, d2, d3,
        z_ref, g_ref, o_ref, wu_ref, wd_ref, sems_u, sems_d,
    ):
        side, n = pl.program_id(0), pl.program_id(1)
        ups = piece_copies(spot_ref, (u0, u1, u2, u3), wu_ref, sems_u, up_col, half)
        downs = piece_copies(spot_ref, (d0, d1, d2, d3), wd_ref, sems_d, down_col, half)

        @pl.when((side == 0) & (n == 0))
        def begin():
            for copy in ups[:16] + downs[:16] + ups[16:] + downs[16:]:
                copy.start()
            if first:
                o_ref[...] = h_ref[...] + t_ref[BD : BD + 1, :]
            else:
                o_ref[...] = h_ref[...]
            for copy in ups[:16] + downs[:16]:
                copy.wait()

        @pl.when((side == 1) & (n == 0))
        def more():
            for copy in ups[16:] + downs[16:]:
                copy.wait()

        owner = jnp.where(side == 0, spot_ref[3], 1 - spot_ref[3])
        at = pl.ds(pl.multiple_of(owner * half + n * tile, LANES), tile)
        u = dot(a_ref[...], wu_ref[:, at]) + b_ref[...]
        cdf, pdf = gelu_parts(u)
        z = (u * cdf).astype(LOW)
        z_ref[...] = z
        g_ref[...] = (cdf + u * pdf).astype(LOW)
        o_ref[...] += dot_nt(z, wd_ref[:, at])

    return pl.pallas_call(
        body,
        out_shape=[
            jax.ShapeDtypeStruct((rows, hidden), LOW),
            jax.ShapeDtypeStruct((rows, hidden), LOW),
            jax.ShapeDtypeStruct((rows, width), WIDE),
        ],
        grid_spec=pltpu.PrefetchScalarGridSpec(
            num_scalar_prefetch=1,
            grid=(2, tiles),
            in_specs=[
                pl.BlockSpec((rows, width), fixed),
                pl.BlockSpec((rows, width), fixed),
                pl.BlockSpec((1, tile), whole),
                pl.BlockSpec((8, width), fixed),
            ]
            + any_specs(8),
            out_specs=[
                pl.BlockSpec((rows, tile), whole),
                pl.BlockSpec((rows, tile), whole),
                pl.BlockSpec((rows, width), fixed),
            ],
            scratch_shapes=[
                pltpu.VMEM((width, hidden), LOW),
                pltpu.VMEM((width, hidden), LOW),
                pltpu.SemaphoreType.DMA((32,)),
                pltpu.SemaphoreType.DMA((32,)),
            ],
        ),
        compiler_params=params(),
        cost_estimate=cost(
            4 * rows * width * hidden, 4 * width * hidden + 4 * rows * hidden, 2 * rows * hidden
        ),
        name="mlp_forward",
    )(spot, base, a2, up_bias, table, *up_refs, *down_refs)


def block_starts(spot, owner, rows):
    z, x, y = spot[0], spot[1], spot[2]
    result = []
    for block in range(16):
        bz, bx, by = block // 4, (block // 2) % 2, block % 2
        zr = lax.rem(z - bz + 4, 4)
        xr = lax.rem(x + bx, 2)
        yr = lax.rem(y + by, 2)
        first = jnp.where(owner == 0, yr, xr)
        second = jnp.where(owner == 0, xr, yr)
        result.append(pl.multiple_of(((first * 2 + second) * 4 + zr) * rows, 16))
    return result


def put_blocks(value, out_ref, starts, column, width):
    rows = value.shape[0] // 16
    low = value.astype(LOW)
    for block, start in enumerate(starts):
        out_ref[pl.ds(start, rows), pl.ds(column, width)] = low[block * rows : (block + 1) * rows]


def column_sum(value):
    return jnp.sum(value.astype(WIDE), axis=0, keepdims=True)


def mlp_backward(spot, up, down, e, a2, z, slope, before, finish):
    rows, width = e.shape
    hidden = z.shape[1]
    half = hidden // 2
    part = width // 2
    wide = 2 * half + (part if finish else 0)
    (up_refs, up_col), (down_refs, down_col) = up, down
    given = [] if before is None else [before]
    if finish:
        (out_refs, out_col), h2, mixed, table = finish
        given += [h2, *mixed, table]
        moved = [*up_refs, *down_refs, *out_refs]
    else:
        moved = [*up_refs, *down_refs]

    def whole(s, spot):
        return 0, jnp.where(s == 0, spot[3], 1 - spot[3])

    def fixed(s, spot):
        return 0, 0

    def body(spot_ref, e_ref, a_ref, z_ref, s_ref, *refs):
        given_refs, refs = refs[: len(given)], refs[len(given) :]
        moved_refs, refs = refs[: len(moved)], refs[len(moved) :]
        sides_out, refs = refs[:2], refs[2:]
        bd_ref, bu_ref = refs[:2]
        if finish:
            e2_ref, da_ref, sums_ref, acc_ref, wo_ref, mt_ref, ey_ref, sems_o = refs[2:10]
            refs = refs[10:]
            h_ref, m0_ref, m1_ref, t_ref = given_refs[-4:]
        else:
            acc_ref, refs = refs[2], refs[3:]
        wu_ref, wd_ref, em_ref, emt_ref, at_ref, grad_ref, sems_u, sems_d, sems_g = refs
        side = pl.program_id(0)
        c = spot_ref[3]
        ups = piece_copies(spot_ref, moved_refs[:4], wu_ref, sems_u, up_col, half)
        downs = piece_copies(spot_ref, moved_refs[4:8], wd_ref, sems_d, down_col, half)
        copies = ups + downs
        if finish:
            outs = piece_copies(spot_ref, moved_refs[8:], wo_ref, sems_o, out_col, part)

        def stored(n, start, size):
            at = pl.ds(start, size)
            return pltpu.make_async_copy(
                grad_ref.at[n, :, at], sides_out[n].at[:, at], sems_g.at[n, start // (2 * half)]
            )

        @pl.when(side == 0)
        def begin():
            for copy in downs[:16] + ups[:16] + downs[16:] + ups[16:]:
                copy.start()
            if finish:
                for copy in outs:
                    copy.start()
            em = e_ref[...].astype(LOW)
            em_ref[...] = em
            bd_ref[...] = column_sum(em)
            emt_ref[...] = em.T
            at_ref[...] = a_ref[...].T
            acc_ref[...] = jnp.zeros_like(acc_ref) if before is None else given_refs[0][...]
            for copy in downs[:16] + ups[:16]:
                copy.wait()

        @pl.when(side == 1)
        def more():
            for copy in downs[16:] + ups[16:]:
                copy.wait()

        owner = jnp.where(side == 0, c, 1 - c)
        at = pl.ds(pl.multiple_of(owner * half, LANES), half)
        starts = block_starts(spot_ref, owner, width // 16)
        grads = grad_ref.at[side]
        du = (dot(em_ref[...], wd_ref[:, at]) * s_ref[...].astype(WIDE)).astype(LOW)
        bu_ref[...] = column_sum(du)
        put_blocks(dot(emt_ref[...], z_ref[...]), grads, starts, 0, half)
        put_blocks(dot(at_ref[...], du), grads, starts, half, half)
        acc_ref[...] += dot_nt(du, wu_ref[:, at])

        @pl.when(side == 0)
        def first_out():
            stored(0, 0, 2 * half).start()

        @pl.when(side == 1)
        def end():
            stored(1, 0, 2 * half).start()
            if finish:
                mt_ref[:part, :] = m0_ref[...].T
                mt_ref[part:, :] = m1_ref[...].T
                dv, gain, shift = norm_back(
                    h_ref[...], t_ref[GAIN2 : GAIN2 + 1, :], acc_ref[...]
                )
                e2 = e_ref[...] + dv
                e2_ref[...] = e2
                ey = e2.astype(LOW)
                ey_ref[...] = ey
                sums_ref[0:1, :] = gain
                sums_ref[1:2, :] = shift
                sums_ref[2:3, :] = column_sum(ey)
                for copy in outs:
                    copy.wait()
                da_ref[...] = dot_nt(ey, wo_ref[...]).astype(LOW)
                for n, holder in enumerate((c, 1 - c)):
                    to = pl.ds(pl.multiple_of(holder * part, LANES), part)
                    put_blocks(
                        dot(mt_ref[...], ey_ref[:, to]),
                        grad_ref.at[n],
                        block_starts(spot_ref, holder, width // 16),
                        2 * half,
                        part,
                    )
                    stored(n, 2 * half, part).start()
                for n in range(2):
                    stored(n, 2 * half, part).wait()
            for n in range(2):
                stored(n, 0, 2 * half).wait()

    out_shape = [jax.ShapeDtypeStruct((width, wide), LOW)] * 2 + [
        jax.ShapeDtypeStruct((1, width), WIDE),
        jax.ShapeDtypeStruct((1, hidden), WIDE),
    ]
    out_specs = any_specs(2) + [
        pl.BlockSpec((1, width), fixed),
        pl.BlockSpec((1, half), whole),
    ]
    scratch = []
    row_spec = pl.BlockSpec((rows, width), fixed)
    if finish:
        out_shape += [
            jax.ShapeDtypeStruct((rows, width), WIDE),
            jax.ShapeDtypeStruct((rows, width), LOW),
            jax.ShapeDtypeStruct((8, width), WIDE),
        ]
        out_specs += [row_spec, row_spec, pl.BlockSpec((8, width), fixed)]
        scratch += [
            pltpu.VMEM((rows, width), WIDE),
            pltpu.VMEM((width, width), LOW),
            pltpu.VMEM((width, rows), LOW),
            pltpu.VMEM((rows, width), LOW),
            pltpu.SemaphoreType.DMA((32,)),
        ]
    else:
        out_shape += [jax.ShapeDtypeStruct((rows, width), WIDE)]
        out_specs += [row_spec]
    return pl.pallas_call(
        body,
        out_shape=out_shape,
        grid_spec=pltpu.PrefetchScalarGridSpec(
            num_scalar_prefetch=1,
            grid=(2,),
            in_specs=[
                row_spec,
                row_spec,
                pl.BlockSpec((rows, half), whole),
                pl.BlockSpec((rows, half), whole),
            ]
            + [pl.BlockSpec(value.shape, fixed) for value in given]
            + any_specs(len(moved)),
            out_specs=out_specs,
            scratch_shapes=scratch
            + [
                pltpu.VMEM((width, hidden), LOW),
                pltpu.VMEM((width, hidden), LOW),
                pltpu.VMEM((rows, width), LOW),
                pltpu.VMEM((width, rows), LOW),
                pltpu.VMEM((width, rows), LOW),
                pltpu.VMEM((2, width, wide), LOW),
                pltpu.SemaphoreType.DMA((32,)),
                pltpu.SemaphoreType.DMA((32,)),
                pltpu.SemaphoreType.DMA((2, 2)),
            ],
        ),
        compiler_params=params(),
        cost_estimate=cost(8 * rows * width * hidden, 8 * width * hidden + 4 * rows * hidden),
        name="mlp_backward",
    )(spot, e, a2, z, slope, *given, *moved)


def attention_backward(lengths, qkv, da, mixed, lse, begin, pairs):
    rows, wide = qkv.shape
    width = pairs * LANES

    def body(len_ref, q_ref, k_ref, v_ref, d_ref, m_ref, lse_ref, out_ref, row_ref):
        pair = pl.program_id(0)

        @pl.when(pair == 0)
        def start():
            row_ref[...] = lse_ref[...].T

        lane = lax.broadcasted_iota(jnp.int32, (1, LANES), 1)
        sub = lax.broadcasted_iota(jnp.int32, (LANES, 1), 0)
        key = lax.broadcasted_iota(jnp.int32, (rows, 1), 0)
        shut = jnp.where(key < len_ref[0], 0.0, -1e30)
        scale = jnp.asarray(HEAD_WIDTH**-0.5, LOW)
        q = q_ref[...] * scale
        k = k_ref[...]
        v = v_ref[...]
        d = d_ref[...]
        kt = k.T * scale
        prod = (d.astype(WIDE) * m_ref[...].astype(WIDE)).T
        dks, dvs = [], []
        dqt = jnp.zeros((LANES, rows), WIDE)
        for side in range(2):
            inside = (lane >= HEAD_WIDTH) == (side == 1)
            down = (sub >= HEAD_WIDTH) == (side == 1)
            ks = jnp.where(inside, k, jnp.zeros_like(k))
            vs = jnp.where(inside, v, jnp.zeros_like(v))
            kts = jnp.where(down, kt, jnp.zeros_like(kt))
            first = side * HEAD_WIDTH
            delta = jnp.sum(prod[first : first + HEAD_WIDTH], axis=0, keepdims=True)
            log_total = row_ref[pl.ds(pair * 2 + side, 1), :]
            p = jnp.exp((dot_nt(ks, q) + shut) - log_total)
            dp = dot_nt(vs, d)
            dvs.append(dot(p.astype(LOW), d))
            ds = (p * (dp - delta)).astype(LOW)
            dks.append(dot(ds, q))
            dqt = dqt + dot(kts, ds)
        dq = dqt.T
        dk = jnp.where(lane < HEAD_WIDTH, dks[0], dks[1])
        dv = jnp.where(lane < HEAD_WIDTH, dvs[0], dvs[1])
        for n, value in enumerate((dq, dk, dv)):
            at = pl.ds(pl.multiple_of(n * width + pair * LANES, LANES), LANES)
            out_ref[:, at] = value.astype(LOW)

    return pl.pallas_call(
        body,
        out_shape=jax.ShapeDtypeStruct((rows, 3 * width), LOW),
        grid_spec=pltpu.PrefetchScalarGridSpec(
            num_scalar_prefetch=1,
            grid=(pairs,),
            in_specs=[
                pl.BlockSpec((rows, LANES), lambda p, n: (0, p + begin)),
                pl.BlockSpec((rows, LANES), lambda p, n: (0, p + begin + PAIRS)),
                pl.BlockSpec((rows, LANES), lambda p, n: (0, p + begin + 2 * PAIRS)),
                pl.BlockSpec((rows, LANES), lambda p, n: (0, p + begin)),
                pl.BlockSpec((rows, LANES), lambda p, n: (0, p)),
                pl.BlockSpec((rows, LANES), lambda p, n: (0, 0)),
            ],
            out_specs=pl.BlockSpec((rows, 3 * width), lambda p, n: (0, 0)),
            scratch_shapes=[pltpu.VMEM((LANES, rows), WIDE)],
        ),
        compiler_params=params(),
        cost_estimate=cost(40 * rows * rows * width, 16 * rows * width, 2 * pairs * rows * rows),
        name="attention_backward",
    )(lengths, qkv, qkv, qkv, da, mixed, lse)


def qkv_backward(spot, weight, dqkv, e2, h, a1, table, others):
    rows, width = e2.shape
    wide = 3 * width
    half = wide // 2
    part = width // 2
    refs, column = weight
    sums, down_sum, up_sums = others
    hidden = sum(value.shape[1] for value in up_sums)

    def body(
        spot_ref, r0, r1, r2, r3, d0_ref, d1_ref, e_ref, h_ref, a_ref, t_ref,
        s_ref, ds_ref, u0_ref, u1_ref, o_ref, mine_ref, rest_ref, sums_ref,
        w_ref, at_ref, d_ref, acc_ref, row_ref, pack_ref, sems,
    ):
        copies = piece_copies(spot_ref, (r0, r1, r2, r3), w_ref, sems, column, half)
        for copy in copies:
            copy.start()
        at_ref[...] = a_ref[...].T
        for n in range(3):
            for side, ref in enumerate((d0_ref, d1_ref)):
                start = n * width + side * part
                d_ref[:, start : start + part] = ref[:, n * part : (n + 1) * part]
        for copy in copies:
            copy.wait()
        c = spot_ref[3]
        order = []
        for owner, out_ref in ((c, mine_ref), (1 - c, rest_ref)):
            starts = block_starts(spot_ref, owner, width // 16)
            at = pl.ds(pl.multiple_of(owner * half, LANES), half)
            put_blocks(dot(at_ref[...], d_ref[:, at]), out_ref, starts, 0, half)
            order.append((starts, out_ref))
        acc_ref[...] = dot_nt(d_ref[...], w_ref[...])
        dv, gain, shift = norm_back(h_ref[...], t_ref[GAIN1 : GAIN1 + 1, :], acc_ref[...])
        o_ref[...] = e_ref[...] + dv
        row_ref[...] = jnp.zeros_like(row_ref)
        for row, value in (
            (GAIN1, gain),
            (GAIN2, s_ref[0:1, :]),
            (BQ, column_sum(d_ref[:, :width])),
            (BV, column_sum(d_ref[:, 2 * width :])),
            (BO, s_ref[2:3, :]),
            (BD, ds_ref[...]),
            (SH1, shift),
            (SH2, s_ref[1:2, :]),
        ):
            row_ref[row : row + 1, :] = value
        sums_ref[...] = row_ref[0:8, :]
        pack_ref[...] = row_ref[...].T
        share = hidden // 32
        per = u0_ref.shape[1] // share
        for device in range(32):
            at = device * (width // 32)
            ref, start = (u0_ref, u1_ref)[device // per], (device % per) * share
            pack_ref[at : at + 1, LANES - share :] = ref[0:1, start : start + share]
        for starts, out_ref in order:
            put_blocks(pack_ref[...], out_ref, starts, half, LANES)

    return pl.pallas_call(
        body,
        out_shape=[
            jax.ShapeDtypeStruct((rows, width), WIDE),
            jax.ShapeDtypeStruct((width, half + LANES), LOW),
            jax.ShapeDtypeStruct((width, half + LANES), LOW),
            jax.ShapeDtypeStruct((8, width), WIDE),
        ],
        in_specs=[pl.BlockSpec(memory_space=pltpu.SMEM)] + any_specs(4) + vmem_specs(10),
        out_specs=vmem_specs(4),
        scratch_shapes=[
            pltpu.VMEM((width, wide), LOW),
            pltpu.VMEM((width, rows), LOW),
            pltpu.VMEM((rows, wide), LOW),
            pltpu.VMEM((rows, width), WIDE),
            pltpu.VMEM((LANES, width), WIDE),
            pltpu.VMEM((width, LANES), WIDE),
            pltpu.SemaphoreType.DMA((32,)),
        ],
        compiler_params=params(),
        cost_estimate=cost(4 * rows * width * wide, 4 * width * wide + 16 * rows * width),
        name="qkv_backward",
    )(spot, *refs, *dqkv, e2, h, a1, table, sums, down_sum, *up_sums)


def small_forward(spot, refs, column, hidden):
    rows = refs[0].shape[0] // 8
    width = 16 * rows

    def body(spot_ref, r0, r1, t_ref, b_ref, w_ref, sems):
        copies = []
        for block in range(16):
            start = pl.multiple_of(place_of(spot_ref, spot_ref[3], block) * rows, 16)
            copies.append(
                pltpu.make_async_copy(
                    (r0, r1)[block // 8].at[pl.ds((block % 8) * rows, rows), pl.ds(column, LANES)],
                    w_ref.at[pl.ds(start, rows), :],
                    sems.at[block],
                )
            )
        for copy in copies:
            copy.start()
        for copy in copies:
            copy.wait()
        values = w_ref[...].astype(WIDE)
        t_ref[...] = values.T[0:8, :]
        share = hidden // 32
        for device in range(32):
            at = device * (width // 32)
            b_ref[0:1, device * share : (device + 1) * share] = values[
                at : at + 1, LANES - share :
            ]

    return pl.pallas_call(
        body,
        out_shape=[
            jax.ShapeDtypeStruct((8, width), WIDE),
            jax.ShapeDtypeStruct((1, hidden), WIDE),
        ],
        in_specs=[pl.BlockSpec(memory_space=pltpu.SMEM)] + any_specs(2),
        out_specs=vmem_specs(2),
        scratch_shapes=[pltpu.VMEM((width, LANES), LOW), pltpu.SemaphoreType.DMA((16,))],
        compiler_params=params(),
        cost_estimate=cost(0, 4 * width * LANES),
        name="small_forward",
    )(spot, *refs[:2])


def finish_mlp(spot, parts, shapes):
    down_shape, up_shape, out_shape = shapes
    layers = len(parts)
    half = up_shape[2] // 4
    small = out_shape[2] // 2

    def body(spot_ref, *refs):
        down_ref, up_ref, out_ref = refs[-3:]
        c = spot_ref[3]
        at = 0
        for layer in range(layers):
            for part in range(2):
                for owner, ref in ((c, refs[at]), (1 - c, refs[at + 1])):
                    start = pl.multiple_of(part * 2 * half + owner * half, LANES)
                    down_ref[layer, :, pl.ds(start, half)] = ref[:, :half].astype(WIDE)
                    up_ref[layer, :, pl.ds(start, half)] = ref[:, half : 2 * half].astype(WIDE)
                    if part == 0:
                        start = pl.multiple_of(owner * small, LANES)
                        out_ref[layer, :, pl.ds(start, small)] = ref[
                            :, 2 * half : 2 * half + small
                        ].astype(WIDE)
                at = at + 2

    flat = [value for layer in parts for part in layer for value in part]
    return pl.pallas_call(
        body,
        out_shape=[jax.ShapeDtypeStruct(shape, WIDE) for shape in shapes],
        in_specs=[pl.BlockSpec(memory_space=pltpu.SMEM)] + vmem_specs(len(flat)),
        out_specs=vmem_specs(3),
        compiler_params=params(),
        cost_estimate=cost(0, 16 * sum(value.size for value in flat)),
        name="finish_mlp",
    )(spot, *flat)


def finish_qkv(spot, parts, shapes):
    share = shapes[3][1]
    half = shapes[0][2] // 2

    def body(spot_ref, *refs):
        qkv_ref, gain_ref, bias_ref, up_ref = refs[-4:]
        c = spot_ref[3]
        for layer in range(len(parts)):
            kept_ref, got_ref = refs[2 * layer], refs[2 * layer + 1]
            for owner, ref in ((c, kept_ref), (1 - c, got_ref)):
                start = pl.multiple_of(owner * half, LANES)
                qkv_ref[layer, :, pl.ds(start, half)] = ref[:, :half].astype(WIDE)
            packed = kept_ref[:, half : half + LANES]
            columns = packed.T
            gain_ref[layer] = columns[0:2, :]
            for n in range(6):
                bias_ref[n, layer : layer + 1, :] = columns[n + 2 : n + 3, :]
            up_ref[layer : layer + 1, :] = packed[0:1, LANES - share :]

    flat = [value for part in parts for value in part]
    return pl.pallas_call(
        body,
        out_shape=[jax.ShapeDtypeStruct(shape, WIDE) for shape in shapes],
        in_specs=[pl.BlockSpec(memory_space=pltpu.SMEM)] + vmem_specs(len(flat)),
        out_specs=vmem_specs(4),
        compiler_params=params(),
        cost_estimate=cost(0, 8 * sum(value.size for value in flat)),
        name="finish_qkv",
    )(spot, *flat)


def linear(z, x, y, c):
    return ((z * 2 + x) * 2 + y) * 2 + c


def pairs_of(step):
    result = []
    for z in range(4):
        for x in range(2):
            for y in range(2):
                for c in range(2):
                    result.append((linear(z, x, y, c), linear(*step(z, x, y, c))))
    return result


TO_CORE = pairs_of(lambda z, x, y, c: (z, x, y, 1 - c))
TO_Z = [pairs_of(lambda z, x, y, c, n=n: ((z + n) % 4, x, y, c)) for n in range(4)]
TO_XY = pairs_of(lambda z, x, y, c: (z, x, 1 - y, c) if c else (z, 1 - x, y, c))
TO_YX = pairs_of(lambda z, x, y, c: (z, 1 - x, y, c) if c else (z, x, 1 - y, c))


def send(value, pairs):
    return lax.ppermute(value, AXES, pairs)


def blocked():
    return lax.axis_size("dp") == 8 and lax.axis_size("fsdp") == 4


def place():
    if not blocked():
        return jnp.zeros((4,), jnp.int32)
    dp = lax.axis_index("dp")
    fsdp = lax.axis_index("fsdp")
    return jnp.stack([dp // 2, dp % 2, fsdp // 2, fsdp % 2]).astype(jnp.int32)


def halves(pieces):
    low = [piece[:, : piece.shape[1] // 2] for piece in pieces]
    high = [piece[:, piece.shape[1] // 2 :] for piece in pieces]
    return jnp.concatenate(low, axis=1), jnp.concatenate(high, axis=1)


class Chain:
    def __init__(self, steps):
        self.steps = steps
        self.result = None
        self.flying = None
        self.resume(None)

    def resume(self, arrived):
        try:
            self.waiting = self.steps.send(arrived)
        except StopIteration as end:
            self.waiting = None
            self.result = end.value

    def start(self):
        if self.waiting is not None:
            assert self.flying is None
            self.flying = [send(value, pairs) for value, pairs in self.waiting]


def slot(begin, end, work):
    for chain in begin:
        chain.start()
    landing = [chain for chain in end if chain.flying is not None]
    outs = work()
    arrived, outs = lax.optimization_barrier(([chain.flying for chain in landing], outs))
    for chain, values in zip(landing, arrived):
        chain.flying = None
        chain.resume(values)
    return outs


def offsets_of(widths):
    offsets = [0]
    for width in widths:
        offsets.append(offsets[-1] + width // 2)
    return offsets


def gather_whole(pieces):
    whole = [lax.all_gather(piece, AXES, axis=0, tiled=True) for piece in pieces]
    low, high = [
        part.reshape(4, 2, 2, -1, part.shape[1])[jnp.array([0, 3, 2, 1])] for part in halves(whole)
    ]
    width = low.shape[-1]
    own = low.transpose(2, 1, 0, 3, 4).reshape(2, -1, width)
    other = high.transpose(1, 2, 0, 3, 4).reshape(2, -1, width)
    return own[0], own[1], other[0], other[1]


def gather_steps(pieces, block):
    if not blocked():
        return gather_whole(pieces)
    ring = yield [(block, TO_Z[n]) for n in (1, 2, 3)]
    stack = jnp.concatenate([block, *ring], axis=0)
    (got,) = yield [(stack, TO_XY)]
    near = jnp.concatenate([stack, got], axis=0)
    far, near_got = yield [(near, TO_YX), (near, TO_CORE)]
    (far_got,) = yield [(far, TO_CORE)]
    return near, far, near_got, far_got


def scatter_whole(mine, rest, start, half):
    mine, rest = mine[:, start : start + half], rest[:, start : start + half]
    rows = mine.shape[0] // 16
    low = mine.reshape(2, 2, 4, rows, half).transpose(2, 1, 0, 3, 4)
    high = rest.reshape(2, 2, 4, rows, half).transpose(2, 0, 1, 3, 4)
    whole = jnp.concatenate([low, high], axis=-1)[jnp.array([0, 3, 2, 1])]
    whole = whole.reshape(16 * rows, 2 * half)
    return lax.psum_scatter(whole, AXES, scatter_dimension=0, tiled=True).astype(WIDE)


def added(parts):
    total = parts[0].astype(WIDE)
    for part in parts[1:]:
        total = total + part.astype(WIDE)
    return total


def scatter_steps(spot, mine, rest):
    if not blocked():
        return mine, rest
    rows = mine.shape[0] // 16
    four, two, one = slice(8 * rows, 16 * rows), slice(4 * rows, 8 * rows), slice(0, 4 * rows)
    (got,) = yield [(rest, TO_CORE)]
    (got_a,) = yield [(added([mine[four], got[four]]).astype(LOW), TO_YX)]
    (got_b,) = yield [(added([mine[two], got[two], got_a[two]]).astype(LOW), TO_XY)]
    total = added([mine[one], got[one], got_a[one], got_b])
    blocks = [total[n * rows : (n + 1) * rows] for n in range(4)]
    arrived = yield [(blocks[n].astype(LOW), TO_Z[4 - n]) for n in (1, 2, 3)]
    total = added([blocks[0], *arrived])
    low, high = total[: rows // 2], total[rows // 2 :]
    kept = jnp.where(spot[3] == 0, low, high)
    (got,) = yield [(jnp.where(spot[3] == 0, high, low).astype(LOW), TO_CORE)]
    return kept, got


def pack_small(gains, shifts, up_bias):
    rows = gains.shape[1]
    columns = jnp.concatenate([gains, shifts], axis=0).T
    share = up_bias.shape[0]
    first = jnp.pad(columns, ((0, 0), (0, LANES - share - columns.shape[1])))
    second = jnp.pad(up_bias[None, :], ((0, rows - 1), (0, 0)))
    packed = jnp.concatenate([first, second], axis=1)
    return jnp.concatenate([packed, packed], axis=1)


def whole_small(gains, shifts, up_bias):
    both = jnp.concatenate([gains, shifts], axis=0)
    table = lax.all_gather(both, AXES, axis=1, tiled=True)
    return table.astype(WIDE), lax.all_gather(up_bias, AXES, axis=0, tiled=True)[None].astype(WIDE)


def local(
    hidden_in,
    cotangent,
    lengths,
    qkv_weight,
    out_weight,
    up_weight,
    down_weight,
    norm_gains,
    biases,
    up_bias,
):
    clips, slots, width = hidden_in.shape
    layers = qkv_weight.shape[0]
    share = up_bias.shape[1]
    hidden = down_weight.shape[1]
    half = hidden // 2
    assert clips == 1 and layers == 2
    spot = place()
    chunks = []
    for i in range(layers):
        gains, shifts, bias = (v[i].astype(LOW) for v in (norm_gains, biases, up_bias))
        up = up_weight[i].astype(LOW)
        down = down_weight[i].T.astype(LOW)
        first = [qkv_weight[i].astype(LOW)]
        if blocked():
            first.append(pack_small(gains, shifts, bias))
        chunks.append(first)
        chunks.append([out_weight[i].astype(LOW), up[:, :half], down[:, :half]])
        chunks.append([up[:, half:], down[:, half:]])
    spots = [offsets_of([piece.shape[1] for piece in pieces]) for pieces in chunks]

    def both_cores(pieces):
        low, high = halves(pieces)
        mine = jnp.where(spot[3] == 0, low, high)
        got = send(jnp.where(spot[3] == 0, high, low), TO_CORE)
        upper = jnp.concatenate([mine, got], axis=0)
        return jnp.where(spot[3] == 0, upper, jnp.concatenate([got, mine], axis=0))

    if blocked():
        rest = both_cores([piece for pieces in chunks[1:] for piece in pieces])
        blocks = [both_cores(chunks[0])]
        start = 0
        for at in spots[1:]:
            blocks.append(rest[:, start : start + at[-1]])
            start = start + at[-1]
    else:
        blocks = [None] * len(chunks)
    q0, a0, b0, q1, a1, b1 = [Chain(gather_steps(p, block)) for p, block in zip(chunks, blocks)]

    def weight(index, member):
        chain = (q0, a0, b0, q1, a1, b1)[index]
        return chain.result, spots[index][member]

    def small_of(i):
        if blocked():
            return small_forward(spot, q0.result if i == 0 else q1.result, spots[3 * i][1], hidden)
        return whole_small(norm_gains[i].astype(LOW), biases[i].astype(LOW), up_bias[i].astype(LOW))

    pairs = PAIRS // 2
    rec = [{"h": hidden_in[0]}, {}]

    def norm_and_qkv(i):
        r = rec[i]
        table, bias = small_of(i)
        qkv, first = qkv_forward(spot, weight(3 * i, 0), r["h"], table)
        return {"table": table, "bias": bias, "qkv": qkv, "a1": first}

    def attend(i, side):
        mixed, lse = attention_forward(lengths, rec[i]["qkv"], side * pairs, pairs)
        return {f"mixed{side}": mixed, f"lse{side}": lse}

    def project(i):
        r = rec[i]
        h2, second = out_forward(
            spot, weight(3 * i + 1, 0), r["h"], (r["mixed0"], r["mixed1"]), r["table"]
        )
        return {"h2": h2, "a2": second}

    def feed_weights(i, side):
        return weight(3 * i + 1 + side, 1 - side), weight(3 * i + 1 + side, 2 - side)

    def feed(i, side):
        r = rec[i]
        z, slope, total = mlp_forward(
            spot,
            *feed_weights(i, side),
            r["total"] if side else r["h2"],
            r["a2"],
            r["bias"][:, side * half : (side + 1) * half],
            r["table"],
            side == 0,
        )
        return {f"z{side}": z, f"slope{side}": slope, "total": total}

    def feed_back(i, side):
        r = rec[i]
        finish = None
        if side == 0:
            finish = (weight(3 * i + 1, 0), r["h2"], (r["mixed0"], r["mixed1"]), r["table"])
        mine, rest, down_sum, up_sum, *others = mlp_backward(
            spot,
            *feed_weights(i, side),
            r["e"],
            r["a2"],
            r[f"z{side}"],
            r[f"slope{side}"],
            None if side else r["acc"],
            finish,
        )
        found = {f"part{side}": (mine, rest), "down_sum": down_sum, f"up_sum{side}": up_sum}
        return {**found, **dict(zip(("e2", "da", "sums2") if finish else ("acc",), others))}

    def attend_back(i, side):
        r = rec[i]
        dqkv = attention_backward(
            lengths, r["qkv"], r["da"], r[f"mixed{side}"], r[f"lse{side}"], side * pairs, pairs
        )
        return {f"dqkv{side}": dqkv}

    def qkv_back(i):
        r = rec[i]
        e, mine, rest, table = qkv_backward(
            spot,
            weight(3 * i, 0),
            (r["dqkv0"], r["dqkv1"]),
            r["e2"],
            r["h"],
            r["a1"],
            r["table"],
            (r["sums2"], r["down_sum"], (r["up_sum0"], r["up_sum1"])),
        )
        return {"e_in": e, "qkv": (mine, rest), "small": table}

    def run(begin, end, *work):
        def todo():
            before = [dict(r) for r in rec]
            found = []
            for function, i, *rest in work:
                new = function(i, *rest)
                rec[i].update(new)
                found.append(new)
            for r, old in zip(rec, before):
                r.clear()
                r.update(old)
            return found

        for (function, i, *rest), new in zip(work, slot(begin, end, todo)):
            rec[i].update(new)

    run([q0], [q0])
    run([q0, a0], [q0])
    run([q0], [q0, a0])
    run([q0, a0, b0], [q0])
    run([], [a0], (norm_and_qkv, 0))
    run([a0], [b0], (attend, 0, 0))
    run([b0, q1], [a0], (attend, 0, 1))
    run([a0], [a0, b0])
    run([b0], [b0, q1], (project, 0), (feed, 0, 0))
    run([b0, q1, a1], [b0, q1])
    run([q1], [q1, a1], (feed, 0, 1))
    rec[1]["h"] = rec[0]["total"]
    run([q1, a1, b1], [q1])
    run([], [a1], (norm_and_qkv, 1))
    run([a1], [b1], (attend, 1, 0))
    run([b1], [a1, b1], (attend, 1, 1))
    run([a1, b1], [a1])
    run([], [b1], (project, 1), (feed, 1, 0))
    run([b1], [b1])
    run([], [], (feed, 1, 1))
    output = rec[1]["total"][None]

    def scatter(i, member):
        return Chain(scatter_steps(spot, *rec[i][member]))

    rec[1]["e"] = cotangent[0]
    run([], [], (feed_back, 1, 1))
    b1 = scatter(1, "part1")
    run([b1], [b1], (feed_back, 1, 0))
    a1 = scatter(1, "part0")
    run([b1, a1], [b1, a1], (attend_back, 1, 0))
    run([b1, a1], [b1], (attend_back, 1, 1))
    run([b1], [b1, a1], (qkv_back, 1))
    rec[0]["e"] = rec[1]["e_in"]
    q1 = scatter(1, "qkv")
    run([b1, a1, q1], [b1, a1, q1], (feed_back, 0, 1))
    b0 = scatter(0, "part1")
    run([a1, q1, b0], [a1, q1, b0], (feed_back, 0, 0))
    a0 = scatter(0, "part0")
    run([a1, q1, b0, a0], [a1, q1, a0], (attend_back, 0, 0))
    run([q1], [b0], (attend_back, 0, 1))
    run([b0, a0], [q1, b0], (qkv_back, 0))
    q0 = scatter(0, "qkv")
    run([b0, q1, q0], [a0, q0])
    run([a0, q0], [b0, a0])
    run([a0, b0], [q0, q1, b0])
    run([q0], [q0, a0])
    run([q0, a0], [a0])

    input_grad = rec[0]["e_in"][None]
    down_shape = (layers, down_weight.shape[2], hidden)
    mlp_shapes = [down_shape, up_weight.shape, out_weight.shape]
    bias_shape = (biases.shape[1], layers, biases.shape[2])
    qkv_shapes = [qkv_weight.shape, norm_gains.shape, bias_shape, up_bias.shape]
    if blocked():
        down_grad, up_grad, out_grad = finish_mlp(
            spot, [(a0.result, b0.result), (a1.result, b1.result)], mlp_shapes
        )
        run([], [q0])
        run([q0], [q0])
        qkv_grad, gains, shifts, up_sums = finish_qkv(spot, [q0.result, q1.result], qkv_shapes)
        shifts = jnp.swapaxes(shifts, 0, 1)
        down_grad = jnp.swapaxes(down_grad, 1, 2)
        return output, input_grad, qkv_grad, out_grad, up_grad, down_grad, gains, shifts, up_sums
    owned = []
    for r, q, a, b in ((rec[0], q0, a0, b0), (rec[1], q1, a1, b1)):
        quarter = half // 2
        down = [scatter_whole(*part.result, 0, quarter) for part in (a, b)]
        up = [scatter_whole(*part.result, quarter, quarter) for part in (a, b)]
        out = scatter_whole(*a.result, half, width // 2)
        up_sum = jnp.concatenate([r["up_sum0"], r["up_sum1"]], axis=1)
        table = lax.psum_scatter(r["small"], AXES, scatter_dimension=1, tiled=True)
        up_sum = lax.psum_scatter(up_sum[0], AXES, scatter_dimension=0, tiled=True)
        down, up = jnp.concatenate(down, axis=1).T, jnp.concatenate(up, axis=1)
        first = scatter_whole(*q.result, 0, 3 * width // 2)
        owned.append((first, out, up, down, table[0:2], table[2:8], up_sum))
    stacked = [jnp.stack([pair[n] for pair in owned]) for n in range(7)]
    return (output, input_grad, *stacked)


def solution(mesh):
    return jax.shard_map(
        local,
        mesh=mesh,
        in_specs=(
            P(("dp", "fsdp"), None, None),
            P(("dp", "fsdp"), None, None),
            P(("dp", "fsdp")),
            P(None, ("dp", "fsdp"), None),
            P(None, ("dp", "fsdp"), None),
            P(None, ("dp", "fsdp"), None),
            P(None, None, ("dp", "fsdp")),
            P(None, None, ("dp", "fsdp")),
            P(None, None, ("dp", "fsdp")),
            P(None, ("dp", "fsdp")),
        ),
        out_specs=(
            P(("dp", "fsdp"), None, None),
            P(("dp", "fsdp"), None, None),
            P(None, ("dp", "fsdp"), None),
            P(None, ("dp", "fsdp"), None),
            P(None, ("dp", "fsdp"), None),
            P(None, None, ("dp", "fsdp")),
            P(None, None, ("dp", "fsdp")),
            P(None, None, ("dp", "fsdp")),
            P(None, ("dp", "fsdp")),
        ),
        check_vma=False,
    )
```

```python
import jax
import jax.numpy as jnp
from jax import lax
from jax.experimental import pallas as pl
from jax.experimental.pallas import tpu as pltpu
from jax.sharding import Mesh
from jax.sharding import PartitionSpec as P

HEADS = 12
HEAD_WIDTH = 64
LANES = 128
PAIRS = HEADS * HEAD_WIDTH // LANES
LOW = jnp.bfloat16
WIDE = jnp.float32
norm_eps = 1e-06
AXES = ("dp", "y", "c")
WHOLE, Z_LAST, Z_NEXT = range(3)
JOINED = (False, False)
ORDERS = (Z_LAST, Z_NEXT)
TURNS = (((1, 2, 3),),) * 6
VMEM_LIMIT = 60 * 1024 * 1024
TILE = 768


def cost(flops, moved, hard=0):
    return pl.CostEstimate(
        flops=int(flops) // 64, bytes_accessed=int(moved) // 64, transcendentals=int(hard) // 64
    )


def params():
    return pltpu.CompilerParams(vmem_limit_bytes=VMEM_LIMIT)


def vmem_specs(count):
    return [pl.BlockSpec(memory_space=pltpu.VMEM)] * count


def any_specs(count):
    return [pl.BlockSpec(memory_space=pl.ANY)] * count


def launch(body, args, after, prefetch, grid, in_specs, out_specs, out_shape, scratch, moved, name):
    count = len(args)

    def trimmed(*refs):
        body(*refs[:count], *refs[count + len(after) :])

    return pl.pallas_call(
        trimmed,
        out_shape=out_shape,
        grid_spec=pltpu.PrefetchScalarGridSpec(
            num_scalar_prefetch=prefetch,
            grid=grid,
            in_specs=in_specs + any_specs(len(after)),
            out_specs=out_specs,
            scratch_shapes=scratch,
        ),
        compiler_params=params(),
        cost_estimate=moved,
        name=name,
    )(*args, *after)


def smem_spec():
    return [pl.BlockSpec(memory_space=pltpu.SMEM)]


def dot(a, b):
    return jnp.dot(a, b, preferred_element_type=WIDE)


def dot_nt(a, b):
    return lax.dot_general(a, b, (((1,), (1,)), ((), ())), preferred_element_type=WIDE)


def dot_tn(a, b):
    return lax.dot_general(a, b, (((0,), (0,)), ((), ())), preferred_element_type=WIDE)


def place_of(spot, owner, block, z_first):
    z, x, y = spot[0], spot[1], spot[2]
    first, second, zr = block // 8, (block // 4) % 2, block % 4
    if not z_first:
        second, zr = block % 2, (block // 2) % 4
    bz = lax.rem(z - zr + 4, 4)
    bx = lax.rem(x + jnp.where(owner == 0, second, first), 2)
    by = lax.rem(y + jnp.where(owner == 0, first, second), 2)
    return (bz * 2 + bx) * 2 + by


def side_copies(spot, weight, refs, side, target, sems, width):
    arrays, column, z_first = weight
    at = pl.ds(column, width)
    if len(arrays) == 2:
        return [pltpu.make_async_copy(refs[side].at[:, at], target, sems.at[side, 0])]
    owner = spot[3] if side == 0 else 1 - spot[3]
    rows = arrays[0].shape[0] // 8
    copies = []
    for block in range(16):
        start = pl.multiple_of(place_of(spot, owner, block, z_first) * rows, 16)
        copies.append(
            pltpu.make_async_copy(
                refs[2 * side + block // 8].at[pl.ds((block % 8) * rows, rows), at],
                target.at[pl.ds(start, rows), :],
                sems.at[side, block],
            )
        )
    return copies


def start_all(*groups):
    for copies in groups:
        for copy in copies:
            copy.start()


def wait_all(*groups):
    for copies in groups:
        for copy in copies:
            copy.wait()


def norm_rows(v):
    center = v - jnp.mean(v, axis=-1, keepdims=True)
    r = lax.rsqrt(jnp.mean(center * center, axis=-1, keepdims=True) + norm_eps)
    return center * r, r


def norm_back(v, gain, d):
    xh, r = norm_rows(v)
    dg = d * gain
    m1 = jnp.mean(dg, axis=-1, keepdims=True)
    m2 = jnp.mean(dg * xh, axis=-1, keepdims=True)
    return (
        r * (dg - m1 - xh * m2),
        jnp.sum(d * xh, axis=0, keepdims=True),
        jnp.sum(d, axis=0, keepdims=True),
    )


GAIN1, GAIN2, BQ, BV, BO, BD, SH1, SH2 = range(8)


def qkv_forward(spot, weight, h, hidden, devices, after):
    rows, width = h.shape
    wide = 3 * width
    half = wide // 2
    refs = weight[0]

    def body(spot_ref, *rest):
        h_ref, qkv_ref, a_ref, t_ref, b_ref = rest[len(refs) : len(refs) + 5]
        w_ref, row_ref, sems = rest[len(refs) + 5 :]
        c = spot_ref[3]
        own, other = [
            side_copies(spot_ref, weight, rest, side, w_ref.at[side], sems, half + LANES)
            for side in range(2)
        ]
        start_all(own, other)
        xh, r = norm_rows(h_ref[...])
        wait_all(own)
        values = w_ref[0, :, half:].astype(WIDE)
        table = values.T[0:8, :]
        t_ref[...] = table
        share = hidden // devices
        for device in range(devices):
            at = device * (width // devices)
            b_ref[0:1, device * share : (device + 1) * share] = values[
                at : at + 1, LANES - share :
            ]
        row_ref[:, :width] = table[BQ : BQ + 1]
        row_ref[:, width : 2 * width] = jnp.zeros((1, width), WIDE)
        row_ref[:, 2 * width :] = table[BV : BV + 1]
        a = (xh * table[GAIN1 : GAIN1 + 1] + table[SH1 : SH1 + 1]).astype(LOW)
        a_ref[...] = a
        for side, owner in enumerate((c, 1 - c)):
            if side == 1:
                wait_all(other)
            to = pl.ds(pl.multiple_of(owner * half, LANES), half)
            qkv_ref[:, to] = (dot(a_ref[...], w_ref[side, :, :half]) + row_ref[:, to]).astype(LOW)

    return launch(
        body,
        [spot, *refs, h],
        after,
        prefetch=0,
        grid=(),
        in_specs=smem_spec() + any_specs(len(refs)) + vmem_specs(1),
        out_specs=vmem_specs(4),
        out_shape=[
            jax.ShapeDtypeStruct((rows, wide), LOW),
            jax.ShapeDtypeStruct((rows, width), LOW),
            jax.ShapeDtypeStruct((8, width), WIDE),
            jax.ShapeDtypeStruct((1, hidden), WIDE),
        ],
        scratch=[
            pltpu.VMEM((2, width, half + LANES), LOW),
            pltpu.VMEM((1, wide), WIDE),
            pltpu.SemaphoreType.DMA((2, 16)),
        ],
        moved=cost(2 * rows * width * wide, 2 * width * wide + 9 * rows * width),
        name="qkv_forward",
    )


def attention_forward(lengths, qkv, after):
    rows, wide = qkv.shape
    width = wide // 3

    def body(len_ref, q_ref, k_ref, v_ref, o_ref, lse_ref):
        pair = pl.program_id(0)
        lane = lax.broadcasted_iota(jnp.int32, (1, LANES), 1)
        key = lax.broadcasted_iota(jnp.int32, (1, rows), 1)
        shut = jnp.where(key < len_ref[0], 0.0, -1e30)
        q = q_ref[...] * jnp.asarray(HEAD_WIDTH**-0.5, LOW)
        k = k_ref[...]
        v = v_ref[...]
        outs = []
        stats = jnp.where(pair == 0, jnp.zeros((rows, LANES), WIDE), lse_ref[...])
        for side in range(2):
            inside = (lane >= HEAD_WIDTH) == (side == 1)
            qs = jnp.where(inside, q, jnp.zeros_like(q))
            s = dot_nt(qs, k) + shut
            peak = jnp.max(s, axis=1, keepdims=True)
            e = jnp.exp(s - peak)
            total = jnp.sum(e, axis=1, keepdims=True)
            p = (e * (1.0 / total)).astype(LOW)
            outs.append(dot(p, v))
            stats = jnp.where(lane == pair * 2 + side, peak + jnp.log(total), stats)
        lse_ref[...] = stats
        o_ref[...] = jnp.where(lane < HEAD_WIDTH, outs[0], outs[1]).astype(LOW)

    return launch(
        body,
        [lengths, qkv, qkv, qkv],
        after,
        out_shape=[
            jax.ShapeDtypeStruct((rows, width), LOW),
            jax.ShapeDtypeStruct((rows, LANES), WIDE),
        ],
        prefetch=1,
        grid=(PAIRS,),
        in_specs=[
            pl.BlockSpec((rows, LANES), lambda p, n: (0, p)),
            pl.BlockSpec((rows, LANES), lambda p, n: (0, p + PAIRS)),
            pl.BlockSpec((rows, LANES), lambda p, n: (0, p + 2 * PAIRS)),
        ],
        out_specs=[
            pl.BlockSpec((rows, LANES), lambda p, n: (0, p)),
            pl.BlockSpec((rows, LANES), lambda p, n: (0, 0)),
        ],
        moved=cost(16 * rows * rows * width, 8 * rows * width, HEADS * rows * rows),
        scratch=[],
        name="attention_forward",
    )


def gelu_parts(u):
    cdf = 0.5 * (1.0 + lax.erf(u * (0.5**0.5)))
    pdf = jnp.exp(-0.5 * u * u) * (0.3989422804014327)
    return cdf, pdf


def up_forward(spot, weight, out_weight, h, mixed, up_bias, table, after):
    rows, width = h.shape
    hidden = up_bias.shape[1]
    half = hidden // 2
    part = width // 2
    tile = TILE
    tiles = half // tile
    refs = weight[0]

    def body(spot_ref, *rest):
        w_refs, rest = rest[: len(refs)], rest[len(refs) :]
        (
            h_ref, m_ref, b_ref, t_ref, h2_ref, a_ref, z_out, s_out,
            w_ref, wo_ref, z_ref, s_ref, sems, sems_o, sems_t,
        ) = rest
        c = spot_ref[3]
        outs = [
            side_copies(spot_ref, out_weight, w_refs, side, wo_ref.at[side], sems_o, part)
            for side in range(2)
        ]
        sides = [
            side_copies(spot_ref, weight, w_refs, side, w_ref.at[side], sems, half)
            for side in range(2)
        ]
        start_all(*outs, *sides)
        wait_all(*outs)
        for side, owner in enumerate((c, 1 - c)):
            to = pl.ds(pl.multiple_of(owner * part, LANES), part)
            h2_ref[:, to] = h_ref[:, to] + (
                dot(m_ref[...], wo_ref[side]) + t_ref[BO : BO + 1, to]
            )
        xh, r = norm_rows(h2_ref[...])
        a_ref[...] = (xh * t_ref[GAIN2 : GAIN2 + 1, :] + t_ref[SH2 : SH2 + 1, :]).astype(LOW)

        def stored(step):
            side, n = step // tiles, lax.rem(step, tiles)
            owner = jnp.where(side == 0, c, 1 - c)
            at = pl.ds(pl.multiple_of(owner * half + n * tile, LANES), tile)
            return side, n, at, [
                pltpu.make_async_copy(ref.at[:, at], out.at[:, at], sems_t.at[which, step])
                for which, (ref, out) in enumerate(((z_ref, z_out), (s_ref, s_out)))
            ]

        def work(step, carry):
            side, n, at, copies = stored(step)

            for which in range(2):

                @pl.when(step == which * tiles)
                def ready():
                    wait_all(sides[which])

            up = pl.ds(pl.multiple_of(n * tile, LANES), tile)
            u = dot(a_ref[...], w_ref[side, :, up]) + b_ref[:, at]
            cdf, pdf = gelu_parts(u)
            z_ref[:, at] = (u * cdf).astype(LOW)
            s_ref[:, at] = (cdf + u * pdf).astype(LOW)
            start_all(copies)
            return carry

        lax.fori_loop(0, 2 * tiles, work, 0)
        for step in range(2 * tiles):
            wait_all(stored(step)[3])

    return launch(
        body,
        [spot, *refs, h, mixed, up_bias, table],
        after,
        prefetch=0,
        grid=(),
        in_specs=smem_spec() + any_specs(len(refs)) + vmem_specs(4),
        out_specs=vmem_specs(2) + any_specs(2),
        out_shape=[
            jax.ShapeDtypeStruct((rows, width), WIDE),
            jax.ShapeDtypeStruct((rows, width), LOW),
            jax.ShapeDtypeStruct((rows, hidden), LOW),
            jax.ShapeDtypeStruct((rows, hidden), LOW),
        ],
        scratch=[
            pltpu.VMEM((2, width, half), LOW),
            pltpu.VMEM((2, width, part), LOW),
            pltpu.VMEM((rows, hidden), LOW),
            pltpu.VMEM((rows, hidden), LOW),
            pltpu.SemaphoreType.DMA((2, 16)),
            pltpu.SemaphoreType.DMA((2, 16)),
            pltpu.SemaphoreType.DMA((2, 2 * tiles)),
        ],
        moved=cost(
            2 * rows * width * hidden, 2 * width * hidden + 4 * rows * hidden, 2 * rows * hidden
        ),
        name="up_forward",
    )


def down_forward(spot, weight, h2, z, table, after):
    rows, width = h2.shape
    hidden = z.shape[1]
    half = hidden // 2
    refs = weight[0]

    def body(spot_ref, *rest):
        h_ref, z_in, t_ref, o_ref, w_ref, z_ref, sems, sems_r = rest[len(refs) :]
        c = spot_ref[3]
        sides = [
            side_copies(spot_ref, weight, rest, side, w_ref.at[side], sems, half)
            for side in range(2)
        ]
        loads = []
        for side, owner in enumerate((c, 1 - c)):
            at = pl.ds(pl.multiple_of(owner * half, LANES), half)
            loads.append(
                [pltpu.make_async_copy(z_in.at[:, at], z_ref.at[side], sems_r.at[side])]
            )
        start_all(sides[0], loads[0], sides[1], loads[1])
        total = h_ref[...] + t_ref[BD : BD + 1, :]
        for side in range(2):
            wait_all(sides[side], loads[side])
            total = total + dot_nt(z_ref[side], w_ref[side])
        o_ref[...] = total

    return launch(
        body,
        [spot, *refs, h2, z, table],
        after,
        prefetch=0,
        grid=(),
        in_specs=smem_spec()
        + any_specs(len(refs))
        + vmem_specs(1)
        + any_specs(1)
        + vmem_specs(1),
        out_specs=vmem_specs(1),
        out_shape=[jax.ShapeDtypeStruct((rows, width), WIDE)],
        scratch=[
            pltpu.VMEM((2, width, half), LOW),
            pltpu.VMEM((2, rows, half), LOW),
            pltpu.SemaphoreType.DMA((2, 16)),
            pltpu.SemaphoreType.DMA((2,)),
        ],
        moved=cost(2 * rows * width * hidden, 2 * width * hidden + 2 * rows * hidden),
        name="down_forward",
    )[0]


def block_starts(spot, owner, rows, order):
    if order == WHOLE:
        return [block * rows for block in range(16)]
    z, x, y = spot[0], spot[1], spot[2]
    result = []
    for block in range(16):
        bz, bx, by = block // 4, (block // 2) % 2, block % 2
        zr = lax.rem(z - bz + 4, 4)
        xr = lax.rem(x + bx, 2)
        yr = lax.rem(y + by, 2)
        first = jnp.where(owner == 0, yr, xr)
        second = jnp.where(owner == 0, xr, yr)
        place = (first * 2 + second) * 4 + zr if order == Z_LAST else (first * 4 + zr) * 2 + second
        result.append(pl.multiple_of(place * rows, 16))
    return result


def put_blocks(value, out_ref, starts, column, width):
    rows = value.shape[0] // 16
    low = value.astype(LOW)
    for block, start in enumerate(starts):
        out_ref[pl.ds(start, rows), pl.ds(column, width)] = low[block * rows : (block + 1) * rows]


def column_sum(value):
    return jnp.sum(value.astype(WIDE), axis=0, keepdims=True)


def mlp_backward(
    spot, up, down, out_weight, e, a2, z, slope, h2, mixed, table, joined, order, after
):
    rows, width = e.shape
    hidden = z.shape[1]
    half = hidden // 2
    part = width // 2
    tile = TILE
    tiles = half // tile
    wide = hidden + part
    refs, down_refs = up[0], down[0]
    near = half + part
    widths = [wide] if joined else [near, half]

    def body(spot_ref, *rest):
        w_refs, rest = rest[: len(refs)], rest[len(refs) :]
        d_refs, rest = rest[: len(down_refs)], rest[len(down_refs) :]
        buffers = [rest[7 + 2 * n : 9 + 2 * n] for n in range(len(widths))]
        rest = rest[:7] + rest[7 + 2 * len(widths) :]
        (
            e_in, a_in, z_in, s_in, h_in, m_in, t_ref,
            bd_ref, bu_ref, e2_ref, da_ref, sums_ref,
            w_ref, wo_ref, e_ref, a_ref, z_ref, s_ref, h_ref, m_ref,
            em_ref, emt_ref, at_ref, acc_ref, grad_ref, sems, sems_d, sems_o, sems_r, sems_g,
        ) = rest
        c = spot_ref[3]
        loads = [
            pltpu.make_async_copy(source, target, sems_r.at[n])
            for n, (source, target) in enumerate(
                (
                    (e_in, e_ref), (a_in, a_ref), (z_in, z_ref), (s_in, s_ref), (h_in, h_ref),
                    (m_in, m_ref),
                )
            )
        ]
        sides = [
            side_copies(spot_ref, down, d_refs, side, w_ref.at[side, 1], sems_d, half)
            + side_copies(spot_ref, up, w_refs, side, w_ref.at[side, 0], sems, half)
            for side in range(2)
        ]
        outs = [
            side_copies(spot_ref, out_weight, w_refs, side, wo_ref.at[side], sems_o, part)
            for side in range(2)
        ]
        start_all(loads[:2], sides[0], loads[2:4], sides[1], loads[4:], *outs)
        wait_all(loads[:1])
        em = e_ref[...].astype(LOW)
        em_ref[...] = em
        bd_ref[...] = column_sum(em)
        emt_ref[...] = em.T
        wait_all(loads[1:2])
        at_ref[...] = a_ref[...].T
        acc_ref[...] = jnp.zeros_like(acc_ref)

        def stored(side, which):
            start, size = ((0, half), (half, part), (near, half))[which]
            out, to = buffers[-1][side], start
            if not joined:
                out, to = (buffers[1][side], 0) if which == 2 else (buffers[0][side], start)
            return pltpu.make_async_copy(
                grad_ref.at[side, :, pl.ds(start, size)],
                out.at[:, pl.ds(to, size)],
                sems_g.at[side, which],
            )

        def work(step, carry):
            side, n = step // tiles, lax.rem(step, tiles)
            owner = jnp.where(side == 0, c, 1 - c)

            @pl.when(step == 0)
            def first_ready():
                wait_all(sides[0], loads[2:4])

            @pl.when(step == tiles)
            def second_ready():
                stored(0, 0).start()
                stored(0, 2).start()
                wait_all(sides[1])

            at = pl.ds(pl.multiple_of(owner * half + n * tile, LANES), tile)
            column = pl.multiple_of(n * tile, LANES)
            tile_at = pl.ds(column, tile)
            starts = block_starts(spot_ref, owner, width // 16, order)
            grads = grad_ref.at[side]
            dz = dot(em_ref[...], w_ref[side, 1, :, tile_at])
            du = (dz * s_ref[:, at].astype(WIDE)).astype(LOW)
            bu_ref[:, at] = column_sum(du)
            put_blocks(dot(emt_ref[...], z_ref[:, at]), grads, starts, near + column, tile)
            put_blocks(dot(at_ref[...], du), grads, starts, column, tile)
            acc_ref[...] += dot_nt(du, w_ref[side, 0, :, tile_at])
            return carry

        lax.fori_loop(0, 2 * tiles, work, 0)
        stored(1, 0).start()
        stored(1, 2).start()
        wait_all(loads[4:])
        at_ref[...] = m_ref[...].T
        dv, gain, shift = norm_back(h_ref[...], t_ref[GAIN2 : GAIN2 + 1, :], acc_ref[...])
        e2 = e_ref[...] + dv
        e2_ref[...] = e2
        em_ref[...] = e2.astype(LOW)
        sums_ref[0:1, :] = gain
        sums_ref[1:2, :] = shift
        sums_ref[2:3, :] = column_sum(em_ref[...])
        wait_all(*outs)
        da = None
        for side, owner in enumerate((c, 1 - c)):
            to = pl.ds(pl.multiple_of(owner * part, LANES), part)
            ey = em_ref[:, to]
            product = dot_nt(ey, wo_ref[side])
            da = product if da is None else da + product
            starts = block_starts(spot_ref, owner, width // 16, order)
            put_blocks(dot(at_ref[...], ey), grad_ref.at[side], starts, half, part)
            stored(side, 1).start()
        da_ref[...] = da.astype(LOW)
        for side in range(2):
            for which in range(3):
                stored(side, which).wait()

    return launch(
        body,
        [spot, *refs, *down_refs, e, a2, z, slope, h2, mixed, table],
        after,
        prefetch=0,
        grid=(),
        in_specs=smem_spec() + any_specs(len(refs) + len(down_refs) + 6) + vmem_specs(1),
        out_specs=any_specs(2 * len(widths)) + vmem_specs(5),
        out_shape=[
            *[jax.ShapeDtypeStruct((width, size), LOW) for size in widths for side in range(2)],
            jax.ShapeDtypeStruct((1, width), WIDE),
            jax.ShapeDtypeStruct((1, hidden), WIDE),
            jax.ShapeDtypeStruct((rows, width), WIDE),
            jax.ShapeDtypeStruct((rows, width), LOW),
            jax.ShapeDtypeStruct((8, width), WIDE),
        ],
        scratch=[
            pltpu.VMEM((2, 2, width, half), LOW),
            pltpu.VMEM((2, width, part), LOW),
            pltpu.VMEM((rows, width), WIDE),
            pltpu.VMEM((rows, width), LOW),
            pltpu.VMEM((rows, hidden), LOW),
            pltpu.VMEM((rows, hidden), LOW),
            pltpu.VMEM((rows, width), WIDE),
            pltpu.VMEM((rows, width), LOW),
            pltpu.VMEM((rows, width), LOW),
            pltpu.VMEM((width, rows), LOW),
            pltpu.VMEM((width, rows), LOW),
            pltpu.VMEM((rows, width), WIDE),
            pltpu.VMEM((2, width, wide), LOW),
            pltpu.SemaphoreType.DMA((2, 16)),
            pltpu.SemaphoreType.DMA((2, 16)),
            pltpu.SemaphoreType.DMA((2, 16)),
            pltpu.SemaphoreType.DMA((6,)),
            pltpu.SemaphoreType.DMA((2, 3)),
        ],
        moved=cost(8 * rows * width * hidden, 8 * width * hidden + 4 * rows * hidden),
        name="mlp_backward",
    )


def attention_backward(lengths, qkv, da, mixed, lse, begin, pairs, after):
    rows, wide = qkv.shape
    width = pairs * LANES

    def body(len_ref, q_ref, k_ref, v_ref, d_ref, m_ref, lse_ref, out_ref, row_ref):
        pair = pl.program_id(0)

        @pl.when(pair == 0)
        def start():
            row_ref[...] = lse_ref[...].T

        lane = lax.broadcasted_iota(jnp.int32, (1, LANES), 1)
        sub = lax.broadcasted_iota(jnp.int32, (LANES, 1), 0)
        key = lax.broadcasted_iota(jnp.int32, (rows, 1), 0)
        shut = jnp.where(key < len_ref[0], 0.0, -1e30)
        scale = jnp.asarray(HEAD_WIDTH**-0.5, LOW)
        q = q_ref[...] * scale
        k = k_ref[...]
        v = v_ref[...]
        d = d_ref[...]
        kt = k.T * scale
        prod = (d.astype(WIDE) * m_ref[...].astype(WIDE)).T
        dks, dvs = [], []
        dqt = jnp.zeros((LANES, rows), WIDE)
        for side in range(2):
            inside = (lane >= HEAD_WIDTH) == (side == 1)
            down = (sub >= HEAD_WIDTH) == (side == 1)
            ks = jnp.where(inside, k, jnp.zeros_like(k))
            vs = jnp.where(inside, v, jnp.zeros_like(v))
            kts = jnp.where(down, kt, jnp.zeros_like(kt))
            first = side * HEAD_WIDTH
            delta = jnp.sum(prod[first : first + HEAD_WIDTH], axis=0, keepdims=True)
            log_total = row_ref[pl.ds((begin + pair) * 2 + side, 1), :]
            p = jnp.exp((dot_nt(ks, q) + shut) - log_total)
            dp = dot_nt(vs, d)
            dvs.append(dot(p.astype(LOW), d))
            ds = (p * (dp - delta)).astype(LOW)
            dks.append(dot(ds, q))
            dqt = dqt + dot(kts, ds)
        dq = dqt.T
        dk = jnp.where(lane < HEAD_WIDTH, dks[0], dks[1])
        dv = jnp.where(lane < HEAD_WIDTH, dvs[0], dvs[1])
        for n, value in enumerate((dq, dk, dv)):
            at = pl.ds(pl.multiple_of(n * width + pair * LANES, LANES), LANES)
            out_ref[:, at] = value.astype(LOW)

    return launch(
        body,
        [lengths, qkv, qkv, qkv, da, mixed, lse],
        after,
        out_shape=jax.ShapeDtypeStruct((rows, 3 * width), LOW),
        prefetch=1,
        grid=(pairs,),
        in_specs=[
            pl.BlockSpec((rows, LANES), lambda p, n: (0, p + begin)),
            pl.BlockSpec((rows, LANES), lambda p, n: (0, p + begin + PAIRS)),
            pl.BlockSpec((rows, LANES), lambda p, n: (0, p + begin + 2 * PAIRS)),
            pl.BlockSpec((rows, LANES), lambda p, n: (0, p + begin)),
            pl.BlockSpec((rows, LANES), lambda p, n: (0, p + begin)),
            pl.BlockSpec((rows, LANES), lambda p, n: (0, 0)),
        ],
        out_specs=pl.BlockSpec((rows, 3 * width), lambda p, n: (0, 0)),
        scratch=[pltpu.VMEM((LANES, rows), WIDE)],
        moved=cost(40 * rows * rows * width, 16 * rows * width, HEADS * rows * rows),
        name="attention_backward",
    )


def qkv_backward(spot, weight, dqkv, e2, h, a1, table, others, order, devices, after):
    rows, width = e2.shape
    wide = 3 * width
    half = wide // 2
    refs = weight[0]
    sums, down_sum, up_sum = others
    hidden = up_sum.shape[1]

    def body(spot_ref, *rest):
        w_refs, rest = rest[: len(refs)], rest[len(refs) :]
        d_ins, rest = rest[: len(dqkv)], rest[len(dqkv) :]
        (
            e_in, h_in, a_in, t_ref, s_ref, ds_ref, u_ref, o_ref, mine_out, rest_out,
            w_ref, d_ref, e_ref, h_ref, a_ref, at_ref, acc_ref, row_ref, pack_ref, grad_ref,
            sems, sems_r, sems_d, sems_g,
        ) = rest
        c = spot_ref[3]
        loads = [
            pltpu.make_async_copy(source, target, sems_r.at[n])
            for n, (source, target) in enumerate(
                ((a_in, a_ref), (h_in, h_ref), (e_in, e_ref))
            )
        ]
        part = width // len(dqkv)
        gathers = [
            pltpu.make_async_copy(
                d_in.at[:, pl.ds(third * part, part)],
                d_ref.at[:, pl.ds(third * width + n * part, part)],
                sems_d.at[n, third],
            )
            for n, d_in in enumerate(d_ins)
            for third in range(3)
        ]
        sides = [
            side_copies(spot_ref, weight, w_refs, side, w_ref.at[side], sems, half)
            for side in range(2)
        ]
        start_all(loads[:1], gathers, sides[0], sides[1], loads[1:])
        wait_all(loads[:1])
        at_ref[...] = a_ref[...].T
        wait_all(gathers)

        def stored(side, which):
            at = pl.ds((0, half)[which], (half, LANES)[which])
            out = (mine_out, rest_out)[side]
            return pltpu.make_async_copy(
                grad_ref.at[side, :, at], out.at[:, at], sems_g.at[side, which]
            )

        placed = []
        for side, owner in enumerate((c, 1 - c)):
            starts = block_starts(spot_ref, owner, width // 16, order)
            placed.append(starts)
            to = pl.ds(pl.multiple_of(owner * half, LANES), half)
            d = d_ref[:, to]
            put_blocks(dot(at_ref[...], d), grad_ref.at[side], starts, 0, half)
            stored(side, 0).start()
            wait_all(sides[side])
            product = dot_nt(d, w_ref[side])
            acc_ref[...] = product if side == 0 else acc_ref[...] + product
        wait_all(loads[1:])
        dv, gain, shift = norm_back(h_ref[...], t_ref[GAIN1 : GAIN1 + 1, :], acc_ref[...])
        o_ref[...] = e_ref[...] + dv
        row_ref[...] = jnp.zeros_like(row_ref)
        for row, value in (
            (GAIN1, gain),
            (GAIN2, s_ref[0:1, :]),
            (BQ, column_sum(d_ref[:, :width])),
            (BV, column_sum(d_ref[:, 2 * width :])),
            (BO, s_ref[2:3, :]),
            (BD, ds_ref[...]),
            (SH1, shift),
            (SH2, s_ref[1:2, :]),
        ):
            row_ref[row : row + 1, :] = value
        pack_ref[...] = row_ref[...].T
        share = hidden // devices
        for device in range(devices):
            at = device * (width // devices)
            pack_ref[at : at + 1, LANES - share :] = u_ref[
                0:1, device * share : (device + 1) * share
            ]
        for side in range(2):
            put_blocks(pack_ref[...], grad_ref.at[side], placed[side], half, LANES)
            stored(side, 1).start()
        for side in range(2):
            for which in range(2):
                stored(side, which).wait()

    return launch(
        body,
        [spot, *refs, *dqkv, e2, h, a1, table, sums, down_sum, up_sum],
        after,
        prefetch=0,
        grid=(),
        in_specs=smem_spec() + any_specs(len(refs) + len(dqkv) + 3) + vmem_specs(4),
        out_specs=vmem_specs(1) + any_specs(2),
        out_shape=[
            jax.ShapeDtypeStruct((rows, width), WIDE),
            jax.ShapeDtypeStruct((width, half + LANES), LOW),
            jax.ShapeDtypeStruct((width, half + LANES), LOW),
        ],
        scratch=[
            pltpu.VMEM((2, width, half), LOW),
            pltpu.VMEM((rows, wide), LOW),
            pltpu.VMEM((rows, width), WIDE),
            pltpu.VMEM((rows, width), WIDE),
            pltpu.VMEM((rows, width), LOW),
            pltpu.VMEM((width, rows), LOW),
            pltpu.VMEM((rows, width), WIDE),
            pltpu.VMEM((LANES, width), WIDE),
            pltpu.VMEM((width, LANES), WIDE),
            pltpu.VMEM((2, width, half + LANES), LOW),
            pltpu.SemaphoreType.DMA((2, 16)),
            pltpu.SemaphoreType.DMA((3,)),
            pltpu.SemaphoreType.DMA((len(dqkv), 3)),
            pltpu.SemaphoreType.DMA((2, 2)),
        ],
        moved=cost(4 * rows * width * wide, 4 * width * wide + 16 * rows * width),
        name="qkv_backward",
    )


def join(pieces):
    return jnp.concatenate(pieces, axis=0)


def finish_mlp(spot, parts, shapes):
    def body(spot_ref, *refs):
        outs = refs[-3:]
        c = spot_ref[3]
        for n, (layer, kept, got, columns) in enumerate(parts):
            for owner, ref in ((c, refs[2 * n]), (1 - c, refs[2 * n + 1])):
                column = 0
                for out, start, size in columns:
                    to = owner * (shapes[out][2] // 2) + start
                    outs[out][layer, :, pl.ds(pl.multiple_of(to, LANES), size)] = ref[
                        :, column : column + size
                    ].astype(WIDE)
                    column = column + size

    flat = [value for layer, kept, got, columns in parts for value in (kept, got)]
    return launch(
        body,
        [spot, *flat],
        [],
        prefetch=0,
        grid=(),
        in_specs=smem_spec() + vmem_specs(len(flat)),
        out_specs=vmem_specs(3),
        out_shape=[jax.ShapeDtypeStruct(shape, WIDE) for shape in shapes],
        scratch=[],
        moved=cost(0, 16 * sum(value.size for value in flat)),
        name="finish_mlp",
    )


def finish_qkv(spot, parts, shapes):
    share = shapes[3][1]
    half = shapes[0][2] // 2

    def body(spot_ref, *refs):
        qkv_ref, gain_ref, bias_ref, up_ref = refs[-4:]
        c = spot_ref[3]
        for layer in range(len(parts)):
            kept_ref, got_ref = refs[2 * layer], refs[2 * layer + 1]
            for owner, ref in ((c, kept_ref), (1 - c, got_ref)):
                start = pl.multiple_of(owner * half, LANES)
                qkv_ref[layer, :, pl.ds(start, half)] = ref[:, :half].astype(WIDE)
            packed = kept_ref[:, half : half + LANES]
            columns = packed.T
            gain_ref[layer] = columns[0:2, :]
            for n in range(6):
                bias_ref[n, layer : layer + 1, :] = columns[n + 2 : n + 3, :]
            up_ref[layer : layer + 1, :] = packed[0:1, LANES - share :]

    flat = [value for part in parts for value in part]
    return launch(
        body,
        [spot, *flat],
        [],
        prefetch=0,
        grid=(),
        in_specs=smem_spec() + vmem_specs(len(flat)),
        out_specs=vmem_specs(4),
        out_shape=[jax.ShapeDtypeStruct(shape, WIDE) for shape in shapes],
        scratch=[],
        moved=cost(0, 8 * sum(value.size for value in flat)),
        name="finish_qkv",
    )


def linear(z, x, y, c):
    return ((z * 2 + x) * 2 + y) * 2 + c


def pairs_of(step):
    result = []
    for z in range(4):
        for x in range(2):
            for y in range(2):
                for c in range(2):
                    result.append((linear(z, x, y, c), linear(*step(z, x, y, c))))
    return result


TO_Z = [pairs_of(lambda z, x, y, c, n=n: ((z + n) % 4, x, y, c)) for n in range(4)]
TO_XY = pairs_of(lambda z, x, y, c: (z, x, 1 - y, c) if c else (z, 1 - x, y, c))
TO_YX = pairs_of(lambda z, x, y, c: (z, 1 - x, y, c) if c else (z, x, 1 - y, c))


def send(value, pairs):
    return lax.ppermute(value, AXES, pairs)


def swap_cores(value):
    chips = lax.axis_size("dp") * lax.axis_size("y")
    return send(value, [(n, n ^ 1) for n in range(2 * chips)])


def stepped():
    return lax.axis_size("dp") == 8 and lax.axis_size("y") == 2


def place():
    dp = lax.axis_index("dp")
    return jnp.stack([dp // 2, dp % 2, lax.axis_index("y"), lax.axis_index("c")]).astype(jnp.int32)


def halves(pieces):
    low = [piece[:, : piece.shape[1] // 2] for piece in pieces]
    high = [piece[:, piece.shape[1] // 2 :] for piece in pieces]
    return jnp.concatenate(low, axis=1), jnp.concatenate(high, axis=1)


def both_cores(c, pieces):
    low, high = halves(pieces)
    mine = jnp.where(c == 0, low, high)
    got = swap_cores(jnp.where(c == 0, high, low))
    upper = jnp.concatenate([mine, got], axis=0)
    return jnp.where(c == 0, upper, jnp.concatenate([got, mine], axis=0))


class Chain:
    def __init__(self, steps):
        self.steps = steps
        self.result = None
        self.flying = None
        self.resume(None)

    def resume(self, arrived):
        try:
            self.waiting = self.steps.send(arrived)
        except StopIteration as end:
            self.waiting = None
            self.result = end.value

    def start(self):
        if self.waiting is not None:
            assert self.flying is None
            self.flying = [begin(value) for value, begin in self.waiting]


def offsets_of(widths):
    offsets = [0]
    for width in widths:
        offsets.append(offsets[-1] + width // 2)
    return offsets


def by(pairs):
    return lambda value: send(value, pairs)


def gather_steps(block, turns):
    ring = {0: block}
    for turn in turns:
        got = yield [(block, by(TO_Z[n])) for n in turn]
        ring.update(zip(turn, got))
    stack = join([ring[n] for n in range(4)])
    (got,) = yield [(stack, by(TO_XY))]
    near = join([stack, got])
    far, near_got = yield [(near, by(TO_YX)), (near, swap_cores)]
    (far_got,) = yield [(far, swap_cores)]
    return near, far, near_got, far_got


def gather_chips(block):
    return lax.all_gather(block, ("dp", "y"), axis=0, tiled=True)


def gather_at_once(block):
    (own,) = yield [(block, gather_chips)]
    (other,) = yield [(own, swap_cores)]
    return own, other


def added(parts):
    total = parts[0].astype(WIDE)
    for part in parts[1:]:
        total = total + part.astype(WIDE)
    return total


def last_step(c, total):
    rows = total.shape[0] // 2
    low, high = total[:rows], total[rows:]
    kept = jnp.where(c == 0, low, high).astype(WIDE)
    (got,) = yield [(jnp.where(c == 0, high, low).astype(LOW), swap_cores)]
    return kept, got


def scatter_steps(c, mine, rest, order):
    rows = mine.shape[0] // 16
    upper, lower = slice(8 * rows, 16 * rows), slice(0, 8 * rows)
    (got,) = yield [(rest, swap_cores)]
    (more,) = yield [(added([mine[upper], got[upper]]).astype(LOW), by(TO_YX))]
    parts = [mine[lower], got[lower], more]
    for along_z in (order == Z_NEXT, order == Z_LAST):
        size = parts[0].shape[0]
        kept = size // (4 if along_z else 2)
        if along_z:
            total = added(parts)
            sent = [
                (total[n * kept : (n + 1) * kept].astype(LOW), by(TO_Z[4 - n])) for n in (1, 2, 3)
            ]
        else:
            sent = [(added([part[kept:] for part in parts]).astype(LOW), by(TO_XY))]
        arrived = yield sent
        parts = [part[:kept] for part in parts] + arrived
    return (yield from last_step(c, added(parts)))


def scatter_chips(value):
    return lax.psum_scatter(value, ("dp", "y"), scatter_dimension=0, tiled=True)


def scatter_at_once(c, mine, rest):
    (got,) = yield [(rest, swap_cores)]
    (total,) = yield [(added([mine, got]).astype(LOW), scatter_chips)]
    return (yield from last_step(c, total))


def pack_small(gains, shifts, up_bias):
    rows = gains.shape[1]
    columns = jnp.concatenate([gains, shifts], axis=0).T
    share = up_bias.shape[0]
    first = jnp.pad(columns, ((0, 0), (0, LANES - share - columns.shape[1])))
    second = jnp.pad(up_bias[None, :], ((0, rows - 1), (0, 0)))
    packed = jnp.concatenate([first, second], axis=1)
    return jnp.concatenate([packed, packed], axis=1)


def local(
    hidden_in,
    cotangent,
    lengths,
    qkv_weight,
    out_weight,
    up_weight,
    down_weight,
    norm_gains,
    biases,
    up_bias,
):
    clips, slots, width = hidden_in.shape
    layers = qkv_weight.shape[0]
    hidden = down_weight.shape[1]
    assert clips == 1 and layers == 2
    by_steps = stepped()
    devices = lax.axis_size(AXES)
    spot = place()
    c = spot[3]
    chunks, spots = [], []
    for i in range(layers):
        gains, shifts, bias = (v[i].astype(LOW) for v in (norm_gains, biases, up_bias))
        chunks += [
            [qkv_weight[i].astype(LOW), pack_small(gains, shifts, bias)],
            [up_weight[i].astype(LOW), out_weight[i].astype(LOW)],
            [down_weight[i].T.astype(LOW)],
        ]
        spots += [offsets_of([piece.shape[1] for piece in chunk]) for chunk in chunks[-3:]]
    blocks = [both_cores(c, chunks[0])]
    rest = both_cores(c, [piece for chunk in chunks[1:] for piece in chunk])
    start = 0
    for at in spots[1:]:
        blocks.append(rest[:, start : start + at[-1]])
        start = start + at[-1]
    if by_steps:
        turns = [TURNS[n] for n in range(len(blocks))]
        gathers = [Chain(gather_steps(block, turn)) for block, turn in zip(blocks, turns)]
    else:
        gathers = [Chain(gather_at_once(block)) for block in blocks]
    q0, u0, d0, q1, u1, d1 = gathers

    def weight(i, chunk, member):
        n = 3 * i + chunk
        return gathers[n].result, spots[n][member], True

    rec = [{"h": hidden_in[0]}, {}]
    awaited = []

    def first_matmul(i):
        qkv, first, table, bias = qkv_forward(
            spot, weight(i, 0, 0), rec[i]["h"], hidden, devices, awaited
        )
        return {"qkv": qkv, "a1": first, "table": table, "bias": bias}

    def attend(i):
        mixed, lse = attention_forward(lengths, rec[i]["qkv"], awaited)
        return {"mixed": mixed, "lse": lse}

    def feed_up(i):
        r = rec[i]
        h2, second, z, slope = up_forward(
            spot,
            weight(i, 1, 0),
            weight(i, 1, 1),
            r["h"],
            r["mixed"],
            r["bias"],
            r["table"],
            awaited,
        )
        return {"h2": h2, "a2": second, "z": z, "slope": slope}

    def feed_down(i):
        r = rec[i]
        total = down_forward(spot, weight(i, 2, 0), r["h2"], r["z"], r["table"], awaited)
        return {"total": total}

    def feed_back(i):
        r = rec[i]
        *grads, down_sum, up_sum, e2, da, sums = mlp_backward(
            spot,
            weight(i, 1, 0),
            weight(i, 2, 0),
            weight(i, 1, 1),
            r["e"],
            r["a2"],
            r["z"],
            r["slope"],
            r["h2"],
            r["mixed"],
            r["table"],
            JOINED[i],
            ORDERS[i] if by_steps else WHOLE,
            awaited,
        )
        others = (sums, down_sum, up_sum)
        return {"first": grads[:2], "second": grads[2:], "e2": e2, "da": da, "others": others}

    def attend_back(i, begin):
        r = rec[i]
        dqkv = attention_backward(
            lengths, r["qkv"], r["da"], r["mixed"], r["lse"], begin, PAIRS // 2, awaited
        )
        return {f"dqkv{begin}": dqkv}

    def qkv_back(i):
        r = rec[i]
        e, mine, rest = qkv_backward(
            spot,
            weight(i, 0, 0),
            (r["dqkv0"], r[f"dqkv{PAIRS // 2}"]),
            r["e2"],
            r["h"],
            r["a1"],
            r["table"],
            r["others"],
            ORDERS[i] if by_steps else WHOLE,
            devices,
            awaited,
        )
        return {"e_in": e, "qkv_grad": (mine, rest)}

    def run(begin, end, *work):
        nonlocal awaited
        for chain in begin:
            chain.start()
        outs = []
        for function, i, *rest in work:
            outs.append(function(i, *rest))
            rec[i].update(outs[-1])
            awaited = []
        landing = [chain for chain in end if chain.flying is not None]
        flying = [chain.flying for chain in landing]
        arrived, outs = lax.optimization_barrier((flying, outs))
        for (function, i, *rest), new in zip(work, outs):
            rec[i].update(new)
        for chain, values in zip(landing, arrived):
            chain.flying = None
            chain.resume(values)
        awaited = awaited + [value for values in arrived for value in values]

    def drain(*chains):
        while any(chain.waiting is not None for chain in chains):
            for chain in chains:
                if chain.flying is not None:
                    values, chain.flying = chain.flying, None
                    chain.resume(values)
            for chain in chains:
                chain.start()

    def scatter(i, member):
        if by_steps:
            return Chain(scatter_steps(c, *rec[i][member], ORDERS[i]))
        return Chain(scatter_at_once(c, *rec[i][member]))

    run([q0], [q0])
    run([q0], [q0])
    run([q0, u0], [q0, u0])
    run([q0, u0, d0], [q0])
    run([], [u0], (first_matmul, 0))
    run([u0], [u0, d0], (attend, 0))
    run([u0, d0, q1], [u0, d0])
    run([d0], [d0, q1], (feed_up, 0))
    run([d0, q1, u1], [d0, q1])
    run([q1], [q1, u1], (feed_down, 0))
    rec[1]["h"] = rec[0]["total"]
    run([q1, u1, d1], [q1])
    run([], [u1], (first_matmul, 1))
    run([u1], [u1, d1], (attend, 1))
    run([u1, d1], [u1, d1])
    run([d1], [d1], (feed_up, 1))
    run([d1], [d1])

    left, right = 0, PAIRS // 2
    rec[1]["e"] = cotangent[0]
    run([], [], (feed_back, 1))
    u1 = scatter(1, "first")
    d1 = scatter(1, "second")
    run([d1, u1], [d1, u1], (attend_back, 1, left), (attend_back, 1, right))
    run([d1], [d1], (qkv_back, 1))
    rec[0]["e"] = rec[1]["e_in"]
    q1 = scatter(1, "qkv_grad")
    run([u1, d1, q1], [u1, d1, q1], (feed_back, 0))
    u0 = scatter(0, "first")
    d0 = scatter(0, "second")
    run([q1, d1, u1, d0, u0], [q1, d1, u1, d0, u0], (attend_back, 0, left), (attend_back, 0, right))
    run([d0, d1], [d0, d1], (qkv_back, 0))
    q0 = scatter(0, "qkv_grad")
    awaited = []
    drain(u0, d0, q0, q1, u1, d1)
    run([], [], (feed_down, 1))
    output = rec[1]["total"][None]
    input_grad = rec[0]["e_in"][None]
    down_shape = (layers, down_weight.shape[2], hidden)
    mlp_shapes = [down_shape, up_weight.shape, out_weight.shape]
    bias_shape = (biases.shape[1], layers, biases.shape[2])
    qkv_shapes = [qkv_weight.shape, norm_gains.shape, bias_shape, up_bias.shape]
    half = hidden // 2
    first, second = [(1, 0, half), (2, 0, width // 2)], [(0, 0, half)]
    parts = [
        (0, *u0.result, first),
        (0, *d0.result, second),
        (1, *u1.result, first),
        (1, *d1.result, second),
    ]
    down_grad, up_grad, out_grad = finish_mlp(spot, parts, mlp_shapes)
    qkv_grad, gains, shifts, up_sums = finish_qkv(spot, [q0.result, q1.result], qkv_shapes)
    shifts = jnp.swapaxes(shifts, 0, 1)
    down_grad = jnp.swapaxes(down_grad, 1, 2)
    return output, input_grad, qkv_grad, out_grad, up_grad, down_grad, gains, shifts, up_sums


def solution(mesh):
    size = dict(mesh.shape)
    fine = Mesh(mesh.devices.reshape(size["dp"], size["fsdp"] // 2, 2), AXES)
    return jax.shard_map(
        local,
        mesh=fine,
        in_specs=(
            P(AXES, None, None),
            P(AXES, None, None),
            P(AXES),
            P(None, AXES, None),
            P(None, AXES, None),
            P(None, AXES, None),
            P(None, None, AXES),
            P(None, None, AXES),
            P(None, None, AXES),
            P(None, AXES),
        ),
        out_specs=(
            P(AXES, None, None),
            P(AXES, None, None),
            P(None, AXES, None),
            P(None, AXES, None),
            P(None, AXES, None),
            P(None, None, AXES),
            P(None, None, AXES),
            P(None, None, AXES),
            P(None, AXES),
        ),
        check_vma=False,
    )
```

```python
import jax
import jax.numpy as jnp
from jax import lax
from jax.experimental import pallas as pl
from jax.experimental.pallas import tpu as pltpu
from jax.sharding import Mesh
from jax.sharding import PartitionSpec as P

HEADS = 12
HEAD_WIDTH = 64
LANES = 128
PAIRS = HEADS * HEAD_WIDTH // LANES
LOW = jnp.bfloat16
WIDE = jnp.float32
norm_eps = 1e-06
AXES = ("dp", "y", "c")
WHOLE, Z_LAST, Z_NEXT = range(3)
JOINED = (False, False)
ORDERS = (Z_LAST, Z_LAST)
TURNS = (((1, 2, 3),),) * 6
VMEM_LIMIT = 60 * 1024 * 1024
TILE = 768


def cost(flops, moved, hard=0):
    return pl.CostEstimate(
        flops=int(flops) // 64, bytes_accessed=int(moved) // 64, transcendentals=int(hard) // 64
    )


def params():
    return pltpu.CompilerParams(vmem_limit_bytes=VMEM_LIMIT)


def vmem_specs(count):
    return [pl.BlockSpec(memory_space=pltpu.VMEM)] * count


def any_specs(count):
    return [pl.BlockSpec(memory_space=pl.ANY)] * count


def launch(body, args, after, prefetch, grid, in_specs, out_specs, out_shape, scratch, moved, name):
    count = len(args)

    def trimmed(*refs):
        body(*refs[:count], *refs[count + len(after) :])

    return pl.pallas_call(
        trimmed,
        out_shape=out_shape,
        grid_spec=pltpu.PrefetchScalarGridSpec(
            num_scalar_prefetch=prefetch,
            grid=grid,
            in_specs=in_specs + any_specs(len(after)),
            out_specs=out_specs,
            scratch_shapes=scratch,
        ),
        compiler_params=params(),
        cost_estimate=moved,
        name=name,
    )(*args, *after)


def smem_spec():
    return [pl.BlockSpec(memory_space=pltpu.SMEM)]


def dot(a, b):
    return jnp.dot(a, b, preferred_element_type=WIDE)


def dot_nt(a, b):
    return lax.dot_general(a, b, (((1,), (1,)), ((), ())), preferred_element_type=WIDE)


def dot_tn(a, b):
    return lax.dot_general(a, b, (((0,), (0,)), ((), ())), preferred_element_type=WIDE)


def place_of(spot, owner, block, z_first):
    z, x, y = spot[0], spot[1], spot[2]
    first, second, zr = block // 8, (block // 4) % 2, block % 4
    if not z_first:
        second, zr = block % 2, (block // 2) % 4
    bz = lax.rem(z - zr + 4, 4)
    bx = lax.rem(x + jnp.where(owner == 0, second, first), 2)
    by = lax.rem(y + jnp.where(owner == 0, first, second), 2)
    return (bz * 2 + bx) * 2 + by


def side_copies(spot, weight, refs, side, target, sems, width):
    arrays, column, z_first = weight
    at = pl.ds(column, width)
    if len(arrays) == 2:
        return [pltpu.make_async_copy(refs[side].at[:, at], target, sems.at[side, 0])]
    owner = spot[3] if side == 0 else 1 - spot[3]
    rows = arrays[0].shape[0] // 8
    copies = []
    for block in range(16):
        start = pl.multiple_of(place_of(spot, owner, block, z_first) * rows, 16)
        copies.append(
            pltpu.make_async_copy(
                refs[2 * side + block // 8].at[pl.ds((block % 8) * rows, rows), at],
                target.at[pl.ds(start, rows), :],
                sems.at[side, block],
            )
        )
    return copies


def start_all(*groups):
    for copies in groups:
        for copy in copies:
            copy.start()


def wait_all(*groups):
    for copies in groups:
        for copy in copies:
            copy.wait()


def norm_rows(v):
    center = v - jnp.mean(v, axis=-1, keepdims=True)
    r = lax.rsqrt(jnp.mean(center * center, axis=-1, keepdims=True) + norm_eps)
    return center * r, r


def norm_back(v, gain, d):
    xh, r = norm_rows(v)
    dg = d * gain
    m1 = jnp.mean(dg, axis=-1, keepdims=True)
    m2 = jnp.mean(dg * xh, axis=-1, keepdims=True)
    return (
        r * (dg - m1 - xh * m2),
        jnp.sum(d * xh, axis=0, keepdims=True),
        jnp.sum(d, axis=0, keepdims=True),
    )


GAIN1, GAIN2, BQ, BV, BO, BD, SH1, SH2 = range(8)


def qkv_forward(spot, weight, h, hidden, devices, after):
    rows, width = h.shape
    wide = 3 * width
    half = wide // 2
    refs = weight[0]

    def body(spot_ref, *rest):
        h_ref, qkv_ref, a_ref, t_ref, b_ref = rest[len(refs) : len(refs) + 5]
        w_ref, row_ref, sems = rest[len(refs) + 5 :]
        c = spot_ref[3]
        own, other = [
            side_copies(spot_ref, weight, rest, side, w_ref.at[side], sems, half + LANES)
            for side in range(2)
        ]
        start_all(own, other)
        xh, r = norm_rows(h_ref[...])
        wait_all(own)
        values = w_ref[0, :, half:].astype(WIDE)
        table = values.T[0:8, :]
        t_ref[...] = table
        share = hidden // devices
        for device in range(devices):
            at = device * (width // devices)
            b_ref[0:1, device * share : (device + 1) * share] = values[
                at : at + 1, LANES - share :
            ]
        row_ref[:, :width] = table[BQ : BQ + 1]
        row_ref[:, width : 2 * width] = jnp.zeros((1, width), WIDE)
        row_ref[:, 2 * width :] = table[BV : BV + 1]
        a = (xh * table[GAIN1 : GAIN1 + 1] + table[SH1 : SH1 + 1]).astype(LOW)
        a_ref[...] = a
        for side, owner in enumerate((c, 1 - c)):
            if side == 1:
                wait_all(other)
            to = pl.ds(pl.multiple_of(owner * half, LANES), half)
            qkv_ref[:, to] = (dot(a_ref[...], w_ref[side, :, :half]) + row_ref[:, to]).astype(LOW)

    return launch(
        body,
        [spot, *refs, h],
        after,
        prefetch=0,
        grid=(),
        in_specs=smem_spec() + any_specs(len(refs)) + vmem_specs(1),
        out_specs=vmem_specs(4),
        out_shape=[
            jax.ShapeDtypeStruct((rows, wide), LOW),
            jax.ShapeDtypeStruct((rows, width), LOW),
            jax.ShapeDtypeStruct((8, width), WIDE),
            jax.ShapeDtypeStruct((1, hidden), WIDE),
        ],
        scratch=[
            pltpu.VMEM((2, width, half + LANES), LOW),
            pltpu.VMEM((1, wide), WIDE),
            pltpu.SemaphoreType.DMA((2, 16)),
        ],
        moved=cost(2 * rows * width * wide, 2 * width * wide + 9 * rows * width),
        name="qkv_forward",
    )


def attention_forward(lengths, qkv, after):
    rows, wide = qkv.shape
    width = wide // 3

    def body(len_ref, q_ref, k_ref, v_ref, o_ref, lse_ref):
        pair = pl.program_id(0)
        lane = lax.broadcasted_iota(jnp.int32, (1, LANES), 1)
        key = lax.broadcasted_iota(jnp.int32, (1, rows), 1)
        shut = jnp.where(key < len_ref[0], 0.0, -1e30)
        q = q_ref[...] * jnp.asarray(HEAD_WIDTH**-0.5, LOW)
        k = k_ref[...]
        v = v_ref[...]
        outs = []
        stats = jnp.where(pair == 0, jnp.zeros((rows, LANES), WIDE), lse_ref[...])
        for side in range(2):
            inside = (lane >= HEAD_WIDTH) == (side == 1)
            qs = jnp.where(inside, q, jnp.zeros_like(q))
            s = dot_nt(qs, k) + shut
            peak = jnp.max(s, axis=1, keepdims=True)
            e = jnp.exp(s - peak)
            total = jnp.sum(e, axis=1, keepdims=True)
            p = (e * (1.0 / total)).astype(LOW)
            outs.append(dot(p, v))
            stats = jnp.where(lane == pair * 2 + side, peak + jnp.log(total), stats)
        lse_ref[...] = stats
        o_ref[...] = jnp.where(lane < HEAD_WIDTH, outs[0], outs[1]).astype(LOW)

    return launch(
        body,
        [lengths, qkv, qkv, qkv],
        after,
        out_shape=[
            jax.ShapeDtypeStruct((rows, width), LOW),
            jax.ShapeDtypeStruct((rows, LANES), WIDE),
        ],
        prefetch=1,
        grid=(PAIRS,),
        in_specs=[
            pl.BlockSpec((rows, LANES), lambda p, n: (0, p)),
            pl.BlockSpec((rows, LANES), lambda p, n: (0, p + PAIRS)),
            pl.BlockSpec((rows, LANES), lambda p, n: (0, p + 2 * PAIRS)),
        ],
        out_specs=[
            pl.BlockSpec((rows, LANES), lambda p, n: (0, p)),
            pl.BlockSpec((rows, LANES), lambda p, n: (0, 0)),
        ],
        moved=cost(16 * rows * rows * width, 8 * rows * width, HEADS * rows * rows),
        scratch=[],
        name="attention_forward",
    )


def gelu_parts(u):
    cdf = 0.5 * (1.0 + lax.erf(u * (0.5**0.5)))
    pdf = jnp.exp(-0.5 * u * u) * (0.3989422804014327)
    return cdf, pdf


def up_forward(spot, weight, out_weight, h, mixed, up_bias, table, after):
    rows, width = h.shape
    hidden = up_bias.shape[1]
    half = hidden // 2
    part = width // 2
    tile = TILE
    tiles = half // tile
    refs = weight[0]

    def body(spot_ref, *rest):
        w_refs, rest = rest[: len(refs)], rest[len(refs) :]
        (
            h_ref, m_ref, b_ref, t_ref, h2_ref, a_ref, z_out, s_out,
            w_ref, wo_ref, z_ref, s_ref, sems, sems_o, sems_t,
        ) = rest
        c = spot_ref[3]
        outs = [
            side_copies(spot_ref, out_weight, w_refs, side, wo_ref.at[side], sems_o, part)
            for side in range(2)
        ]
        sides = [
            side_copies(spot_ref, weight, w_refs, side, w_ref.at[side], sems, half)
            for side in range(2)
        ]
        start_all(*outs, *sides)
        wait_all(*outs)
        for side, owner in enumerate((c, 1 - c)):
            to = pl.ds(pl.multiple_of(owner * part, LANES), part)
            h2_ref[:, to] = h_ref[:, to] + (
                dot(m_ref[...], wo_ref[side]) + t_ref[BO : BO + 1, to]
            )
        xh, r = norm_rows(h2_ref[...])
        a_ref[...] = (xh * t_ref[GAIN2 : GAIN2 + 1, :] + t_ref[SH2 : SH2 + 1, :]).astype(LOW)

        def stored(step):
            side, n = step // tiles, lax.rem(step, tiles)
            owner = jnp.where(side == 0, c, 1 - c)
            at = pl.ds(pl.multiple_of(owner * half + n * tile, LANES), tile)
            return side, n, at, [
                pltpu.make_async_copy(ref.at[:, at], out.at[:, at], sems_t.at[which, step])
                for which, (ref, out) in enumerate(((z_ref, z_out), (s_ref, s_out)))
            ]

        def work(step, carry):
            side, n, at, copies = stored(step)

            for which in range(2):

                @pl.when(step == which * tiles)
                def ready():
                    wait_all(sides[which])

            up = pl.ds(pl.multiple_of(n * tile, LANES), tile)
            u = dot(a_ref[...], w_ref[side, :, up]) + b_ref[:, at]
            cdf, pdf = gelu_parts(u)
            z_ref[:, at] = (u * cdf).astype(LOW)
            s_ref[:, at] = (cdf + u * pdf).astype(LOW)
            start_all(copies)
            return carry

        lax.fori_loop(0, 2 * tiles, work, 0)
        for step in range(2 * tiles):
            wait_all(stored(step)[3])

    return launch(
        body,
        [spot, *refs, h, mixed, up_bias, table],
        after,
        prefetch=0,
        grid=(),
        in_specs=smem_spec() + any_specs(len(refs)) + vmem_specs(4),
        out_specs=vmem_specs(2) + any_specs(2),
        out_shape=[
            jax.ShapeDtypeStruct((rows, width), WIDE),
            jax.ShapeDtypeStruct((rows, width), LOW),
            jax.ShapeDtypeStruct((rows, hidden), LOW),
            jax.ShapeDtypeStruct((rows, hidden), LOW),
        ],
        scratch=[
            pltpu.VMEM((2, width, half), LOW),
            pltpu.VMEM((2, width, part), LOW),
            pltpu.VMEM((rows, hidden), LOW),
            pltpu.VMEM((rows, hidden), LOW),
            pltpu.SemaphoreType.DMA((2, 16)),
            pltpu.SemaphoreType.DMA((2, 16)),
            pltpu.SemaphoreType.DMA((2, 2 * tiles)),
        ],
        moved=cost(
            2 * rows * width * hidden, 2 * width * hidden + 4 * rows * hidden, 2 * rows * hidden
        ),
        name="up_forward",
    )


def down_forward(spot, weight, h2, z, table, after):
    rows, width = h2.shape
    hidden = z.shape[1]
    half = hidden // 2
    refs = weight[0]

    def body(spot_ref, *rest):
        h_ref, z_in, t_ref, o_ref, w_ref, z_ref, sems, sems_r = rest[len(refs) :]
        c = spot_ref[3]
        sides = [
            side_copies(spot_ref, weight, rest, side, w_ref.at[side], sems, half)
            for side in range(2)
        ]
        loads = []
        for side, owner in enumerate((c, 1 - c)):
            at = pl.ds(pl.multiple_of(owner * half, LANES), half)
            loads.append(
                [pltpu.make_async_copy(z_in.at[:, at], z_ref.at[side], sems_r.at[side])]
            )
        start_all(sides[0], loads[0], sides[1], loads[1])
        total = h_ref[...] + t_ref[BD : BD + 1, :]
        for side in range(2):
            wait_all(sides[side], loads[side])
            total = total + dot_nt(z_ref[side], w_ref[side])
        o_ref[...] = total

    return launch(
        body,
        [spot, *refs, h2, z, table],
        after,
        prefetch=0,
        grid=(),
        in_specs=smem_spec()
        + any_specs(len(refs))
        + vmem_specs(1)
        + any_specs(1)
        + vmem_specs(1),
        out_specs=vmem_specs(1),
        out_shape=[jax.ShapeDtypeStruct((rows, width), WIDE)],
        scratch=[
            pltpu.VMEM((2, width, half), LOW),
            pltpu.VMEM((2, rows, half), LOW),
            pltpu.SemaphoreType.DMA((2, 16)),
            pltpu.SemaphoreType.DMA((2,)),
        ],
        moved=cost(2 * rows * width * hidden, 2 * width * hidden + 2 * rows * hidden),
        name="down_forward",
    )[0]


def block_starts(spot, owner, rows, order):
    if order == WHOLE:
        return [block * rows for block in range(16)]
    z, x, y = spot[0], spot[1], spot[2]
    result = []
    for block in range(16):
        bz, bx, by = block // 4, (block // 2) % 2, block % 2
        zr = lax.rem(z - bz + 4, 4)
        xr = lax.rem(x + bx, 2)
        yr = lax.rem(y + by, 2)
        first = jnp.where(owner == 0, yr, xr)
        second = jnp.where(owner == 0, xr, yr)
        place = (first * 2 + second) * 4 + zr if order == Z_LAST else (first * 4 + zr) * 2 + second
        result.append(pl.multiple_of(place * rows, 16))
    return result


def put_blocks(value, out_ref, starts, column, width):
    rows = value.shape[0] // 16
    low = value.astype(LOW)
    for block, start in enumerate(starts):
        out_ref[pl.ds(start, rows), pl.ds(column, width)] = low[block * rows : (block + 1) * rows]


def column_sum(value):
    return jnp.sum(value.astype(WIDE), axis=0, keepdims=True)


def mlp_backward(
    spot, up, down, out_weight, e, a2, z, slope, h2, mixed, table, joined, order, after
):
    rows, width = e.shape
    hidden = z.shape[1]
    half = hidden // 2
    part = width // 2
    tile = TILE
    tiles = half // tile
    wide = hidden + part
    refs, down_refs = up[0], down[0]
    near = half + part
    widths = [wide] if joined else [near, half]

    def body(spot_ref, *rest):
        w_refs, rest = rest[: len(refs)], rest[len(refs) :]
        d_refs, rest = rest[: len(down_refs)], rest[len(down_refs) :]
        buffers = [rest[7 + 2 * n : 9 + 2 * n] for n in range(len(widths))]
        rest = rest[:7] + rest[7 + 2 * len(widths) :]
        (
            e_in, a_in, z_in, s_in, h_in, m_in, t_ref,
            bd_ref, bu_ref, e2_ref, da_ref, sums_ref,
            w_ref, wo_ref, e_ref, a_ref, z_ref, s_ref, h_ref, m_ref,
            em_ref, emt_ref, at_ref, acc_ref, grad_ref, sems, sems_d, sems_o, sems_r, sems_g,
        ) = rest
        c = spot_ref[3]
        loads = [
            pltpu.make_async_copy(source, target, sems_r.at[n])
            for n, (source, target) in enumerate(
                (
                    (e_in, e_ref), (a_in, a_ref), (z_in, z_ref), (s_in, s_ref), (h_in, h_ref),
                    (m_in, m_ref),
                )
            )
        ]
        sides = [
            side_copies(spot_ref, down, d_refs, side, w_ref.at[side, 1], sems_d, half)
            + side_copies(spot_ref, up, w_refs, side, w_ref.at[side, 0], sems, half)
            for side in range(2)
        ]
        outs = [
            side_copies(spot_ref, out_weight, w_refs, side, wo_ref.at[side], sems_o, part)
            for side in range(2)
        ]
        start_all(loads[:2], sides[0], loads[2:4], sides[1], loads[4:], *outs)
        wait_all(loads[:1])
        em = e_ref[...].astype(LOW)
        em_ref[...] = em
        bd_ref[...] = column_sum(em)
        emt_ref[...] = em.T
        wait_all(loads[1:2])
        at_ref[...] = a_ref[...].T
        acc_ref[...] = jnp.zeros_like(acc_ref)

        def stored(side, which):
            start, size = ((0, half), (half, part), (near, half))[which]
            out, to = buffers[-1][side], start
            if not joined:
                out, to = (buffers[1][side], 0) if which == 2 else (buffers[0][side], start)
            return pltpu.make_async_copy(
                grad_ref.at[side, :, pl.ds(start, size)],
                out.at[:, pl.ds(to, size)],
                sems_g.at[side, which],
            )

        def work(step, carry):
            side, n = step // tiles, lax.rem(step, tiles)
            owner = jnp.where(side == 0, c, 1 - c)

            @pl.when(step == 0)
            def first_ready():
                wait_all(sides[0], loads[2:4])

            @pl.when(step == tiles)
            def second_ready():
                stored(0, 0).start()
                stored(0, 2).start()
                wait_all(sides[1])

            at = pl.ds(pl.multiple_of(owner * half + n * tile, LANES), tile)
            column = pl.multiple_of(n * tile, LANES)
            tile_at = pl.ds(column, tile)
            starts = block_starts(spot_ref, owner, width // 16, order)
            grads = grad_ref.at[side]
            dz = dot(em_ref[...], w_ref[side, 1, :, tile_at])
            du = (dz * s_ref[:, at].astype(WIDE)).astype(LOW)
            bu_ref[:, at] = column_sum(du)
            put_blocks(dot(emt_ref[...], z_ref[:, at]), grads, starts, near + column, tile)
            put_blocks(dot(at_ref[...], du), grads, starts, column, tile)
            acc_ref[...] += dot_nt(du, w_ref[side, 0, :, tile_at])
            return carry

        lax.fori_loop(0, 2 * tiles, work, 0)
        stored(1, 0).start()
        stored(1, 2).start()
        wait_all(loads[4:])
        at_ref[...] = m_ref[...].T
        dv, gain, shift = norm_back(h_ref[...], t_ref[GAIN2 : GAIN2 + 1, :], acc_ref[...])
        e2 = e_ref[...] + dv
        e2_ref[...] = e2
        em_ref[...] = e2.astype(LOW)
        sums_ref[0:1, :] = gain
        sums_ref[1:2, :] = shift
        sums_ref[2:3, :] = column_sum(em_ref[...])
        wait_all(*outs)
        da = None
        for side, owner in enumerate((c, 1 - c)):
            to = pl.ds(pl.multiple_of(owner * part, LANES), part)
            ey = em_ref[:, to]
            product = dot_nt(ey, wo_ref[side])
            da = product if da is None else da + product
            starts = block_starts(spot_ref, owner, width // 16, order)
            put_blocks(dot(at_ref[...], ey), grad_ref.at[side], starts, half, part)
            stored(side, 1).start()
        da_ref[...] = da.astype(LOW)
        for side in range(2):
            for which in range(3):
                stored(side, which).wait()

    return launch(
        body,
        [spot, *refs, *down_refs, e, a2, z, slope, h2, mixed, table],
        after,
        prefetch=0,
        grid=(),
        in_specs=smem_spec() + any_specs(len(refs) + len(down_refs) + 6) + vmem_specs(1),
        out_specs=any_specs(2 * len(widths)) + vmem_specs(5),
        out_shape=[
            *[jax.ShapeDtypeStruct((width, size), LOW) for size in widths for side in range(2)],
            jax.ShapeDtypeStruct((1, width), WIDE),
            jax.ShapeDtypeStruct((1, hidden), WIDE),
            jax.ShapeDtypeStruct((rows, width), WIDE),
            jax.ShapeDtypeStruct((rows, width), LOW),
            jax.ShapeDtypeStruct((8, width), WIDE),
        ],
        scratch=[
            pltpu.VMEM((2, 2, width, half), LOW),
            pltpu.VMEM((2, width, part), LOW),
            pltpu.VMEM((rows, width), WIDE),
            pltpu.VMEM((rows, width), LOW),
            pltpu.VMEM((rows, hidden), LOW),
            pltpu.VMEM((rows, hidden), LOW),
            pltpu.VMEM((rows, width), WIDE),
            pltpu.VMEM((rows, width), LOW),
            pltpu.VMEM((rows, width), LOW),
            pltpu.VMEM((width, rows), LOW),
            pltpu.VMEM((width, rows), LOW),
            pltpu.VMEM((rows, width), WIDE),
            pltpu.VMEM((2, width, wide), LOW),
            pltpu.SemaphoreType.DMA((2, 16)),
            pltpu.SemaphoreType.DMA((2, 16)),
            pltpu.SemaphoreType.DMA((2, 16)),
            pltpu.SemaphoreType.DMA((6,)),
            pltpu.SemaphoreType.DMA((2, 3)),
        ],
        moved=cost(8 * rows * width * hidden, 8 * width * hidden + 4 * rows * hidden),
        name="mlp_backward",
    )


def attention_backward(lengths, qkv, da, mixed, lse, begin, pairs, after):
    rows, wide = qkv.shape
    width = pairs * LANES

    def body(len_ref, q_ref, k_ref, v_ref, d_ref, m_ref, lse_ref, out_ref, row_ref):
        pair = pl.program_id(0)

        @pl.when(pair == 0)
        def start():
            row_ref[...] = lse_ref[...].T

        lane = lax.broadcasted_iota(jnp.int32, (1, LANES), 1)
        sub = lax.broadcasted_iota(jnp.int32, (LANES, 1), 0)
        key = lax.broadcasted_iota(jnp.int32, (rows, 1), 0)
        shut = jnp.where(key < len_ref[0], 0.0, -1e30)
        scale = jnp.asarray(HEAD_WIDTH**-0.5, LOW)
        q = q_ref[...] * scale
        k = k_ref[...]
        v = v_ref[...]
        d = d_ref[...]
        kt = k.T * scale
        prod = (d.astype(WIDE) * m_ref[...].astype(WIDE)).T
        dks, dvs = [], []
        dqt = jnp.zeros((LANES, rows), WIDE)
        for side in range(2):
            inside = (lane >= HEAD_WIDTH) == (side == 1)
            down = (sub >= HEAD_WIDTH) == (side == 1)
            ks = jnp.where(inside, k, jnp.zeros_like(k))
            vs = jnp.where(inside, v, jnp.zeros_like(v))
            kts = jnp.where(down, kt, jnp.zeros_like(kt))
            first = side * HEAD_WIDTH
            delta = jnp.sum(prod[first : first + HEAD_WIDTH], axis=0, keepdims=True)
            log_total = row_ref[pl.ds((begin + pair) * 2 + side, 1), :]
            p = jnp.exp((dot_nt(ks, q) + shut) - log_total)
            dp = dot_nt(vs, d)
            dvs.append(dot(p.astype(LOW), d))
            ds = (p * (dp - delta)).astype(LOW)
            dks.append(dot(ds, q))
            dqt = dqt + dot(kts, ds)
        dq = dqt.T
        dk = jnp.where(lane < HEAD_WIDTH, dks[0], dks[1])
        dv = jnp.where(lane < HEAD_WIDTH, dvs[0], dvs[1])
        for n, value in enumerate((dq, dk, dv)):
            at = pl.ds(pl.multiple_of(n * width + pair * LANES, LANES), LANES)
            out_ref[:, at] = value.astype(LOW)

    return launch(
        body,
        [lengths, qkv, qkv, qkv, da, mixed, lse],
        after,
        out_shape=jax.ShapeDtypeStruct((rows, 3 * width), LOW),
        prefetch=1,
        grid=(pairs,),
        in_specs=[
            pl.BlockSpec((rows, LANES), lambda p, n: (0, p + begin)),
            pl.BlockSpec((rows, LANES), lambda p, n: (0, p + begin + PAIRS)),
            pl.BlockSpec((rows, LANES), lambda p, n: (0, p + begin + 2 * PAIRS)),
            pl.BlockSpec((rows, LANES), lambda p, n: (0, p + begin)),
            pl.BlockSpec((rows, LANES), lambda p, n: (0, p + begin)),
            pl.BlockSpec((rows, LANES), lambda p, n: (0, 0)),
        ],
        out_specs=pl.BlockSpec((rows, 3 * width), lambda p, n: (0, 0)),
        scratch=[pltpu.VMEM((LANES, rows), WIDE)],
        moved=cost(40 * rows * rows * width, 16 * rows * width, HEADS * rows * rows),
        name="attention_backward",
    )


def qkv_backward(spot, weight, dqkv, e2, h, a1, table, others, order, devices, after):
    rows, width = e2.shape
    wide = 3 * width
    half = wide // 2
    refs = weight[0]
    sums, down_sum, up_sum = others
    hidden = up_sum.shape[1]

    def body(spot_ref, *rest):
        w_refs, rest = rest[: len(refs)], rest[len(refs) :]
        d_ins, rest = rest[: len(dqkv)], rest[len(dqkv) :]
        (
            e_in, h_in, a_in, t_ref, s_ref, ds_ref, u_ref, o_ref, mine_out, rest_out,
            w_ref, d_ref, e_ref, h_ref, a_ref, at_ref, acc_ref, row_ref, pack_ref, grad_ref,
            sems, sems_r, sems_d, sems_g,
        ) = rest
        c = spot_ref[3]
        loads = [
            pltpu.make_async_copy(source, target, sems_r.at[n])
            for n, (source, target) in enumerate(
                ((a_in, a_ref), (h_in, h_ref), (e_in, e_ref))
            )
        ]
        part = width // len(dqkv)
        gathers = [
            pltpu.make_async_copy(
                d_in.at[:, pl.ds(third * part, part)],
                d_ref.at[:, pl.ds(third * width + n * part, part)],
                sems_d.at[n, third],
            )
            for n, d_in in enumerate(d_ins)
            for third in range(3)
        ]
        sides = [
            side_copies(spot_ref, weight, w_refs, side, w_ref.at[side], sems, half)
            for side in range(2)
        ]
        start_all(loads[:1], gathers, sides[0], sides[1], loads[1:])
        wait_all(loads[:1])
        at_ref[...] = a_ref[...].T
        wait_all(gathers)

        def stored(side, which):
            at = pl.ds((0, half)[which], (half, LANES)[which])
            out = (mine_out, rest_out)[side]
            return pltpu.make_async_copy(
                grad_ref.at[side, :, at], out.at[:, at], sems_g.at[side, which]
            )

        placed = []
        for side, owner in enumerate((c, 1 - c)):
            starts = block_starts(spot_ref, owner, width // 16, order)
            placed.append(starts)
            to = pl.ds(pl.multiple_of(owner * half, LANES), half)
            d = d_ref[:, to]
            put_blocks(dot(at_ref[...], d), grad_ref.at[side], starts, 0, half)
            stored(side, 0).start()
            wait_all(sides[side])
            product = dot_nt(d, w_ref[side])
            acc_ref[...] = product if side == 0 else acc_ref[...] + product
        wait_all(loads[1:])
        dv, gain, shift = norm_back(h_ref[...], t_ref[GAIN1 : GAIN1 + 1, :], acc_ref[...])
        o_ref[...] = e_ref[...] + dv
        row_ref[...] = jnp.zeros_like(row_ref)
        for row, value in (
            (GAIN1, gain),
            (GAIN2, s_ref[0:1, :]),
            (BQ, column_sum(d_ref[:, :width])),
            (BV, column_sum(d_ref[:, 2 * width :])),
            (BO, s_ref[2:3, :]),
            (BD, ds_ref[...]),
            (SH1, shift),
            (SH2, s_ref[1:2, :]),
        ):
            row_ref[row : row + 1, :] = value
        pack_ref[...] = row_ref[...].T
        share = hidden // devices
        for device in range(devices):
            at = device * (width // devices)
            pack_ref[at : at + 1, LANES - share :] = u_ref[
                0:1, device * share : (device + 1) * share
            ]
        for side in range(2):
            put_blocks(pack_ref[...], grad_ref.at[side], placed[side], half, LANES)
            stored(side, 1).start()
        for side in range(2):
            for which in range(2):
                stored(side, which).wait()

    return launch(
        body,
        [spot, *refs, *dqkv, e2, h, a1, table, sums, down_sum, up_sum],
        after,
        prefetch=0,
        grid=(),
        in_specs=smem_spec() + any_specs(len(refs) + len(dqkv) + 3) + vmem_specs(4),
        out_specs=vmem_specs(1) + any_specs(2),
        out_shape=[
            jax.ShapeDtypeStruct((rows, width), WIDE),
            jax.ShapeDtypeStruct((width, half + LANES), LOW),
            jax.ShapeDtypeStruct((width, half + LANES), LOW),
        ],
        scratch=[
            pltpu.VMEM((2, width, half), LOW),
            pltpu.VMEM((rows, wide), LOW),
            pltpu.VMEM((rows, width), WIDE),
            pltpu.VMEM((rows, width), WIDE),
            pltpu.VMEM((rows, width), LOW),
            pltpu.VMEM((width, rows), LOW),
            pltpu.VMEM((rows, width), WIDE),
            pltpu.VMEM((LANES, width), WIDE),
            pltpu.VMEM((width, LANES), WIDE),
            pltpu.VMEM((2, width, half + LANES), LOW),
            pltpu.SemaphoreType.DMA((2, 16)),
            pltpu.SemaphoreType.DMA((3,)),
            pltpu.SemaphoreType.DMA((len(dqkv), 3)),
            pltpu.SemaphoreType.DMA((2, 2)),
        ],
        moved=cost(4 * rows * width * wide, 4 * width * wide + 16 * rows * width),
        name="qkv_backward",
    )


def join(pieces):
    return jnp.concatenate(pieces, axis=0)


def finish_mlp(spot, parts, shapes):
    def body(spot_ref, *refs):
        outs = refs[-3:]
        c = spot_ref[3]
        for n, (layer, kept, got, columns) in enumerate(parts):
            for owner, ref in ((c, refs[2 * n]), (1 - c, refs[2 * n + 1])):
                column = 0
                for out, start, size in columns:
                    to = owner * (shapes[out][2] // 2) + start
                    outs[out][layer, :, pl.ds(pl.multiple_of(to, LANES), size)] = ref[
                        :, column : column + size
                    ].astype(WIDE)
                    column = column + size

    flat = [value for layer, kept, got, columns in parts for value in (kept, got)]
    return launch(
        body,
        [spot, *flat],
        [],
        prefetch=0,
        grid=(),
        in_specs=smem_spec() + vmem_specs(len(flat)),
        out_specs=vmem_specs(3),
        out_shape=[jax.ShapeDtypeStruct(shape, WIDE) for shape in shapes],
        scratch=[],
        moved=cost(0, 16 * sum(value.size for value in flat)),
        name="finish_mlp",
    )


def finish_qkv(spot, parts, shapes):
    share = shapes[3][1]
    half = shapes[0][2] // 2

    def body(spot_ref, *refs):
        qkv_ref, gain_ref, bias_ref, up_ref = refs[-4:]
        c = spot_ref[3]
        for layer in range(len(parts)):
            kept_ref, got_ref = refs[2 * layer], refs[2 * layer + 1]
            for owner, ref in ((c, kept_ref), (1 - c, got_ref)):
                start = pl.multiple_of(owner * half, LANES)
                qkv_ref[layer, :, pl.ds(start, half)] = ref[:, :half].astype(WIDE)
            packed = kept_ref[:, half : half + LANES]
            columns = packed.T
            gain_ref[layer] = columns[0:2, :]
            for n in range(6):
                bias_ref[n, layer : layer + 1, :] = columns[n + 2 : n + 3, :]
            up_ref[layer : layer + 1, :] = packed[0:1, LANES - share :]

    flat = [value for part in parts for value in part]
    return launch(
        body,
        [spot, *flat],
        [],
        prefetch=0,
        grid=(),
        in_specs=smem_spec() + vmem_specs(len(flat)),
        out_specs=vmem_specs(4),
        out_shape=[jax.ShapeDtypeStruct(shape, WIDE) for shape in shapes],
        scratch=[],
        moved=cost(0, 8 * sum(value.size for value in flat)),
        name="finish_qkv",
    )


def linear(z, x, y, c):
    return ((z * 2 + x) * 2 + y) * 2 + c


def pairs_of(step):
    result = []
    for z in range(4):
        for x in range(2):
            for y in range(2):
                for c in range(2):
                    result.append((linear(z, x, y, c), linear(*step(z, x, y, c))))
    return result


TO_Z = [pairs_of(lambda z, x, y, c, n=n: ((z + n) % 4, x, y, c)) for n in range(4)]
TO_XY = pairs_of(lambda z, x, y, c: (z, x, 1 - y, c) if c else (z, 1 - x, y, c))
TO_YX = pairs_of(lambda z, x, y, c: (z, 1 - x, y, c) if c else (z, x, 1 - y, c))


def send(value, pairs):
    return lax.ppermute(value, AXES, pairs)


def swap_cores(value):
    chips = lax.axis_size("dp") * lax.axis_size("y")
    return send(value, [(n, n ^ 1) for n in range(2 * chips)])


def stepped():
    return lax.axis_size("dp") == 8 and lax.axis_size("y") == 2


def place():
    dp = lax.axis_index("dp")
    return jnp.stack([dp // 2, dp % 2, lax.axis_index("y"), lax.axis_index("c")]).astype(jnp.int32)


def halves(pieces):
    low = [piece[:, : piece.shape[1] // 2] for piece in pieces]
    high = [piece[:, piece.shape[1] // 2 :] for piece in pieces]
    return jnp.concatenate(low, axis=1), jnp.concatenate(high, axis=1)


def both_cores(c, pieces):
    low, high = halves(pieces)
    mine = jnp.where(c == 0, low, high)
    got = swap_cores(jnp.where(c == 0, high, low))
    upper = jnp.concatenate([mine, got], axis=0)
    return jnp.where(c == 0, upper, jnp.concatenate([got, mine], axis=0))


class Chain:
    def __init__(self, steps):
        self.steps = steps
        self.result = None
        self.flying = None
        self.resume(None)

    def resume(self, arrived):
        try:
            self.waiting = self.steps.send(arrived)
        except StopIteration as end:
            self.waiting = None
            self.result = end.value

    def start(self):
        if self.waiting is not None:
            assert self.flying is None
            self.flying = [begin(value) for value, begin in self.waiting]


def offsets_of(widths):
    offsets = [0]
    for width in widths:
        offsets.append(offsets[-1] + width // 2)
    return offsets


def by(pairs):
    return lambda value: send(value, pairs)


def gather_steps(block, turns):
    ring = {0: block}
    for turn in turns:
        got = yield [(block, by(TO_Z[n])) for n in turn]
        ring.update(zip(turn, got))
    stack = join([ring[n] for n in range(4)])
    (got,) = yield [(stack, by(TO_XY))]
    near = join([stack, got])
    far, near_got = yield [(near, by(TO_YX)), (near, swap_cores)]
    (far_got,) = yield [(far, swap_cores)]
    return near, far, near_got, far_got


def gather_chips(block):
    return lax.all_gather(block, ("dp", "y"), axis=0, tiled=True)


def gather_at_once(block):
    (own,) = yield [(block, gather_chips)]
    (other,) = yield [(own, swap_cores)]
    return own, other


def added(parts):
    total = parts[0].astype(WIDE)
    for part in parts[1:]:
        total = total + part.astype(WIDE)
    return total


def last_step(c, total):
    rows = total.shape[0] // 2
    low, high = total[:rows], total[rows:]
    kept = jnp.where(c == 0, low, high).astype(WIDE)
    (got,) = yield [(jnp.where(c == 0, high, low).astype(LOW), swap_cores)]
    return kept, got


def scatter_steps(c, mine, rest, order):
    rows = mine.shape[0] // 16
    upper, lower = slice(8 * rows, 16 * rows), slice(0, 8 * rows)
    (got,) = yield [(rest, swap_cores)]
    (more,) = yield [(added([mine[upper], got[upper]]).astype(LOW), by(TO_YX))]
    parts = [mine[lower], got[lower], more]
    for along_z in (order == Z_NEXT, order == Z_LAST):
        size = parts[0].shape[0]
        kept = size // (4 if along_z else 2)
        if along_z:
            total = added(parts)
            sent = [
                (total[n * kept : (n + 1) * kept].astype(LOW), by(TO_Z[4 - n])) for n in (1, 2, 3)
            ]
        else:
            sent = [(added([part[kept:] for part in parts]).astype(LOW), by(TO_XY))]
        arrived = yield sent
        parts = [part[:kept] for part in parts] + arrived
    return (yield from last_step(c, added(parts)))


def scatter_chips(value):
    return lax.psum_scatter(value, ("dp", "y"), scatter_dimension=0, tiled=True)


def scatter_at_once(c, mine, rest):
    (got,) = yield [(rest, swap_cores)]
    (total,) = yield [(added([mine, got]).astype(LOW), scatter_chips)]
    return (yield from last_step(c, total))


def pack_small(gains, shifts, up_bias):
    rows = gains.shape[1]
    columns = jnp.concatenate([gains, shifts], axis=0).T
    share = up_bias.shape[0]
    first = jnp.pad(columns, ((0, 0), (0, LANES - share - columns.shape[1])))
    second = jnp.pad(up_bias[None, :], ((0, rows - 1), (0, 0)))
    packed = jnp.concatenate([first, second], axis=1)
    return jnp.concatenate([packed, packed], axis=1)


def local(
    hidden_in,
    cotangent,
    lengths,
    qkv_weight,
    out_weight,
    up_weight,
    down_weight,
    norm_gains,
    biases,
    up_bias,
):
    clips, slots, width = hidden_in.shape
    layers = qkv_weight.shape[0]
    hidden = down_weight.shape[1]
    assert clips == 1 and layers == 2
    by_steps = stepped()
    devices = lax.axis_size(AXES)
    spot = place()
    c = spot[3]
    chunks, spots = [], []
    for i in range(layers):
        gains, shifts, bias = (v[i].astype(LOW) for v in (norm_gains, biases, up_bias))
        chunks += [
            [qkv_weight[i].astype(LOW), pack_small(gains, shifts, bias)],
            [up_weight[i].astype(LOW), out_weight[i].astype(LOW)],
            [down_weight[i].T.astype(LOW)],
        ]
        spots += [offsets_of([piece.shape[1] for piece in chunk]) for chunk in chunks[-3:]]
    blocks = [both_cores(c, chunks[0])]
    rest = both_cores(c, [piece for chunk in chunks[1:] for piece in chunk])
    start = 0
    for at in spots[1:]:
        blocks.append(rest[:, start : start + at[-1]])
        start = start + at[-1]
    if by_steps:
        turns = [TURNS[n] for n in range(len(blocks))]
        gathers = [Chain(gather_steps(block, turn)) for block, turn in zip(blocks, turns)]
    else:
        gathers = [Chain(gather_at_once(block)) for block in blocks]
    q0, u0, d0, q1, u1, d1 = gathers

    def weight(i, chunk, member):
        n = 3 * i + chunk
        return gathers[n].result, spots[n][member], True

    rec = [{"h": hidden_in[0]}, {}]
    awaited = []

    def first_matmul(i):
        qkv, first, table, bias = qkv_forward(
            spot, weight(i, 0, 0), rec[i]["h"], hidden, devices, awaited
        )
        return {"qkv": qkv, "a1": first, "table": table, "bias": bias}

    def attend(i):
        mixed, lse = attention_forward(lengths, rec[i]["qkv"], awaited)
        return {"mixed": mixed, "lse": lse}

    def feed_up(i):
        r = rec[i]
        h2, second, z, slope = up_forward(
            spot,
            weight(i, 1, 0),
            weight(i, 1, 1),
            r["h"],
            r["mixed"],
            r["bias"],
            r["table"],
            awaited,
        )
        return {"h2": h2, "a2": second, "z": z, "slope": slope}

    def feed_down(i):
        r = rec[i]
        total = down_forward(spot, weight(i, 2, 0), r["h2"], r["z"], r["table"], awaited)
        return {"total": total}

    def feed_back(i):
        r = rec[i]
        *grads, down_sum, up_sum, e2, da, sums = mlp_backward(
            spot,
            weight(i, 1, 0),
            weight(i, 2, 0),
            weight(i, 1, 1),
            r["e"],
            r["a2"],
            r["z"],
            r["slope"],
            r["h2"],
            r["mixed"],
            r["table"],
            JOINED[i],
            ORDERS[i] if by_steps else WHOLE,
            awaited,
        )
        others = (sums, down_sum, up_sum)
        return {"first": grads[:2], "second": grads[2:], "e2": e2, "da": da, "others": others}

    def attend_back(i, begin):
        r = rec[i]
        dqkv = attention_backward(
            lengths, r["qkv"], r["da"], r["mixed"], r["lse"], begin, PAIRS // 2, awaited
        )
        return {f"dqkv{begin}": dqkv}

    def qkv_back(i):
        r = rec[i]
        e, mine, rest = qkv_backward(
            spot,
            weight(i, 0, 0),
            (r["dqkv0"], r[f"dqkv{PAIRS // 2}"]),
            r["e2"],
            r["h"],
            r["a1"],
            r["table"],
            r["others"],
            ORDERS[i] if by_steps else WHOLE,
            devices,
            awaited,
        )
        return {"e_in": e, "qkv_grad": (mine, rest)}

    def run(begin, end, *work):
        nonlocal awaited
        for chain in begin:
            chain.start()
        outs = []
        for function, i, *rest in work:
            outs.append(function(i, *rest))
            rec[i].update(outs[-1])
            awaited = []
        landing = [chain for chain in end if chain.flying is not None]
        flying = [chain.flying for chain in landing]
        arrived, outs = lax.optimization_barrier((flying, outs))
        for (function, i, *rest), new in zip(work, outs):
            rec[i].update(new)
        for chain, values in zip(landing, arrived):
            chain.flying = None
            chain.resume(values)
        awaited = awaited + [value for values in arrived for value in values]

    def drain(*chains):
        while any(chain.waiting is not None for chain in chains):
            for chain in chains:
                if chain.flying is not None:
                    values, chain.flying = chain.flying, None
                    chain.resume(values)
            for chain in chains:
                chain.start()

    def scatter(i, member):
        if by_steps:
            return Chain(scatter_steps(c, *rec[i][member], ORDERS[i]))
        return Chain(scatter_at_once(c, *rec[i][member]))

    run([q0], [q0])
    run([q0], [q0])
    run([q0, u0], [q0, u0])
    run([q0, u0, d0], [q0])
    run([], [u0], (first_matmul, 0))
    run([u0], [u0, d0], (attend, 0))
    run([u0, d0, q1], [u0, d0])
    run([d0], [d0, q1], (feed_up, 0))
    run([d0, q1, u1], [d0, q1])
    run([q1], [q1, u1], (feed_down, 0))
    rec[1]["h"] = rec[0]["total"]
    run([q1, u1, d1], [q1])
    run([], [u1], (first_matmul, 1))
    run([u1], [u1, d1], (attend, 1))
    run([u1, d1], [u1, d1])
    run([d1], [d1], (feed_up, 1))
    run([d1], [d1])

    left, right = 0, PAIRS // 2
    rec[1]["e"] = cotangent[0]
    run([], [], (feed_back, 1))
    u1, d1 = scatter(1, "first"), scatter(1, "second")
    run([d1], [d1], (attend_back, 1, left))
    run([d1, u1], [u1, d1], (attend_back, 1, right))
    run([u1], [u1], (qkv_back, 1))
    rec[0]["e"] = rec[1]["e_in"]
    q1 = scatter(1, "qkv_grad")
    run([q1], [q1])
    run([q1, d1], [q1, d1], (feed_back, 0))
    u0, d0 = scatter(0, "first"), scatter(0, "second")
    run([d0, u1, q1], [d0, u1, q1], (attend_back, 0, left))
    run([d0, u0, d1], [u0, d0, d1], (attend_back, 0, right))
    run([u0, u1, q1], [u0, u1, q1], (qkv_back, 0))
    q0 = scatter(0, "qkv_grad")
    run([q0, d0], [q0, d0])
    run([q0, u0, d0], [q0, u0, d0])
    run([q0, u0], [q0])
    run([q0], [u0, q0], (feed_down, 1))
    output = rec[1]["total"][None]
    drain(q0, u0, d0, q1, u1, d1)
    input_grad = rec[0]["e_in"][None]
    down_shape = (layers, down_weight.shape[2], hidden)
    mlp_shapes = [down_shape, up_weight.shape, out_weight.shape]
    bias_shape = (biases.shape[1], layers, biases.shape[2])
    qkv_shapes = [qkv_weight.shape, norm_gains.shape, bias_shape, up_bias.shape]
    half = hidden // 2
    first, second = [(1, 0, half), (2, 0, width // 2)], [(0, 0, half)]
    parts = [
        (0, *u0.result, first),
        (0, *d0.result, second),
        (1, *u1.result, first),
        (1, *d1.result, second),
    ]
    down_grad, up_grad, out_grad = finish_mlp(spot, parts, mlp_shapes)
    qkv_grad, gains, shifts, up_sums = finish_qkv(spot, [q0.result, q1.result], qkv_shapes)
    shifts = jnp.swapaxes(shifts, 0, 1)
    down_grad = jnp.swapaxes(down_grad, 1, 2)
    return output, input_grad, qkv_grad, out_grad, up_grad, down_grad, gains, shifts, up_sums


def solution(mesh):
    size = dict(mesh.shape)
    fine = Mesh(mesh.devices.reshape(size["dp"], size["fsdp"] // 2, 2), AXES)
    return jax.shard_map(
        local,
        mesh=fine,
        in_specs=(
            P(AXES, None, None),
            P(AXES, None, None),
            P(AXES),
            P(None, AXES, None),
            P(None, AXES, None),
            P(None, AXES, None),
            P(None, None, AXES),
            P(None, None, AXES),
            P(None, None, AXES),
            P(None, AXES),
        ),
        out_specs=(
            P(AXES, None, None),
            P(AXES, None, None),
            P(None, AXES, None),
            P(None, AXES, None),
            P(None, AXES, None),
            P(None, None, AXES),
            P(None, None, AXES),
            P(None, None, AXES),
            P(None, AXES),
        ),
        check_vma=False,
    )
```

```python
import jax
import jax.numpy as jnp
from jax import lax
from jax.experimental import pallas as pl
from jax.experimental.pallas import tpu as pltpu
from jax.sharding import Mesh
from jax.sharding import PartitionSpec as P

HEADS = 12
HEAD_WIDTH = 64
LANES = 128
PAIRS = HEADS * HEAD_WIDTH // LANES
LOW = jnp.bfloat16
WIDE = jnp.float32
norm_eps = 1e-06
AXES = ("dp", "y", "c")
WHOLE, Z_LAST, Z_NEXT = range(3)
JOINED = (False, False)
ORDERS = (Z_LAST, Z_LAST)
TURNS = (((1, 2, 3),),) * 6
VMEM_LIMIT = 60 * 1024 * 1024
TILE = 768


def cost(flops, moved, hard=0):
    return pl.CostEstimate(
        flops=int(flops) // 64, bytes_accessed=int(moved) // 64, transcendentals=int(hard) // 64
    )


def params():
    return pltpu.CompilerParams(vmem_limit_bytes=VMEM_LIMIT)


def vmem_specs(count):
    return [pl.BlockSpec(memory_space=pltpu.VMEM)] * count


def any_specs(count):
    return [pl.BlockSpec(memory_space=pl.ANY)] * count


def launch(body, args, after, prefetch, grid, in_specs, out_specs, out_shape, scratch, moved, name):
    count = len(args)

    def trimmed(*refs):
        body(*refs[:count], *refs[count + len(after) :])

    return pl.pallas_call(
        trimmed,
        out_shape=out_shape,
        grid_spec=pltpu.PrefetchScalarGridSpec(
            num_scalar_prefetch=prefetch,
            grid=grid,
            in_specs=in_specs + any_specs(len(after)),
            out_specs=out_specs,
            scratch_shapes=scratch,
        ),
        compiler_params=params(),
        cost_estimate=moved,
        name=name,
    )(*args, *after)


def smem_spec():
    return [pl.BlockSpec(memory_space=pltpu.SMEM)]


def dot(a, b):
    return jnp.dot(a, b, preferred_element_type=WIDE)


def dot_nt(a, b):
    return lax.dot_general(a, b, (((1,), (1,)), ((), ())), preferred_element_type=WIDE)


def dot_tn(a, b):
    return lax.dot_general(a, b, (((0,), (0,)), ((), ())), preferred_element_type=WIDE)


def place_of(spot, owner, block, z_first):
    z, x, y = spot[0], spot[1], spot[2]
    first, second, zr = block // 8, (block // 4) % 2, block % 4
    if not z_first:
        second, zr = block % 2, (block // 2) % 4
    bz = lax.rem(z - zr + 4, 4)
    bx = lax.rem(x + jnp.where(owner == 0, second, first), 2)
    by = lax.rem(y + jnp.where(owner == 0, first, second), 2)
    return (bz * 2 + bx) * 2 + by


def side_copies(spot, weight, refs, side, target, sems, width):
    arrays, column, z_first = weight
    at = pl.ds(column, width)
    if len(arrays) == 2:
        return [pltpu.make_async_copy(refs[side].at[:, at], target, sems.at[side, 0])]
    owner = spot[3] if side == 0 else 1 - spot[3]
    rows = arrays[0].shape[0] // 8
    copies = []
    for block in range(16):
        start = pl.multiple_of(place_of(spot, owner, block, z_first) * rows, 16)
        copies.append(
            pltpu.make_async_copy(
                refs[2 * side + block // 8].at[pl.ds((block % 8) * rows, rows), at],
                target.at[pl.ds(start, rows), :],
                sems.at[side, block],
            )
        )
    return copies


def start_all(*groups):
    for copies in groups:
        for copy in copies:
            copy.start()


def wait_all(*groups):
    for copies in groups:
        for copy in copies:
            copy.wait()


def norm_rows(v):
    center = v - jnp.mean(v, axis=-1, keepdims=True)
    r = lax.rsqrt(jnp.mean(center * center, axis=-1, keepdims=True) + norm_eps)
    return center * r, r


def norm_back(v, gain, d):
    xh, r = norm_rows(v)
    dg = d * gain
    m1 = jnp.mean(dg, axis=-1, keepdims=True)
    m2 = jnp.mean(dg * xh, axis=-1, keepdims=True)
    return (
        r * (dg - m1 - xh * m2),
        jnp.sum(d * xh, axis=0, keepdims=True),
        jnp.sum(d, axis=0, keepdims=True),
    )


GAIN1, GAIN2, BQ, BV, BO, BD, SH1, SH2 = range(8)


def qkv_forward(spot, weight, h, hidden, devices, after):
    rows, width = h.shape
    wide = 3 * width
    half = wide // 2
    refs = weight[0]

    def body(spot_ref, *rest):
        h_ref, qkv_ref, a_ref, t_ref, b_ref = rest[len(refs) : len(refs) + 5]
        w_ref, row_ref, sems = rest[len(refs) + 5 :]
        c = spot_ref[3]
        own, other = [
            side_copies(spot_ref, weight, rest, side, w_ref.at[side], sems, half + LANES)
            for side in range(2)
        ]
        start_all(own, other)
        xh, r = norm_rows(h_ref[...])
        wait_all(own)
        values = w_ref[0, :, half:].astype(WIDE)
        table = values.T[0:8, :]
        t_ref[...] = table
        share = hidden // devices
        for device in range(devices):
            at = device * (width // devices)
            b_ref[0:1, device * share : (device + 1) * share] = values[
                at : at + 1, LANES - share :
            ]
        row_ref[:, :width] = table[BQ : BQ + 1]
        row_ref[:, width : 2 * width] = jnp.zeros((1, width), WIDE)
        row_ref[:, 2 * width :] = table[BV : BV + 1]
        a = (xh * table[GAIN1 : GAIN1 + 1] + table[SH1 : SH1 + 1]).astype(LOW)
        a_ref[...] = a
        for side, owner in enumerate((c, 1 - c)):
            if side == 1:
                wait_all(other)
            to = pl.ds(pl.multiple_of(owner * half, LANES), half)
            qkv_ref[:, to] = (dot(a_ref[...], w_ref[side, :, :half]) + row_ref[:, to]).astype(LOW)

    return launch(
        body,
        [spot, *refs, h],
        after,
        prefetch=0,
        grid=(),
        in_specs=smem_spec() + any_specs(len(refs)) + vmem_specs(1),
        out_specs=vmem_specs(4),
        out_shape=[
            jax.ShapeDtypeStruct((rows, wide), LOW),
            jax.ShapeDtypeStruct((rows, width), LOW),
            jax.ShapeDtypeStruct((8, width), WIDE),
            jax.ShapeDtypeStruct((1, hidden), WIDE),
        ],
        scratch=[
            pltpu.VMEM((2, width, half + LANES), LOW),
            pltpu.VMEM((1, wide), WIDE),
            pltpu.SemaphoreType.DMA((2, 16)),
        ],
        moved=cost(2 * rows * width * wide, 2 * width * wide + 9 * rows * width),
        name="qkv_forward",
    )


def attention_forward(lengths, qkv, after):
    rows, wide = qkv.shape
    width = wide // 3

    def body(len_ref, q_ref, k_ref, v_ref, o_ref, lse_ref):
        pair = pl.program_id(0)
        lane = lax.broadcasted_iota(jnp.int32, (1, LANES), 1)
        key = lax.broadcasted_iota(jnp.int32, (1, rows), 1)
        shut = jnp.where(key < len_ref[0], 0.0, -1e30)
        q = q_ref[...] * jnp.asarray(HEAD_WIDTH**-0.5, LOW)
        k = k_ref[...]
        v = v_ref[...]
        outs = []
        stats = jnp.where(pair == 0, jnp.zeros((rows, LANES), WIDE), lse_ref[...])
        for side in range(2):
            inside = (lane >= HEAD_WIDTH) == (side == 1)
            qs = jnp.where(inside, q, jnp.zeros_like(q))
            s = dot_nt(qs, k) + shut
            peak = jnp.max(s, axis=1, keepdims=True)
            e = jnp.exp(s - peak)
            total = jnp.sum(e, axis=1, keepdims=True)
            p = (e * (1.0 / total)).astype(LOW)
            outs.append(dot(p, v))
            stats = jnp.where(lane == pair * 2 + side, peak + jnp.log(total), stats)
        lse_ref[...] = stats
        o_ref[...] = jnp.where(lane < HEAD_WIDTH, outs[0], outs[1]).astype(LOW)

    return launch(
        body,
        [lengths, qkv, qkv, qkv],
        after,
        out_shape=[
            jax.ShapeDtypeStruct((rows, width), LOW),
            jax.ShapeDtypeStruct((rows, LANES), WIDE),
        ],
        prefetch=1,
        grid=(PAIRS,),
        in_specs=[
            pl.BlockSpec((rows, LANES), lambda p, n: (0, p)),
            pl.BlockSpec((rows, LANES), lambda p, n: (0, p + PAIRS)),
            pl.BlockSpec((rows, LANES), lambda p, n: (0, p + 2 * PAIRS)),
        ],
        out_specs=[
            pl.BlockSpec((rows, LANES), lambda p, n: (0, p)),
            pl.BlockSpec((rows, LANES), lambda p, n: (0, 0)),
        ],
        moved=cost(16 * rows * rows * width, 8 * rows * width, HEADS * rows * rows),
        scratch=[],
        name="attention_forward",
    )


def gelu_parts(u):
    cdf = 0.5 * (1.0 + lax.erf(u * (0.5**0.5)))
    pdf = jnp.exp(-0.5 * u * u) * (0.3989422804014327)
    return cdf, pdf


def up_forward(spot, weight, out_weight, h, mixed, up_bias, table, after):
    rows, width = h.shape
    hidden = up_bias.shape[1]
    half = hidden // 2
    part = width // 2
    tile = TILE
    tiles = half // tile
    refs = weight[0]

    def body(spot_ref, *rest):
        w_refs, rest = rest[: len(refs)], rest[len(refs) :]
        (
            h_ref, m_ref, b_ref, t_ref, h2_ref, a_ref, z_out, s_out,
            w_ref, wo_ref, z_ref, s_ref, sems, sems_o, sems_t,
        ) = rest
        c = spot_ref[3]
        outs = [
            side_copies(spot_ref, out_weight, w_refs, side, wo_ref.at[side], sems_o, part)
            for side in range(2)
        ]
        sides = [
            side_copies(spot_ref, weight, w_refs, side, w_ref.at[side], sems, half)
            for side in range(2)
        ]
        start_all(*outs, *sides)
        wait_all(*outs)
        for side, owner in enumerate((c, 1 - c)):
            to = pl.ds(pl.multiple_of(owner * part, LANES), part)
            h2_ref[:, to] = h_ref[:, to] + (
                dot(m_ref[...], wo_ref[side]) + t_ref[BO : BO + 1, to]
            )
        xh, r = norm_rows(h2_ref[...])
        a_ref[...] = (xh * t_ref[GAIN2 : GAIN2 + 1, :] + t_ref[SH2 : SH2 + 1, :]).astype(LOW)

        def stored(step):
            side, n = step // tiles, lax.rem(step, tiles)
            owner = jnp.where(side == 0, c, 1 - c)
            at = pl.ds(pl.multiple_of(owner * half + n * tile, LANES), tile)
            return side, n, at, [
                pltpu.make_async_copy(ref.at[:, at], out.at[:, at], sems_t.at[which, step])
                for which, (ref, out) in enumerate(((z_ref, z_out), (s_ref, s_out)))
            ]

        def work(step, carry):
            side, n, at, copies = stored(step)

            for which in range(2):

                @pl.when(step == which * tiles)
                def ready():
                    wait_all(sides[which])

            up = pl.ds(pl.multiple_of(n * tile, LANES), tile)
            u = dot(a_ref[...], w_ref[side, :, up]) + b_ref[:, at]
            cdf, pdf = gelu_parts(u)
            z_ref[:, at] = (u * cdf).astype(LOW)
            s_ref[:, at] = (cdf + u * pdf).astype(LOW)
            start_all(copies)
            return carry

        lax.fori_loop(0, 2 * tiles, work, 0)
        for step in range(2 * tiles):
            wait_all(stored(step)[3])

    return launch(
        body,
        [spot, *refs, h, mixed, up_bias, table],
        after,
        prefetch=0,
        grid=(),
        in_specs=smem_spec() + any_specs(len(refs)) + vmem_specs(4),
        out_specs=vmem_specs(2) + any_specs(2),
        out_shape=[
            jax.ShapeDtypeStruct((rows, width), WIDE),
            jax.ShapeDtypeStruct((rows, width), LOW),
            jax.ShapeDtypeStruct((rows, hidden), LOW),
            jax.ShapeDtypeStruct((rows, hidden), LOW),
        ],
        scratch=[
            pltpu.VMEM((2, width, half), LOW),
            pltpu.VMEM((2, width, part), LOW),
            pltpu.VMEM((rows, hidden), LOW),
            pltpu.VMEM((rows, hidden), LOW),
            pltpu.SemaphoreType.DMA((2, 16)),
            pltpu.SemaphoreType.DMA((2, 16)),
            pltpu.SemaphoreType.DMA((2, 2 * tiles)),
        ],
        moved=cost(
            2 * rows * width * hidden, 2 * width * hidden + 4 * rows * hidden, 2 * rows * hidden
        ),
        name="up_forward",
    )


def down_forward(spot, weight, h2, z, table, after):
    rows, width = h2.shape
    hidden = z.shape[1]
    half = hidden // 2
    refs = weight[0]

    def body(spot_ref, *rest):
        h_ref, z_in, t_ref, o_ref, w_ref, z_ref, sems, sems_r = rest[len(refs) :]
        c = spot_ref[3]
        sides = [
            side_copies(spot_ref, weight, rest, side, w_ref.at[side], sems, half)
            for side in range(2)
        ]
        loads = []
        for side, owner in enumerate((c, 1 - c)):
            at = pl.ds(pl.multiple_of(owner * half, LANES), half)
            loads.append(
                [pltpu.make_async_copy(z_in.at[:, at], z_ref.at[side], sems_r.at[side])]
            )
        start_all(sides[0], loads[0], sides[1], loads[1])
        total = h_ref[...] + t_ref[BD : BD + 1, :]
        for side in range(2):
            wait_all(sides[side], loads[side])
            total = total + dot_nt(z_ref[side], w_ref[side])
        o_ref[...] = total

    return launch(
        body,
        [spot, *refs, h2, z, table],
        after,
        prefetch=0,
        grid=(),
        in_specs=smem_spec()
        + any_specs(len(refs))
        + vmem_specs(1)
        + any_specs(1)
        + vmem_specs(1),
        out_specs=vmem_specs(1),
        out_shape=[jax.ShapeDtypeStruct((rows, width), WIDE)],
        scratch=[
            pltpu.VMEM((2, width, half), LOW),
            pltpu.VMEM((2, rows, half), LOW),
            pltpu.SemaphoreType.DMA((2, 16)),
            pltpu.SemaphoreType.DMA((2,)),
        ],
        moved=cost(2 * rows * width * hidden, 2 * width * hidden + 2 * rows * hidden),
        name="down_forward",
    )[0]


def block_starts(spot, owner, rows, order):
    if order == WHOLE:
        return [block * rows for block in range(16)]
    z, x, y = spot[0], spot[1], spot[2]
    result = []
    for block in range(16):
        bz, bx, by = block // 4, (block // 2) % 2, block % 2
        zr = lax.rem(z - bz + 4, 4)
        xr = lax.rem(x + bx, 2)
        yr = lax.rem(y + by, 2)
        first = jnp.where(owner == 0, yr, xr)
        second = jnp.where(owner == 0, xr, yr)
        place = (first * 2 + second) * 4 + zr if order == Z_LAST else (first * 4 + zr) * 2 + second
        result.append(pl.multiple_of(place * rows, 16))
    return result


def put_blocks(value, out_ref, starts, column, width):
    rows = value.shape[0] // 16
    low = value.astype(LOW)
    for block, start in enumerate(starts):
        out_ref[pl.ds(start, rows), pl.ds(column, width)] = low[block * rows : (block + 1) * rows]


def column_sum(value):
    return jnp.sum(value.astype(WIDE), axis=0, keepdims=True)


def mlp_backward(
    spot, up, down, out_weight, e, a2, z, slope, h2, mixed, table, joined, order, after
):
    rows, width = e.shape
    hidden = z.shape[1]
    half = hidden // 2
    part = width // 2
    tile = TILE
    tiles = half // tile
    wide = hidden + part
    refs, down_refs = up[0], down[0]
    near = half + part
    widths = [wide] if joined else [near, half]

    def body(spot_ref, *rest):
        w_refs, rest = rest[: len(refs)], rest[len(refs) :]
        d_refs, rest = rest[: len(down_refs)], rest[len(down_refs) :]
        buffers = [rest[7 + 2 * n : 9 + 2 * n] for n in range(len(widths))]
        rest = rest[:7] + rest[7 + 2 * len(widths) :]
        (
            e_in, a_in, z_in, s_in, h_in, m_in, t_ref,
            bd_ref, bu_ref, e2_ref, da_ref, sums_ref,
            w_ref, wo_ref, e_ref, a_ref, z_ref, s_ref, h_ref, m_ref,
            em_ref, emt_ref, at_ref, acc_ref, grad_ref, sems, sems_d, sems_o, sems_r, sems_g,
        ) = rest
        c = spot_ref[3]
        loads = [
            pltpu.make_async_copy(source, target, sems_r.at[n])
            for n, (source, target) in enumerate(
                (
                    (e_in, e_ref), (a_in, a_ref), (z_in, z_ref), (s_in, s_ref), (h_in, h_ref),
                    (m_in, m_ref),
                )
            )
        ]
        sides = [
            side_copies(spot_ref, down, d_refs, side, w_ref.at[side, 1], sems_d, half)
            + side_copies(spot_ref, up, w_refs, side, w_ref.at[side, 0], sems, half)
            for side in range(2)
        ]
        outs = [
            side_copies(spot_ref, out_weight, w_refs, side, wo_ref.at[side], sems_o, part)
            for side in range(2)
        ]
        start_all(loads[:2], sides[0], loads[2:4], sides[1], loads[4:], *outs)
        wait_all(loads[:1])
        em = e_ref[...].astype(LOW)
        em_ref[...] = em
        bd_ref[...] = column_sum(em)
        emt_ref[...] = em.T
        wait_all(loads[1:2])
        at_ref[...] = a_ref[...].T
        acc_ref[...] = jnp.zeros_like(acc_ref)

        def stored(side, which):
            start, size = ((0, half), (half, part), (near, half))[which]
            out, to = buffers[-1][side], start
            if not joined:
                out, to = (buffers[1][side], 0) if which == 2 else (buffers[0][side], start)
            return pltpu.make_async_copy(
                grad_ref.at[side, :, pl.ds(start, size)],
                out.at[:, pl.ds(to, size)],
                sems_g.at[side, which],
            )

        def work(step, carry):
            side, n = step // tiles, lax.rem(step, tiles)
            owner = jnp.where(side == 0, c, 1 - c)

            @pl.when(step == 0)
            def first_ready():
                wait_all(sides[0], loads[2:4])

            @pl.when(step == tiles)
            def second_ready():
                stored(0, 0).start()
                stored(0, 2).start()
                wait_all(sides[1])

            at = pl.ds(pl.multiple_of(owner * half + n * tile, LANES), tile)
            column = pl.multiple_of(n * tile, LANES)
            tile_at = pl.ds(column, tile)
            starts = block_starts(spot_ref, owner, width // 16, order)
            grads = grad_ref.at[side]
            dz = dot(em_ref[...], w_ref[side, 1, :, tile_at])
            du = (dz * s_ref[:, at].astype(WIDE)).astype(LOW)
            bu_ref[:, at] = column_sum(du)
            put_blocks(dot(emt_ref[...], z_ref[:, at]), grads, starts, near + column, tile)
            put_blocks(dot(at_ref[...], du), grads, starts, column, tile)
            acc_ref[...] += dot_nt(du, w_ref[side, 0, :, tile_at])
            return carry

        lax.fori_loop(0, 2 * tiles, work, 0)
        stored(1, 0).start()
        stored(1, 2).start()
        wait_all(loads[4:])
        at_ref[...] = m_ref[...].T
        dv, gain, shift = norm_back(h_ref[...], t_ref[GAIN2 : GAIN2 + 1, :], acc_ref[...])
        e2 = e_ref[...] + dv
        e2_ref[...] = e2
        em_ref[...] = e2.astype(LOW)
        sums_ref[0:1, :] = gain
        sums_ref[1:2, :] = shift
        sums_ref[2:3, :] = column_sum(em_ref[...])
        wait_all(*outs)
        da = None
        for side, owner in enumerate((c, 1 - c)):
            to = pl.ds(pl.multiple_of(owner * part, LANES), part)
            ey = em_ref[:, to]
            product = dot_nt(ey, wo_ref[side])
            da = product if da is None else da + product
            starts = block_starts(spot_ref, owner, width // 16, order)
            put_blocks(dot(at_ref[...], ey), grad_ref.at[side], starts, half, part)
            stored(side, 1).start()
        da_ref[...] = da.astype(LOW)
        for side in range(2):
            for which in range(3):
                stored(side, which).wait()

    return launch(
        body,
        [spot, *refs, *down_refs, e, a2, z, slope, h2, mixed, table],
        after,
        prefetch=0,
        grid=(),
        in_specs=smem_spec() + any_specs(len(refs) + len(down_refs) + 6) + vmem_specs(1),
        out_specs=any_specs(2 * len(widths)) + vmem_specs(5),
        out_shape=[
            *[jax.ShapeDtypeStruct((width, size), LOW) for size in widths for side in range(2)],
            jax.ShapeDtypeStruct((1, width), WIDE),
            jax.ShapeDtypeStruct((1, hidden), WIDE),
            jax.ShapeDtypeStruct((rows, width), WIDE),
            jax.ShapeDtypeStruct((rows, width), LOW),
            jax.ShapeDtypeStruct((8, width), WIDE),
        ],
        scratch=[
            pltpu.VMEM((2, 2, width, half), LOW),
            pltpu.VMEM((2, width, part), LOW),
            pltpu.VMEM((rows, width), WIDE),
            pltpu.VMEM((rows, width), LOW),
            pltpu.VMEM((rows, hidden), LOW),
            pltpu.VMEM((rows, hidden), LOW),
            pltpu.VMEM((rows, width), WIDE),
            pltpu.VMEM((rows, width), LOW),
            pltpu.VMEM((rows, width), LOW),
            pltpu.VMEM((width, rows), LOW),
            pltpu.VMEM((width, rows), LOW),
            pltpu.VMEM((rows, width), WIDE),
            pltpu.VMEM((2, width, wide), LOW),
            pltpu.SemaphoreType.DMA((2, 16)),
            pltpu.SemaphoreType.DMA((2, 16)),
            pltpu.SemaphoreType.DMA((2, 16)),
            pltpu.SemaphoreType.DMA((6,)),
            pltpu.SemaphoreType.DMA((2, 3)),
        ],
        moved=cost(8 * rows * width * hidden, 8 * width * hidden + 4 * rows * hidden),
        name="mlp_backward",
    )


def attention_backward(lengths, qkv, da, mixed, lse, begin, pairs, after):
    rows, wide = qkv.shape
    width = pairs * LANES

    def body(len_ref, q_ref, k_ref, v_ref, d_ref, m_ref, lse_ref, out_ref, row_ref):
        pair = pl.program_id(0)

        @pl.when(pair == 0)
        def start():
            row_ref[...] = lse_ref[...].T

        lane = lax.broadcasted_iota(jnp.int32, (1, LANES), 1)
        sub = lax.broadcasted_iota(jnp.int32, (LANES, 1), 0)
        key = lax.broadcasted_iota(jnp.int32, (rows, 1), 0)
        shut = jnp.where(key < len_ref[0], 0.0, -1e30)
        scale = jnp.asarray(HEAD_WIDTH**-0.5, LOW)
        q = q_ref[...] * scale
        k = k_ref[...]
        v = v_ref[...]
        d = d_ref[...]
        kt = k.T * scale
        prod = (d.astype(WIDE) * m_ref[...].astype(WIDE)).T
        dks, dvs = [], []
        dqt = jnp.zeros((LANES, rows), WIDE)
        for side in range(2):
            inside = (lane >= HEAD_WIDTH) == (side == 1)
            down = (sub >= HEAD_WIDTH) == (side == 1)
            ks = jnp.where(inside, k, jnp.zeros_like(k))
            vs = jnp.where(inside, v, jnp.zeros_like(v))
            kts = jnp.where(down, kt, jnp.zeros_like(kt))
            first = side * HEAD_WIDTH
            delta = jnp.sum(prod[first : first + HEAD_WIDTH], axis=0, keepdims=True)
            log_total = row_ref[pl.ds((begin + pair) * 2 + side, 1), :]
            p = jnp.exp((dot_nt(ks, q) + shut) - log_total)
            dp = dot_nt(vs, d)
            dvs.append(dot(p.astype(LOW), d))
            ds = (p * (dp - delta)).astype(LOW)
            dks.append(dot(ds, q))
            dqt = dqt + dot(kts, ds)
        dq = dqt.T
        dk = jnp.where(lane < HEAD_WIDTH, dks[0], dks[1])
        dv = jnp.where(lane < HEAD_WIDTH, dvs[0], dvs[1])
        for n, value in enumerate((dq, dk, dv)):
            at = pl.ds(pl.multiple_of(n * width + pair * LANES, LANES), LANES)
            out_ref[:, at] = value.astype(LOW)

    return launch(
        body,
        [lengths, qkv, qkv, qkv, da, mixed, lse],
        after,
        out_shape=jax.ShapeDtypeStruct((rows, 3 * width), LOW),
        prefetch=1,
        grid=(pairs,),
        in_specs=[
            pl.BlockSpec((rows, LANES), lambda p, n: (0, p + begin)),
            pl.BlockSpec((rows, LANES), lambda p, n: (0, p + begin + PAIRS)),
            pl.BlockSpec((rows, LANES), lambda p, n: (0, p + begin + 2 * PAIRS)),
            pl.BlockSpec((rows, LANES), lambda p, n: (0, p + begin)),
            pl.BlockSpec((rows, LANES), lambda p, n: (0, p + begin)),
            pl.BlockSpec((rows, LANES), lambda p, n: (0, 0)),
        ],
        out_specs=pl.BlockSpec((rows, 3 * width), lambda p, n: (0, 0)),
        scratch=[pltpu.VMEM((LANES, rows), WIDE)],
        moved=cost(40 * rows * rows * width, 16 * rows * width, HEADS * rows * rows),
        name="attention_backward",
    )


def qkv_backward(spot, weight, dqkv, e2, h, a1, table, others, order, devices, after):
    rows, width = e2.shape
    wide = 3 * width
    half = wide // 2
    refs = weight[0]
    sums, down_sum, up_sum = others
    hidden = up_sum.shape[1]

    def body(spot_ref, *rest):
        w_refs, rest = rest[: len(refs)], rest[len(refs) :]
        d_ins, rest = rest[: len(dqkv)], rest[len(dqkv) :]
        (
            e_in, h_in, a_in, t_ref, s_ref, ds_ref, u_ref, o_ref, mine_out, rest_out,
            w_ref, d_ref, e_ref, h_ref, a_ref, at_ref, acc_ref, row_ref, pack_ref, grad_ref,
            sems, sems_r, sems_d, sems_g,
        ) = rest
        c = spot_ref[3]
        loads = [
            pltpu.make_async_copy(source, target, sems_r.at[n])
            for n, (source, target) in enumerate(
                ((a_in, a_ref), (h_in, h_ref), (e_in, e_ref))
            )
        ]
        part = width // len(dqkv)
        gathers = [
            pltpu.make_async_copy(
                d_in.at[:, pl.ds(third * part, part)],
                d_ref.at[:, pl.ds(third * width + n * part, part)],
                sems_d.at[n, third],
            )
            for n, d_in in enumerate(d_ins)
            for third in range(3)
        ]
        sides = [
            side_copies(spot_ref, weight, w_refs, side, w_ref.at[side], sems, half)
            for side in range(2)
        ]
        start_all(loads[:1], gathers, sides[0], sides[1], loads[1:])
        wait_all(loads[:1])
        at_ref[...] = a_ref[...].T
        wait_all(gathers)

        def stored(side, which):
            at = pl.ds((0, half)[which], (half, LANES)[which])
            out = (mine_out, rest_out)[side]
            return pltpu.make_async_copy(
                grad_ref.at[side, :, at], out.at[:, at], sems_g.at[side, which]
            )

        placed = []
        for side, owner in enumerate((c, 1 - c)):
            starts = block_starts(spot_ref, owner, width // 16, order)
            placed.append(starts)
            to = pl.ds(pl.multiple_of(owner * half, LANES), half)
            d = d_ref[:, to]
            put_blocks(dot(at_ref[...], d), grad_ref.at[side], starts, 0, half)
            stored(side, 0).start()
            wait_all(sides[side])
            product = dot_nt(d, w_ref[side])
            acc_ref[...] = product if side == 0 else acc_ref[...] + product
        wait_all(loads[1:])
        dv, gain, shift = norm_back(h_ref[...], t_ref[GAIN1 : GAIN1 + 1, :], acc_ref[...])
        o_ref[...] = e_ref[...] + dv
        row_ref[...] = jnp.zeros_like(row_ref)
        for row, value in (
            (GAIN1, gain),
            (GAIN2, s_ref[0:1, :]),
            (BQ, column_sum(d_ref[:, :width])),
            (BV, column_sum(d_ref[:, 2 * width :])),
            (BO, s_ref[2:3, :]),
            (BD, ds_ref[...]),
            (SH1, shift),
            (SH2, s_ref[1:2, :]),
        ):
            row_ref[row : row + 1, :] = value
        pack_ref[...] = row_ref[...].T
        share = hidden // devices
        for device in range(devices):
            at = device * (width // devices)
            pack_ref[at : at + 1, LANES - share :] = u_ref[
                0:1, device * share : (device + 1) * share
            ]
        for side in range(2):
            put_blocks(pack_ref[...], grad_ref.at[side], placed[side], half, LANES)
            stored(side, 1).start()
        for side in range(2):
            for which in range(2):
                stored(side, which).wait()

    return launch(
        body,
        [spot, *refs, *dqkv, e2, h, a1, table, sums, down_sum, up_sum],
        after,
        prefetch=0,
        grid=(),
        in_specs=smem_spec() + any_specs(len(refs) + len(dqkv) + 3) + vmem_specs(4),
        out_specs=vmem_specs(1) + any_specs(2),
        out_shape=[
            jax.ShapeDtypeStruct((rows, width), WIDE),
            jax.ShapeDtypeStruct((width, half + LANES), LOW),
            jax.ShapeDtypeStruct((width, half + LANES), LOW),
        ],
        scratch=[
            pltpu.VMEM((2, width, half), LOW),
            pltpu.VMEM((rows, wide), LOW),
            pltpu.VMEM((rows, width), WIDE),
            pltpu.VMEM((rows, width), WIDE),
            pltpu.VMEM((rows, width), LOW),
            pltpu.VMEM((width, rows), LOW),
            pltpu.VMEM((rows, width), WIDE),
            pltpu.VMEM((LANES, width), WIDE),
            pltpu.VMEM((width, LANES), WIDE),
            pltpu.VMEM((2, width, half + LANES), LOW),
            pltpu.SemaphoreType.DMA((2, 16)),
            pltpu.SemaphoreType.DMA((3,)),
            pltpu.SemaphoreType.DMA((len(dqkv), 3)),
            pltpu.SemaphoreType.DMA((2, 2)),
        ],
        moved=cost(4 * rows * width * wide, 4 * width * wide + 16 * rows * width),
        name="qkv_backward",
    )


def join(pieces):
    return jnp.concatenate(pieces, axis=0)


def finish_mlp(spot, parts, shapes):
    def body(spot_ref, *refs):
        outs = refs[-3:]
        c = spot_ref[3]
        for n, (layer, kept, got, columns) in enumerate(parts):
            for owner, ref in ((c, refs[2 * n]), (1 - c, refs[2 * n + 1])):
                column = 0
                for out, start, size in columns:
                    to = owner * (shapes[out][2] // 2) + start
                    outs[out][layer, :, pl.ds(pl.multiple_of(to, LANES), size)] = ref[
                        :, column : column + size
                    ].astype(WIDE)
                    column = column + size

    flat = [value for layer, kept, got, columns in parts for value in (kept, got)]
    return launch(
        body,
        [spot, *flat],
        [],
        prefetch=0,
        grid=(),
        in_specs=smem_spec() + vmem_specs(len(flat)),
        out_specs=vmem_specs(3),
        out_shape=[jax.ShapeDtypeStruct(shape, WIDE) for shape in shapes],
        scratch=[],
        moved=cost(0, 16 * sum(value.size for value in flat)),
        name="finish_mlp",
    )


def finish_qkv(spot, parts, shapes):
    share = shapes[3][1]
    half = shapes[0][2] // 2

    def body(spot_ref, *refs):
        qkv_ref, gain_ref, bias_ref, up_ref = refs[-4:]
        c = spot_ref[3]
        for layer in range(len(parts)):
            kept_ref, got_ref = refs[2 * layer], refs[2 * layer + 1]
            for owner, ref in ((c, kept_ref), (1 - c, got_ref)):
                start = pl.multiple_of(owner * half, LANES)
                qkv_ref[layer, :, pl.ds(start, half)] = ref[:, :half].astype(WIDE)
            packed = kept_ref[:, half : half + LANES]
            columns = packed.T
            gain_ref[layer] = columns[0:2, :]
            for n in range(6):
                bias_ref[n, layer : layer + 1, :] = columns[n + 2 : n + 3, :]
            up_ref[layer : layer + 1, :] = packed[0:1, LANES - share :]

    flat = [value for part in parts for value in part]
    return launch(
        body,
        [spot, *flat],
        [],
        prefetch=0,
        grid=(),
        in_specs=smem_spec() + vmem_specs(len(flat)),
        out_specs=vmem_specs(4),
        out_shape=[jax.ShapeDtypeStruct(shape, WIDE) for shape in shapes],
        scratch=[],
        moved=cost(0, 8 * sum(value.size for value in flat)),
        name="finish_qkv",
    )


def linear(z, x, y, c):
    return ((z * 2 + x) * 2 + y) * 2 + c


def pairs_of(step):
    result = []
    for z in range(4):
        for x in range(2):
            for y in range(2):
                for c in range(2):
                    result.append((linear(z, x, y, c), linear(*step(z, x, y, c))))
    return result


TO_Z = [pairs_of(lambda z, x, y, c, n=n: ((z + n) % 4, x, y, c)) for n in range(4)]
TO_XY = pairs_of(lambda z, x, y, c: (z, x, 1 - y, c) if c else (z, 1 - x, y, c))
TO_YX = pairs_of(lambda z, x, y, c: (z, 1 - x, y, c) if c else (z, x, 1 - y, c))


def send(value, pairs):
    return lax.ppermute(value, AXES, pairs)


def swap_cores(value):
    chips = lax.axis_size("dp") * lax.axis_size("y")
    return send(value, [(n, n ^ 1) for n in range(2 * chips)])


def stepped():
    return lax.axis_size("dp") == 8 and lax.axis_size("y") == 2


def place():
    dp = lax.axis_index("dp")
    return jnp.stack([dp // 2, dp % 2, lax.axis_index("y"), lax.axis_index("c")]).astype(jnp.int32)


def halves(pieces):
    low = [piece[:, : piece.shape[1] // 2] for piece in pieces]
    high = [piece[:, piece.shape[1] // 2 :] for piece in pieces]
    return jnp.concatenate(low, axis=1), jnp.concatenate(high, axis=1)


def both_cores(c, pieces):
    low, high = halves(pieces)
    mine = jnp.where(c == 0, low, high)
    got = swap_cores(jnp.where(c == 0, high, low))
    upper = jnp.concatenate([mine, got], axis=0)
    return jnp.where(c == 0, upper, jnp.concatenate([got, mine], axis=0))


class Chain:
    def __init__(self, steps):
        self.steps = steps
        self.result = None
        self.flying = None
        self.resume(None)

    def resume(self, arrived):
        try:
            self.waiting = self.steps.send(arrived)
        except StopIteration as end:
            self.waiting = None
            self.result = end.value

    def start(self):
        if self.waiting is not None:
            assert self.flying is None
            self.flying = [begin(value) for value, begin in self.waiting]


def offsets_of(widths):
    offsets = [0]
    for width in widths:
        offsets.append(offsets[-1] + width // 2)
    return offsets


def by(pairs):
    return lambda value: send(value, pairs)


def gather_steps(block, turns):
    ring = {0: block}
    for turn in turns:
        got = yield [(block, by(TO_Z[n])) for n in turn]
        ring.update(zip(turn, got))
    stack = lax.optimization_barrier(join([ring[n] for n in range(4)]))
    (got,) = yield [(stack, by(TO_XY))]
    near = join([stack, got])
    far, near_got = yield [(near, by(TO_YX)), (near, swap_cores)]
    (far_got,) = yield [(far, swap_cores)]
    return near, far, near_got, far_got


def gather_chips(block):
    return lax.all_gather(block, ("dp", "y"), axis=0, tiled=True)


def gather_at_once(block):
    (own,) = yield [(block, gather_chips)]
    (other,) = yield [(own, swap_cores)]
    return own, other


def added(parts):
    total = parts[0].astype(WIDE)
    for part in parts[1:]:
        total = total + part.astype(WIDE)
    return total


def last_step(c, total):
    rows = total.shape[0] // 2
    low, high = total[:rows], total[rows:]
    kept = jnp.where(c == 0, low, high).astype(WIDE)
    (got,) = yield [(jnp.where(c == 0, high, low).astype(LOW), swap_cores)]
    return kept, got


def scatter_steps(c, mine, rest, order):
    rows = mine.shape[0] // 16
    upper, lower = slice(8 * rows, 16 * rows), slice(0, 8 * rows)
    (got,) = yield [(rest, swap_cores)]
    (more,) = yield [(added([mine[upper], got[upper]]).astype(LOW), by(TO_YX))]
    parts = [mine[lower], got[lower], more]
    for along_z in (order == Z_NEXT, order == Z_LAST):
        size = parts[0].shape[0]
        kept = size // (4 if along_z else 2)
        if along_z:
            total = added(parts)
            sent = [
                (total[n * kept : (n + 1) * kept].astype(LOW), by(TO_Z[4 - n])) for n in (1, 2, 3)
            ]
        else:
            sent = [(added([part[kept:] for part in parts]).astype(LOW), by(TO_XY))]
        arrived = yield sent
        parts = [part[:kept] for part in parts] + arrived
    return (yield from last_step(c, added(parts)))


def scatter_chips(value):
    return lax.psum_scatter(value, ("dp", "y"), scatter_dimension=0, tiled=True)


def scatter_at_once(c, mine, rest):
    (got,) = yield [(rest, swap_cores)]
    (total,) = yield [(added([mine, got]).astype(LOW), scatter_chips)]
    return (yield from last_step(c, total))


def pack_small(gains, shifts, up_bias):
    rows = gains.shape[1]
    columns = jnp.concatenate([gains, shifts], axis=0).T
    share = up_bias.shape[0]
    first = jnp.pad(columns, ((0, 0), (0, LANES - share - columns.shape[1])))
    second = jnp.pad(up_bias[None, :], ((0, rows - 1), (0, 0)))
    packed = jnp.concatenate([first, second], axis=1)
    return jnp.concatenate([packed, packed], axis=1)


def local(
    hidden_in,
    cotangent,
    lengths,
    qkv_weight,
    out_weight,
    up_weight,
    down_weight,
    norm_gains,
    biases,
    up_bias,
):
    clips, slots, width = hidden_in.shape
    layers = qkv_weight.shape[0]
    hidden = down_weight.shape[1]
    assert clips == 1 and layers == 2
    by_steps = stepped()
    devices = lax.axis_size(AXES)
    spot = place()
    c = spot[3]
    chunks, spots = [], []
    for i in range(layers):
        gains, shifts, bias = (v[i].astype(LOW) for v in (norm_gains, biases, up_bias))
        chunks += [
            [qkv_weight[i].astype(LOW), pack_small(gains, shifts, bias)],
            [up_weight[i].astype(LOW), out_weight[i].astype(LOW)],
            [down_weight[i].T.astype(LOW)],
        ]
        spots += [offsets_of([piece.shape[1] for piece in chunk]) for chunk in chunks[-3:]]
    blocks = [both_cores(c, chunks[0])]
    rest = both_cores(c, [piece for chunk in chunks[1:] for piece in chunk])
    start = 0
    for at in spots[1:]:
        blocks.append(rest[:, start : start + at[-1]])
        start = start + at[-1]
    if by_steps:
        turns = [TURNS[n] for n in range(len(blocks))]
        gathers = [Chain(gather_steps(block, turn)) for block, turn in zip(blocks, turns)]
    else:
        gathers = [Chain(gather_at_once(block)) for block in blocks]
    q0, u0, d0, q1, u1, d1 = gathers

    def weight(i, chunk, member):
        n = 3 * i + chunk
        return gathers[n].result, spots[n][member], True

    rec = [{"h": hidden_in[0]}, {}]
    awaited = []

    def first_matmul(i):
        qkv, first, table, bias = qkv_forward(
            spot, weight(i, 0, 0), rec[i]["h"], hidden, devices, awaited
        )
        return {"qkv": qkv, "a1": first, "table": table, "bias": bias}

    def attend(i):
        mixed, lse = attention_forward(lengths, rec[i]["qkv"], awaited)
        return {"mixed": mixed, "lse": lse}

    def feed_up(i):
        r = rec[i]
        h2, second, z, slope = up_forward(
            spot,
            weight(i, 1, 0),
            weight(i, 1, 1),
            r["h"],
            r["mixed"],
            r["bias"],
            r["table"],
            awaited,
        )
        return {"h2": h2, "a2": second, "z": z, "slope": slope}

    def feed_down(i):
        r = rec[i]
        total = down_forward(spot, weight(i, 2, 0), r["h2"], r["z"], r["table"], awaited)
        return {"total": total}

    def feed_back(i):
        r = rec[i]
        *grads, down_sum, up_sum, e2, da, sums = mlp_backward(
            spot,
            weight(i, 1, 0),
            weight(i, 2, 0),
            weight(i, 1, 1),
            r["e"],
            r["a2"],
            r["z"],
            r["slope"],
            r["h2"],
            r["mixed"],
            r["table"],
            JOINED[i],
            ORDERS[i] if by_steps else WHOLE,
            awaited,
        )
        others = (sums, down_sum, up_sum)
        return {"first": grads[:2], "second": grads[2:], "e2": e2, "da": da, "others": others}

    def attend_back(i, begin):
        r = rec[i]
        dqkv = attention_backward(
            lengths, r["qkv"], r["da"], r["mixed"], r["lse"], begin, PAIRS // 2, awaited
        )
        return {f"dqkv{begin}": dqkv}

    def qkv_back(i):
        r = rec[i]
        e, mine, rest = qkv_backward(
            spot,
            weight(i, 0, 0),
            (r["dqkv0"], r[f"dqkv{PAIRS // 2}"]),
            r["e2"],
            r["h"],
            r["a1"],
            r["table"],
            r["others"],
            ORDERS[i] if by_steps else WHOLE,
            devices,
            awaited,
        )
        return {"e_in": e, "qkv_grad": (mine, rest)}

    def run(begin, end, *work):
        nonlocal awaited
        for chain in begin:
            chain.start()
        outs = []
        for function, i, *rest in work:
            outs.append(function(i, *rest))
            rec[i].update(outs[-1])
            awaited = []
        landing = [chain for chain in end if chain.flying is not None]
        flying = [chain.flying for chain in landing]
        arrived, outs = lax.optimization_barrier((flying, outs))
        for (function, i, *rest), new in zip(work, outs):
            rec[i].update(new)
        for chain, values in zip(landing, arrived):
            chain.flying = None
            chain.resume(values)
        awaited = awaited + [value for values in arrived for value in values]

    def drain(*chains):
        while any(chain.waiting is not None for chain in chains):
            for chain in chains:
                if chain.flying is not None:
                    values, chain.flying = chain.flying, None
                    chain.resume(values)
            for chain in chains:
                chain.start()

    def scatter(i, member):
        if by_steps:
            return Chain(scatter_steps(c, *rec[i][member], ORDERS[i]))
        return Chain(scatter_at_once(c, *rec[i][member]))

    run([q0], [q0])
    run([q0], [q0])
    run([q0, u0], [q0, u0])
    run([q0, u0], [q0])
    run([q1], [u0, q1], (first_matmul, 0))
    run([u0, d0], [u0, d0], (attend, 0))
    run([u0, d0, q1], [u0, d0, q1])
    run([d0, u1], [d0, u1], (feed_up, 0))
    run([d0], [d0])
    run([q1, d1], [q1, d1], (feed_down, 0))
    rec[1]["h"] = rec[0]["total"]
    run([q1, u1], [q1])
    run([], [u1], (first_matmul, 1))
    run([u1], [u1], (attend, 1))
    run([u1, d1], [u1, d1])
    run([d1], [d1], (feed_up, 1))
    run([d1], [d1])

    left, right = 0, PAIRS // 2
    rec[1]["e"] = cotangent[0]
    run([], [], (feed_back, 1))
    u1, d1 = scatter(1, "first"), scatter(1, "second")
    run([d1], [d1], (attend_back, 1, left))
    run([d1, u1], [u1, d1], (attend_back, 1, right))
    run([u1], [u1], (qkv_back, 1))
    rec[0]["e"] = rec[1]["e_in"]
    q1 = scatter(1, "qkv_grad")
    run([q1], [q1])
    run([q1, d1], [q1, d1], (feed_back, 0))
    u0, d0 = scatter(0, "first"), scatter(0, "second")
    run([d0, u1, q1], [d0, u1, q1], (attend_back, 0, left))
    run([d0, u0, d1], [u0, d0, d1], (attend_back, 0, right))
    run([u0, u1, q1], [u0, u1, q1], (qkv_back, 0))
    q0 = scatter(0, "qkv_grad")
    run([q0, d0], [q0, d0])
    run([q0, u0, d0], [q0, u0, d0])
    run([q0, u0], [q0])
    run([q0], [u0, q0], (feed_down, 1))
    output = rec[1]["total"][None]
    drain(q0, u0, d0, q1, u1, d1)
    input_grad = rec[0]["e_in"][None]
    down_shape = (layers, down_weight.shape[2], hidden)
    mlp_shapes = [down_shape, up_weight.shape, out_weight.shape]
    bias_shape = (biases.shape[1], layers, biases.shape[2])
    qkv_shapes = [qkv_weight.shape, norm_gains.shape, bias_shape, up_bias.shape]
    half = hidden // 2
    first, second = [(1, 0, half), (2, 0, width // 2)], [(0, 0, half)]
    parts = [
        (0, *u0.result, first),
        (0, *d0.result, second),
        (1, *u1.result, first),
        (1, *d1.result, second),
    ]
    down_grad, up_grad, out_grad = finish_mlp(spot, parts, mlp_shapes)
    qkv_grad, gains, shifts, up_sums = finish_qkv(spot, [q0.result, q1.result], qkv_shapes)
    shifts = jnp.swapaxes(shifts, 0, 1)
    down_grad = jnp.swapaxes(down_grad, 1, 2)
    return output, input_grad, qkv_grad, out_grad, up_grad, down_grad, gains, shifts, up_sums


def solution(mesh):
    size = dict(mesh.shape)
    fine = Mesh(mesh.devices.reshape(size["dp"], size["fsdp"] // 2, 2), AXES)
    return jax.shard_map(
        local,
        mesh=fine,
        in_specs=(
            P(AXES, None, None),
            P(AXES, None, None),
            P(AXES),
            P(None, AXES, None),
            P(None, AXES, None),
            P(None, AXES, None),
            P(None, None, AXES),
            P(None, None, AXES),
            P(None, None, AXES),
            P(None, AXES),
        ),
        out_specs=(
            P(AXES, None, None),
            P(AXES, None, None),
            P(None, AXES, None),
            P(None, AXES, None),
            P(None, AXES, None),
            P(None, None, AXES),
            P(None, None, AXES),
            P(None, None, AXES),
            P(None, AXES),
        ),
        check_vma=False,
    )
```

```python
import jax
import jax.numpy as jnp
from jax import lax
from jax.experimental import pallas as pl
from jax.experimental.pallas import tpu as pltpu
from jax.sharding import Mesh
from jax.sharding import PartitionSpec as P

HEADS = 12
HEAD_WIDTH = 64
LANES = 128
PAIRS = HEADS * HEAD_WIDTH // LANES
LOW = jnp.bfloat16
WIDE = jnp.float32
norm_eps = 1e-06
AXES = ("dp", "y", "c")
WHOLE, Z_LAST, Z_NEXT = range(3)
ORDERS = (Z_LAST, Z_LAST)
TURNS = (((1, 2, 3),),) * 6
VMEM_LIMIT = 60 * 1024 * 1024
TILE = 768


def cost(flops, moved, hard=0):
    return pl.CostEstimate(
        flops=int(flops) // 64, bytes_accessed=int(moved) // 64, transcendentals=int(hard) // 64
    )


def params():
    return pltpu.CompilerParams(vmem_limit_bytes=VMEM_LIMIT)


def vmem_specs(count):
    return [pl.BlockSpec(memory_space=pltpu.VMEM)] * count


def any_specs(count):
    return [pl.BlockSpec(memory_space=pl.ANY)] * count


def launch(body, args, after, prefetch, grid, in_specs, out_specs, out_shape, scratch, moved, name):
    count = len(args)

    def trimmed(*refs):
        body(*refs[:count], *refs[count + len(after) :])

    return pl.pallas_call(
        trimmed,
        out_shape=out_shape,
        grid_spec=pltpu.PrefetchScalarGridSpec(
            num_scalar_prefetch=prefetch,
            grid=grid,
            in_specs=in_specs + any_specs(len(after)),
            out_specs=out_specs,
            scratch_shapes=scratch,
        ),
        compiler_params=params(),
        cost_estimate=moved,
        name=name,
    )(*args, *after)


def smem_spec():
    return [pl.BlockSpec(memory_space=pltpu.SMEM)]


def dot(a, b):
    return jnp.dot(a, b, preferred_element_type=WIDE)


def dot_nt(a, b):
    return lax.dot_general(a, b, (((1,), (1,)), ((), ())), preferred_element_type=WIDE)


def dot_tn(a, b):
    return lax.dot_general(a, b, (((0,), (0,)), ((), ())), preferred_element_type=WIDE)


def place_of(spot, owner, block, z_first):
    z, x, y = spot[0], spot[1], spot[2]
    first, second, zr = block // 8, (block // 4) % 2, block % 4
    if not z_first:
        second, zr = block % 2, (block // 2) % 4
    bz = lax.rem(z - zr + 4, 4)
    bx = lax.rem(x + jnp.where(owner == 0, second, first), 2)
    by = lax.rem(y + jnp.where(owner == 0, first, second), 2)
    return (bz * 2 + bx) * 2 + by


def side_copies(spot, weight, refs, side, target, sems, width):
    arrays, column, z_first = weight
    at = pl.ds(column, width)
    if len(arrays) == 2:
        return [pltpu.make_async_copy(refs[side].at[:, at], target, sems.at[side, 0])]
    owner = spot[3] if side == 0 else 1 - spot[3]
    rows = arrays[0].shape[0] // 8
    copies = []
    for block in range(16):
        start = pl.multiple_of(place_of(spot, owner, block, z_first) * rows, 16)
        copies.append(
            pltpu.make_async_copy(
                refs[2 * side + block // 8].at[pl.ds((block % 8) * rows, rows), at],
                target.at[pl.ds(start, rows), :],
                sems.at[side, block],
            )
        )
    return copies


def start_all(*groups):
    for copies in groups:
        for copy in copies:
            copy.start()


def wait_all(*groups):
    for copies in groups:
        for copy in copies:
            copy.wait()


def norm_rows(v):
    center = v - jnp.mean(v, axis=-1, keepdims=True)
    r = lax.rsqrt(jnp.mean(center * center, axis=-1, keepdims=True) + norm_eps)
    return center * r, r


def norm_back(v, gain, d):
    xh, r = norm_rows(v)
    dg = d * gain
    m1 = jnp.mean(dg, axis=-1, keepdims=True)
    m2 = jnp.mean(dg * xh, axis=-1, keepdims=True)
    return (
        r * (dg - m1 - xh * m2),
        jnp.sum(d * xh, axis=0, keepdims=True),
        jnp.sum(d, axis=0, keepdims=True),
    )


GAIN1, GAIN2, BQ, BV, BO, BD, SH1, SH2 = range(8)


def qkv_forward(spot, weight, h, hidden, devices, after):
    rows, width = h.shape
    wide = 3 * width
    half = wide // 2
    refs = weight[0]

    def body(spot_ref, *rest):
        h_ref, qkv_ref, a_ref, t_ref, b_ref = rest[len(refs) : len(refs) + 5]
        w_ref, row_ref, sems = rest[len(refs) + 5 :]
        c = spot_ref[3]
        own, other = [
            side_copies(spot_ref, weight, rest, side, w_ref.at[side], sems, half + LANES)
            for side in range(2)
        ]
        start_all(own, other)
        xh, r = norm_rows(h_ref[...])
        wait_all(own)
        values = w_ref[0, :, half:].astype(WIDE)
        table = values.T[0:8, :]
        t_ref[...] = table
        share = hidden // devices
        for device in range(devices):
            at = device * (width // devices)
            b_ref[0:1, device * share : (device + 1) * share] = values[
                at : at + 1, LANES - share :
            ]
        row_ref[:, :width] = table[BQ : BQ + 1]
        row_ref[:, width : 2 * width] = jnp.zeros((1, width), WIDE)
        row_ref[:, 2 * width :] = table[BV : BV + 1]
        a = (xh * table[GAIN1 : GAIN1 + 1] + table[SH1 : SH1 + 1]).astype(LOW)
        a_ref[...] = a
        for side, owner in enumerate((c, 1 - c)):
            if side == 1:
                wait_all(other)
            to = pl.ds(pl.multiple_of(owner * half, LANES), half)
            qkv_ref[:, to] = (dot(a_ref[...], w_ref[side, :, :half]) + row_ref[:, to]).astype(LOW)

    return launch(
        body,
        [spot, *refs, h],
        after,
        prefetch=0,
        grid=(),
        in_specs=smem_spec() + any_specs(len(refs)) + vmem_specs(1),
        out_specs=vmem_specs(4),
        out_shape=[
            jax.ShapeDtypeStruct((rows, wide), LOW),
            jax.ShapeDtypeStruct((rows, width), LOW),
            jax.ShapeDtypeStruct((8, width), WIDE),
            jax.ShapeDtypeStruct((1, hidden), WIDE),
        ],
        scratch=[
            pltpu.VMEM((2, width, half + LANES), LOW),
            pltpu.VMEM((1, wide), WIDE),
            pltpu.SemaphoreType.DMA((2, 16)),
        ],
        moved=cost(2 * rows * width * wide, 2 * width * wide + 9 * rows * width),
        name="qkv_forward",
    )


def attention_forward(lengths, qkv, after):
    rows, wide = qkv.shape
    width = wide // 3

    def body(len_ref, q_ref, k_ref, v_ref, o_ref, lse_ref):
        pair = pl.program_id(0)
        lane = lax.broadcasted_iota(jnp.int32, (1, LANES), 1)
        key = lax.broadcasted_iota(jnp.int32, (1, rows), 1)
        shut = jnp.where(key < len_ref[0], 0.0, -1e30)
        q = q_ref[...] * jnp.asarray(HEAD_WIDTH**-0.5, LOW)
        k = k_ref[...]
        v = v_ref[...]
        outs = []
        stats = jnp.where(pair == 0, jnp.zeros((rows, LANES), WIDE), lse_ref[...])
        for side in range(2):
            inside = (lane >= HEAD_WIDTH) == (side == 1)
            qs = jnp.where(inside, q, jnp.zeros_like(q))
            s = dot_nt(qs, k) + shut
            peak = jnp.max(s, axis=1, keepdims=True)
            e = jnp.exp(s - peak)
            total = jnp.sum(e, axis=1, keepdims=True)
            p = (e * (1.0 / total)).astype(LOW)
            outs.append(dot(p, v))
            stats = jnp.where(lane == pair * 2 + side, peak + jnp.log(total), stats)
        lse_ref[...] = stats
        o_ref[...] = jnp.where(lane < HEAD_WIDTH, outs[0], outs[1]).astype(LOW)

    return launch(
        body,
        [lengths, qkv, qkv, qkv],
        after,
        out_shape=[
            jax.ShapeDtypeStruct((rows, width), LOW),
            jax.ShapeDtypeStruct((rows, LANES), WIDE),
        ],
        prefetch=1,
        grid=(PAIRS,),
        in_specs=[
            pl.BlockSpec((rows, LANES), lambda p, n: (0, p)),
            pl.BlockSpec((rows, LANES), lambda p, n: (0, p + PAIRS)),
            pl.BlockSpec((rows, LANES), lambda p, n: (0, p + 2 * PAIRS)),
        ],
        out_specs=[
            pl.BlockSpec((rows, LANES), lambda p, n: (0, p)),
            pl.BlockSpec((rows, LANES), lambda p, n: (0, 0)),
        ],
        moved=cost(16 * rows * rows * width, 8 * rows * width, HEADS * rows * rows),
        scratch=[],
        name="attention_forward",
    )


def gelu_parts(u):
    cdf = 0.5 * (1.0 + lax.erf(u * (0.5**0.5)))
    pdf = jnp.exp(-0.5 * u * u) * (0.3989422804014327)
    return cdf, pdf


def up_forward(spot, weight, out_weight, h, mixed, up_bias, table, after):
    rows, width = h.shape
    hidden = up_bias.shape[1]
    half = hidden // 2
    part = width // 2
    tile = TILE
    tiles = half // tile
    refs = weight[0]

    def body(spot_ref, *rest):
        w_refs, rest = rest[: len(refs)], rest[len(refs) :]
        (
            h_ref, m_ref, b_ref, t_ref, h2_ref, a_ref, z_out, s_out,
            w_ref, wo_ref, z_ref, s_ref, sems, sems_o, sems_t,
        ) = rest
        c = spot_ref[3]
        outs = [
            side_copies(spot_ref, out_weight, w_refs, side, wo_ref.at[side], sems_o, part)
            for side in range(2)
        ]
        sides = [
            side_copies(spot_ref, weight, w_refs, side, w_ref.at[side], sems, half)
            for side in range(2)
        ]
        start_all(*outs, *sides)
        wait_all(*outs)
        for side, owner in enumerate((c, 1 - c)):
            to = pl.ds(pl.multiple_of(owner * part, LANES), part)
            h2_ref[:, to] = h_ref[:, to] + (
                dot(m_ref[...], wo_ref[side]) + t_ref[BO : BO + 1, to]
            )
        xh, r = norm_rows(h2_ref[...])
        a_ref[...] = (xh * t_ref[GAIN2 : GAIN2 + 1, :] + t_ref[SH2 : SH2 + 1, :]).astype(LOW)

        def stored(step):
            side, n = step // tiles, lax.rem(step, tiles)
            owner = jnp.where(side == 0, c, 1 - c)
            at = pl.ds(pl.multiple_of(owner * half + n * tile, LANES), tile)
            return side, n, at, [
                pltpu.make_async_copy(ref.at[:, at], out.at[:, at], sems_t.at[which, step])
                for which, (ref, out) in enumerate(((z_ref, z_out), (s_ref, s_out)))
            ]

        def work(step, carry):
            side, n, at, copies = stored(step)

            for which in range(2):

                @pl.when(step == which * tiles)
                def ready():
                    wait_all(sides[which])

            up = pl.ds(pl.multiple_of(n * tile, LANES), tile)
            u = dot(a_ref[...], w_ref[side, :, up]) + b_ref[:, at]
            cdf, pdf = gelu_parts(u)
            z_ref[:, at] = (u * cdf).astype(LOW)
            s_ref[:, at] = (cdf + u * pdf).astype(LOW)
            start_all(copies)
            return carry

        lax.fori_loop(0, 2 * tiles, work, 0)
        for step in range(2 * tiles):
            wait_all(stored(step)[3])

    return launch(
        body,
        [spot, *refs, h, mixed, up_bias, table],
        after,
        prefetch=0,
        grid=(),
        in_specs=smem_spec() + any_specs(len(refs)) + vmem_specs(4),
        out_specs=vmem_specs(2) + any_specs(2),
        out_shape=[
            jax.ShapeDtypeStruct((rows, width), WIDE),
            jax.ShapeDtypeStruct((rows, width), LOW),
            jax.ShapeDtypeStruct((rows, hidden), LOW),
            jax.ShapeDtypeStruct((rows, hidden), LOW),
        ],
        scratch=[
            pltpu.VMEM((2, width, half), LOW),
            pltpu.VMEM((2, width, part), LOW),
            pltpu.VMEM((rows, hidden), LOW),
            pltpu.VMEM((rows, hidden), LOW),
            pltpu.SemaphoreType.DMA((2, 16)),
            pltpu.SemaphoreType.DMA((2, 16)),
            pltpu.SemaphoreType.DMA((2, 2 * tiles)),
        ],
        moved=cost(
            2 * rows * width * hidden, 2 * width * hidden + 4 * rows * hidden, 2 * rows * hidden
        ),
        name="up_forward",
    )


def down_forward(spot, weight, h2, z, table, after):
    rows, width = h2.shape
    hidden = z.shape[1]
    half = hidden // 2
    refs = weight[0]

    def body(spot_ref, *rest):
        h_ref, z_in, t_ref, o_ref, w_ref, z_ref, sems, sems_r = rest[len(refs) :]
        c = spot_ref[3]
        sides = [
            side_copies(spot_ref, weight, rest, side, w_ref.at[side], sems, half)
            for side in range(2)
        ]
        loads = []
        for side, owner in enumerate((c, 1 - c)):
            at = pl.ds(pl.multiple_of(owner * half, LANES), half)
            loads.append(
                [pltpu.make_async_copy(z_in.at[:, at], z_ref.at[side], sems_r.at[side])]
            )
        start_all(sides[0], loads[0], sides[1], loads[1])
        total = h_ref[...] + t_ref[BD : BD + 1, :]
        for side in range(2):
            wait_all(sides[side], loads[side])
            total = total + dot_nt(z_ref[side], w_ref[side])
        o_ref[...] = total

    return launch(
        body,
        [spot, *refs, h2, z, table],
        after,
        prefetch=0,
        grid=(),
        in_specs=smem_spec()
        + any_specs(len(refs))
        + vmem_specs(1)
        + any_specs(1)
        + vmem_specs(1),
        out_specs=vmem_specs(1),
        out_shape=[jax.ShapeDtypeStruct((rows, width), WIDE)],
        scratch=[
            pltpu.VMEM((2, width, half), LOW),
            pltpu.VMEM((2, rows, half), LOW),
            pltpu.SemaphoreType.DMA((2, 16)),
            pltpu.SemaphoreType.DMA((2,)),
        ],
        moved=cost(2 * rows * width * hidden, 2 * width * hidden + 2 * rows * hidden),
        name="down_forward",
    )[0]


def block_starts(spot, owner, rows, order):
    if order == WHOLE:
        return [block * rows for block in range(16)]
    z, x, y = spot[0], spot[1], spot[2]
    result = []
    for block in range(16):
        bz, bx, by = block // 4, (block // 2) % 2, block % 2
        zr = lax.rem(z - bz + 4, 4)
        xr = lax.rem(x + bx, 2)
        yr = lax.rem(y + by, 2)
        first = jnp.where(owner == 0, yr, xr)
        second = jnp.where(owner == 0, xr, yr)
        place = (first * 2 + second) * 4 + zr if order == Z_LAST else (first * 4 + zr) * 2 + second
        result.append(pl.multiple_of(place * rows, 16))
    return result


def put_blocks(value, out_ref, starts, column, width):
    rows = value.shape[0] // 16
    low = value.astype(LOW)
    for block, start in enumerate(starts):
        out_ref[pl.ds(start, rows), pl.ds(column, width)] = low[block * rows : (block + 1) * rows]


def column_sum(value):
    return jnp.sum(value.astype(WIDE), axis=0, keepdims=True)


def down_backward(spot, e, z, order, after):
    rows, width = e.shape
    hidden = z.shape[1]
    half = hidden // 2
    tile = TILE
    tiles = half // tile

    def body(spot_ref, e_ref, z_in, mine_out, rest_out, bd_ref, z_ref, emt_ref, grad_ref, sems, sems_g):
        c = spot_ref[3]
        loads, stores = [], []
        for side, owner in enumerate((c, 1 - c)):
            at = pl.ds(pl.multiple_of(owner * half, LANES), half)
            loads.append(pltpu.make_async_copy(z_in.at[:, at], z_ref.at[side], sems.at[side]))
            stores.append(
                pltpu.make_async_copy(
                    grad_ref.at[side], (mine_out, rest_out)[side], sems_g.at[side]
                )
            )
        start_all(loads)
        em = e_ref[...].astype(LOW)
        bd_ref[...] = column_sum(em)
        emt_ref[...] = em.T
        for side, owner in enumerate((c, 1 - c)):
            wait_all(loads[side : side + 1])
            starts = block_starts(spot_ref, owner, width // 16, order)

            def work(n, carry):
                column = pl.multiple_of(n * tile, LANES)
                product = dot(emt_ref[...], z_ref[side, :, pl.ds(column, tile)])
                put_blocks(product, grad_ref.at[side], starts, column, tile)
                return carry

            lax.fori_loop(0, tiles, work, 0)
            start_all(stores[side : side + 1])
        wait_all(stores)

    return launch(
        body,
        [spot, e, z],
        after,
        prefetch=0,
        grid=(),
        in_specs=smem_spec() + vmem_specs(1) + any_specs(1),
        out_specs=any_specs(2) + vmem_specs(1),
        out_shape=[
            jax.ShapeDtypeStruct((width, half), LOW),
            jax.ShapeDtypeStruct((width, half), LOW),
            jax.ShapeDtypeStruct((1, width), WIDE),
        ],
        scratch=[
            pltpu.VMEM((2, rows, half), LOW),
            pltpu.VMEM((width, rows), LOW),
            pltpu.VMEM((2, width, half), LOW),
            pltpu.SemaphoreType.DMA((2,)),
            pltpu.SemaphoreType.DMA((2,)),
        ],
        moved=cost(2 * rows * width * hidden, 2 * width * hidden + 2 * rows * hidden),
        name="down_backward",
    )


def mlp_backward(
    spot, up, down, out_weight, e, a2, slope, h2, mixed, table, order, after
):
    rows, width = e.shape
    hidden = slope.shape[1]
    half = hidden // 2
    part = width // 2
    tile = TILE
    tiles = half // tile
    refs, down_refs = up[0], down[0]
    near = half + part

    def body(spot_ref, *rest):
        w_refs, rest = rest[: len(refs)], rest[len(refs) :]
        d_refs, rest = rest[: len(down_refs)], rest[len(down_refs) :]
        (
            e_in, a_in, s_in, h_in, m_in, t_ref, mine_out, rest_out,
            bu_ref, e2_ref, da_ref, sums_ref,
            w_ref, wo_ref, e_ref, a_ref, s_ref, h_ref, m_ref,
            em_ref, at_ref, acc_ref, grad_ref, sems, sems_d, sems_o, sems_r, sems_g,
        ) = rest
        c = spot_ref[3]
        loads = [
            pltpu.make_async_copy(source, target, sems_r.at[n])
            for n, (source, target) in enumerate(
                (
                    (e_in, e_ref), (a_in, a_ref), (s_in, s_ref), (h_in, h_ref),
                    (m_in, m_ref),
                )
            )
        ]
        sides = [
            side_copies(spot_ref, down, d_refs, side, w_ref.at[side, 1], sems_d, half)
            + side_copies(spot_ref, up, w_refs, side, w_ref.at[side, 0], sems, half)
            for side in range(2)
        ]
        outs = [
            side_copies(spot_ref, out_weight, w_refs, side, wo_ref.at[side], sems_o, part)
            for side in range(2)
        ]
        start_all(loads[:2], sides[0], loads[2:3], sides[1], loads[3:], *outs)
        wait_all(loads[:1])
        em_ref[...] = e_ref[...].astype(LOW)
        wait_all(loads[1:2])
        at_ref[...] = a_ref[...].T
        acc_ref[...] = jnp.zeros_like(acc_ref)

        def stored(side, which):
            start, size = ((0, half), (half, part))[which]
            at = pl.ds(start, size)
            return pltpu.make_async_copy(
                grad_ref.at[side, :, at],
                (mine_out, rest_out)[side].at[:, at],
                sems_g.at[side, which],
            )

        def work(step, carry):
            side, n = step // tiles, lax.rem(step, tiles)
            owner = jnp.where(side == 0, c, 1 - c)

            @pl.when(step == 0)
            def first_ready():
                wait_all(sides[0], loads[2:3])

            @pl.when(step == tiles)
            def second_ready():
                stored(0, 0).start()
                wait_all(sides[1])

            at = pl.ds(pl.multiple_of(owner * half + n * tile, LANES), tile)
            column = pl.multiple_of(n * tile, LANES)
            tile_at = pl.ds(column, tile)
            starts = block_starts(spot_ref, owner, width // 16, order)
            grads = grad_ref.at[side]
            dz = dot(em_ref[...], w_ref[side, 1, :, tile_at])
            du = (dz * s_ref[:, at].astype(WIDE)).astype(LOW)
            bu_ref[:, at] = column_sum(du)
            put_blocks(dot(at_ref[...], du), grads, starts, column, tile)
            acc_ref[...] += dot_nt(du, w_ref[side, 0, :, tile_at])
            return carry

        lax.fori_loop(0, 2 * tiles, work, 0)
        stored(1, 0).start()
        wait_all(loads[3:])
        at_ref[...] = m_ref[...].T
        dv, gain, shift = norm_back(h_ref[...], t_ref[GAIN2 : GAIN2 + 1, :], acc_ref[...])
        e2 = e_ref[...] + dv
        e2_ref[...] = e2
        em_ref[...] = e2.astype(LOW)
        sums_ref[0:1, :] = gain
        sums_ref[1:2, :] = shift
        sums_ref[2:3, :] = column_sum(em_ref[...])
        wait_all(*outs)
        da = None
        for side, owner in enumerate((c, 1 - c)):
            to = pl.ds(pl.multiple_of(owner * part, LANES), part)
            ey = em_ref[:, to]
            product = dot_nt(ey, wo_ref[side])
            da = product if da is None else da + product
            starts = block_starts(spot_ref, owner, width // 16, order)
            put_blocks(dot(at_ref[...], ey), grad_ref.at[side], starts, half, part)
            stored(side, 1).start()
        da_ref[...] = da.astype(LOW)
        for side in range(2):
            for which in range(2):
                stored(side, which).wait()

    return launch(
        body,
        [spot, *refs, *down_refs, e, a2, slope, h2, mixed, table],
        after,
        prefetch=0,
        grid=(),
        in_specs=smem_spec() + any_specs(len(refs) + len(down_refs) + 5) + vmem_specs(1),
        out_specs=any_specs(2) + vmem_specs(4),
        out_shape=[
            jax.ShapeDtypeStruct((width, near), LOW),
            jax.ShapeDtypeStruct((width, near), LOW),
            jax.ShapeDtypeStruct((1, hidden), WIDE),
            jax.ShapeDtypeStruct((rows, width), WIDE),
            jax.ShapeDtypeStruct((rows, width), LOW),
            jax.ShapeDtypeStruct((8, width), WIDE),
        ],
        scratch=[
            pltpu.VMEM((2, 2, width, half), LOW),
            pltpu.VMEM((2, width, part), LOW),
            pltpu.VMEM((rows, width), WIDE),
            pltpu.VMEM((rows, width), LOW),
            pltpu.VMEM((rows, hidden), LOW),
            pltpu.VMEM((rows, width), WIDE),
            pltpu.VMEM((rows, width), LOW),
            pltpu.VMEM((rows, width), LOW),
            pltpu.VMEM((width, rows), LOW),
            pltpu.VMEM((rows, width), WIDE),
            pltpu.VMEM((2, width, near), LOW),
            pltpu.SemaphoreType.DMA((2, 16)),
            pltpu.SemaphoreType.DMA((2, 16)),
            pltpu.SemaphoreType.DMA((2, 16)),
            pltpu.SemaphoreType.DMA((5,)),
            pltpu.SemaphoreType.DMA((2, 2)),
        ],
        moved=cost(8 * rows * width * hidden, 8 * width * hidden + 4 * rows * hidden),
        name="mlp_backward",
    )


def attention_backward(lengths, qkv, da, mixed, lse, begin, pairs, after):
    rows, wide = qkv.shape
    width = pairs * LANES

    def body(len_ref, q_ref, k_ref, v_ref, d_ref, m_ref, lse_ref, out_ref, row_ref):
        pair = pl.program_id(0)

        @pl.when(pair == 0)
        def start():
            row_ref[...] = lse_ref[...].T

        lane = lax.broadcasted_iota(jnp.int32, (1, LANES), 1)
        sub = lax.broadcasted_iota(jnp.int32, (LANES, 1), 0)
        key = lax.broadcasted_iota(jnp.int32, (rows, 1), 0)
        shut = jnp.where(key < len_ref[0], 0.0, -1e30)
        scale = jnp.asarray(HEAD_WIDTH**-0.5, LOW)
        q = q_ref[...] * scale
        k = k_ref[...]
        v = v_ref[...]
        d = d_ref[...]
        kt = k.T * scale
        prod = (d.astype(WIDE) * m_ref[...].astype(WIDE)).T
        dks, dvs = [], []
        dqt = jnp.zeros((LANES, rows), WIDE)
        for side in range(2):
            inside = (lane >= HEAD_WIDTH) == (side == 1)
            down = (sub >= HEAD_WIDTH) == (side == 1)
            ks = jnp.where(inside, k, jnp.zeros_like(k))
            vs = jnp.where(inside, v, jnp.zeros_like(v))
            kts = jnp.where(down, kt, jnp.zeros_like(kt))
            first = side * HEAD_WIDTH
            delta = jnp.sum(prod[first : first + HEAD_WIDTH], axis=0, keepdims=True)
            log_total = row_ref[pl.ds((begin + pair) * 2 + side, 1), :]
            p = jnp.exp((dot_nt(ks, q) + shut) - log_total)
            dp = dot_nt(vs, d)
            dvs.append(dot(p.astype(LOW), d))
            ds = (p * (dp - delta)).astype(LOW)
            dks.append(dot(ds, q))
            dqt = dqt + dot(kts, ds)
        dq = dqt.T
        dk = jnp.where(lane < HEAD_WIDTH, dks[0], dks[1])
        dv = jnp.where(lane < HEAD_WIDTH, dvs[0], dvs[1])
        for n, value in enumerate((dq, dk, dv)):
            at = pl.ds(pl.multiple_of(n * width + pair * LANES, LANES), LANES)
            out_ref[:, at] = value.astype(LOW)

    return launch(
        body,
        [lengths, qkv, qkv, qkv, da, mixed, lse],
        after,
        out_shape=jax.ShapeDtypeStruct((rows, 3 * width), LOW),
        prefetch=1,
        grid=(pairs,),
        in_specs=[
            pl.BlockSpec((rows, LANES), lambda p, n: (0, p + begin)),
            pl.BlockSpec((rows, LANES), lambda p, n: (0, p + begin + PAIRS)),
            pl.BlockSpec((rows, LANES), lambda p, n: (0, p + begin + 2 * PAIRS)),
            pl.BlockSpec((rows, LANES), lambda p, n: (0, p + begin)),
            pl.BlockSpec((rows, LANES), lambda p, n: (0, p + begin)),
            pl.BlockSpec((rows, LANES), lambda p, n: (0, 0)),
        ],
        out_specs=pl.BlockSpec((rows, 3 * width), lambda p, n: (0, 0)),
        scratch=[pltpu.VMEM((LANES, rows), WIDE)],
        moved=cost(40 * rows * rows * width, 16 * rows * width, HEADS * rows * rows),
        name="attention_backward",
    )


def qkv_backward(spot, weight, dqkv, e2, h, a1, table, others, order, devices, after):
    rows, width = e2.shape
    wide = 3 * width
    half = wide // 2
    refs = weight[0]
    sums, down_sum, up_sum = others
    hidden = up_sum.shape[1]

    def body(spot_ref, *rest):
        w_refs, rest = rest[: len(refs)], rest[len(refs) :]
        d_ins, rest = rest[: len(dqkv)], rest[len(dqkv) :]
        (
            e_in, h_in, a_in, t_ref, s_ref, ds_ref, u_ref, o_ref, mine_out, rest_out,
            w_ref, d_ref, e_ref, h_ref, a_ref, at_ref, acc_ref, row_ref, pack_ref, grad_ref,
            sems, sems_r, sems_d, sems_g,
        ) = rest
        c = spot_ref[3]
        loads = [
            pltpu.make_async_copy(source, target, sems_r.at[n])
            for n, (source, target) in enumerate(
                ((a_in, a_ref), (h_in, h_ref), (e_in, e_ref))
            )
        ]
        part = width // len(dqkv)
        gathers = [
            pltpu.make_async_copy(
                d_in.at[:, pl.ds(third * part, part)],
                d_ref.at[:, pl.ds(third * width + n * part, part)],
                sems_d.at[n, third],
            )
            for n, d_in in enumerate(d_ins)
            for third in range(3)
        ]
        sides = [
            side_copies(spot_ref, weight, w_refs, side, w_ref.at[side], sems, half)
            for side in range(2)
        ]
        start_all(loads[:1], gathers, sides[0], sides[1], loads[1:])
        wait_all(loads[:1])
        at_ref[...] = a_ref[...].T
        wait_all(gathers)

        def stored(side, which):
            at = pl.ds((0, half)[which], (half, LANES)[which])
            out = (mine_out, rest_out)[side]
            return pltpu.make_async_copy(
                grad_ref.at[side, :, at], out.at[:, at], sems_g.at[side, which]
            )

        placed = []
        for side, owner in enumerate((c, 1 - c)):
            starts = block_starts(spot_ref, owner, width // 16, order)
            placed.append(starts)
            to = pl.ds(pl.multiple_of(owner * half, LANES), half)
            d = d_ref[:, to]
            put_blocks(dot(at_ref[...], d), grad_ref.at[side], starts, 0, half)
            stored(side, 0).start()
            wait_all(sides[side])
            product = dot_nt(d, w_ref[side])
            acc_ref[...] = product if side == 0 else acc_ref[...] + product
        wait_all(loads[1:])
        dv, gain, shift = norm_back(h_ref[...], t_ref[GAIN1 : GAIN1 + 1, :], acc_ref[...])
        o_ref[...] = e_ref[...] + dv
        row_ref[...] = jnp.zeros_like(row_ref)
        for row, value in (
            (GAIN1, gain),
            (GAIN2, s_ref[0:1, :]),
            (BQ, column_sum(d_ref[:, :width])),
            (BV, column_sum(d_ref[:, 2 * width :])),
            (BO, s_ref[2:3, :]),
            (BD, ds_ref[...]),
            (SH1, shift),
            (SH2, s_ref[1:2, :]),
        ):
            row_ref[row : row + 1, :] = value
        pack_ref[...] = row_ref[...].T
        share = hidden // devices
        for device in range(devices):
            at = device * (width // devices)
            pack_ref[at : at + 1, LANES - share :] = u_ref[
                0:1, device * share : (device + 1) * share
            ]
        for side in range(2):
            put_blocks(pack_ref[...], grad_ref.at[side], placed[side], half, LANES)
            stored(side, 1).start()
        for side in range(2):
            for which in range(2):
                stored(side, which).wait()

    return launch(
        body,
        [spot, *refs, *dqkv, e2, h, a1, table, sums, down_sum, up_sum],
        after,
        prefetch=0,
        grid=(),
        in_specs=smem_spec() + any_specs(len(refs) + len(dqkv) + 3) + vmem_specs(4),
        out_specs=vmem_specs(1) + any_specs(2),
        out_shape=[
            jax.ShapeDtypeStruct((rows, width), WIDE),
            jax.ShapeDtypeStruct((width, half + LANES), LOW),
            jax.ShapeDtypeStruct((width, half + LANES), LOW),
        ],
        scratch=[
            pltpu.VMEM((2, width, half), LOW),
            pltpu.VMEM((rows, wide), LOW),
            pltpu.VMEM((rows, width), WIDE),
            pltpu.VMEM((rows, width), WIDE),
            pltpu.VMEM((rows, width), LOW),
            pltpu.VMEM((width, rows), LOW),
            pltpu.VMEM((rows, width), WIDE),
            pltpu.VMEM((LANES, width), WIDE),
            pltpu.VMEM((width, LANES), WIDE),
            pltpu.VMEM((2, width, half + LANES), LOW),
            pltpu.SemaphoreType.DMA((2, 16)),
            pltpu.SemaphoreType.DMA((3,)),
            pltpu.SemaphoreType.DMA((len(dqkv), 3)),
            pltpu.SemaphoreType.DMA((2, 2)),
        ],
        moved=cost(4 * rows * width * wide, 4 * width * wide + 16 * rows * width),
        name="qkv_backward",
    )


def join(pieces):
    return jnp.concatenate(pieces, axis=0)


def finish_mlp(spot, parts, shapes):
    def body(spot_ref, *refs):
        outs = refs[-3:]
        c = spot_ref[3]
        for n, (layer, kept, got, columns) in enumerate(parts):
            for owner, ref in ((c, refs[2 * n]), (1 - c, refs[2 * n + 1])):
                column = 0
                for out, start, size in columns:
                    to = owner * (shapes[out][2] // 2) + start
                    outs[out][layer, :, pl.ds(pl.multiple_of(to, LANES), size)] = ref[
                        :, column : column + size
                    ].astype(WIDE)
                    column = column + size

    flat = [value for layer, kept, got, columns in parts for value in (kept, got)]
    return launch(
        body,
        [spot, *flat],
        [],
        prefetch=0,
        grid=(),
        in_specs=smem_spec() + vmem_specs(len(flat)),
        out_specs=vmem_specs(3),
        out_shape=[jax.ShapeDtypeStruct(shape, WIDE) for shape in shapes],
        scratch=[],
        moved=cost(0, 16 * sum(value.size for value in flat)),
        name="finish_mlp",
    )


def finish_qkv(spot, parts, shapes, after):
    share = shapes[3][1]
    half = shapes[0][2] // 2

    def body(spot_ref, *refs):
        qkv_ref, gain_ref, bias_ref, up_ref = refs[-4:]
        c = spot_ref[3]
        for layer in range(len(parts)):
            kept_ref, got_ref = refs[2 * layer], refs[2 * layer + 1]
            for owner, ref in ((c, kept_ref), (1 - c, got_ref)):
                start = pl.multiple_of(owner * half, LANES)
                qkv_ref[layer, :, pl.ds(start, half)] = ref[:, :half].astype(WIDE)
            packed = kept_ref[:, half : half + LANES]
            columns = packed.T
            gain_ref[layer] = columns[0:2, :]
            for n in range(6):
                bias_ref[n, layer : layer + 1, :] = columns[n + 2 : n + 3, :]
            up_ref[layer : layer + 1, :] = packed[0:1, LANES - share :]

    flat = [value for part in parts for value in part]
    return launch(
        body,
        [spot, *flat],
        after,
        prefetch=0,
        grid=(),
        in_specs=smem_spec() + vmem_specs(len(flat)),
        out_specs=vmem_specs(4),
        out_shape=[jax.ShapeDtypeStruct(shape, WIDE) for shape in shapes],
        scratch=[],
        moved=cost(0, 8 * sum(value.size for value in flat)),
        name="finish_qkv",
    )


def linear(z, x, y, c):
    return ((z * 2 + x) * 2 + y) * 2 + c


def pairs_of(step):
    result = []
    for z in range(4):
        for x in range(2):
            for y in range(2):
                for c in range(2):
                    result.append((linear(z, x, y, c), linear(*step(z, x, y, c))))
    return result


TO_Z = [pairs_of(lambda z, x, y, c, n=n: ((z + n) % 4, x, y, c)) for n in range(4)]
TO_XY = pairs_of(lambda z, x, y, c: (z, x, 1 - y, c) if c else (z, 1 - x, y, c))
TO_YX = pairs_of(lambda z, x, y, c: (z, 1 - x, y, c) if c else (z, x, 1 - y, c))


def send(value, pairs):
    return lax.ppermute(value, AXES, pairs)


def swap_cores(value):
    chips = lax.axis_size("dp") * lax.axis_size("y")
    return send(value, [(n, n ^ 1) for n in range(2 * chips)])


def stepped():
    return lax.axis_size("dp") == 8 and lax.axis_size("y") == 2


def place():
    dp = lax.axis_index("dp")
    return jnp.stack([dp // 2, dp % 2, lax.axis_index("y"), lax.axis_index("c")]).astype(jnp.int32)


def halves(pieces):
    low = [piece[:, : piece.shape[1] // 2] for piece in pieces]
    high = [piece[:, piece.shape[1] // 2 :] for piece in pieces]
    return jnp.concatenate(low, axis=1), jnp.concatenate(high, axis=1)


def both_cores(c, pieces):
    low, high = halves(pieces)
    mine = jnp.where(c == 0, low, high)
    got = swap_cores(jnp.where(c == 0, high, low))
    upper = jnp.concatenate([mine, got], axis=0)
    return jnp.where(c == 0, upper, jnp.concatenate([got, mine], axis=0))


class Chain:
    def __init__(self, steps):
        self.steps = steps
        self.result = None
        self.flying = None
        self.resume(None)

    def resume(self, arrived):
        try:
            self.waiting = self.steps.send(arrived)
        except StopIteration as end:
            self.waiting = None
            self.result = end.value

    def start(self):
        if self.waiting is not None:
            assert self.flying is None
            self.flying = [begin(value) for value, begin in self.waiting]


def offsets_of(widths):
    offsets = [0]
    for width in widths:
        offsets.append(offsets[-1] + width // 2)
    return offsets


def by(pairs):
    return lambda value: send(value, pairs)


def gather_steps(block, turns):
    ring = {0: block}
    for turn in turns:
        got = yield [(block, by(TO_Z[n])) for n in turn]
        ring.update(zip(turn, got))
    stack = lax.optimization_barrier(join([ring[n] for n in range(4)]))
    (got,) = yield [(stack, by(TO_XY))]
    near = join([stack, got])
    far, near_got = yield [(near, by(TO_YX)), (near, swap_cores)]
    (far_got,) = yield [(far, swap_cores)]
    return near, far, near_got, far_got


def gather_chips(block):
    return lax.all_gather(block, ("dp", "y"), axis=0, tiled=True)


def gather_at_once(block):
    (own,) = yield [(block, gather_chips)]
    (other,) = yield [(own, swap_cores)]
    return own, other


def added(parts):
    total = parts[0].astype(WIDE)
    for part in parts[1:]:
        total = total + part.astype(WIDE)
    return total


def last_step(c, total):
    rows = total.shape[0] // 2
    low, high = total[:rows], total[rows:]
    kept = jnp.where(c == 0, low, high).astype(WIDE)
    (got,) = yield [(jnp.where(c == 0, high, low).astype(LOW), swap_cores)]
    return kept, got


def scatter_steps(c, mine, rest, order):
    rows = mine.shape[0] // 16
    upper, lower = slice(8 * rows, 16 * rows), slice(0, 8 * rows)
    (got,) = yield [(rest, swap_cores)]
    (more,) = yield [(added([mine[upper], got[upper]]).astype(LOW), by(TO_YX))]
    parts = [mine[lower], got[lower], more]
    for along_z in (order == Z_NEXT, order == Z_LAST):
        size = parts[0].shape[0]
        kept = size // (4 if along_z else 2)
        if along_z:
            total = added(parts)
            sent = [
                (total[n * kept : (n + 1) * kept].astype(LOW), by(TO_Z[4 - n])) for n in (1, 2, 3)
            ]
        else:
            sent = [(added([part[kept:] for part in parts]).astype(LOW), by(TO_XY))]
        arrived = yield sent
        parts = [part[:kept] for part in parts] + arrived
    return (yield from last_step(c, added(parts)))


def scatter_chips(value):
    return lax.psum_scatter(value, ("dp", "y"), scatter_dimension=0, tiled=True)


def scatter_at_once(c, mine, rest):
    (got,) = yield [(rest, swap_cores)]
    (total,) = yield [(added([mine, got]).astype(LOW), scatter_chips)]
    return (yield from last_step(c, total))


def pack_small(gains, shifts, up_bias):
    rows = gains.shape[1]
    columns = jnp.concatenate([gains, shifts], axis=0).T
    share = up_bias.shape[0]
    first = jnp.pad(columns, ((0, 0), (0, LANES - share - columns.shape[1])))
    second = jnp.pad(up_bias[None, :], ((0, rows - 1), (0, 0)))
    packed = jnp.concatenate([first, second], axis=1)
    return jnp.concatenate([packed, packed], axis=1)


def local(
    hidden_in,
    cotangent,
    lengths,
    qkv_weight,
    out_weight,
    up_weight,
    down_weight,
    norm_gains,
    biases,
    up_bias,
):
    clips, slots, width = hidden_in.shape
    layers = qkv_weight.shape[0]
    hidden = down_weight.shape[1]
    assert clips == 1 and layers == 2
    by_steps = stepped()
    devices = lax.axis_size(AXES)
    spot = place()
    c = spot[3]
    chunks, spots = [], []
    for i in range(layers):
        gains, shifts, bias = (v[i].astype(LOW) for v in (norm_gains, biases, up_bias))
        chunks += [
            [qkv_weight[i].astype(LOW), pack_small(gains, shifts, bias)],
            [up_weight[i].astype(LOW), out_weight[i].astype(LOW)],
            [down_weight[i].T.astype(LOW)],
        ]
        spots += [offsets_of([piece.shape[1] for piece in chunk]) for chunk in chunks[-3:]]
    blocks = [both_cores(c, chunks[0])]
    rest = both_cores(c, [piece for chunk in chunks[1:] for piece in chunk])
    start = 0
    for at in spots[1:]:
        blocks.append(rest[:, start : start + at[-1]])
        start = start + at[-1]
    if by_steps:
        turns = [TURNS[n] for n in range(len(blocks))]
        gathers = [Chain(gather_steps(block, turn)) for block, turn in zip(blocks, turns)]
    else:
        gathers = [Chain(gather_at_once(block)) for block in blocks]
    q0, u0, d0, q1, u1, d1 = gathers

    def weight(i, chunk, member):
        n = 3 * i + chunk
        return gathers[n].result, spots[n][member], True

    rec = [{"h": hidden_in[0]}, {}]
    awaited = []

    def first_matmul(i):
        qkv, first, table, bias = qkv_forward(
            spot, weight(i, 0, 0), rec[i]["h"], hidden, devices, awaited
        )
        return {"qkv": qkv, "a1": first, "table": table, "bias": bias}

    def attend(i):
        mixed, lse = attention_forward(lengths, rec[i]["qkv"], awaited)
        return {"mixed": mixed, "lse": lse}

    def feed_up(i):
        r = rec[i]
        h2, second, z, slope = up_forward(
            spot,
            weight(i, 1, 0),
            weight(i, 1, 1),
            r["h"],
            r["mixed"],
            r["bias"],
            r["table"],
            awaited,
        )
        return {"h2": h2, "a2": second, "z": z, "slope": slope}

    def feed_down(i):
        r = rec[i]
        total = down_forward(spot, weight(i, 2, 0), r["h2"], r["z"], r["table"], awaited)
        return {"total": total}

    def down_back(i):
        r = rec[i]
        order = ORDERS[i] if by_steps else WHOLE
        mine, rest, down_sum = down_backward(spot, r["e"], r["z"], order, awaited)
        return {"second": (mine, rest), "down_sum": down_sum}

    def feed_back(i):
        r = rec[i]
        mine, rest, up_sum, e2, da, sums = mlp_backward(
            spot,
            weight(i, 1, 0),
            weight(i, 2, 0),
            weight(i, 1, 1),
            r["e"],
            r["a2"],
            r["slope"],
            r["h2"],
            r["mixed"],
            r["table"],
            ORDERS[i] if by_steps else WHOLE,
            awaited,
        )
        others = (sums, r["down_sum"], up_sum)
        return {"first": (mine, rest), "e2": e2, "da": da, "others": others}

    def attend_back(i, begin):
        r = rec[i]
        dqkv = attention_backward(
            lengths, r["qkv"], r["da"], r["mixed"], r["lse"], begin, PAIRS // 2, awaited
        )
        return {f"dqkv{begin}": dqkv}

    def qkv_back(i):
        r = rec[i]
        e, mine, rest = qkv_backward(
            spot,
            weight(i, 0, 0),
            (r["dqkv0"], r[f"dqkv{PAIRS // 2}"]),
            r["e2"],
            r["h"],
            r["a1"],
            r["table"],
            r["others"],
            ORDERS[i] if by_steps else WHOLE,
            devices,
            awaited,
        )
        return {"e_in": e, "qkv_grad": (mine, rest)}

    def run(begin, end, *work):
        nonlocal awaited
        for chain in begin:
            chain.start()
        outs = []
        for function, i, *rest in work:
            outs.append(function(i, *rest))
            rec[i].update(outs[-1])
            awaited = []
        landing = [chain for chain in end if chain.flying is not None]
        flying = [chain.flying for chain in landing]
        arrived, outs = lax.optimization_barrier((flying, outs))
        for (function, i, *rest), new in zip(work, outs):
            rec[i].update(new)
        for chain, values in zip(landing, arrived):
            chain.flying = None
            chain.resume(values)
        awaited = awaited + [value for values in arrived for value in values]

    def drain(*chains):
        while any(chain.waiting is not None for chain in chains):
            for chain in chains:
                if chain.flying is not None:
                    values, chain.flying = chain.flying, None
                    chain.resume(values)
            for chain in chains:
                chain.start()

    def scatter(i, member):
        if by_steps:
            return Chain(scatter_steps(c, *rec[i][member], ORDERS[i]))
        return Chain(scatter_at_once(c, *rec[i][member]))

    run([q0], [q0])
    run([q0], [q0])
    run([q0, u0], [q0, u0])
    run([q0, u0], [q0])
    run([q1], [u0, q1], (first_matmul, 0))
    run([u0, d0], [u0, d0], (attend, 0))
    run([u0, d0, q1], [u0, d0, q1])
    run([d0, u1], [d0, u1], (feed_up, 0))
    run([d0], [d0])
    run([q1, d1], [q1, d1], (feed_down, 0))
    rec[1]["h"] = rec[0]["total"]
    run([q1, u1], [q1])
    run([], [u1], (first_matmul, 1))
    run([u1], [u1], (attend, 1))
    run([u1, d1], [u1, d1])
    run([d1], [d1], (feed_up, 1))
    left, right = 0, PAIRS // 2
    rec[1]["e"] = cotangent[0]
    run([d1], [d1], (down_back, 1))
    d1 = scatter(1, "second")
    run([d1], [d1], (feed_back, 1))
    u1 = scatter(1, "first")
    run([d1, u1], [d1, u1], (attend_back, 1, left), (attend_back, 1, right))
    run([u1], [u1], (qkv_back, 1))
    rec[0]["e"] = rec[1]["e_in"]
    q1 = scatter(1, "qkv_grad")
    run([q1], [q1], (down_back, 0))
    d0 = scatter(0, "second")
    run([q1, d1, d0], [q1, d1, d0], (feed_back, 0))
    u0 = scatter(0, "first")
    run([u0, d0, u1, d1, q1], [u0, d0, u1, d1, q1], (attend_back, 0, left), (attend_back, 0, right))
    run([u0, u1, q1], [u0, u1, q1], (qkv_back, 0))
    q0 = scatter(0, "qkv_grad")
    run([q0, d0], [q0, d0])
    run([q0, u0, d0], [q0, u0, d0])
    run([q0, u0], [q0])
    run([q0], [u0, q0], (feed_down, 1))
    output = rec[1]["total"][None]
    drain(q0, u0, d0, q1, u1, d1)
    input_grad = rec[0]["e_in"][None]
    down_shape = (layers, down_weight.shape[2], hidden)
    mlp_shapes = [down_shape, up_weight.shape, out_weight.shape]
    bias_shape = (biases.shape[1], layers, biases.shape[2])
    qkv_shapes = [qkv_weight.shape, norm_gains.shape, bias_shape, up_bias.shape]
    half = hidden // 2
    first, second = [(1, 0, half), (2, 0, width // 2)], [(0, 0, half)]
    parts = [
        (0, *u0.result, first),
        (0, *d0.result, second),
        (1, *u1.result, first),
        (1, *d1.result, second),
    ]
    down_grad, up_grad, out_grad = finish_mlp(spot, parts, mlp_shapes)
    qkv_grad, gains, shifts, up_sums = finish_qkv(spot, [q0.result, q1.result], qkv_shapes, [])
    shifts = jnp.swapaxes(shifts, 0, 1)
    down_grad = jnp.swapaxes(down_grad, 1, 2)
    return output, input_grad, qkv_grad, out_grad, up_grad, down_grad, gains, shifts, up_sums


def solution(mesh):
    size = dict(mesh.shape)
    fine = Mesh(mesh.devices.reshape(size["dp"], size["fsdp"] // 2, 2), AXES)
    return jax.shard_map(
        local,
        mesh=fine,
        in_specs=(
            P(AXES, None, None),
            P(AXES, None, None),
            P(AXES),
            P(None, AXES, None),
            P(None, AXES, None),
            P(None, AXES, None),
            P(None, None, AXES),
            P(None, None, AXES),
            P(None, None, AXES),
            P(None, AXES),
        ),
        out_specs=(
            P(AXES, None, None),
            P(AXES, None, None),
            P(None, AXES, None),
            P(None, AXES, None),
            P(None, AXES, None),
            P(None, None, AXES),
            P(None, None, AXES),
            P(None, None, AXES),
            P(None, AXES),
        ),
        check_vma=False,
    )
```

```python
import jax
import jax.numpy as jnp
from jax import lax
from jax.experimental import pallas as pl
from jax.experimental.pallas import tpu as pltpu
from jax.sharding import Mesh
from jax.sharding import PartitionSpec as P

HEADS = 12
HEAD_WIDTH = 64
LANES = 128
PAIRS = HEADS * HEAD_WIDTH // LANES
LOW = jnp.bfloat16
WIDE = jnp.float32
norm_eps = 1e-06
AXES = ("dp", "y", "c")
WHOLE, Z_LAST, Z_NEXT = range(3)
ORDERS = (Z_LAST, Z_LAST)
TURNS = (((1, 2, 3),),) * 6
VMEM_LIMIT = 60 * 1024 * 1024
TILE = 768


def cost(flops, moved, hard=0):
    return pl.CostEstimate(
        flops=int(flops) // 64, bytes_accessed=int(moved) // 64, transcendentals=int(hard) // 64
    )


def params():
    return pltpu.CompilerParams(vmem_limit_bytes=VMEM_LIMIT)


def vmem_specs(count):
    return [pl.BlockSpec(memory_space=pltpu.VMEM)] * count


def any_specs(count):
    return [pl.BlockSpec(memory_space=pl.ANY)] * count


def launch(body, args, after, prefetch, grid, in_specs, out_specs, out_shape, scratch, moved, name):
    count = len(args)

    def trimmed(*refs):
        body(*refs[:count], *refs[count + len(after) :])

    return pl.pallas_call(
        trimmed,
        out_shape=out_shape,
        grid_spec=pltpu.PrefetchScalarGridSpec(
            num_scalar_prefetch=prefetch,
            grid=grid,
            in_specs=in_specs + any_specs(len(after)),
            out_specs=out_specs,
            scratch_shapes=scratch,
        ),
        compiler_params=params(),
        cost_estimate=moved,
        name=name,
    )(*args, *after)


def smem_spec():
    return [pl.BlockSpec(memory_space=pltpu.SMEM)]


def dot(a, b):
    return jnp.dot(a, b, preferred_element_type=WIDE)


def dot_nt(a, b):
    return lax.dot_general(a, b, (((1,), (1,)), ((), ())), preferred_element_type=WIDE)


def dot_tn(a, b):
    return lax.dot_general(a, b, (((0,), (0,)), ((), ())), preferred_element_type=WIDE)


def place_of(spot, owner, block, z_first):
    z, x, y = spot[0], spot[1], spot[2]
    first, second, zr = block // 8, (block // 4) % 2, block % 4
    if not z_first:
        second, zr = block % 2, (block // 2) % 4
    bz = lax.rem(z - zr + 4, 4)
    bx = lax.rem(x + jnp.where(owner == 0, second, first), 2)
    by = lax.rem(y + jnp.where(owner == 0, first, second), 2)
    return (bz * 2 + bx) * 2 + by


def side_copies(spot, weight, refs, side, target, sems, width):
    arrays, column, z_first = weight
    at = pl.ds(column, width)
    if len(arrays) == 2:
        return [pltpu.make_async_copy(refs[side].at[:, at], target, sems.at[side, 0])]
    owner = spot[3] if side == 0 else 1 - spot[3]
    rows = arrays[0].shape[0] // 8
    copies = []
    for block in range(16):
        start = pl.multiple_of(place_of(spot, owner, block, z_first) * rows, 16)
        copies.append(
            pltpu.make_async_copy(
                refs[2 * side + block // 8].at[pl.ds((block % 8) * rows, rows), at],
                target.at[pl.ds(start, rows), :],
                sems.at[side, block],
            )
        )
    return copies


def start_all(*groups):
    for copies in groups:
        for copy in copies:
            copy.start()


def wait_all(*groups):
    for copies in groups:
        for copy in copies:
            copy.wait()


def norm_rows(v):
    center = v - jnp.mean(v, axis=-1, keepdims=True)
    r = lax.rsqrt(jnp.mean(center * center, axis=-1, keepdims=True) + norm_eps)
    return center * r, r


def norm_back(v, gain, d):
    xh, r = norm_rows(v)
    dg = d * gain
    m1 = jnp.mean(dg, axis=-1, keepdims=True)
    m2 = jnp.mean(dg * xh, axis=-1, keepdims=True)
    return (
        r * (dg - m1 - xh * m2),
        jnp.sum(d * xh, axis=0, keepdims=True),
        jnp.sum(d, axis=0, keepdims=True),
    )


GAIN1, GAIN2, BQ, BV, BO, BD, SH1, SH2 = range(8)


def qkv_forward(spot, weight, h, hidden, devices, after):
    rows, width = h.shape
    wide = 3 * width
    half = wide // 2
    refs = weight[0]

    def body(spot_ref, *rest):
        h_ref, qkv_ref, a_ref, t_ref, b_ref = rest[len(refs) : len(refs) + 5]
        w_ref, row_ref, sems = rest[len(refs) + 5 :]
        c = spot_ref[3]
        own, other = [
            side_copies(spot_ref, weight, rest, side, w_ref.at[side], sems, half + LANES)
            for side in range(2)
        ]
        start_all(own, other)
        xh, r = norm_rows(h_ref[...])
        wait_all(own)
        values = w_ref[0, :, half:].astype(WIDE)
        table = values.T[0:8, :]
        t_ref[...] = table
        share = hidden // devices
        for device in range(devices):
            at = device * (width // devices)
            b_ref[0:1, device * share : (device + 1) * share] = values[
                at : at + 1, LANES - share :
            ]
        row_ref[:, :width] = table[BQ : BQ + 1]
        row_ref[:, width : 2 * width] = jnp.zeros((1, width), WIDE)
        row_ref[:, 2 * width :] = table[BV : BV + 1]
        a = (xh * table[GAIN1 : GAIN1 + 1] + table[SH1 : SH1 + 1]).astype(LOW)
        a_ref[...] = a
        for side, owner in enumerate((c, 1 - c)):
            if side == 1:
                wait_all(other)
            to = pl.ds(pl.multiple_of(owner * half, LANES), half)
            qkv_ref[:, to] = (dot(a_ref[...], w_ref[side, :, :half]) + row_ref[:, to]).astype(LOW)

    return launch(
        body,
        [spot, *refs, h],
        after,
        prefetch=0,
        grid=(),
        in_specs=smem_spec() + any_specs(len(refs)) + vmem_specs(1),
        out_specs=vmem_specs(4),
        out_shape=[
            jax.ShapeDtypeStruct((rows, wide), LOW),
            jax.ShapeDtypeStruct((rows, width), LOW),
            jax.ShapeDtypeStruct((8, width), WIDE),
            jax.ShapeDtypeStruct((1, hidden), WIDE),
        ],
        scratch=[
            pltpu.VMEM((2, width, half + LANES), LOW),
            pltpu.VMEM((1, wide), WIDE),
            pltpu.SemaphoreType.DMA((2, 16)),
        ],
        moved=cost(2 * rows * width * wide, 2 * width * wide + 9 * rows * width),
        name="qkv_forward",
    )


def attention_forward(lengths, qkv, after):
    rows, wide = qkv.shape
    width = wide // 3

    def body(len_ref, q_ref, k_ref, v_ref, o_ref, lse_ref):
        pair = pl.program_id(0)
        lane = lax.broadcasted_iota(jnp.int32, (1, LANES), 1)
        key = lax.broadcasted_iota(jnp.int32, (1, rows), 1)
        shut = jnp.where(key < len_ref[0], 0.0, -1e30)
        q = q_ref[...] * jnp.asarray(HEAD_WIDTH**-0.5, LOW)
        k = k_ref[...]
        v = v_ref[...]
        outs = []
        stats = jnp.where(pair == 0, jnp.zeros((rows, LANES), WIDE), lse_ref[...])
        for side in range(2):
            inside = (lane >= HEAD_WIDTH) == (side == 1)
            qs = jnp.where(inside, q, jnp.zeros_like(q))
            s = dot_nt(qs, k) + shut
            peak = jnp.max(s, axis=1, keepdims=True)
            e = jnp.exp(s - peak)
            total = jnp.sum(e, axis=1, keepdims=True)
            p = (e * (1.0 / total)).astype(LOW)
            outs.append(dot(p, v))
            stats = jnp.where(lane == pair * 2 + side, peak + jnp.log(total), stats)
        lse_ref[...] = stats
        o_ref[...] = jnp.where(lane < HEAD_WIDTH, outs[0], outs[1]).astype(LOW)

    return launch(
        body,
        [lengths, qkv, qkv, qkv],
        after,
        out_shape=[
            jax.ShapeDtypeStruct((rows, width), LOW),
            jax.ShapeDtypeStruct((rows, LANES), WIDE),
        ],
        prefetch=1,
        grid=(PAIRS,),
        in_specs=[
            pl.BlockSpec((rows, LANES), lambda p, n: (0, p)),
            pl.BlockSpec((rows, LANES), lambda p, n: (0, p + PAIRS)),
            pl.BlockSpec((rows, LANES), lambda p, n: (0, p + 2 * PAIRS)),
        ],
        out_specs=[
            pl.BlockSpec((rows, LANES), lambda p, n: (0, p)),
            pl.BlockSpec((rows, LANES), lambda p, n: (0, 0)),
        ],
        moved=cost(16 * rows * rows * width, 8 * rows * width, HEADS * rows * rows),
        scratch=[],
        name="attention_forward",
    )


def gelu_parts(u):
    cdf = 0.5 * (1.0 + lax.erf(u * (0.5**0.5)))
    pdf = jnp.exp(-0.5 * u * u) * (0.3989422804014327)
    return cdf, pdf


def up_forward(spot, weight, out_weight, h, mixed, up_bias, table, after):
    rows, width = h.shape
    hidden = up_bias.shape[1]
    half = hidden // 2
    part = width // 2
    tile = TILE
    tiles = half // tile
    refs = weight[0]

    def body(spot_ref, *rest):
        w_refs, rest = rest[: len(refs)], rest[len(refs) :]
        (
            h_ref, m_ref, b_ref, t_ref, h2_ref, a_ref, z_out, s_out,
            w_ref, wo_ref, z_ref, s_ref, sems, sems_o, sems_t,
        ) = rest
        c = spot_ref[3]
        outs = [
            side_copies(spot_ref, out_weight, w_refs, side, wo_ref.at[side], sems_o, part)
            for side in range(2)
        ]
        sides = [
            side_copies(spot_ref, weight, w_refs, side, w_ref.at[side], sems, half)
            for side in range(2)
        ]
        start_all(*outs, *sides)
        wait_all(*outs)
        for side, owner in enumerate((c, 1 - c)):
            to = pl.ds(pl.multiple_of(owner * part, LANES), part)
            h2_ref[:, to] = h_ref[:, to] + (
                dot(m_ref[...], wo_ref[side]) + t_ref[BO : BO + 1, to]
            )
        xh, r = norm_rows(h2_ref[...])
        a_ref[...] = (xh * t_ref[GAIN2 : GAIN2 + 1, :] + t_ref[SH2 : SH2 + 1, :]).astype(LOW)

        def stored(step):
            side, n = step // tiles, lax.rem(step, tiles)
            owner = jnp.where(side == 0, c, 1 - c)
            at = pl.ds(pl.multiple_of(owner * half + n * tile, LANES), tile)
            return side, n, at, [
                pltpu.make_async_copy(ref.at[:, at], out.at[:, at], sems_t.at[which, step])
                for which, (ref, out) in enumerate(((z_ref, z_out), (s_ref, s_out)))
            ]

        def work(step, carry):
            side, n, at, copies = stored(step)

            for which in range(2):

                @pl.when(step == which * tiles)
                def ready():
                    wait_all(sides[which])

            up = pl.ds(pl.multiple_of(n * tile, LANES), tile)
            u = dot(a_ref[...], w_ref[side, :, up]) + b_ref[:, at]
            cdf, pdf = gelu_parts(u)
            z_ref[:, at] = (u * cdf).astype(LOW)
            s_ref[:, at] = (cdf + u * pdf).astype(LOW)
            start_all(copies)
            return carry

        lax.fori_loop(0, 2 * tiles, work, 0)
        for step in range(2 * tiles):
            wait_all(stored(step)[3])

    return launch(
        body,
        [spot, *refs, h, mixed, up_bias, table],
        after,
        prefetch=0,
        grid=(),
        in_specs=smem_spec() + any_specs(len(refs)) + vmem_specs(4),
        out_specs=vmem_specs(2) + any_specs(2),
        out_shape=[
            jax.ShapeDtypeStruct((rows, width), WIDE),
            jax.ShapeDtypeStruct((rows, width), LOW),
            jax.ShapeDtypeStruct((rows, hidden), LOW),
            jax.ShapeDtypeStruct((rows, hidden), LOW),
        ],
        scratch=[
            pltpu.VMEM((2, width, half), LOW),
            pltpu.VMEM((2, width, part), LOW),
            pltpu.VMEM((rows, hidden), LOW),
            pltpu.VMEM((rows, hidden), LOW),
            pltpu.SemaphoreType.DMA((2, 16)),
            pltpu.SemaphoreType.DMA((2, 16)),
            pltpu.SemaphoreType.DMA((2, 2 * tiles)),
        ],
        moved=cost(
            2 * rows * width * hidden, 2 * width * hidden + 4 * rows * hidden, 2 * rows * hidden
        ),
        name="up_forward",
    )


def down_forward(spot, weight, h2, z, table, after):
    rows, width = h2.shape
    hidden = z.shape[1]
    half = hidden // 2
    refs = weight[0]

    def body(spot_ref, *rest):
        h_ref, z_in, t_ref, o_ref, w_ref, z_ref, sems, sems_r = rest[len(refs) :]
        c = spot_ref[3]
        sides = [
            side_copies(spot_ref, weight, rest, side, w_ref.at[side], sems, half)
            for side in range(2)
        ]
        loads = []
        for side, owner in enumerate((c, 1 - c)):
            at = pl.ds(pl.multiple_of(owner * half, LANES), half)
            loads.append(
                [pltpu.make_async_copy(z_in.at[:, at], z_ref.at[side], sems_r.at[side])]
            )
        start_all(sides[0], loads[0], sides[1], loads[1])
        total = h_ref[...] + t_ref[BD : BD + 1, :]
        for side in range(2):
            wait_all(sides[side], loads[side])
            total = total + dot_nt(z_ref[side], w_ref[side])
        o_ref[...] = total

    return launch(
        body,
        [spot, *refs, h2, z, table],
        after,
        prefetch=0,
        grid=(),
        in_specs=smem_spec()
        + any_specs(len(refs))
        + vmem_specs(1)
        + any_specs(1)
        + vmem_specs(1),
        out_specs=vmem_specs(1),
        out_shape=[jax.ShapeDtypeStruct((rows, width), WIDE)],
        scratch=[
            pltpu.VMEM((2, width, half), LOW),
            pltpu.VMEM((2, rows, half), LOW),
            pltpu.SemaphoreType.DMA((2, 16)),
            pltpu.SemaphoreType.DMA((2,)),
        ],
        moved=cost(2 * rows * width * hidden, 2 * width * hidden + 2 * rows * hidden),
        name="down_forward",
    )[0]


def block_starts(spot, owner, rows, order):
    if order == WHOLE:
        return [block * rows for block in range(16)]
    z, x, y = spot[0], spot[1], spot[2]
    result = []
    for block in range(16):
        bz, bx, by = block // 4, (block // 2) % 2, block % 2
        zr = lax.rem(z - bz + 4, 4)
        xr = lax.rem(x + bx, 2)
        yr = lax.rem(y + by, 2)
        first = jnp.where(owner == 0, yr, xr)
        second = jnp.where(owner == 0, xr, yr)
        place = (first * 2 + second) * 4 + zr if order == Z_LAST else (first * 4 + zr) * 2 + second
        result.append(pl.multiple_of(place * rows, 16))
    return result


def put_blocks(value, out_ref, starts, column, width):
    rows = value.shape[0] // 16
    low = value.astype(LOW)
    for block, start in enumerate(starts):
        out_ref[pl.ds(start, rows), pl.ds(column, width)] = low[block * rows : (block + 1) * rows]


def column_sum(value):
    return jnp.sum(value.astype(WIDE), axis=0, keepdims=True)


def down_backward(spot, e, z, order, after):
    rows, width = e.shape
    hidden = z.shape[1]
    half = hidden // 2
    tile = TILE
    tiles = half // tile

    def body(spot_ref, e_ref, z_in, mine_out, rest_out, bd_ref, z_ref, emt_ref, grad_ref, sems, sems_g):
        c = spot_ref[3]
        loads, stores = [], []
        for side, owner in enumerate((c, 1 - c)):
            at = pl.ds(pl.multiple_of(owner * half, LANES), half)
            loads.append(pltpu.make_async_copy(z_in.at[:, at], z_ref.at[side], sems.at[side]))
            stores.append(
                pltpu.make_async_copy(
                    grad_ref.at[side], (mine_out, rest_out)[side], sems_g.at[side]
                )
            )
        start_all(loads)
        em = e_ref[...].astype(LOW)
        bd_ref[...] = column_sum(em)
        emt_ref[...] = em.T
        for side, owner in enumerate((c, 1 - c)):
            wait_all(loads[side : side + 1])
            starts = block_starts(spot_ref, owner, width // 16, order)

            def work(n, carry):
                column = pl.multiple_of(n * tile, LANES)
                product = dot(emt_ref[...], z_ref[side, :, pl.ds(column, tile)])
                put_blocks(product, grad_ref.at[side], starts, column, tile)
                return carry

            lax.fori_loop(0, tiles, work, 0)
            start_all(stores[side : side + 1])
        wait_all(stores)

    return launch(
        body,
        [spot, e, z],
        after,
        prefetch=0,
        grid=(),
        in_specs=smem_spec() + vmem_specs(1) + any_specs(1),
        out_specs=any_specs(2) + vmem_specs(1),
        out_shape=[
            jax.ShapeDtypeStruct((width, half), LOW),
            jax.ShapeDtypeStruct((width, half), LOW),
            jax.ShapeDtypeStruct((1, width), WIDE),
        ],
        scratch=[
            pltpu.VMEM((2, rows, half), LOW),
            pltpu.VMEM((width, rows), LOW),
            pltpu.VMEM((2, width, half), LOW),
            pltpu.SemaphoreType.DMA((2,)),
            pltpu.SemaphoreType.DMA((2,)),
        ],
        moved=cost(2 * rows * width * hidden, 2 * width * hidden + 2 * rows * hidden),
        name="down_backward",
    )


def mlp_backward(
    spot, up, down, out_weight, e, a2, slope, h2, mixed, table, order, after
):
    rows, width = e.shape
    hidden = slope.shape[1]
    half = hidden // 2
    part = width // 2
    tile = TILE
    tiles = half // tile
    refs, down_refs = up[0], down[0]
    near = half + part

    def body(spot_ref, *rest):
        w_refs, rest = rest[: len(refs)], rest[len(refs) :]
        d_refs, rest = rest[: len(down_refs)], rest[len(down_refs) :]
        (
            e_in, a_in, s_in, h_in, m_in, t_ref, mine_out, rest_out,
            bu_ref, e2_ref, da_ref, sums_ref,
            w_ref, wo_ref, e_ref, a_ref, s_ref, h_ref, m_ref,
            em_ref, at_ref, acc_ref, grad_ref, sems, sems_d, sems_o, sems_r, sems_g,
        ) = rest
        c = spot_ref[3]
        loads = [
            pltpu.make_async_copy(source, target, sems_r.at[n])
            for n, (source, target) in enumerate(
                (
                    (e_in, e_ref), (a_in, a_ref), (s_in, s_ref), (h_in, h_ref),
                    (m_in, m_ref),
                )
            )
        ]
        sides = [
            side_copies(spot_ref, down, d_refs, side, w_ref.at[side, 1], sems_d, half)
            + side_copies(spot_ref, up, w_refs, side, w_ref.at[side, 0], sems, half)
            for side in range(2)
        ]
        outs = [
            side_copies(spot_ref, out_weight, w_refs, side, wo_ref.at[side], sems_o, part)
            for side in range(2)
        ]
        start_all(loads[:2], sides[0], loads[2:3], sides[1], loads[3:], *outs)
        wait_all(loads[:1])
        em_ref[...] = e_ref[...].astype(LOW)
        wait_all(loads[1:2])
        at_ref[...] = a_ref[...].T
        acc_ref[...] = jnp.zeros_like(acc_ref)

        def stored(side, which):
            start, size = ((0, half), (half, part))[which]
            at = pl.ds(start, size)
            return pltpu.make_async_copy(
                grad_ref.at[side, :, at],
                (mine_out, rest_out)[side].at[:, at],
                sems_g.at[side, which],
            )

        def work(step, carry):
            side, n = step // tiles, lax.rem(step, tiles)
            owner = jnp.where(side == 0, c, 1 - c)

            @pl.when(step == 0)
            def first_ready():
                wait_all(sides[0], loads[2:3])

            @pl.when(step == tiles)
            def second_ready():
                stored(0, 0).start()
                wait_all(sides[1])

            at = pl.ds(pl.multiple_of(owner * half + n * tile, LANES), tile)
            column = pl.multiple_of(n * tile, LANES)
            tile_at = pl.ds(column, tile)
            starts = block_starts(spot_ref, owner, width // 16, order)
            grads = grad_ref.at[side]
            dz = dot(em_ref[...], w_ref[side, 1, :, tile_at])
            du = (dz * s_ref[:, at].astype(WIDE)).astype(LOW)
            bu_ref[:, at] = column_sum(du)
            put_blocks(dot(at_ref[...], du), grads, starts, column, tile)
            acc_ref[...] += dot_nt(du, w_ref[side, 0, :, tile_at])
            return carry

        lax.fori_loop(0, 2 * tiles, work, 0)
        stored(1, 0).start()
        wait_all(loads[3:])
        at_ref[...] = m_ref[...].T
        dv, gain, shift = norm_back(h_ref[...], t_ref[GAIN2 : GAIN2 + 1, :], acc_ref[...])
        e2 = e_ref[...] + dv
        e2_ref[...] = e2
        em_ref[...] = e2.astype(LOW)
        sums_ref[0:1, :] = gain
        sums_ref[1:2, :] = shift
        sums_ref[2:3, :] = column_sum(em_ref[...])
        wait_all(*outs)
        da = None
        for side, owner in enumerate((c, 1 - c)):
            to = pl.ds(pl.multiple_of(owner * part, LANES), part)
            ey = em_ref[:, to]
            product = dot_nt(ey, wo_ref[side])
            da = product if da is None else da + product
            starts = block_starts(spot_ref, owner, width // 16, order)
            put_blocks(dot(at_ref[...], ey), grad_ref.at[side], starts, half, part)
            stored(side, 1).start()
        da_ref[...] = da.astype(LOW)
        for side in range(2):
            for which in range(2):
                stored(side, which).wait()

    return launch(
        body,
        [spot, *refs, *down_refs, e, a2, slope, h2, mixed, table],
        after,
        prefetch=0,
        grid=(),
        in_specs=smem_spec() + any_specs(len(refs) + len(down_refs) + 5) + vmem_specs(1),
        out_specs=any_specs(2) + vmem_specs(4),
        out_shape=[
            jax.ShapeDtypeStruct((width, near), LOW),
            jax.ShapeDtypeStruct((width, near), LOW),
            jax.ShapeDtypeStruct((1, hidden), WIDE),
            jax.ShapeDtypeStruct((rows, width), WIDE),
            jax.ShapeDtypeStruct((rows, width), LOW),
            jax.ShapeDtypeStruct((8, width), WIDE),
        ],
        scratch=[
            pltpu.VMEM((2, 2, width, half), LOW),
            pltpu.VMEM((2, width, part), LOW),
            pltpu.VMEM((rows, width), WIDE),
            pltpu.VMEM((rows, width), LOW),
            pltpu.VMEM((rows, hidden), LOW),
            pltpu.VMEM((rows, width), WIDE),
            pltpu.VMEM((rows, width), LOW),
            pltpu.VMEM((rows, width), LOW),
            pltpu.VMEM((width, rows), LOW),
            pltpu.VMEM((rows, width), WIDE),
            pltpu.VMEM((2, width, near), LOW),
            pltpu.SemaphoreType.DMA((2, 16)),
            pltpu.SemaphoreType.DMA((2, 16)),
            pltpu.SemaphoreType.DMA((2, 16)),
            pltpu.SemaphoreType.DMA((5,)),
            pltpu.SemaphoreType.DMA((2, 2)),
        ],
        moved=cost(8 * rows * width * hidden, 8 * width * hidden + 4 * rows * hidden),
        name="mlp_backward",
    )


def attention_backward(lengths, qkv, da, mixed, lse, begin, pairs, after):
    rows, wide = qkv.shape
    width = pairs * LANES

    def body(len_ref, q_ref, k_ref, v_ref, d_ref, m_ref, lse_ref, out_ref, row_ref):
        pair = pl.program_id(0)

        @pl.when(pair == 0)
        def start():
            row_ref[...] = lse_ref[...].T

        lane = lax.broadcasted_iota(jnp.int32, (1, LANES), 1)
        sub = lax.broadcasted_iota(jnp.int32, (LANES, 1), 0)
        key = lax.broadcasted_iota(jnp.int32, (rows, 1), 0)
        shut = jnp.where(key < len_ref[0], 0.0, -1e30)
        scale = jnp.asarray(HEAD_WIDTH**-0.5, LOW)
        q = q_ref[...] * scale
        k = k_ref[...]
        v = v_ref[...]
        d = d_ref[...]
        kt = k.T * scale
        prod = (d.astype(WIDE) * m_ref[...].astype(WIDE)).T
        dks, dvs = [], []
        dqt = jnp.zeros((LANES, rows), WIDE)
        for side in range(2):
            inside = (lane >= HEAD_WIDTH) == (side == 1)
            down = (sub >= HEAD_WIDTH) == (side == 1)
            ks = jnp.where(inside, k, jnp.zeros_like(k))
            vs = jnp.where(inside, v, jnp.zeros_like(v))
            kts = jnp.where(down, kt, jnp.zeros_like(kt))
            first = side * HEAD_WIDTH
            delta = jnp.sum(prod[first : first + HEAD_WIDTH], axis=0, keepdims=True)
            log_total = row_ref[pl.ds((begin + pair) * 2 + side, 1), :]
            p = jnp.exp((dot_nt(ks, q) + shut) - log_total)
            dp = dot_nt(vs, d)
            dvs.append(dot(p.astype(LOW), d))
            ds = (p * (dp - delta)).astype(LOW)
            dks.append(dot(ds, q))
            dqt = dqt + dot(kts, ds)
        dq = dqt.T
        dk = jnp.where(lane < HEAD_WIDTH, dks[0], dks[1])
        dv = jnp.where(lane < HEAD_WIDTH, dvs[0], dvs[1])
        for n, value in enumerate((dq, dk, dv)):
            at = pl.ds(pl.multiple_of(n * width + pair * LANES, LANES), LANES)
            out_ref[:, at] = value.astype(LOW)

    return launch(
        body,
        [lengths, qkv, qkv, qkv, da, mixed, lse],
        after,
        out_shape=jax.ShapeDtypeStruct((rows, 3 * width), LOW),
        prefetch=1,
        grid=(pairs,),
        in_specs=[
            pl.BlockSpec((rows, LANES), lambda p, n: (0, p + begin)),
            pl.BlockSpec((rows, LANES), lambda p, n: (0, p + begin + PAIRS)),
            pl.BlockSpec((rows, LANES), lambda p, n: (0, p + begin + 2 * PAIRS)),
            pl.BlockSpec((rows, LANES), lambda p, n: (0, p + begin)),
            pl.BlockSpec((rows, LANES), lambda p, n: (0, p + begin)),
            pl.BlockSpec((rows, LANES), lambda p, n: (0, 0)),
        ],
        out_specs=pl.BlockSpec((rows, 3 * width), lambda p, n: (0, 0)),
        scratch=[pltpu.VMEM((LANES, rows), WIDE)],
        moved=cost(40 * rows * rows * width, 16 * rows * width, HEADS * rows * rows),
        name="attention_backward",
    )


def qkv_backward(spot, weight, dqkv, e2, h, a1, table, others, order, devices, after):
    rows, width = e2.shape
    wide = 3 * width
    half = wide // 2
    refs = weight[0]
    sums, down_sum, up_sum = others
    hidden = up_sum.shape[1]

    def body(spot_ref, *rest):
        w_refs, rest = rest[: len(refs)], rest[len(refs) :]
        d_ins, rest = rest[: len(dqkv)], rest[len(dqkv) :]
        (
            e_in, h_in, a_in, t_ref, s_ref, ds_ref, u_ref, o_ref, mine_out, rest_out,
            w_ref, d_ref, e_ref, h_ref, a_ref, at_ref, acc_ref, row_ref, pack_ref, grad_ref,
            sems, sems_r, sems_d, sems_g,
        ) = rest
        c = spot_ref[3]
        loads = [
            pltpu.make_async_copy(source, target, sems_r.at[n])
            for n, (source, target) in enumerate(
                ((a_in, a_ref), (h_in, h_ref), (e_in, e_ref))
            )
        ]
        part = width // len(dqkv)
        gathers = [
            pltpu.make_async_copy(
                d_in.at[:, pl.ds(third * part, part)],
                d_ref.at[:, pl.ds(third * width + n * part, part)],
                sems_d.at[n, third],
            )
            for n, d_in in enumerate(d_ins)
            for third in range(3)
        ]
        sides = [
            side_copies(spot_ref, weight, w_refs, side, w_ref.at[side], sems, half)
            for side in range(2)
        ]
        start_all(loads[:1], gathers, sides[0], sides[1], loads[1:])
        wait_all(loads[:1])
        at_ref[...] = a_ref[...].T
        wait_all(gathers)

        def stored(side, which):
            at = pl.ds((0, half)[which], (half, LANES)[which])
            out = (mine_out, rest_out)[side]
            return pltpu.make_async_copy(
                grad_ref.at[side, :, at], out.at[:, at], sems_g.at[side, which]
            )

        placed = []
        for side, owner in enumerate((c, 1 - c)):
            starts = block_starts(spot_ref, owner, width // 16, order)
            placed.append(starts)
            to = pl.ds(pl.multiple_of(owner * half, LANES), half)
            d = d_ref[:, to]
            put_blocks(dot(at_ref[...], d), grad_ref.at[side], starts, 0, half)
            stored(side, 0).start()
            wait_all(sides[side])
            product = dot_nt(d, w_ref[side])
            acc_ref[...] = product if side == 0 else acc_ref[...] + product
        wait_all(loads[1:])
        dv, gain, shift = norm_back(h_ref[...], t_ref[GAIN1 : GAIN1 + 1, :], acc_ref[...])
        o_ref[...] = e_ref[...] + dv
        row_ref[...] = jnp.zeros_like(row_ref)
        for row, value in (
            (GAIN1, gain),
            (GAIN2, s_ref[0:1, :]),
            (BQ, column_sum(d_ref[:, :width])),
            (BV, column_sum(d_ref[:, 2 * width :])),
            (BO, s_ref[2:3, :]),
            (BD, ds_ref[...]),
            (SH1, shift),
            (SH2, s_ref[1:2, :]),
        ):
            row_ref[row : row + 1, :] = value
        pack_ref[...] = row_ref[...].T
        share = hidden // devices
        for device in range(devices):
            at = device * (width // devices)
            pack_ref[at : at + 1, LANES - share :] = u_ref[
                0:1, device * share : (device + 1) * share
            ]
        for side in range(2):
            put_blocks(pack_ref[...], grad_ref.at[side], placed[side], half, LANES)
            stored(side, 1).start()
        for side in range(2):
            for which in range(2):
                stored(side, which).wait()

    return launch(
        body,
        [spot, *refs, *dqkv, e2, h, a1, table, sums, down_sum, up_sum],
        after,
        prefetch=0,
        grid=(),
        in_specs=smem_spec() + any_specs(len(refs) + len(dqkv) + 3) + vmem_specs(4),
        out_specs=vmem_specs(1) + any_specs(2),
        out_shape=[
            jax.ShapeDtypeStruct((rows, width), WIDE),
            jax.ShapeDtypeStruct((width, half + LANES), LOW),
            jax.ShapeDtypeStruct((width, half + LANES), LOW),
        ],
        scratch=[
            pltpu.VMEM((2, width, half), LOW),
            pltpu.VMEM((rows, wide), LOW),
            pltpu.VMEM((rows, width), WIDE),
            pltpu.VMEM((rows, width), WIDE),
            pltpu.VMEM((rows, width), LOW),
            pltpu.VMEM((width, rows), LOW),
            pltpu.VMEM((rows, width), WIDE),
            pltpu.VMEM((LANES, width), WIDE),
            pltpu.VMEM((width, LANES), WIDE),
            pltpu.VMEM((2, width, half + LANES), LOW),
            pltpu.SemaphoreType.DMA((2, 16)),
            pltpu.SemaphoreType.DMA((3,)),
            pltpu.SemaphoreType.DMA((len(dqkv), 3)),
            pltpu.SemaphoreType.DMA((2, 2)),
        ],
        moved=cost(4 * rows * width * wide, 4 * width * wide + 16 * rows * width),
        name="qkv_backward",
    )


def join(pieces):
    return jnp.concatenate(pieces, axis=0)


def finish_mlp(spot, parts, shapes):
    def body(spot_ref, *refs):
        outs = refs[-3:]
        c = spot_ref[3]
        for n, (layer, kept, got, columns) in enumerate(parts):
            for owner, ref in ((c, refs[2 * n]), (1 - c, refs[2 * n + 1])):
                column = 0
                for out, start, size in columns:
                    to = owner * (shapes[out][2] // 2) + start
                    outs[out][layer, :, pl.ds(pl.multiple_of(to, LANES), size)] = ref[
                        :, column : column + size
                    ].astype(WIDE)
                    column = column + size

    flat = [value for layer, kept, got, columns in parts for value in (kept, got)]
    return launch(
        body,
        [spot, *flat],
        [],
        prefetch=0,
        grid=(),
        in_specs=smem_spec() + vmem_specs(len(flat)),
        out_specs=vmem_specs(3),
        out_shape=[jax.ShapeDtypeStruct(shape, WIDE) for shape in shapes],
        scratch=[],
        moved=cost(0, 16 * sum(value.size for value in flat)),
        name="finish_mlp",
    )


def finish_qkv(spot, parts, shapes, after):
    share = shapes[3][1]
    half = shapes[0][2] // 2

    def body(spot_ref, *refs):
        qkv_ref, gain_ref, bias_ref, up_ref = refs[-4:]
        c = spot_ref[3]
        for layer in range(len(parts)):
            kept_ref, got_ref = refs[2 * layer], refs[2 * layer + 1]
            for owner, ref in ((c, kept_ref), (1 - c, got_ref)):
                start = pl.multiple_of(owner * half, LANES)
                qkv_ref[layer, :, pl.ds(start, half)] = ref[:, :half].astype(WIDE)
            packed = kept_ref[:, half : half + LANES]
            columns = packed.T
            gain_ref[layer] = columns[0:2, :]
            for n in range(6):
                bias_ref[n, layer : layer + 1, :] = columns[n + 2 : n + 3, :]
            up_ref[layer : layer + 1, :] = packed[0:1, LANES - share :]

    flat = [value for part in parts for value in part]
    return launch(
        body,
        [spot, *flat],
        after,
        prefetch=0,
        grid=(),
        in_specs=smem_spec() + vmem_specs(len(flat)),
        out_specs=vmem_specs(4),
        out_shape=[jax.ShapeDtypeStruct(shape, WIDE) for shape in shapes],
        scratch=[],
        moved=cost(0, 8 * sum(value.size for value in flat)),
        name="finish_qkv",
    )


def linear(z, x, y, c):
    return ((z * 2 + x) * 2 + y) * 2 + c


def pairs_of(step):
    result = []
    for z in range(4):
        for x in range(2):
            for y in range(2):
                for c in range(2):
                    result.append((linear(z, x, y, c), linear(*step(z, x, y, c))))
    return result


TO_Z = [pairs_of(lambda z, x, y, c, n=n: ((z + n) % 4, x, y, c)) for n in range(4)]
TO_XY = pairs_of(lambda z, x, y, c: (z, x, 1 - y, c) if c else (z, 1 - x, y, c))
TO_YX = pairs_of(lambda z, x, y, c: (z, 1 - x, y, c) if c else (z, x, 1 - y, c))


def send(value, pairs):
    return lax.ppermute(value, AXES, pairs)


def swap_cores(value):
    chips = lax.axis_size("dp") * lax.axis_size("y")
    return send(value, [(n, n ^ 1) for n in range(2 * chips)])


def stepped():
    return lax.axis_size("dp") == 8 and lax.axis_size("y") == 2


def place():
    dp = lax.axis_index("dp")
    return jnp.stack([dp // 2, dp % 2, lax.axis_index("y"), lax.axis_index("c")]).astype(jnp.int32)


def halves(pieces):
    low = [piece[:, : piece.shape[1] // 2] for piece in pieces]
    high = [piece[:, piece.shape[1] // 2 :] for piece in pieces]
    return jnp.concatenate(low, axis=1), jnp.concatenate(high, axis=1)


def both_cores(c, pieces):
    low, high = halves(pieces)
    mine = jnp.where(c == 0, low, high)
    got = swap_cores(jnp.where(c == 0, high, low))
    upper = jnp.concatenate([mine, got], axis=0)
    return jnp.where(c == 0, upper, jnp.concatenate([got, mine], axis=0))


class Chain:
    def __init__(self, steps):
        self.steps = steps
        self.result = None
        self.flying = None
        self.resume(None)

    def resume(self, arrived):
        try:
            self.waiting = self.steps.send(arrived)
        except StopIteration as end:
            self.waiting = None
            self.result = end.value

    def start(self):
        if self.waiting is not None:
            assert self.flying is None
            self.flying = [begin(value) for value, begin in self.waiting]


def offsets_of(widths):
    offsets = [0]
    for width in widths:
        offsets.append(offsets[-1] + width // 2)
    return offsets


def by(pairs):
    return lambda value: send(value, pairs)


def gather_steps(block, turns):
    ring = {0: block}
    for turn in turns:
        got = yield [(block, by(TO_Z[n])) for n in turn]
        ring.update(zip(turn, got))
    stack = lax.optimization_barrier(join([ring[n] for n in range(4)]))
    (got,) = yield [(stack, by(TO_XY))]
    near = join([stack, got])
    far, near_got = yield [(near, by(TO_YX)), (near, swap_cores)]
    (far_got,) = yield [(far, swap_cores)]
    return near, far, near_got, far_got


def gather_chips(block):
    return lax.all_gather(block, ("dp", "y"), axis=0, tiled=True)


def gather_at_once(block):
    (own,) = yield [(block, gather_chips)]
    (other,) = yield [(own, swap_cores)]
    return own, other


def added(parts):
    total = parts[0].astype(WIDE)
    for part in parts[1:]:
        total = total + part.astype(WIDE)
    return total


def last_step(c, total):
    rows = total.shape[0] // 2
    low, high = total[:rows], total[rows:]
    kept = jnp.where(c == 0, low, high).astype(WIDE)
    (got,) = yield [(jnp.where(c == 0, high, low).astype(LOW), swap_cores)]
    return kept, got


def scatter_steps(c, mine, rest, order):
    rows = mine.shape[0] // 16
    upper, lower = slice(8 * rows, 16 * rows), slice(0, 8 * rows)
    (got,) = yield [(rest, swap_cores)]
    (more,) = yield [(added([mine[upper], got[upper]]).astype(LOW), by(TO_YX))]
    parts = [mine[lower], got[lower], more]
    for along_z in (order == Z_NEXT, order == Z_LAST):
        size = parts[0].shape[0]
        kept = size // (4 if along_z else 2)
        if along_z:
            total = added(parts)
            sent = [
                (total[n * kept : (n + 1) * kept].astype(LOW), by(TO_Z[4 - n])) for n in (1, 2, 3)
            ]
        else:
            sent = [(added([part[kept:] for part in parts]).astype(LOW), by(TO_XY))]
        arrived = yield sent
        parts = [part[:kept] for part in parts] + arrived
    return (yield from last_step(c, added(parts)))


def scatter_chips(value):
    return lax.psum_scatter(value, ("dp", "y"), scatter_dimension=0, tiled=True)


def scatter_at_once(c, mine, rest):
    (got,) = yield [(rest, swap_cores)]
    (total,) = yield [(added([mine, got]).astype(LOW), scatter_chips)]
    return (yield from last_step(c, total))


def pack_small(gains, shifts, up_bias):
    rows = gains.shape[1]
    columns = jnp.concatenate([gains, shifts], axis=0).T
    share = up_bias.shape[0]
    first = jnp.pad(columns, ((0, 0), (0, LANES - share - columns.shape[1])))
    second = jnp.pad(up_bias[None, :], ((0, rows - 1), (0, 0)))
    packed = jnp.concatenate([first, second], axis=1)
    return jnp.concatenate([packed, packed], axis=1)


def local(
    hidden_in,
    cotangent,
    lengths,
    qkv_weight,
    out_weight,
    up_weight,
    down_weight,
    norm_gains,
    biases,
    up_bias,
):
    clips, slots, width = hidden_in.shape
    layers = qkv_weight.shape[0]
    hidden = down_weight.shape[1]
    assert clips == 1 and layers == 2
    by_steps = stepped()
    devices = lax.axis_size(AXES)
    spot = place()
    c = spot[3]
    chunks, spots = [], []
    for i in range(layers):
        gains, shifts, bias = (v[i].astype(LOW) for v in (norm_gains, biases, up_bias))
        chunks += [
            [qkv_weight[i].astype(LOW), pack_small(gains, shifts, bias)],
            [up_weight[i].astype(LOW), out_weight[i].astype(LOW)],
            [down_weight[i].T.astype(LOW)],
        ]
        spots += [offsets_of([piece.shape[1] for piece in chunk]) for chunk in chunks[-3:]]
    blocks = [both_cores(c, chunks[0])]
    rest = both_cores(c, [piece for chunk in chunks[1:] for piece in chunk])
    start = 0
    for at in spots[1:]:
        blocks.append(rest[:, start : start + at[-1]])
        start = start + at[-1]
    if by_steps:
        turns = [TURNS[n] for n in range(len(blocks))]
        gathers = [Chain(gather_steps(block, turn)) for block, turn in zip(blocks, turns)]
    else:
        gathers = [Chain(gather_at_once(block)) for block in blocks]
    q0, u0, d0, q1, u1, d1 = gathers

    def weight(i, chunk, member):
        n = 3 * i + chunk
        return gathers[n].result, spots[n][member], True

    rec = [{"h": hidden_in[0]}, {}]
    awaited = []

    def first_matmul(i):
        qkv, first, table, bias = qkv_forward(
            spot, weight(i, 0, 0), rec[i]["h"], hidden, devices, awaited
        )
        return {"qkv": qkv, "a1": first, "table": table, "bias": bias}

    def attend(i):
        mixed, lse = attention_forward(lengths, rec[i]["qkv"], awaited)
        return {"mixed": mixed, "lse": lse}

    def feed_up(i):
        r = rec[i]
        h2, second, z, slope = up_forward(
            spot,
            weight(i, 1, 0),
            weight(i, 1, 1),
            r["h"],
            r["mixed"],
            r["bias"],
            r["table"],
            awaited,
        )
        return {"h2": h2, "a2": second, "z": z, "slope": slope}

    def feed_down(i):
        r = rec[i]
        total = down_forward(spot, weight(i, 2, 0), r["h2"], r["z"], r["table"], awaited)
        return {"total": total}

    def down_back(i):
        r = rec[i]
        order = ORDERS[i] if by_steps else WHOLE
        mine, rest, down_sum = down_backward(spot, r["e"], r["z"], order, awaited)
        return {"second": (mine, rest), "down_sum": down_sum}

    def feed_back(i):
        r = rec[i]
        mine, rest, up_sum, e2, da, sums = mlp_backward(
            spot,
            weight(i, 1, 0),
            weight(i, 2, 0),
            weight(i, 1, 1),
            r["e"],
            r["a2"],
            r["slope"],
            r["h2"],
            r["mixed"],
            r["table"],
            ORDERS[i] if by_steps else WHOLE,
            awaited,
        )
        others = (sums, r["down_sum"], up_sum)
        return {"first": (mine, rest), "e2": e2, "da": da, "others": others}

    def attend_back(i, begin):
        r = rec[i]
        dqkv = attention_backward(
            lengths, r["qkv"], r["da"], r["mixed"], r["lse"], begin, PAIRS // 2, awaited
        )
        return {f"dqkv{begin}": dqkv}

    def qkv_back(i):
        r = rec[i]
        e, mine, rest = qkv_backward(
            spot,
            weight(i, 0, 0),
            (r["dqkv0"], r[f"dqkv{PAIRS // 2}"]),
            r["e2"],
            r["h"],
            r["a1"],
            r["table"],
            r["others"],
            ORDERS[i] if by_steps else WHOLE,
            devices,
            awaited,
        )
        return {"e_in": e, "qkv_grad": (mine, rest)}

    def run(begin, end, *work):
        nonlocal awaited
        for chain in begin:
            chain.start()
        outs = []
        for function, i, *rest in work:
            outs.append(function(i, *rest))
            rec[i].update(outs[-1])
            awaited = []
        landing = [chain for chain in end if chain.flying is not None]
        flying = [chain.flying for chain in landing]
        arrived, outs = lax.optimization_barrier((flying, outs))
        for (function, i, *rest), new in zip(work, outs):
            rec[i].update(new)
        for chain, values in zip(landing, arrived):
            chain.flying = None
            chain.resume(values)
        awaited = awaited + [value for values in arrived for value in values]

    def drain(*chains):
        while any(chain.waiting is not None for chain in chains):
            for chain in chains:
                if chain.flying is not None:
                    values, chain.flying = chain.flying, None
                    chain.resume(values)
            for chain in chains:
                chain.start()

    def scatter(i, member):
        if by_steps:
            return Chain(scatter_steps(c, *rec[i][member], ORDERS[i]))
        return Chain(scatter_at_once(c, *rec[i][member]))

    run([q0], [q0])
    run([q0], [q0])
    run([q0, u0], [q0, u0])
    run([q0, u0], [q0])
    run([q1], [u0, q1], (first_matmul, 0))
    run([u0, d0], [u0, d0], (attend, 0))
    run([u0, d0, q1], [u0, d0, q1])
    run([d0, u1], [d0, u1], (feed_up, 0))
    run([d0], [d0])
    run([q1, d1], [q1, d1], (feed_down, 0))
    rec[1]["h"] = rec[0]["total"]
    run([q1, u1], [q1])
    run([], [u1], (first_matmul, 1))
    run([u1], [u1], (attend, 1))
    run([u1, d1], [u1, d1])
    run([d1], [d1], (feed_up, 1))
    left, right = 0, PAIRS // 2
    rec[1]["e"] = cotangent[0]
    run([d1], [d1], (down_back, 1))
    d1 = scatter(1, "second")
    run([d1], [d1], (feed_back, 1))
    u1 = scatter(1, "first")
    run([d1, u1], [d1, u1], (attend_back, 1, left), (attend_back, 1, right))
    run([u1], [u1], (qkv_back, 1))
    rec[0]["e"] = rec[1]["e_in"]
    q1 = scatter(1, "qkv_grad")
    run([q1], [q1], (down_back, 0))
    d0 = scatter(0, "second")
    run([q1, d1, d0], [q1, d1, d0], (feed_back, 0))
    u0 = scatter(0, "first")
    run([u0, d0, u1, d1], [u0, d0, u1, d1], (attend_back, 0, left), (attend_back, 0, right))
    run([u0, u1, q1], [u0, u1, q1], (qkv_back, 0))
    q0 = scatter(0, "qkv_grad")
    run([q0, d0, q1], [q0, d0, q1])
    run([q0, u0, d0], [q0, u0, d0])
    run([q0, u0], [q0])
    run([q0], [u0, q0], (feed_down, 1))
    output = rec[1]["total"][None]
    drain(q0, u0, d0, q1, u1, d1)
    input_grad = rec[0]["e_in"][None]
    down_shape = (layers, down_weight.shape[2], hidden)
    mlp_shapes = [down_shape, up_weight.shape, out_weight.shape]
    bias_shape = (biases.shape[1], layers, biases.shape[2])
    qkv_shapes = [qkv_weight.shape, norm_gains.shape, bias_shape, up_bias.shape]
    half = hidden // 2
    first, second = [(1, 0, half), (2, 0, width // 2)], [(0, 0, half)]
    parts = [
        (0, *u0.result, first),
        (0, *d0.result, second),
        (1, *u1.result, first),
        (1, *d1.result, second),
    ]
    down_grad, up_grad, out_grad = finish_mlp(spot, parts, mlp_shapes)
    qkv_grad, gains, shifts, up_sums = finish_qkv(spot, [q0.result, q1.result], qkv_shapes, [])
    shifts = jnp.swapaxes(shifts, 0, 1)
    down_grad = jnp.swapaxes(down_grad, 1, 2)
    return output, input_grad, qkv_grad, out_grad, up_grad, down_grad, gains, shifts, up_sums


def solution(mesh):
    size = dict(mesh.shape)
    fine = Mesh(mesh.devices.reshape(size["dp"], size["fsdp"] // 2, 2), AXES)
    return jax.shard_map(
        local,
        mesh=fine,
        in_specs=(
            P(AXES, None, None),
            P(AXES, None, None),
            P(AXES),
            P(None, AXES, None),
            P(None, AXES, None),
            P(None, AXES, None),
            P(None, None, AXES),
            P(None, None, AXES),
            P(None, None, AXES),
            P(None, AXES),
        ),
        out_specs=(
            P(AXES, None, None),
            P(AXES, None, None),
            P(None, AXES, None),
            P(None, AXES, None),
            P(None, AXES, None),
            P(None, None, AXES),
            P(None, None, AXES),
            P(None, None, AXES),
            P(None, AXES),
        ),
        check_vma=False,
    )
```
